32 devices in a mesh: dp: 8 (over y, x, core), fsdp: 4 (over z).
Axes of the slice: x: 2, y: 2, z: 4, core: 2. Of those that a mesh axis runs over, the one named last changes fastest.
Arguments:
- patches: bfloat16 [2, 32, 256, 768], P(None, ('dp', 'fsdp')), may hold values from -6 to 6
- grid: int32 [2, 32, 4, 256], P(None, ('dp', 'fsdp')), may hold values from 0 to 63, as said below
- segments: int32 [2, 32, 256], P(None, ('dp', 'fsdp')), may hold values from 0 to 7, as said below
- text_ids: int32 [2, 32, 8, 16], P(None, ('dp', 'fsdp')), may hold values from 0 to 31999
- table: bfloat16 [32000, 768], P('fsdp'), may hold values from -6 to 6
- weights: float32 [26, 768, 768], P(None, 'fsdp')
- momenta: float32 [26, 768, 768], P(None, 'fsdp'), may hold values from -1.9073486e-05 to 1.9073486e-05
- gains: float32 [79, 768], replicated
- gains_m: float32 [79, 768], replicated, may hold values from -1.9073486e-05 to 1.9073486e-05
- gains_v: float32 [79, 768], replicated, may hold values from 1.7e-13 to 7e-13
- step: int32 [1], replicated, may hold values from 2 to 20
Outputs:
- loss: float32 [], replicated
- grad_norm: float32 [], replicated
- weights_new: float32 [26, 768, 768], P(None, 'fsdp')
- weights_low: bfloat16 [26, 768, 768], P(None, 'fsdp')
- momenta_new: float32 [26, 768, 768], P(None, 'fsdp')
- gains_new: float32 [79, 768], replicated
- gains_m_new: float32 [79, 768], replicated
- gains_v_new: float32 [79, 768], replicated
- final_shift_grad: float32 [768], replicated
The draws below stay inside these ranges and needn't reach their ends.
Inputs may be any that keep to these rules, and one draw needn't show every extreme that they name: Rows 0 and 1 of grid are below rows 2 and 3 at the same patch; heights and widths are given per patch, 1 to 63. `segments`: slot numbers never fall along a sequence and start at 0; some slots may be empty.
All inputs are finite; a program needn't handle non-finite values.
Results may differ from the reference program's by a relative error of at most 0.015.
Values may be sent and summed in bfloat16 or wider, within the bound.
A program may use at most 384 MiB of HBM per device.

```python
import math
import jax
import jax.numpy as jnp
import numpy as np
from jax import lax

D = 768
HEADS = 12
FF = 3072
VOCAB = 32000
LAYERS = 2
SEQ = 256
IMGS = 8
TXT = 16
POS = 32
MB = 2
NS_ITERS = 5
HD = 64
SEQS = 32
MATS = 26
GROWS = 79


def draw_grid(key, part):
    first, second, third, fourth = jax.random.split(key, 4)
    shape = (MB, SEQS, 1, SEQ)
    height = jax.random.randint(first, shape, 1, 2 * POS)
    width = jax.random.randint(second, shape, 1, 2 * POS)
    row = jax.random.randint(third, shape, 0, 4096) % height
    col = jax.random.randint(fourth, shape, 0, 4096) % width
    return jnp.concatenate([row, col, height, width], 2).astype(jnp.int32)


def draw_segments(key, part):
    first, second = jax.random.split(key)
    order = jnp.arange(SEQS, dtype=jnp.int32)
    rising = 1 + ((IMGS - 1) * order + (SEQS - 1) // 2) // (SEQS - 1)
    jitter = jax.random.randint(first, (MB, SEQS), -1, 2)
    counts = jnp.clip(rising[None, :] + jitter, 1, IMGS)
    counts = counts.at[:, SEQS - 1].set(IMGS)[:, :, None]
    cuts = jnp.sort(jax.random.randint(second, (MB, SEQS, IMGS - 1), 1, SEQ), -1)
    places = jnp.arange(SEQ, dtype=jnp.int32)
    index = jnp.sum((places[None, None, :, None] >= cuts[:, :, None, :]).astype(jnp.int32), -1)
    return jnp.minimum(index, counts - 1).astype(jnp.int32)


def draw_weights(key, part):
    base = jax.random.normal(key, (MATS, D, D), jnp.float32)
    kind = jnp.arange(MATS)
    offset = (kind - 2) % 12
    layered = kind >= 2
    factor = jnp.where(layered & (offset == 3), 6.0, jnp.where(layered & (offset >= 8), 0.5, 1.0))
    place = jnp.arange(D, dtype=jnp.float32) / (D - 1.0)
    rise = jnp.exp(math.log(3.0) * (place - 0.5))
    return base * factor[:, None, None].astype(jnp.float32) * rise[None, :, None] * (1.0 / math.sqrt(D))


def draw_gains(key, part):
    base = jax.random.normal(key, (GROWS, D), jnp.float32)
    row = jnp.arange(GROWS)[:, None]
    fin = 6 * LAYERS
    inside = row < fin
    slot = row % 6
    gainlike = inside & ((slot == 0) | (slot == 2) | (slot >= 4)) | (row == fin)
    shiftlike = inside & ((slot == 1) | (slot == 3)) | (row == fin + 1)
    query = row == fin + 2
    return jnp.where(gainlike, 1.0 + 0.1 * base, jnp.where(shiftlike, 0.2 * base, jnp.where(query, 1.5 * base, 0.5 * base)))


def touch_ends(entries, stream_key, low, largest):
    spot = [jax.random.randint(jax.random.fold_in(stream_key, axis), (), 0, length) for axis, length in enumerate(entries.shape)]
    main_axis = entries.shape.index(max(entries.shape))
    next_to = spot[:main_axis] + [(spot[main_axis] + 1) % entries.shape[main_axis]] + spot[main_axis + 1:]
    return entries.at[tuple(spot)].set(low).at[tuple(next_to)].set(largest)


def block_scale(own_key, extent, shards, least, high):
    loudness = 1.0
    for position, blocks in shards:
        steps = jax.random.uniform(jax.random.fold_in(jax.random.fold_in(own_key, 6), position), (blocks,), jnp.float32, least / len(shards), high / len(shards))
        loudness = loudness * jnp.repeat(jnp.exp(steps), extent[position] // blocks).reshape((-1,) + (1,) * (len(extent) - 1 - position))
    return loudness


def cumulative_ranks(number_of, slope):
    weights = [(1 << 20) // math.isqrt(grade ** slope) + 1 for grade in range(1, number_of + 1)]
    deviation = 1 + sum(weights) // (1 << 30)
    return np.cumsum(np.array([max(1, weight // deviation) for weight in weights]))


def skewed_ids(key, extent, amount, slope):
    listing = cumulative_ranks(amount, slope)
    pick = jax.random.randint(jax.random.fold_in(key, 1), extent, 0, int(listing[amount - 1]))
    standing = jnp.searchsorted(jnp.asarray(listing, jnp.int32), pick, side="right")
    return jax.random.permutation(jax.random.fold_in(key, 2), amount)[standing].astype(jnp.int32)


def scatter_about(key, extent, scale, limit, cuts=(), kind=jnp.bfloat16):
    factor_of = block_scale(key, extent, cuts, -0.22, 0.18) if cuts else 1.0
    entries = jax.random.normal(key, extent, jnp.float32) * scale * factor_of
    return jnp.minimum(jnp.maximum(entries, -limit), limit).astype(kind)


def setup_inputs(seed: int = 0) -> dict:
    arg_keys = jax.random.split(jax.random.key(seed), 12)
    patches = scatter_about(arg_keys[0], (MB, SEQS, SEQ, D), 1.0, 6.0, ((1, 32),))
    grid = draw_grid(jax.random.fold_in(arg_keys[11], 71), 0)
    segments = draw_segments(jax.random.fold_in(arg_keys[11], 71), 0)
    text_ids = touch_ends(skewed_ids(arg_keys[3], (MB, SEQS, IMGS, TXT), VOCAB, 2), jax.random.fold_in(arg_keys[3], 3), 0, VOCAB - 1).astype(jnp.int32)
    table = scatter_about(arg_keys[4], (VOCAB, D), 1.0, 6.0, ((0, 4),))
    weights = draw_weights(jax.random.fold_in(arg_keys[11], 71), 0)
    momenta = scatter_about(arg_keys[6], (MATS, D, D), (1.3e-6), 1.9073486328125e-05, ((1, 4),), jnp.float32)
    gains = draw_gains(jax.random.fold_in(arg_keys[11], 71), 0)
    gains_m = scatter_about(arg_keys[8], (GROWS, D), (1.4e-6), 1.9073486328125e-05, (), jnp.float32)
    gains_v = jnp.clip(jnp.exp(jax.random.uniform(arg_keys[9], (GROWS, D), jnp.float32, math.log(1.700000004049157e-13), math.log(7.000000080449598e-13))), 1.700000004049157e-13, 7.000000080449598e-13)
    step = jax.random.randint(arg_keys[10], (1,), 2, 21).astype(jnp.int32)
    return {"patches": patches, "grid": grid, "segments": segments, "text_ids": text_ids, "table": table, "weights": weights, "momenta": momenta, "gains": gains, "gains_m": gains_m, "gains_v": gains_v, "step": step}


HIGH = lax.Precision.HIGHEST
LOGIT_SCALE = 50.0
CLIP_LIMIT = 0.005
MOMENT = 0.95
MUON_RATE = 0.5
MUON_DECAY = 0.01
ADAM_RATE = 0.4
BETA_ONE = 0.9
BETA_TWO = 0.999
ADAM_EPS = 1e-08
ADAM_DECAY = 0.01
COEF_A = 3.4445
COEF_B = -4.775
COEF_C = 2.0315

@jax.custom_vjp
def low(v):
    return lax.optimization_barrier(v.astype(jnp.bfloat16)).astype(jnp.float32)

@jax.custom_vjp
def low_back(v):
    return v

def low_keep(v):
    return (low(v), None)

def low_pass(kept, grad):
    return (grad,)

def back_keep(v):
    return (v, None)

def back_low(kept, grad):
    return (low(grad),)
low.defvjp(low_keep, low_pass)
low_back.defvjp(back_keep, back_low)

def layer_norm(value, gain, shift):
    centred = value - lax.optimization_barrier(jnp.mean(value, -1, keepdims=True))
    spread = lax.optimization_barrier(jnp.mean(centred * centred, -1, keepdims=True))
    return centred * lax.rsqrt(spread + 1e-06) * gain + shift

def head_norm(value, gain):
    heads = value.reshape(value.shape[0], HEADS, HD)
    centred = heads - lax.optimization_barrier(jnp.mean(heads, -1, keepdims=True))
    spread = lax.optimization_barrier(jnp.mean(centred * centred, -1, keepdims=True))
    return centred * lax.rsqrt(spread + 1e-06) * gain.reshape(HEADS, HD)

def unit_rows(value):
    return value * lax.rsqrt(lax.optimization_barrier(jnp.mean(value * value, -1, keepdims=True)) + 1e-06) * (1.0 / math.sqrt(D))

def dense_rows(inputs, matrix):
    return low_back(jnp.dot(low(inputs), low(matrix).T, precision=HIGH))

def dense_cols(inputs, matrix):
    return low_back(jnp.dot(low(inputs), low(matrix), precision=HIGH))

def positions(grid):
    slots = jnp.arange(POS, dtype=jnp.int32)
    row_index = grid[0] * POS // grid[2]
    col_index = grid[1] * POS // grid[3]
    return ((row_index[:, None] == slots[None]).astype(jnp.float32), (col_index[:, None] == slots[None]).astype(jnp.float32))

def layer(state, blocks, gains, segment):
    heads_in = layer_norm(state, gains[0], gains[1])
    mixed = dense_rows(heads_in, blocks[0:3].reshape(3 * D, D))
    query = head_norm(mixed[:, :D], gains[4])
    key = head_norm(mixed[:, D:2 * D], gains[5])
    value = mixed[:, 2 * D:].reshape(SEQ, HEADS, HD)
    scores = low_back(jnp.einsum('shd,thd->hst', low(query), low(key), precision=HIGH)) * (1.0 / math.sqrt(HD))
    same = segment[:, None] == segment[None, :]
    scores = jnp.where(same[None], scores, -1e+30)
    weights = jax.nn.softmax(scores, -1)
    attended = low_back(jnp.einsum('hst,thd->shd', low(weights), low(value), precision=HIGH)).reshape(SEQ, D)
    state = state + dense_cols(attended, blocks[3])
    normed = layer_norm(state, gains[2], gains[3])
    hidden = jax.nn.gelu(dense_rows(normed, blocks[4:8].reshape(FF, D)))
    return state + dense_cols(hidden, blocks[8:12].reshape(FF, D))

def sequence(weights, gains, patches, grid, segment):
    fin = 6 * LAYERS
    base = fin + 3
    rows_hot, cols_hot = positions(grid)
    state = dense_rows(patches, weights[0])
    state = state + jnp.dot(rows_hot, gains[base:base + POS], precision=HIGH)
    state = state + jnp.dot(cols_hot, gains[base + POS:base + 2 * POS], precision=HIGH)
    for index in range(LAYERS):
        state = layer(state, weights[2 + 12 * index:14 + 12 * index], gains[6 * index:6 * index + 6], segment)
    final = layer_norm(state, gains[fin], gains[fin + 1])
    split = final.reshape(SEQ, HEADS, HD)
    logits = jnp.einsum('shd,hd->hs', split, gains[fin + 2].reshape(HEADS, HD), precision=HIGH) * (1.0 / math.sqrt(HD))
    member = segment[None, :] == jnp.arange(IMGS, dtype=jnp.int32)[:, None]
    logits = jnp.where(member[:, None, :], logits[None], -1e+30)
    share = jax.nn.softmax(logits, -1)
    pooled = jnp.einsum('khs,shd->khd', share, split, precision=HIGH).reshape(IMGS, D)
    return unit_rows(dense_cols(pooled, weights[1]))

def contrast(images, texts, live):
    image_low = low(images)
    forward = LOGIT_SCALE * low_back(jnp.dot(image_low, texts.T, precision=HIGH))
    backward = LOGIT_SCALE * low_back(jnp.dot(texts, image_low.T, precision=HIGH))
    total = jnp.float32(0.0)
    for scores in (forward, backward):
        masked = jnp.where(live[None, :] > 0, scores, -1e+30)
        top = jax.scipy.special.logsumexp(masked, axis=1)
        total = total + jnp.sum((top - jnp.diagonal(scores)) * live)
    return total

def objective(weights, gains, patches, grid, segments, texts, live, count):
    total = jnp.float32(0.0)
    for part in range(MB):

        def one(items):
            return sequence(weights, gains, items[0], items[1], items[2])
        images = lax.map(jax.checkpoint(one), (patches[part], grid[part], segments[part]))
        total = total + contrast(images.reshape(SEQS * IMGS, D), texts[part], live[part])
    return total / (2.0 * count)

def muon_groups():
    found = [(0, 1), (1, 1)]
    for index in range(LAYERS):
        base = 2 + 12 * index
        found = found + [(base, 3), (base + 3, 1), (base + 4, 4), (base + 8, 4)]
    return found

def orthogonal(momentum):
    flat = momentum.reshape(-1, D)
    start_low = low(flat)
    gram = jnp.dot(start_low.T, start_low, precision=HIGH)
    size = jnp.sqrt(jnp.trace(gram)) + 1e-07
    current = flat / size
    gram = gram / (size * size)
    for turn in range(NS_ITERS):
        if turn > 0:
            current_low = low(current)
            gram = jnp.dot(current_low.T, current_low, precision=HIGH)
        gram_low = low(gram)
        first = jnp.dot(low(current), gram_low, precision=HIGH)
        second = jnp.dot(low(first), gram_low, precision=HIGH)
        current = COEF_A * current + COEF_B * first + COEF_C * second
    return current.reshape(momentum.shape)

def reference(patches, grid, segments, text_ids, table, weights, momenta, gains, gains_m, gains_v, step):
    slots = jnp.arange(IMGS, dtype=jnp.int32)
    live = jnp.any(segments[:, :, None, :] == slots[None, None, :, None], -1).astype(jnp.float32)
    live = live.reshape(MB, SEQS * IMGS)
    count = jnp.sum(live)
    rows = jnp.take(table.astype(jnp.float32), text_ids, axis=0)
    texts = low(unit_rows(lax.optimization_barrier(jnp.mean(rows, axis=-2)))).reshape(MB, SEQS * IMGS, D)
    inputs = patches.astype(jnp.float32)

    def loss_of(weight_arg, gain_arg):
        return objective(weight_arg, gain_arg, inputs, grid, segments, texts, live, count)
    loss, pullback = jax.vjp(loss_of, weights, gains)
    grad_w, grad_g = pullback(jnp.ones_like(loss))
    norm = jnp.sqrt(jnp.sum(grad_w * grad_w) + jnp.sum(grad_g * grad_g))
    clip = jnp.minimum(1.0, CLIP_LIMIT / (norm + 1e-06))
    momenta_new = MOMENT * momenta + clip * grad_w
    updated = []
    for start, number in muon_groups():
        direction = orthogonal(momenta_new[start:start + number])
        old = weights[start:start + number]
        updated.append(old * (1.0 - MUON_RATE * MUON_DECAY) - MUON_RATE * math.sqrt(number) * direction)
    weights_new = jnp.concatenate(updated, 0)
    grad_small = clip * grad_g
    moment_one = BETA_ONE * gains_m + (1.0 - BETA_ONE) * grad_small
    moment_two = BETA_TWO * gains_v + (1.0 - BETA_TWO) * grad_small * grad_small
    count_steps = step[0].astype(jnp.float32)
    corrected_one = moment_one / (1.0 - jnp.power(BETA_ONE, count_steps))
    corrected_two = moment_two / (1.0 - jnp.power(BETA_TWO, count_steps))
    gains_new = gains - ADAM_RATE * (corrected_one / (jnp.sqrt(corrected_two) + ADAM_EPS) + ADAM_DECAY * gains)
    shift_grad = grad_small[6 * LAYERS + 1]
    return (loss, norm, weights_new, weights_new.astype(jnp.bfloat16), momenta_new, gains_new, moment_one, moment_two, shift_grad)
```

```python
import functools
import math

import jax
import jax.numpy as jnp
import numpy as np
from jax import lax
from jax.sharding import PartitionSpec as P

D = 768
HEADS = 12
FF = 3072
LAYERS = 2
IMGS = 8
POS = 32
MB = 2
NS_ITERS = 5
HD = 64


HIGH = lax.Precision.HIGHEST
LOGIT_SCALE = 50.0
CLIP_LIMIT = 0.005
MOMENT = 0.95
MUON_RATE = 0.5
MUON_DECAY = 0.01
ADAM_RATE = 0.4
BETA_ONE = 0.9
BETA_TWO = 0.999
ADAM_EPS = 1e-08
ADAM_DECAY = 0.01
COEF_A = 3.4445
COEF_B = -4.775
COEF_C = 2.0315


def rounded(value):
    return value.astype(jnp.bfloat16)


def product(left, right, form):
    return jnp.einsum(form, left, right, preferred_element_type=jnp.float32)


def layer_norm(value, gain, shift):
    centred = value - jnp.mean(value, -1, keepdims=True)
    spread = jnp.mean(centred * centred, -1, keepdims=True)
    return centred * lax.rsqrt(spread + 1e-06) * gain + shift


def head_norm(value, gain):
    heads = value.reshape(value.shape[0], HEADS, HD)
    centred = heads - jnp.mean(heads, -1, keepdims=True)
    spread = jnp.mean(centred * centred, -1, keepdims=True)
    return centred * lax.rsqrt(spread + 1e-06) * gain.reshape(HEADS, HD)


def both_norms(query, key, gain_query, gain_key):
    return (head_norm(query, gain_query), head_norm(key, gain_key))


def unit_rows(value):
    return (
        value
        * lax.rsqrt(jnp.mean(value * value, -1, keepdims=True) + 1e-06)
        * (1.0 / math.sqrt(value.shape[-1]))
    )


def positions(grid):
    slots = jnp.arange(POS, dtype=jnp.int32)
    row_index = grid[0] * POS // grid[2]
    col_index = grid[1] * POS // grid[3]
    return (
        (row_index[:, None] == slots[None]).astype(jnp.float32),
        (col_index[:, None] == slots[None]).astype(jnp.float32),
    )


def pooling(segment):
    member = segment[None, :] == jnp.arange(IMGS, dtype=jnp.int32)[:, None]

    def pooled_of(final, query):
        split = final.reshape(-1, HEADS, HD)
        logits = jnp.einsum("shd,hd->hs", split, query.reshape(HEADS, HD), precision=HIGH) * (
            1.0 / math.sqrt(HD)
        )
        logits = jnp.where(member[:, None, :], logits[None], -1e30)
        share = jax.nn.softmax(logits, -1)
        return jnp.einsum("khs,shd->khd", share, split, precision=HIGH).reshape(IMGS, -1)

    return pooled_of


def fetch(blocks):
    return lax.all_gather(rounded(blocks), "fsdp", axis=1, tiled=True)


def masked_scores(query_low, key_low, same):
    scores = product(query_low, key_low, "bshd,bthd->bhst") * (1.0 / math.sqrt(HD))
    return jnp.where(same[:, None], scores, -1e30)


def layer_forward(state, blocks, gains, same):
    heads_in, norm_one = jax.vjp(layer_norm, state, gains[0], gains[1])
    heads_low = rounded(heads_in)
    mixed = product(heads_low, blocks[0:3].reshape(3 * D, D), "sd,rd->sr")
    (query, key), norms_back = jax.vjp(
        both_norms, mixed[:, :D], mixed[:, D : 2 * D], gains[4], gains[5]
    )
    query_low = rounded(query).reshape(MB, -1, HEADS, HD)
    key_low = rounded(key).reshape(MB, -1, HEADS, HD)
    value_low = rounded(mixed[:, 2 * D :]).reshape(MB, -1, HEADS, HD)
    scores = masked_scores(query_low, key_low, same)
    top = jax.scipy.special.logsumexp(scores, axis=-1, keepdims=True)
    weights_low = rounded(jnp.exp(scores - top))
    attended_low = rounded(product(weights_low, value_low, "bhst,bthd->bshd").reshape(-1, D))
    state = state + product(attended_low, blocks[3], "sr,rd->sd")
    normed, norm_two = jax.vjp(layer_norm, state, gains[2], gains[3])
    normed_low = rounded(normed)
    hidden, gelu_back = jax.vjp(
        jax.nn.gelu, product(normed_low, blocks[4:8].reshape(FF, D), "sd,rd->sr")
    )
    hidden_low = rounded(hidden)
    state = state + product(hidden_low, blocks[8:12].reshape(FF, D), "sr,rd->sd")
    kept = (
        norm_one,
        heads_low,
        norms_back,
        query_low,
        key_low,
        value_low,
        top,
        attended_low,
        norm_two,
        normed_low,
        gelu_back,
        hidden_low,
    )
    return (state, kept)


def layer_backward(grad, kept, blocks, same):
    (
        norm_one,
        heads_low,
        norms_back,
        query_low,
        key_low,
        value_low,
        top,
        attended_low,
        norm_two,
        normed_low,
        gelu_back,
        hidden_low,
    ) = kept
    down = blocks[8:12].reshape(FF, D)
    upward = blocks[4:8].reshape(FF, D)
    grad_low = rounded(grad)
    grad_down = rounded(product(hidden_low, grad_low, "sr,sd->rd"))
    (grad_hidden,) = gelu_back(product(grad_low, down, "sd,rd->sr"))
    hidden_grad = rounded(grad_hidden)
    grad_up = rounded(product(hidden_grad, normed_low, "sr,sd->rd"))
    inner, gain_two, shift_two = norm_two(product(hidden_grad, upward, "sr,rd->sd"))
    grad = grad + inner
    grad_low = rounded(grad)
    grad_out = rounded(product(attended_low, grad_low, "sr,sd->rd"))
    attended_grad = rounded(product(grad_low, blocks[3], "sd,rd->sr")).reshape(MB, -1, HEADS, HD)
    weights = jnp.exp(masked_scores(query_low, key_low, same) - top)
    weights_low = rounded(weights)
    value_grad = product(weights_low, attended_grad, "bhst,bshd->bthd")
    weight_grad = product(attended_grad, value_low, "bshd,bthd->bhst")
    score_grad = weights * (weight_grad - jnp.sum(weights * weight_grad, -1, keepdims=True))
    score_low = rounded(score_grad * (1.0 / math.sqrt(HD)))
    query_grad = product(score_low, key_low, "bhst,bthd->bshd").reshape(-1, HEADS, HD)
    key_grad = product(score_low, query_low, "bhst,bshd->bthd").reshape(-1, HEADS, HD)
    query_in, key_in, gain_query, gain_key = norms_back((query_grad, key_grad))
    mixed_low = rounded(jnp.concatenate([query_in, key_in, value_grad.reshape(-1, D)], 1))
    grad_mixed = rounded(product(mixed_low, heads_low, "sr,sd->rd"))
    inner, gain_one, shift_one = norm_one(
        product(mixed_low, blocks[0:3].reshape(3 * D, D), "sr,rd->sd")
    )
    grad = grad + inner
    block_grads = jnp.concatenate(
        [
            grad_mixed.reshape(3, D, D),
            grad_out[None],
            grad_up.reshape(4, D, D),
            grad_down.reshape(4, D, D),
        ],
        0,
    )
    gain_grads = jnp.stack([gain_one, shift_one, gain_two, shift_two, gain_query, gain_key])
    return (grad, block_grads, gain_grads)


def contrast_rows(scores, alive, own_live, offset):
    masked = jnp.where(alive[None, :] > 0, scores, -1e30)
    top = jax.scipy.special.logsumexp(masked, axis=1, keepdims=True)
    share = jnp.exp(masked - top)
    columns = jnp.arange(scores.shape[1], dtype=jnp.int32)
    target = (
        columns[None, :] == offset + jnp.arange(scores.shape[0], dtype=jnp.int32)[:, None]
    ).astype(jnp.float32)
    diagonal = jnp.sum(scores * target, 1)
    term = jnp.sum((top[:, 0] - diagonal) * own_live)
    return (term, (share - target) * own_live[:, None])


def muon_groups():
    found = [(0, 1), (1, 1)]
    for index in range(LAYERS):
        base = 2 + 12 * index
        found = found + [(base, 3), (base + 3, 1), (base + 4, 4), (base + 8, 4)]
    return found


def lane_plan(lanes):
    plan = [[] for _ in range(lanes)]
    for start, number in sorted(muon_groups(), key=lambda group: -group[1]):
        lane = min(range(lanes), key=lambda i: (sum(n for _, n in plan[i]), len(plan[i]), i))
        plan[lane].append((start, number))
    depth = max(len(entry) for entry in plan)
    widths = [
        max([entry[slot][1] for entry in plan if slot < len(entry)]) for slot in range(depth)
    ]
    return (plan, widths)


def lane_tables(plan, widths):
    index = np.zeros((len(plan), sum(widths)), np.int32)
    mask = np.zeros((len(plan), sum(widths)), np.float32)
    number = np.ones((len(plan), sum(widths)), np.float32)
    home = {}
    for lane, entry in enumerate(plan):
        first = 0
        for slot, width in enumerate(widths):
            if slot < len(entry):
                start, count = entry[slot]
                for place in range(count):
                    index[lane, first + place] = start + place
                    mask[lane, first + place] = 1.0
                    number[lane, first + place] = count
                    home[start + place] = (lane, first + place)
            first += width
    return (index, mask, number, home)


def orthogonal_factor(gram):
    size = jnp.sqrt(jnp.trace(gram)) + 1e-07
    state = gram / (size * size)
    total = None
    for turn in range(NS_ITERS):
        low = rounded(state)
        change = COEF_B * state + COEF_C * jnp.dot(low, low, preferred_element_type=jnp.float32)
        change_low = rounded(change)
        if total is None:
            total = COEF_A * jnp.eye(D, dtype=jnp.float32) + change
        else:
            total = COEF_A * total + jnp.dot(
                rounded(total), change_low, preferred_element_type=jnp.float32
            )
        if turn < NS_ITERS - 1:
            for _ in range(2):
                state = COEF_A * state + jnp.dot(
                    rounded(state), change_low, preferred_element_type=jnp.float32
                )
    return total / size


def per_device(
    patches, grid, segments, text_ids, table, weights, momenta, gains, gains_m, gains_v, step
):
    fin = 6 * LAYERS
    base = fin + 3
    lanes = lax.axis_size("dp")
    slots = jnp.arange(IMGS, dtype=jnp.int32)
    live = jnp.any(segments[:, 0, None, :] == slots[None, :, None], -1).astype(jnp.float32)
    count = lax.psum(jnp.sum(live), ("dp", "fsdp"))
    factor = 1.0 / (2.0 * count)
    group_ids = lax.all_gather(text_ids, "fsdp", axis=1, tiled=True)
    flat_ids = jnp.transpose(group_ids, (1, 0, 2, 3)).reshape(-1, group_ids.shape[3])
    share_rows = table.shape[0]
    first_row = lax.axis_index("fsdp") * share_rows
    picked = flat_ids - first_row
    hits = jnp.sum(
        (picked[:, :, None] == jnp.arange(share_rows, dtype=jnp.int32)[None, None, :]).astype(
            jnp.int32
        ),
        1,
    )
    text_sum = lax.psum_scatter(
        jnp.dot(
            rounded(hits.astype(jnp.float32)), table, preferred_element_type=jnp.float32
        ).astype(jnp.bfloat16),
        "fsdp",
        scatter_dimension=0,
        tiled=True,
    ).astype(jnp.float32)
    text_low = rounded(unit_rows(text_sum / text_ids.shape[-1])).reshape(MB, IMGS, -1)
    me = lax.axis_index(("dp", "fsdp"))
    rows_local = weights.shape[1]
    segment = segments[:, 0]
    same = segment[:, :, None] == segment[:, None, :]
    rows_hot, cols_hot = jax.vmap(positions)(grid[:, 0])
    rows_hot = rows_hot.reshape(-1, POS)
    cols_hot = cols_hot.reshape(-1, POS)
    patch_low = patches.reshape(-1, D)
    stem = fetch(weights[0:2])
    state = product(patch_low, stem[0], "sd,rd->sr")
    state = state + jnp.dot(rows_hot, gains[base : base + POS], precision=HIGH)
    state = state + jnp.dot(cols_hot, gains[base + POS : base + 2 * POS], precision=HIGH)
    saved = []
    for index in range(LAYERS):
        blocks = fetch(weights[2 + 12 * index : 14 + 12 * index])
        state, kept = layer_forward(state, blocks, gains[6 * index : 6 * index + 6], same)
        saved.append((kept, blocks))
    final, norm_final = jax.vjp(layer_norm, state, gains[fin], gains[fin + 1])

    def pool_all(values, query):
        split = values.reshape(MB, -1, D)
        return jnp.concatenate([pooling(segment[part])(split[part], query) for part in range(MB)])

    pooled, pool_back = jax.vjp(pool_all, final, gains[fin + 2])
    pooled_low = rounded(pooled)
    embedded, unit_back = jax.vjp(unit_rows, product(pooled_low, stem[1], "kr,rd->kd"))
    image_low = rounded(embedded)
    both = jnp.concatenate([image_low, text_low.reshape(MB * IMGS, D)], 0)
    whole = lax.all_gather(both, ("dp", "fsdp"), axis=0)
    alive = lax.all_gather(rounded(live), ("dp", "fsdp"), axis=1, tiled=True).astype(jnp.float32)
    loss_part = jnp.float32(0.0)
    image_grads = []
    spreads = []
    for part in range(MB):
        images = whole[:, part * IMGS : (part + 1) * IMGS].reshape(-1, D)
        texts = whole[:, (MB + part) * IMGS : (MB + part + 1) * IMGS].reshape(-1, D)
        own_image = image_low[part * IMGS : (part + 1) * IMGS]
        own_text = text_low[part]
        forward = LOGIT_SCALE * product(own_image, texts, "kd,nd->kn")
        backward = LOGIT_SCALE * product(own_text, images, "kd,nd->kn")
        term_f, grad_f = contrast_rows(forward, alive[part], live[part], me * IMGS)
        term_b, grad_b = contrast_rows(backward, alive[part], live[part], me * IMGS)
        loss_part = loss_part + (term_f + term_b) * factor
        forward_low = rounded(grad_f * factor * LOGIT_SCALE)
        backward_low = rounded(grad_b * factor * LOGIT_SCALE)
        spreads.append(product(backward_low, own_text, "kn,kd->nd"))
        image_grads.append(product(forward_low, texts, "kn,nd->kd"))
    spread = jnp.stack([value.reshape(-1, IMGS, D) for value in spreads], 1)
    text_side = lax.psum_scatter(spread, ("dp", "fsdp"), scatter_dimension=0)
    image_grad = jnp.concatenate(image_grads, 0) + text_side.reshape(MB * IMGS, D)
    (embed_grad,) = unit_back(image_grad)
    embed_low = rounded(embed_grad)
    grad_pool = rounded(product(pooled_low, embed_low, "kr,kd->rd"))
    final_grad, query_grad = pool_back(product(embed_low, stem[1], "kd,rd->kr"))
    grad, gain_final, shift_final = norm_final(final_grad)
    gain_parts = [None] * LAYERS
    shards = [None] * (LAYERS + 1)
    for index in reversed(range(LAYERS)):
        kept, blocks = saved[index]
        grad, block_grads, gain_parts[index] = layer_backward(grad, kept, blocks, same)
        shards[index + 1] = lax.psum(
            lax.psum_scatter(block_grads, "fsdp", scatter_dimension=1, tiled=True), "dp"
        )
    grad_low = rounded(grad)
    grad_patch = rounded(product(grad_low, patch_low, "sr,sd->rd"))
    shards[0] = lax.psum(
        lax.psum_scatter(
            jnp.stack([grad_patch, grad_pool]), "fsdp", scatter_dimension=1, tiled=True
        ),
        "dp",
    )
    grad_rows = jnp.dot(rows_hot.T, grad, precision=HIGH)
    grad_cols = jnp.dot(cols_hot.T, grad, precision=HIGH)
    gains_grad = jnp.concatenate(
        gain_parts
        + [jnp.stack([gain_final, shift_final, query_grad]), grad_rows, grad_cols],
        0,
    )
    gains_grad, loss = lax.psum((gains_grad, loss_part), ("dp", "fsdp"))
    shard_grads = jnp.concatenate(shards, 0).astype(jnp.float32)
    squares = lax.psum(jnp.sum(shard_grads * shard_grads), "fsdp")
    norm = jnp.sqrt(squares + jnp.sum(gains_grad * gains_grad))
    clip = jnp.minimum(1.0, CLIP_LIMIT / (norm + 1e-06))
    momenta_new = MOMENT * momenta + clip * shard_grads
    plan, widths = lane_plan(lanes)
    index, mask, number, home = lane_tables(plan, widths)
    lane = lax.axis_index("dp")
    own = jnp.stack(
        [
            lax.dynamic_index_in_dim(momenta_new, jnp.asarray(index)[lane, place], 0, False)
            * jnp.asarray(mask)[lane, place]
            for place in range(index.shape[1])
        ]
    )
    own_low = rounded(own)
    bounds = np.cumsum([0] + widths)
    grams = jnp.stack(
        [
            product(own_low[a:b], own_low[a:b], "brd,bre->de")
            for a, b in zip(bounds[:-1], bounds[1:])
        ]
    )
    grams = lax.psum(grams, "fsdp")
    turned = jnp.concatenate(
        [
            product(
                own_low[bounds[slot] : bounds[slot + 1]],
                rounded(orthogonal_factor(grams[slot])),
                "brd,de->bre",
            )
            for slot in range(len(widths))
        ],
        0,
    )
    spread_rows = lax.all_gather(rounded(turned), "dp", axis=0)
    current = jnp.stack(
        [spread_rows[home[block][0], home[block][1]] for block in range(weights.shape[0])]
    ).astype(jnp.float32)
    scale = np.ones((weights.shape[0], 1, 1), np.float32)
    for start, count_blocks in muon_groups():
        scale[start : start + count_blocks] = MUON_RATE * math.sqrt(count_blocks)
    weights_new = weights * (1.0 - MUON_RATE * MUON_DECAY) - jnp.asarray(scale) * current
    grad_small = clip * gains_grad
    moment_one = BETA_ONE * gains_m + (1.0 - BETA_ONE) * grad_small
    moment_two = BETA_TWO * gains_v + (1.0 - BETA_TWO) * grad_small * grad_small
    count_steps = step[0].astype(jnp.float32)
    corrected_one = moment_one / (1.0 - jnp.power(BETA_ONE, count_steps))
    corrected_two = moment_two / (1.0 - jnp.power(BETA_TWO, count_steps))
    gains_new = gains - ADAM_RATE * (
        corrected_one / (jnp.sqrt(corrected_two) + ADAM_EPS) + ADAM_DECAY * gains
    )
    shift_grad = grad_small[fin + 1]
    return (
        loss,
        norm,
        weights_new,
        rounded(weights_new),
        momenta_new,
        gains_new,
        moment_one,
        moment_two,
        shift_grad,
    )


def solution(mesh):
    placed = (
        P(None, ("dp", "fsdp"), None, None),
        P(None, ("dp", "fsdp"), None, None),
        P(None, ("dp", "fsdp"), None),
        P(None, ("dp", "fsdp"), None, None),
        P("fsdp", None),
        P(None, "fsdp", None),
        P(None, "fsdp", None),
        P(),
        P(),
        P(),
        P(),
    )
    return jax.shard_map(
        per_device,
        mesh=mesh,
        in_specs=placed,
        out_specs=(
            P(),
            P(),
            P(None, "fsdp", None),
            P(None, "fsdp", None),
            P(None, "fsdp", None),
            P(),
            P(),
            P(),
            P(),
        ),
        check_vma=False,
    )
```

```python
import functools
import math

import jax
import jax.numpy as jnp
import numpy as np
from jax import lax
from jax.experimental import pallas as pl
from jax.experimental.pallas import tpu as pltpu
from jax.sharding import PartitionSpec as P

D = 768
HEADS = 12
FF = 3072
LAYERS = 2
IMGS = 8
POS = 32
MB = 2
NS_ITERS = 5
HD = 64


MESH = pl.DeviceIdType.MESH
VMEM_LIMIT = 56 * 1024 * 1024
HIGH = lax.Precision.HIGHEST
LOGIT_SCALE = 50.0
CLIP_LIMIT = 0.005
MOMENT = 0.95
MUON_RATE = 0.5
MUON_DECAY = 0.01
ADAM_RATE = 0.4
BETA_ONE = 0.9
BETA_TWO = 0.999
ADAM_EPS = 1e-08
ADAM_DECAY = 0.01
COEF_A = 3.4445
COEF_B = -4.775
COEF_C = 2.0315


def rounded(value):
    return value.astype(jnp.bfloat16)


def product(left, right, form):
    return jnp.einsum(form, left, right, preferred_element_type=jnp.float32)


def layer_norm(value, gain, shift):
    centred = value - jnp.mean(value, -1, keepdims=True)
    spread = jnp.mean(centred * centred, -1, keepdims=True)
    return centred * lax.rsqrt(spread + 1e-06) * gain + shift


def head_norm(value, gain):
    heads = value.reshape(value.shape[0], HEADS, HD)
    centred = heads - jnp.mean(heads, -1, keepdims=True)
    spread = jnp.mean(centred * centred, -1, keepdims=True)
    return centred * lax.rsqrt(spread + 1e-06) * gain.reshape(HEADS, HD)


def both_norms(query, key, gain_query, gain_key):
    return (head_norm(query, gain_query), head_norm(key, gain_key))


def unit_rows(value):
    return (
        value
        * lax.rsqrt(jnp.mean(value * value, -1, keepdims=True) + 1e-06)
        * (1.0 / math.sqrt(value.shape[-1]))
    )


def positions(grid):
    slots = jnp.arange(POS, dtype=jnp.int32)
    row_index = grid[0] * POS // grid[2]
    col_index = grid[1] * POS // grid[3]
    return (
        (row_index[:, None] == slots[None]).astype(jnp.float32),
        (col_index[:, None] == slots[None]).astype(jnp.float32),
    )


def pooling(segment):
    member = segment[None, :] == jnp.arange(IMGS, dtype=jnp.int32)[:, None]

    def pooled_of(final, query):
        split = final.reshape(-1, HEADS, HD)
        logits = jnp.einsum("shd,hd->hs", split, query.reshape(HEADS, HD), precision=HIGH) * (
            1.0 / math.sqrt(HD)
        )
        logits = jnp.where(member[:, None, :], logits[None], -1e30)
        share = jax.nn.softmax(logits, -1)
        return jnp.einsum("khs,shd->khd", share, split, precision=HIGH).reshape(IMGS, -1)

    return pooled_of


def flip(index, bit):
    return index + bit - 2 * bit * lax.rem(index // bit, 2)


def greet(peers):
    barrier = pltpu.get_barrier_semaphore()
    for peer in peers:
        pl.semaphore_signal(barrier, inc=1, device_id=peer, device_id_type=MESH)
    pl.semaphore_wait(barrier, len(peers))


def places():
    d = lax.axis_index("dp")
    z = lax.axis_index("fsdp")
    return (d, z, [lax.rem(z + step, 4) for step in range(4)])


def fetch_kernel(chunks, sizes, weights, *refs):
    outs = refs[: len(sizes)]
    full, low, load_sem, store_sem, send, recv = refs[len(sizes) :]
    d, z, zs = places()
    sib, near_x, near_y = flip(d, 1), flip(d, 2), flip(d, 4)
    diagonal = flip(near_x, 4)
    starts = [sum(chunk[3] for chunk in chunks[:k]) for k in range(len(chunks))]
    loads = []
    for k, (source, _, _, n) in enumerate(chunks):
        loads.append(
            pltpu.make_async_copy(
                weights.at[pl.ds(source, n)], full.at[pl.ds(starts[k], n)], load_sem.at[k]
            )
        )
        loads[k].start()
    greet([(d, zs[1]), (d, zs[2]), (d, zs[3]), (sib, z), (near_x, z), (near_y, z)])
    pending = []

    def push(k, slot, first, n, zz, dd, to, source=None):
        out = outs[chunks[k][1]]
        rows = pl.ds(chunks[k][2] + first, n)
        copy = pltpu.make_async_remote_copy(
            src_ref=out.at[rows, zz, dd] if source is None else source,
            dst_ref=out.at[rows, zz, dd],
            send_sem=send.at[k, slot],
            recv_sem=recv.at[k, slot],
            device_id=to,
            device_id_type=MESH,
        )
        copy.start()
        pending.append(copy)
        return copy

    along_z = []
    stores = []
    for k, (_, out, offset, n) in enumerate(chunks):
        loads[k].wait()

        @pl.loop(starts[k], starts[k] + n)
        def _(i):
            low[i] = full[i].astype(low.dtype)

        along_z.append(
            [
                push(k, o - 1, 0, n, z, d, (d, zs[o]), low.at[pl.ds(starts[k], n), d])
                for o in (1, 2, 3)
            ]
        )
        stores.append(
            pltpu.make_async_copy(
                low.at[pl.ds(starts[k], n)],
                outs[out].at[pl.ds(offset, n), z],
                store_sem.at[k],
            )
        )
        stores[k].start()
    along_x, along_y, turn_y, turn_x, last = {}, {}, {}, {}, []
    count = len(chunks)
    for step in range(count + 2):
        if step < count:
            k, n = step, chunks[step][3]
            along_x[k], along_y[k] = [], []
            for o in (1, 2, 3):
                zz = zs[4 - o]
                along_z[k][o - 1].wait_recv()
                along_x[k].append(push(k, 2 + o, 0, n, zz, d, (near_x, z)))
                along_y[k].append(push(k, 5 + o, 0, n, zz, d, (near_y, z)))
                last.append(push(k, 14 + o, 0, n, zz, d, (sib, z)))
        if 1 <= step <= count:
            k, n = step - 1, chunks[step - 1][3]
            half = n // 2
            turn_y[k], turn_x[k] = [], []
            for o in (1, 2, 3):
                zz = zs[4 - o]
                along_x[k][o - 1].wait_recv()
                if half:
                    turn_y[k].append(push(k, 8 + o, 0, half, zz, near_x, (near_y, z)))
                last.append(push(k, 17 + o, 0, n, zz, near_x, (sib, z)))
                along_y[k][o - 1].wait_recv()
                turn_x[k].append(push(k, 11 + o, half, n - half, zz, near_y, (near_x, z)))
                last.append(push(k, 20 + o, 0, n, zz, near_y, (sib, z)))
        if step >= 2:
            k, n = step - 2, chunks[step - 2][3]
            for o in (1, 2, 3):
                for copies in (turn_y[k], turn_x[k]):
                    if copies:
                        copies[o - 1].wait_recv()
                last.append(push(k, 23 + o, 0, n, zs[4 - o], diagonal, (sib, z)))
    for copy in last:
        copy.wait_recv()
    for copy in pending:
        copy.wait_send()
    for copy in stores:
        copy.wait()


def fetch(weights, pieces, collective):
    depth, eighths = lax.axis_size("fsdp"), lax.axis_size("dp")
    if depth != 4 or eighths != 8:
        return [
            lax.all_gather(rounded(weights[a : a + n]), "fsdp", axis=1, tiled=True)
            for a, n in pieces
        ]
    blocks, rows, width = weights.shape
    part = (eighths, rows // eighths, width)
    chunks = []
    for out, (a, n) in enumerate(pieces):
        for first in range(0, n, 2):
            chunks.append((a + first, out, first, min(2, n - first)))
    total = sum(n for _, n in pieces)
    outs = pl.pallas_call(
        functools.partial(fetch_kernel, chunks, [n for _, n in pieces]),
        out_shape=[
            jax.ShapeDtypeStruct((n, depth) + part, jnp.bfloat16) for _, n in pieces
        ],
        in_specs=[pl.BlockSpec(memory_space=pl.ANY)],
        out_specs=[pl.BlockSpec(memory_space=pl.ANY)] * len(pieces),
        scratch_shapes=[
            pltpu.VMEM((total,) + part, jnp.float32),
            pltpu.VMEM((total,) + part, jnp.bfloat16),
            pltpu.SemaphoreType.DMA((len(chunks),)),
            pltpu.SemaphoreType.DMA((len(chunks),)),
            pltpu.SemaphoreType.DMA((len(chunks), 27)),
            pltpu.SemaphoreType.DMA((len(chunks), 27)),
        ],
        compiler_params=pltpu.CompilerParams(
            collective_id=collective, has_side_effects=True, vmem_limit_bytes=VMEM_LIMIT
        ),
        name=f"fetch_{collective}",
    )(weights.reshape((blocks,) + part))
    return [out.reshape(-1, width, width) for out in outs]


def share_kernel(own, out, send, recv):
    d, z, zs = places()
    sib, near_x, near_y = flip(d, 1), flip(d, 2), flip(d, 4)
    diagonal = flip(near_x, 4)
    greet(
        [(d, zs[1]), (d, zs[2]), (d, zs[3]), (sib, z), (near_x, z), (near_y, z), (diagonal, z)]
    )
    out[d, z] = own[...]

    def push(slot, source, target, to):
        copy = pltpu.make_async_remote_copy(
            src_ref=source,
            dst_ref=target,
            send_sem=send.at[slot],
            recv_sem=recv.at[slot],
            device_id=to,
            device_id_type=MESH,
        )
        copy.start()
        return copy

    first = [push(o - 1, own, out.at[d, z], (d, zs[o])) for o in (1, 2, 3)]
    for copy in first:
        copy.wait_recv()
    second = [
        push(3 + i, out.at[d], out.at[d], (to, z)) for i, to in enumerate((near_x, near_y, diagonal))
    ]
    last = [push(6, out.at[d], out.at[d], (sib, z))]
    for i, origin in enumerate((near_x, near_y, diagonal)):
        second[i].wait_recv()
        last.append(push(7 + i, out.at[origin], out.at[origin], (sib, z)))
    for copy in last:
        copy.wait_recv()
    for copy in first + second + last:
        copy.wait_send()


def share(own, collective):
    lanes, depth = lax.axis_size("dp"), lax.axis_size("fsdp")
    if depth != 4 or lanes != 8:
        return lax.all_gather(own, ("dp", "fsdp"), axis=0).reshape((lanes, depth) + own.shape)
    return pl.pallas_call(
        share_kernel,
        out_shape=jax.ShapeDtypeStruct((lanes, depth) + own.shape, own.dtype),
        in_specs=[pl.BlockSpec(memory_space=pltpu.VMEM)],
        out_specs=pl.BlockSpec(memory_space=pltpu.VMEM),
        scratch_shapes=[pltpu.SemaphoreType.DMA((10,)), pltpu.SemaphoreType.DMA((10,))],
        compiler_params=pltpu.CompilerParams(collective_id=collective, has_side_effects=True),
        name=f"share_{collective}",
    )(own)


def swap_kernel(parts, out, send, recv):
    d, z, zs = places()
    greet([(d, zs[1]), (d, zs[2]), (d, zs[3])])
    out[z] = parts[z]
    copies = []
    for o in (1, 2, 3):
        copies.append(
            pltpu.make_async_remote_copy(
                src_ref=parts.at[zs[o]],
                dst_ref=out.at[z],
                send_sem=send.at[o - 1],
                recv_sem=recv.at[o - 1],
                device_id=(d, zs[o]),
                device_id_type=MESH,
            )
        )
        copies[-1].start()
    for copy in copies:
        copy.wait()


def swap(parts, collective):
    depth = lax.axis_size("fsdp")
    if depth != 4 or lax.axis_size("dp") != 8:
        return lax.all_to_all(parts, "fsdp", 0, 0)
    return pl.pallas_call(
        swap_kernel,
        out_shape=jax.ShapeDtypeStruct(parts.shape, parts.dtype),
        in_specs=[pl.BlockSpec(memory_space=pltpu.VMEM)],
        out_specs=pl.BlockSpec(memory_space=pltpu.VMEM),
        scratch_shapes=[pltpu.SemaphoreType.DMA((3,)), pltpu.SemaphoreType.DMA((3,))],
        compiler_params=pltpu.CompilerParams(collective_id=collective, has_side_effects=True),
        name=f"swap_{collective}",
    )(parts)


class Reduction:
    def __init__(self, source, start, first, n, buffers, k, semaphores, spots):
        self.source, self.start, self.first, self.n, self.k = (source, start, first, n, k)
        self.held, self.from_core, self.from_near, self.from_turn, self.ready, self.from_z = buffers
        self.local_sem, self.send, self.recv = semaphores
        self.spots = spots
        self.rows = pl.ds(first, n)
        self.started = []

    def push(self, slot, source, target, to):
        copy = pltpu.make_async_remote_copy(
            src_ref=source,
            dst_ref=target,
            send_sem=self.send.at[self.k, slot],
            recv_sem=self.recv.at[self.k, slot],
            device_id=to,
            device_id_type=MESH,
        )
        copy.start()
        self.started.append(copy)
        return copy

    def begin(self):
        d, z, zs, x, y, c = self.spots
        blocks = pl.ds(self.start, self.n)
        self.local = pltpu.make_async_copy(
            self.source.at[blocks, :, :, :, c], self.held.at[self.rows], self.local_sem.at[self.k]
        )
        self.local.start()
        self.core = self.push(
            0,
            self.source.at[blocks, :, :, :, 1 - c],
            self.from_core.at[self.rows],
            (flip(d, 1), z),
        )

    def add(self, count, place):
        @pl.loop(0, self.n * count)
        def _(i):
            target, other = place(self.first + i // count, lax.rem(i, count))
            total = self.held[target].astype(jnp.float32) + other.astype(jnp.float32)
            self.held[target] = total.astype(self.held.dtype)

    def across_plane(self):
        d, z, zs, x, y, c = self.spots
        self.local.wait()
        self.core.wait_recv()

        def place(b, i):
            target = (b, i // 4, lax.rem(i // 2, 2), lax.rem(i, 2))
            return (target, self.from_core[target])

        self.add(16, place)
        self.near = [
            self.push(
                1,
                self.held.at[self.rows, 0:2, :, 1 - x],
                self.from_near.at[self.rows, 0:2],
                (flip(d, 2), z),
            ),
            self.push(
                2,
                self.held.at[self.rows, 2:4, 1 - y],
                self.from_near.at[self.rows, 2:4],
                (flip(d, 4), z),
            ),
        ]

    def turn(self):
        d, z, zs, x, y, c = self.spots

        def place_a(b, i):
            return ((b, i // 2, lax.rem(i, 2), x), self.from_near[b, i // 2, lax.rem(i, 2)])

        def place_b(b, i):
            return ((b, 2 + i // 2, y, lax.rem(i, 2)), self.from_near[b, 2 + i // 2, lax.rem(i, 2)])

        self.near[0].wait_recv()
        self.add(4, place_a)
        a = self.push(
            3,
            self.held.at[self.rows, 0:2, 1 - y, x],
            self.from_turn.at[self.rows, 0:2],
            (flip(d, 4), z),
        )
        self.near[1].wait_recv()
        self.add(4, place_b)
        b = self.push(
            4,
            self.held.at[self.rows, 2:4, y, 1 - x],
            self.from_turn.at[self.rows, 2:4],
            (flip(d, 2), z),
        )
        self.turned = [a, b]

    def along_z(self):
        d, z, zs, x, y, c = self.spots
        for copy in self.turned:
            copy.wait_recv()

        @pl.loop(0, self.n * 4)
        def _(i):
            b, zz = (self.first + i // 4, lax.rem(i, 4))
            total = self.held[b, zz, y, x].astype(jnp.float32) + self.from_turn[b, zz].astype(
                jnp.float32
            )
            self.ready[b, zz] = total.astype(self.ready.dtype)

        self.spread = [
            self.push(
                4 + o,
                self.ready.at[self.rows, zs[o]],
                self.from_z.at[self.rows, o - 1],
                (d, zs[o]),
            )
            for o in (1, 2, 3)
        ]

    def finish(self, out):
        d, z, zs, x, y, c = self.spots
        for copy in self.spread:
            copy.wait_recv()

        @pl.loop(self.first, self.first + self.n)
        def _(b):
            total = self.held[b, z, y, x].astype(jnp.float32) + self.from_turn[b, z].astype(
                jnp.float32
            )
            for o in range(3):
                total = total + self.from_z[b, o].astype(jnp.float32)
            out[b] = total

        for copy in self.started:
            copy.wait_send()


def reduce_kernel(chunks, sources, sets, *refs):
    ins = refs[:sources]
    outs = refs[sources : sources + sets]
    buffers = [refs[sources + sets + 6 * i : sources + sets + 6 * i + 6] for i in range(sets)]
    semaphores = refs[sources + 7 * sets :]
    d, z, zs = places()
    spots = (d, z, zs, lax.rem(d // 2, 2), d // 4, lax.rem(d, 2))
    greet([(d, zs[1]), (d, zs[2]), (d, zs[3]), (flip(d, 1), z), (flip(d, 2), z), (flip(d, 4), z)])
    work = []
    for k, (source, start, first, n, which) in enumerate(chunks):
        work.append(
            Reduction(ins[source], start, first, n, buffers[which], k, semaphores, spots)
        )
        work[k].begin()
    count = len(chunks)
    for step in range(count + 3):
        if step < count:
            work[step].across_plane()
        if 1 <= step <= count:
            work[step - 1].turn()
        if 2 <= step <= count + 1:
            work[step - 2].along_z()
        if step >= 3:
            work[step - 3].finish(outs[chunks[step - 3][4]])


def reduce_grads(grads, small, collective):
    lanes, depth = lax.axis_size("dp"), lax.axis_size("fsdp")
    rows = D // (lanes * depth)
    tail = (depth, 2, 2, 2)
    sources = [grad.reshape((-1,) + tail + (rows, D)) for grad in grads]
    chunks = []
    first = 0
    for i, source in enumerate(sources):
        for start in range(0, source.shape[0], 2):
            n = min(2, source.shape[0] - start)
            chunks.append((i, start, first, n, 0))
            first += n
    sets = [(first, (rows, D), jnp.bfloat16)]
    if small is not None:
        sources.append(small.reshape((1,) + tail + small.shape[1:]))
        chunks.insert(1, (len(sources) - 1, 0, 0, 1, 1))
        sets.append((1, small.shape[1:], jnp.float32))
    scratch = []
    for n, shape, kind in sets:
        scratch += [
            pltpu.VMEM((n, depth, 2, 2) + shape, kind),
            pltpu.VMEM((n, depth, 2, 2) + shape, kind),
            pltpu.VMEM((n, depth, 2) + shape, kind),
            pltpu.VMEM((n, depth) + shape, kind),
            pltpu.VMEM((n, depth) + shape, kind),
            pltpu.VMEM((n, 3) + shape, kind),
        ]
    outs = pl.pallas_call(
        functools.partial(reduce_kernel, chunks, len(sources), len(sets)),
        out_shape=[jax.ShapeDtypeStruct((n,) + shape, jnp.float32) for n, shape, _ in sets],
        in_specs=[pl.BlockSpec(memory_space=pl.ANY)] * len(sources),
        out_specs=[pl.BlockSpec(memory_space=pltpu.VMEM)] * len(sets),
        scratch_shapes=scratch
        + [
            pltpu.SemaphoreType.DMA((len(chunks),)),
            pltpu.SemaphoreType.DMA((len(chunks), 8)),
            pltpu.SemaphoreType.DMA((len(chunks), 8)),
        ],
        compiler_params=pltpu.CompilerParams(
            collective_id=collective, has_side_effects=True, vmem_limit_bytes=VMEM_LIMIT
        ),
        name=f"reduce_{collective}",
    )(*sources)
    return (outs[0], outs[1] if small is not None else None)


def spread_kernel(own, out, local_sem, send, recv):
    d, z, _ = places()
    sib, near_x, near_y = flip(d, 1), flip(d, 2), flip(d, 4)
    diagonal = flip(near_x, 4)
    greet([(sib, z), (near_x, z), (near_y, z)])
    half = own.shape[0] // 2
    first, second = (pl.ds(0, half), pl.ds(half, own.shape[0] - half))
    started = []

    def push(slot, origin, part, to, source=None):
        copy = pltpu.make_async_remote_copy(
            src_ref=out.at[part, origin] if source is None else source,
            dst_ref=out.at[part, origin],
            send_sem=send.at[slot],
            recv_sem=recv.at[slot],
            device_id=to,
            device_id_type=MESH,
        )
        copy.start()
        started.append(copy)
        return copy

    near = []
    for i, part in enumerate((first, second)):
        near.append(
            [
                push(2 * i, d, part, (near_x, z), own.at[part]),
                push(2 * i + 1, d, part, (near_y, z), own.at[part]),
            ]
        )
    keep = pltpu.make_async_copy(own, out.at[:, d], local_sem)
    keep.start()
    last = [push(4 + i, d, part, (sib, z), own.at[part]) for i, part in enumerate((first, second))]
    near[0][0].wait_recv()
    turn_y = push(6, near_x, first, (near_y, z))
    last.append(push(7, near_x, first, (sib, z)))
    near[1][1].wait_recv()
    turn_x = push(8, near_y, second, (near_x, z))
    last.append(push(9, near_y, second, (sib, z)))
    near[0][1].wait_recv()
    last.append(push(10, near_y, first, (sib, z)))
    near[1][0].wait_recv()
    last.append(push(11, near_x, second, (sib, z)))
    turn_y.wait_recv()
    last.append(push(12, diagonal, first, (sib, z)))
    turn_x.wait_recv()
    last.append(push(13, diagonal, second, (sib, z)))
    for copy in last:
        copy.wait_recv()
    for copy in started:
        copy.wait_send()
    keep.wait()


def spread(own, collective):
    lanes = lax.axis_size("dp")
    if lax.axis_size("fsdp") != 4 or lanes != 8:
        return lax.all_gather(own, "dp", axis=1)
    return pl.pallas_call(
        spread_kernel,
        out_shape=jax.ShapeDtypeStruct(own.shape[:1] + (lanes,) + own.shape[1:], own.dtype),
        in_specs=[pl.BlockSpec(memory_space=pltpu.VMEM)],
        out_specs=pl.BlockSpec(memory_space=pl.ANY),
        scratch_shapes=[
            pltpu.SemaphoreType.DMA,
            pltpu.SemaphoreType.DMA((14,)),
            pltpu.SemaphoreType.DMA((14,)),
        ],
        compiler_params=pltpu.CompilerParams(
            collective_id=collective, has_side_effects=True, vmem_limit_bytes=VMEM_LIMIT
        ),
        name=f"spread_{collective}",
    )(own)


def masked_scores(query_low, key_low, same):
    scores = product(query_low, key_low, "bshd,bthd->bhst") * (1.0 / math.sqrt(HD))
    return jnp.where(same[:, None], scores, -1e30)


def layer_forward(state, blocks, gains, same):
    heads_in, norm_one = jax.vjp(layer_norm, state, gains[0], gains[1])
    heads_low = rounded(heads_in)
    mixed = product(heads_low, blocks[0].reshape(3 * D, D), "sd,rd->sr")
    (query, key), norms_back = jax.vjp(
        both_norms, mixed[:, :D], mixed[:, D : 2 * D], gains[4], gains[5]
    )
    query_low = rounded(query).reshape(MB, -1, HEADS, HD)
    key_low = rounded(key).reshape(MB, -1, HEADS, HD)
    value_low = rounded(mixed[:, 2 * D :]).reshape(MB, -1, HEADS, HD)
    scores = masked_scores(query_low, key_low, same)
    top = jax.scipy.special.logsumexp(scores, axis=-1, keepdims=True)
    weights_low = rounded(jnp.exp(scores - top))
    attended_low = rounded(product(weights_low, value_low, "bhst,bthd->bshd").reshape(-1, D))
    state = state + product(attended_low, blocks[1].reshape(D, D), "sr,rd->sd")
    normed, norm_two = jax.vjp(layer_norm, state, gains[2], gains[3])
    normed_low = rounded(normed)
    hidden, gelu_back = jax.vjp(
        jax.nn.gelu, product(normed_low, blocks[2].reshape(FF, D), "sd,rd->sr")
    )
    hidden_low = rounded(hidden)
    state = state + product(hidden_low, blocks[3].reshape(FF, D), "sr,rd->sd")
    kept = (
        norm_one,
        heads_low,
        norms_back,
        query_low,
        key_low,
        value_low,
        top,
        attended_low,
        norm_two,
        normed_low,
        gelu_back,
        hidden_low,
    )
    return (state, kept)


def layer_backward(grad, kept, blocks, same):
    (
        norm_one,
        heads_low,
        norms_back,
        query_low,
        key_low,
        value_low,
        top,
        attended_low,
        norm_two,
        normed_low,
        gelu_back,
        hidden_low,
    ) = kept
    down = blocks[3].reshape(FF, D)
    upward = blocks[2].reshape(FF, D)
    grad_low = rounded(grad)
    grad_down = rounded(product(hidden_low, grad_low, "sr,sd->rd"))
    (grad_hidden,) = gelu_back(product(grad_low, down, "sd,rd->sr"))
    hidden_grad = rounded(grad_hidden)
    grad_up = rounded(product(hidden_grad, normed_low, "sr,sd->rd"))
    inner, gain_two, shift_two = norm_two(product(hidden_grad, upward, "sr,rd->sd"))
    grad = grad + inner
    grad_low = rounded(grad)
    grad_out = rounded(product(attended_low, grad_low, "sr,sd->rd"))
    attended_grad = rounded(product(grad_low, blocks[1].reshape(D, D), "sd,rd->sr")).reshape(MB, -1, HEADS, HD)
    weights = jnp.exp(masked_scores(query_low, key_low, same) - top)
    weights_low = rounded(weights)
    value_grad = product(weights_low, attended_grad, "bhst,bshd->bthd")
    weight_grad = product(attended_grad, value_low, "bshd,bthd->bhst")
    score_grad = weights * (weight_grad - jnp.sum(weights * weight_grad, -1, keepdims=True))
    score_low = rounded(score_grad * (1.0 / math.sqrt(HD)))
    query_grad = product(score_low, key_low, "bhst,bthd->bshd").reshape(-1, HEADS, HD)
    key_grad = product(score_low, query_low, "bhst,bshd->bthd").reshape(-1, HEADS, HD)
    query_in, key_in, gain_query, gain_key = norms_back((query_grad, key_grad))
    mixed_low = rounded(jnp.concatenate([query_in, key_in, value_grad.reshape(-1, D)], 1))
    grad_mixed = rounded(product(mixed_low, heads_low, "sr,sd->rd"))
    inner, gain_one, shift_one = norm_one(
        product(mixed_low, blocks[0].reshape(3 * D, D), "sr,rd->sd")
    )
    grad = grad + inner
    block_grads = [grad_mixed, grad_out, grad_up, grad_down]
    gain_grads = jnp.stack([gain_one, shift_one, gain_two, shift_two, gain_query, gain_key])
    return (grad, block_grads, gain_grads)


def contrast_rows(scores, alive, own_live, rows):
    masked = jnp.where(alive[None, :] > 0, scores, -1e30)
    top = jax.scipy.special.logsumexp(masked, axis=1, keepdims=True)
    share = jnp.exp(masked - top)
    columns = jnp.arange(scores.shape[1], dtype=jnp.int32)
    target = (columns[None, :] == rows[:, None]).astype(jnp.float32)
    diagonal = jnp.sum(scores * target, 1)
    return ((top[:, 0] - diagonal) * own_live, (share - target) * own_live[:, None])


def muon_groups():
    found = [(0, 1), (1, 1)]
    for index in range(LAYERS):
        base = 2 + 12 * index
        found = found + [(base, 3), (base + 3, 1), (base + 4, 4), (base + 8, 4)]
    return found


def lane_plan(lanes):
    plan = [[] for _ in range(lanes)]
    for start, number in sorted(muon_groups(), key=lambda group: -group[1]):
        lane = min(range(lanes), key=lambda i: (sum(n for _, n in plan[i]), len(plan[i]), i))
        plan[lane].append((start, number))
    depth = max(len(entry) for entry in plan)
    widths = [
        max([entry[slot][1] for entry in plan if slot < len(entry)]) for slot in range(depth)
    ]
    return (plan, widths)


def lane_tables(plan, widths):
    index = np.zeros((len(plan), sum(widths)), np.int32)
    mask = np.zeros((len(plan), sum(widths)), np.float32)
    number = np.ones((len(plan), sum(widths)), np.float32)
    home = {}
    for lane, entry in enumerate(plan):
        first = 0
        for slot, width in enumerate(widths):
            if slot < len(entry):
                start, count = entry[slot]
                for place in range(count):
                    index[lane, first + place] = start + place
                    mask[lane, first + place] = 1.0
                    number[lane, first + place] = count
                    home[start + place] = (lane, first + place)
            first += width
    return (index, mask, number, home)


def orthogonal_factor(gram):
    size = jnp.sqrt(jnp.trace(gram)) + 1e-07
    state = gram / (size * size)
    total = None
    for turn in range(NS_ITERS):
        low = rounded(state)
        change = COEF_B * state + COEF_C * jnp.dot(low, low, preferred_element_type=jnp.float32)
        change_low = rounded(change)
        if total is None:
            total = COEF_A * jnp.eye(D, dtype=jnp.float32) + change
        else:
            total = COEF_A * total + jnp.dot(
                rounded(total), change_low, preferred_element_type=jnp.float32
            )
        if turn < NS_ITERS - 1:
            for _ in range(2):
                state = COEF_A * state + jnp.dot(
                    rounded(state), change_low, preferred_element_type=jnp.float32
                )
    return total / size


def per_device(
    patches, grid, segments, text_ids, table, weights, momenta, gains, gains_m, gains_v, step
):
    fin = 6 * LAYERS
    base = fin + 3
    lanes = lax.axis_size("dp")
    slots = jnp.arange(IMGS, dtype=jnp.int32)
    live = jnp.any(segments[:, 0, None, :] == slots[None, :, None], -1).astype(jnp.float32)
    depth = lax.axis_size("fsdp")
    captions = MB * IMGS
    ids = jnp.broadcast_to(text_ids.reshape(1, captions, -1), (depth, captions, text_ids.shape[3]))
    ids = swap(ids, 10)
    stem, *first_blocks = fetch(weights, [(0, 1), (2, 3), (5, 1), (6, 4), (10, 4)], 1)
    flat_ids = ids.reshape(depth * captions, -1)
    share_rows = table.shape[0]
    picked = flat_ids - lax.axis_index("fsdp") * share_rows
    hits = jnp.sum(
        (picked[:, :, None] == jnp.arange(share_rows, dtype=jnp.int32)[None, None, :]).astype(
            jnp.int32
        ),
        1,
    )
    parts = jnp.dot(rounded(hits.astype(jnp.float32)), table, preferred_element_type=jnp.float32)
    text_sum = jnp.sum(swap(parts.reshape(depth, captions, D), 11), 0)
    text_low = rounded(unit_rows(text_sum / text_ids.shape[-1]))
    me = lax.axis_index(("dp", "fsdp"))
    segment = segments[:, 0]
    same = segment[:, :, None] == segment[:, None, :]
    rows_hot, cols_hot = jax.vmap(positions)(grid[:, 0])
    rows_hot = rows_hot.reshape(-1, POS)
    cols_hot = cols_hot.reshape(-1, POS)
    patch_low = patches.reshape(-1, D)
    state = product(patch_low, stem[0], "sd,rd->sr")
    state = state + jnp.dot(rows_hot, gains[base : base + POS], precision=HIGH)
    state = state + jnp.dot(cols_hot, gains[base + POS : base + 2 * POS], precision=HIGH)
    saved = []
    for index in range(LAYERS):
        if index == 0:
            blocks = first_blocks
        else:
            start = 2 + 12 * index
            pieces = [(start, 3), (start + 3, 1), (start + 4, 4), (start + 8, 4)]
            if index == 1:
                pieces = pieces + [(1, 1)]
            blocks = fetch(weights, pieces, 2 + index)
            if index == 1:
                pooling_matrix = blocks.pop()[0]
        state, kept = layer_forward(state, blocks, gains[6 * index : 6 * index + 6], same)
        saved.append((kept, blocks))
    final, norm_final = jax.vjp(layer_norm, state, gains[fin], gains[fin + 1])

    def pool_all(values, query):
        split = values.reshape(MB, -1, D)
        return jnp.concatenate([pooling(segment[part])(split[part], query) for part in range(MB)])

    pooled, pool_back = jax.vjp(pool_all, final, gains[fin + 2])
    pooled_low = rounded(pooled)
    embedded, unit_back = jax.vjp(unit_rows, product(pooled_low, pooling_matrix, "kr,rd->kd"))
    image_low = rounded(embedded)
    flags = jnp.broadcast_to(live.reshape(1, captions, 1), (1, captions, D)).astype(jnp.bfloat16)
    both = jnp.concatenate([image_low[None], text_low[None], flags], 0).reshape(3 * captions, D)
    whole = share(both, 8).reshape(-1, 3, MB, IMGS, D)
    flags = whole[:, 2, :, :, 0].astype(jnp.float32)
    count = jnp.sum(flags)
    factor = 1.0 / (2.0 * count)
    loss_part = jnp.float32(0.0)
    image_grads = []
    for part in range(MB):
        images = whole[:, 0, part].reshape(-1, D)
        texts = whole[:, 1, part].reshape(-1, D)
        alive = flags[:, part].reshape(-1)
        own_image = image_low[part * IMGS : (part + 1) * IMGS]
        forward = LOGIT_SCALE * product(own_image, texts, "kd,nd->kn")
        backward = LOGIT_SCALE * product(texts, images, "kd,nd->kn")
        own = me * IMGS + jnp.arange(IMGS, dtype=jnp.int32)
        everyone = jnp.arange(alive.shape[0], dtype=jnp.int32)
        term_f, grad_f = contrast_rows(forward, alive, live[part], own)
        term_b, grad_b = contrast_rows(backward, alive, alive, everyone)
        own_terms = jnp.sum(jnp.where((everyone // IMGS) == me, term_b, 0.0))
        loss_part = loss_part + (jnp.sum(term_f) + own_terms) * factor
        forward_low = rounded(grad_f * factor * LOGIT_SCALE)
        backward_low = rounded(
            lax.dynamic_slice_in_dim(grad_b, me * IMGS, IMGS, 1) * factor * LOGIT_SCALE
        )
        image_grads.append(
            product(forward_low, texts, "kn,nd->kd") + product(backward_low, texts, "nk,nd->kd")
        )
    image_grad = jnp.concatenate(image_grads, 0)
    (embed_grad,) = unit_back(image_grad)
    embed_low = rounded(embed_grad)
    grad_pool = rounded(product(pooled_low, embed_low, "kr,kd->rd"))
    final_grad, query_grad = pool_back(product(embed_low, pooling_matrix, "kd,rd->kr"))
    grad, gain_final, shift_final = norm_final(final_grad)
    gain_parts = [None] * LAYERS
    block_grads = [None] * LAYERS
    fast = depth == 4 and lanes == 8
    slices = [None] * LAYERS
    for index in reversed(range(LAYERS)):
        kept, blocks = saved[index]
        grad, block_grads[index], gain_parts[index] = layer_backward(grad, kept, blocks, same)
        if index == 1:
            block_grads[index].append(grad_pool)
        if fast and index > 0:
            slices[index], _ = reduce_grads(block_grads[index], None, 4 + index)
    grad_low = rounded(grad)
    grad_patch = rounded(product(grad_low, patch_low, "sr,sd->rd"))
    block_grads[0].append(grad_patch)
    grad_rows = jnp.dot(rows_hot.T, grad, precision=HIGH)
    grad_cols = jnp.dot(cols_hot.T, grad, precision=HIGH)
    gains_grad = jnp.concatenate(
        gain_parts
        + [jnp.stack([gain_final, shift_final, query_grad]), grad_rows, grad_cols],
        0,
    )
    if fast:
        width = 256
        small = jnp.concatenate([gains_grad.reshape(-1), loss_part[None]])
        small = jnp.pad(small, (0, lanes * depth * 8 * width - small.shape[0]))
        slices[0], small = reduce_grads(
            block_grads[0], small.reshape(lanes * depth, 8, width), 4
        )
        slices = jnp.concatenate(
            [slices[0][12:], slices[1][12:]] + [values[:12] for values in slices], 0
        )
        squares = jnp.broadcast_to(jnp.sum(slices * slices), (8, width))
        shared = share(jnp.concatenate([small[0], squares], 0), 9)
        flat = jnp.transpose(shared[:, :, :8], (1, 0, 2, 3)).reshape(-1)
        gains_grad, loss = (flat[: gains.size].reshape(gains.shape), flat[gains.size])
        squares = jnp.sum(shared[:, :, 8, 0])
        shard_grads = spread(rounded(slices), 12).reshape(weights.shape).astype(jnp.float32)
    else:
        stack = jnp.concatenate(
            [block_grads[index].pop().reshape(1, D, D) for index in range(LAYERS)]
            + [value.reshape(-1, D, D) for values in block_grads for value in values],
            0,
        )
        shard_grads = lax.psum(
            lax.psum_scatter(stack, "fsdp", scatter_dimension=1, tiled=True), "dp"
        ).astype(jnp.float32)
        gains_grad, loss = lax.psum((gains_grad, loss_part), ("dp", "fsdp"))
        squares = lax.psum(jnp.sum(shard_grads * shard_grads), "fsdp")
    norm = jnp.sqrt(squares + jnp.sum(gains_grad * gains_grad))
    clip = jnp.minimum(1.0, CLIP_LIMIT / (norm + 1e-06))
    momenta_new = MOMENT * momenta + clip * shard_grads
    plan, widths = lane_plan(lanes)
    index, mask, number, home = lane_tables(plan, widths)
    lane = lax.axis_index("dp")
    own = jnp.stack(
        [
            lax.dynamic_index_in_dim(momenta_new, jnp.asarray(index)[lane, place], 0, False)
            * jnp.asarray(mask)[lane, place]
            for place in range(index.shape[1])
        ]
    )
    own_low = rounded(own)
    bounds = np.cumsum([0] + widths)
    grams = jnp.stack(
        [
            product(own_low[a:b], own_low[a:b], "brd,bre->de")
            for a, b in zip(bounds[:-1], bounds[1:])
        ]
    )
    grams = lax.psum(grams, "fsdp")
    turned = jnp.concatenate(
        [
            product(
                own_low[bounds[slot] : bounds[slot + 1]],
                rounded(orthogonal_factor(grams[slot])),
                "brd,de->bre",
            )
            for slot in range(len(widths))
        ],
        0,
    )
    spread_rows = lax.all_gather(rounded(turned), "dp", axis=0)
    current = jnp.stack(
        [spread_rows[home[block][0], home[block][1]] for block in range(weights.shape[0])]
    ).astype(jnp.float32)
    scale = np.ones((weights.shape[0], 1, 1), np.float32)
    for start, count_blocks in muon_groups():
        scale[start : start + count_blocks] = MUON_RATE * math.sqrt(count_blocks)
    weights_new = weights * (1.0 - MUON_RATE * MUON_DECAY) - jnp.asarray(scale) * current
    grad_small = clip * gains_grad
    moment_one = BETA_ONE * gains_m + (1.0 - BETA_ONE) * grad_small
    moment_two = BETA_TWO * gains_v + (1.0 - BETA_TWO) * grad_small * grad_small
    count_steps = step[0].astype(jnp.float32)
    corrected_one = moment_one / (1.0 - jnp.power(BETA_ONE, count_steps))
    corrected_two = moment_two / (1.0 - jnp.power(BETA_TWO, count_steps))
    gains_new = gains - ADAM_RATE * (
        corrected_one / (jnp.sqrt(corrected_two) + ADAM_EPS) + ADAM_DECAY * gains
    )
    shift_grad = grad_small[fin + 1]
    return (
        loss,
        norm,
        weights_new,
        rounded(weights_new),
        momenta_new,
        gains_new,
        moment_one,
        moment_two,
        shift_grad,
    )


def solution(mesh):
    placed = (
        P(None, ("dp", "fsdp"), None, None),
        P(None, ("dp", "fsdp"), None, None),
        P(None, ("dp", "fsdp"), None),
        P(None, ("dp", "fsdp"), None, None),
        P("fsdp", None),
        P(None, "fsdp", None),
        P(None, "fsdp", None),
        P(),
        P(),
        P(),
        P(),
    )
    return jax.shard_map(
        per_device,
        mesh=mesh,
        in_specs=placed,
        out_specs=(
            P(),
            P(),
            P(None, "fsdp", None),
            P(None, "fsdp", None),
            P(None, "fsdp", None),
            P(),
            P(),
            P(),
            P(),
        ),
        check_vma=False,
    )
```

```python
import functools
import math

import jax
import jax.numpy as jnp
import numpy as np
from jax import lax
from jax.experimental import pallas as pl
from jax.experimental.pallas import tpu as pltpu
from jax.sharding import PartitionSpec as P

D = 768
HEADS = 12
FF = 3072
LAYERS = 2
IMGS = 8
POS = 32
MB = 2
NS_ITERS = 5
HD = 64


MESH = pl.DeviceIdType.MESH
VMEM_LIMIT = 56 * 1024 * 1024
HIGH = lax.Precision.HIGHEST
LOGIT_SCALE = 50.0
CLIP_LIMIT = 0.005
MOMENT = 0.95
MUON_RATE = 0.5
MUON_DECAY = 0.01
ADAM_RATE = 0.4
BETA_ONE = 0.9
BETA_TWO = 0.999
ADAM_EPS = 1e-08
ADAM_DECAY = 0.01
COEF_A = 3.4445
COEF_B = -4.775
COEF_C = 2.0315


def rounded(value):
    return value.astype(jnp.bfloat16)


def product(left, right, form):
    return jnp.einsum(form, left, right, preferred_element_type=jnp.float32)


def layer_norm(value, gain, shift):
    centred = value - jnp.mean(value, -1, keepdims=True)
    spread = jnp.mean(centred * centred, -1, keepdims=True)
    return centred * lax.rsqrt(spread + 1e-06) * gain + shift


def unit_rows(value):
    return (
        value
        * lax.rsqrt(jnp.mean(value * value, -1, keepdims=True) + 1e-06)
        * (1.0 / math.sqrt(value.shape[-1]))
    )


def positions(grid):
    slots = jnp.arange(POS, dtype=jnp.int32)
    row_index = grid[0] * POS // grid[2]
    col_index = grid[1] * POS // grid[3]
    return (
        (row_index[:, None] == slots[None]).astype(jnp.float32),
        (col_index[:, None] == slots[None]).astype(jnp.float32),
    )


def pooling(segment):
    member = segment[None, :] == jnp.arange(IMGS, dtype=jnp.int32)[:, None]

    def pooled_of(final, query):
        split = final.reshape(-1, HEADS, HD)
        logits = jnp.einsum("shd,hd->hs", split, query.reshape(HEADS, HD), precision=HIGH) * (
            1.0 / math.sqrt(HD)
        )
        logits = jnp.where(member[:, None, :], logits[None], -1e30)
        share = jax.nn.softmax(logits, -1)
        return jnp.einsum("khs,shd->khd", share, split, precision=HIGH).reshape(IMGS, -1)

    return pooled_of


def flip(index, bit):
    return index + bit - 2 * bit * lax.rem(index // bit, 2)


def greet(peers):
    barrier = pltpu.get_barrier_semaphore()
    for peer in peers:
        pl.semaphore_signal(barrier, inc=1, device_id=peer, device_id_type=MESH)
    pl.semaphore_wait(barrier, len(peers))


def places():
    d = lax.axis_index("dp")
    z = lax.axis_index("fsdp")
    return (d, z, [lax.rem(z + step, 4) for step in range(4)])


def fetch_kernel(chunks, sizes, weights, *refs):
    outs = refs[: len(sizes)]
    full, low, load_sem, store_sem, send, recv = refs[len(sizes) :]
    d, z, zs = places()
    sib, near_x, near_y = flip(d, 1), flip(d, 2), flip(d, 4)
    diagonal = flip(near_x, 4)
    starts = [sum(chunk[3] for chunk in chunks[:k]) for k in range(len(chunks))]
    loads = []
    for k, (source, _, _, n) in enumerate(chunks):
        loads.append(
            pltpu.make_async_copy(
                weights.at[pl.ds(source, n)], full.at[pl.ds(starts[k], n)], load_sem.at[k]
            )
        )
        loads[k].start()
    greet([(d, zs[1]), (d, zs[2]), (d, zs[3]), (sib, z), (near_x, z), (near_y, z)])
    pending = []

    def push(k, slot, first, n, zz, dd, to, source=None):
        out = outs[chunks[k][1]]
        rows = pl.ds(chunks[k][2] + first, n)
        copy = pltpu.make_async_remote_copy(
            src_ref=out.at[rows, zz, dd] if source is None else source,
            dst_ref=out.at[rows, zz, dd],
            send_sem=send.at[k, slot],
            recv_sem=recv.at[k, slot],
            device_id=to,
            device_id_type=MESH,
        )
        copy.start()
        pending.append(copy)
        return copy

    along_z = []
    stores = []
    for k, (_, out, offset, n) in enumerate(chunks):
        loads[k].wait()

        @pl.loop(starts[k], starts[k] + n)
        def _(i):
            low[i] = full[i].astype(low.dtype)

        along_z.append(
            [
                push(k, o - 1, 0, n, z, d, (d, zs[o]), low.at[pl.ds(starts[k], n), d])
                for o in (1, 2, 3)
            ]
        )
        stores.append(
            pltpu.make_async_copy(
                low.at[pl.ds(starts[k], n)],
                outs[out].at[pl.ds(offset, n), z],
                store_sem.at[k],
            )
        )
        stores[k].start()
    along_x, along_y, turn_y, turn_x, last = {}, {}, {}, {}, []
    count = len(chunks)
    for step in range(count + 2):
        if step < count:
            k, n = step, chunks[step][3]
            along_x[k], along_y[k] = [], []
            for o in (1, 2, 3):
                zz = zs[4 - o]
                along_z[k][o - 1].wait_recv()
                along_x[k].append(push(k, 2 + o, 0, n, zz, d, (near_x, z)))
                along_y[k].append(push(k, 5 + o, 0, n, zz, d, (near_y, z)))
                last.append(push(k, 14 + o, 0, n, zz, d, (sib, z)))
        if 1 <= step <= count:
            k, n = step - 1, chunks[step - 1][3]
            half = n // 2
            turn_y[k], turn_x[k] = [], []
            for o in (1, 2, 3):
                zz = zs[4 - o]
                along_x[k][o - 1].wait_recv()
                if half:
                    turn_y[k].append(push(k, 8 + o, 0, half, zz, near_x, (near_y, z)))
                last.append(push(k, 17 + o, 0, n, zz, near_x, (sib, z)))
                along_y[k][o - 1].wait_recv()
                turn_x[k].append(push(k, 11 + o, half, n - half, zz, near_y, (near_x, z)))
                last.append(push(k, 20 + o, 0, n, zz, near_y, (sib, z)))
        if step >= 2:
            k, n = step - 2, chunks[step - 2][3]
            for o in (1, 2, 3):
                for copies in (turn_y[k], turn_x[k]):
                    if copies:
                        copies[o - 1].wait_recv()
                last.append(push(k, 23 + o, 0, n, zs[4 - o], diagonal, (sib, z)))
    for copy in last:
        copy.wait_recv()
    for copy in pending:
        copy.wait_send()
    for copy in stores:
        copy.wait()


def fetch(weights, pieces, collective):
    depth, eighths = lax.axis_size("fsdp"), lax.axis_size("dp")
    if depth != 4 or eighths != 8:
        return [
            lax.all_gather(rounded(weights[a : a + n]), "fsdp", axis=1, tiled=True)
            for a, n in pieces
        ]
    blocks, rows, width = weights.shape
    part = (eighths, rows // eighths, width)
    chunks = []
    for out, (a, n) in enumerate(pieces):
        for first in range(0, n, 2):
            chunks.append((a + first, out, first, min(2, n - first)))
    total = sum(n for _, n in pieces)
    outs = pl.pallas_call(
        functools.partial(fetch_kernel, chunks, [n for _, n in pieces]),
        out_shape=[
            jax.ShapeDtypeStruct((n, depth) + part, jnp.bfloat16) for _, n in pieces
        ],
        in_specs=[pl.BlockSpec(memory_space=pl.ANY)],
        out_specs=[pl.BlockSpec(memory_space=pl.ANY)] * len(pieces),
        scratch_shapes=[
            pltpu.VMEM((total,) + part, jnp.float32),
            pltpu.VMEM((total,) + part, jnp.bfloat16),
            pltpu.SemaphoreType.DMA((len(chunks),)),
            pltpu.SemaphoreType.DMA((len(chunks),)),
            pltpu.SemaphoreType.DMA((len(chunks), 27)),
            pltpu.SemaphoreType.DMA((len(chunks), 27)),
        ],
        compiler_params=pltpu.CompilerParams(
            collective_id=collective, has_side_effects=True, vmem_limit_bytes=VMEM_LIMIT
        ),
        name=f"fetch_{collective}",
    )(weights.reshape((blocks,) + part))
    return [out.reshape(-1, width, width) for out in outs]


def share_kernel(own, out, send, recv):
    d, z, zs = places()
    sib, near_x, near_y = flip(d, 1), flip(d, 2), flip(d, 4)
    diagonal = flip(near_x, 4)
    greet(
        [(d, zs[1]), (d, zs[2]), (d, zs[3]), (sib, z), (near_x, z), (near_y, z), (diagonal, z)]
    )
    out[d, z] = own[...]

    def push(slot, source, target, to):
        copy = pltpu.make_async_remote_copy(
            src_ref=source,
            dst_ref=target,
            send_sem=send.at[slot],
            recv_sem=recv.at[slot],
            device_id=to,
            device_id_type=MESH,
        )
        copy.start()
        return copy

    first = [push(o - 1, own, out.at[d, z], (d, zs[o])) for o in (1, 2, 3)]
    for copy in first:
        copy.wait_recv()
    second = [
        push(3 + i, out.at[d], out.at[d], (to, z)) for i, to in enumerate((near_x, near_y, diagonal))
    ]
    last = [push(6, out.at[d], out.at[d], (sib, z))]
    for i, origin in enumerate((near_x, near_y, diagonal)):
        second[i].wait_recv()
        last.append(push(7 + i, out.at[origin], out.at[origin], (sib, z)))
    for copy in last:
        copy.wait_recv()
    for copy in first + second + last:
        copy.wait_send()


def share(own, collective):
    lanes, depth = lax.axis_size("dp"), lax.axis_size("fsdp")
    if depth != 4 or lanes != 8:
        return lax.all_gather(own, ("dp", "fsdp"), axis=0).reshape((lanes, depth) + own.shape)
    return pl.pallas_call(
        share_kernel,
        out_shape=jax.ShapeDtypeStruct((lanes, depth) + own.shape, own.dtype),
        in_specs=[pl.BlockSpec(memory_space=pltpu.VMEM)],
        out_specs=pl.BlockSpec(memory_space=pltpu.VMEM),
        scratch_shapes=[pltpu.SemaphoreType.DMA((10,)), pltpu.SemaphoreType.DMA((10,))],
        compiler_params=pltpu.CompilerParams(collective_id=collective, has_side_effects=True),
        name=f"share_{collective}",
    )(own)


def swap_kernel(parts, out, send, recv):
    d, z, zs = places()
    greet([(d, zs[1]), (d, zs[2]), (d, zs[3])])
    out[z] = parts[z]
    copies = []
    for o in (1, 2, 3):
        copies.append(
            pltpu.make_async_remote_copy(
                src_ref=parts.at[zs[o]],
                dst_ref=out.at[z],
                send_sem=send.at[o - 1],
                recv_sem=recv.at[o - 1],
                device_id=(d, zs[o]),
                device_id_type=MESH,
            )
        )
        copies[-1].start()
    for copy in copies:
        copy.wait()


def swap(parts, collective):
    depth = lax.axis_size("fsdp")
    if depth != 4 or lax.axis_size("dp") != 8:
        return lax.all_to_all(parts, "fsdp", 0, 0)
    return pl.pallas_call(
        swap_kernel,
        out_shape=jax.ShapeDtypeStruct(parts.shape, parts.dtype),
        in_specs=[pl.BlockSpec(memory_space=pltpu.VMEM)],
        out_specs=pl.BlockSpec(memory_space=pltpu.VMEM),
        scratch_shapes=[pltpu.SemaphoreType.DMA((3,)), pltpu.SemaphoreType.DMA((3,))],
        compiler_params=pltpu.CompilerParams(collective_id=collective, has_side_effects=True),
        name=f"swap_{collective}",
    )(parts)


class Reduction:
    def __init__(self, source, start, first, n, buffers, k, semaphores, spots):
        self.source, self.start, self.first, self.n, self.k = (source, start, first, n, k)
        self.held, self.from_core, self.from_near, self.from_turn, self.ready, self.from_z = buffers
        self.local_sem, self.send, self.recv = semaphores
        self.spots = spots
        self.rows = pl.ds(first, n)
        self.started = []

    def push(self, slot, source, target, to):
        copy = pltpu.make_async_remote_copy(
            src_ref=source,
            dst_ref=target,
            send_sem=self.send.at[self.k, slot],
            recv_sem=self.recv.at[self.k, slot],
            device_id=to,
            device_id_type=MESH,
        )
        copy.start()
        self.started.append(copy)
        return copy

    def begin(self):
        d, z, zs, x, y, c = self.spots
        blocks = pl.ds(self.start, self.n)
        self.local = pltpu.make_async_copy(
            self.source.at[blocks, :, :, :, c], self.held.at[self.rows], self.local_sem.at[self.k]
        )
        self.local.start()
        self.core = self.push(
            0,
            self.source.at[blocks, :, :, :, 1 - c],
            self.from_core.at[self.rows],
            (flip(d, 1), z),
        )

    def add(self, count, place):
        @pl.loop(0, self.n * count)
        def _(i):
            target, other = place(self.first + i // count, lax.rem(i, count))
            total = self.held[target].astype(jnp.float32) + other.astype(jnp.float32)
            self.held[target] = total.astype(self.held.dtype)

    def across_plane(self):
        d, z, zs, x, y, c = self.spots
        self.local.wait()
        self.core.wait_recv()

        def place(b, i):
            target = (b, i // 4, lax.rem(i // 2, 2), lax.rem(i, 2))
            return (target, self.from_core[target])

        self.add(16, place)
        self.near = [
            self.push(
                1,
                self.held.at[self.rows, 0:2, :, 1 - x],
                self.from_near.at[self.rows, 0:2],
                (flip(d, 2), z),
            ),
            self.push(
                2,
                self.held.at[self.rows, 2:4, 1 - y],
                self.from_near.at[self.rows, 2:4],
                (flip(d, 4), z),
            ),
        ]

    def turn(self):
        d, z, zs, x, y, c = self.spots

        def place_a(b, i):
            return ((b, i // 2, lax.rem(i, 2), x), self.from_near[b, i // 2, lax.rem(i, 2)])

        def place_b(b, i):
            return ((b, 2 + i // 2, y, lax.rem(i, 2)), self.from_near[b, 2 + i // 2, lax.rem(i, 2)])

        self.near[0].wait_recv()
        self.add(4, place_a)
        a = self.push(
            3,
            self.held.at[self.rows, 0:2, 1 - y, x],
            self.from_turn.at[self.rows, 0:2],
            (flip(d, 4), z),
        )
        self.near[1].wait_recv()
        self.add(4, place_b)
        b = self.push(
            4,
            self.held.at[self.rows, 2:4, y, 1 - x],
            self.from_turn.at[self.rows, 2:4],
            (flip(d, 2), z),
        )
        self.turned = [a, b]

    def along_z(self):
        d, z, zs, x, y, c = self.spots
        for copy in self.turned:
            copy.wait_recv()

        @pl.loop(0, self.n * 4)
        def _(i):
            b, zz = (self.first + i // 4, lax.rem(i, 4))
            total = self.held[b, zz, y, x].astype(jnp.float32) + self.from_turn[b, zz].astype(
                jnp.float32
            )
            self.ready[b, zz] = total.astype(self.ready.dtype)

        self.spread = [
            self.push(
                4 + o,
                self.ready.at[self.rows, zs[o]],
                self.from_z.at[self.rows, o - 1],
                (d, zs[o]),
            )
            for o in (1, 2, 3)
        ]

    def finish(self, out):
        d, z, zs, x, y, c = self.spots
        for copy in self.spread:
            copy.wait_recv()

        @pl.loop(self.first, self.first + self.n)
        def _(b):
            total = self.held[b, z, y, x].astype(jnp.float32) + self.from_turn[b, z].astype(
                jnp.float32
            )
            for o in range(3):
                total = total + self.from_z[b, o].astype(jnp.float32)
            out[b] = total

        for copy in self.started:
            copy.wait_send()


def reduce_kernel(chunks, sources, sets, *refs):
    ins = refs[:sources]
    outs = refs[sources : sources + sets]
    buffers = [refs[sources + sets + 6 * i : sources + sets + 6 * i + 6] for i in range(sets)]
    semaphores = refs[sources + 7 * sets :]
    d, z, zs = places()
    spots = (d, z, zs, lax.rem(d // 2, 2), d // 4, lax.rem(d, 2))
    greet([(d, zs[1]), (d, zs[2]), (d, zs[3]), (flip(d, 1), z), (flip(d, 2), z), (flip(d, 4), z)])
    work = []
    for k, (source, start, first, n, which) in enumerate(chunks):
        work.append(
            Reduction(ins[source], start, first, n, buffers[which], k, semaphores, spots)
        )
        work[k].begin()
    count = len(chunks)
    for step in range(count + 3):
        if step < count:
            work[step].across_plane()
        if 1 <= step <= count:
            work[step - 1].turn()
        if 2 <= step <= count + 1:
            work[step - 2].along_z()
        if step >= 3:
            work[step - 3].finish(outs[chunks[step - 3][4]])


def reduce_grads(grads, small, collective):
    lanes, depth = lax.axis_size("dp"), lax.axis_size("fsdp")
    rows = D // (lanes * depth)
    tail = (depth, 2, 2, 2)
    sources = [grad.reshape((-1,) + tail + (rows, D)) for grad in grads]
    chunks = []
    first = 0
    for i, source in enumerate(sources):
        for start in range(0, source.shape[0], 2):
            n = min(2, source.shape[0] - start)
            chunks.append((i, start, first, n, 0))
            first += n
    sets = [(first, (rows, D), jnp.bfloat16)]
    if small is not None:
        sources.append(small.reshape((1,) + tail + small.shape[1:]))
        chunks.insert(1, (len(sources) - 1, 0, 0, 1, 1))
        sets.append((1, small.shape[1:], jnp.float32))
    scratch = []
    for n, shape, kind in sets:
        scratch += [
            pltpu.VMEM((n, depth, 2, 2) + shape, kind),
            pltpu.VMEM((n, depth, 2, 2) + shape, kind),
            pltpu.VMEM((n, depth, 2) + shape, kind),
            pltpu.VMEM((n, depth) + shape, kind),
            pltpu.VMEM((n, depth) + shape, kind),
            pltpu.VMEM((n, 3) + shape, kind),
        ]
    outs = pl.pallas_call(
        functools.partial(reduce_kernel, chunks, len(sources), len(sets)),
        out_shape=[jax.ShapeDtypeStruct((n,) + shape, jnp.float32) for n, shape, _ in sets],
        in_specs=[pl.BlockSpec(memory_space=pl.ANY)] * len(sources),
        out_specs=[pl.BlockSpec(memory_space=pltpu.VMEM)] * len(sets),
        scratch_shapes=scratch
        + [
            pltpu.SemaphoreType.DMA((len(chunks),)),
            pltpu.SemaphoreType.DMA((len(chunks), 8)),
            pltpu.SemaphoreType.DMA((len(chunks), 8)),
        ],
        compiler_params=pltpu.CompilerParams(
            collective_id=collective, has_side_effects=True, vmem_limit_bytes=VMEM_LIMIT
        ),
        name=f"reduce_{collective}",
    )(*sources)
    return (outs[0], outs[1] if small is not None else None)


def spread_stages(own, out, local_sem, send, recv):
    d, z, _ = places()
    sib, near_x, near_y = flip(d, 1), flip(d, 2), flip(d, 4)
    diagonal = flip(near_x, 4)
    half = own.shape[0] // 2
    parts = (pl.ds(0, half), pl.ds(half, own.shape[0] - half))
    started = []
    last = []

    def push(slot, origin, part, to, source=None):
        copy = pltpu.make_async_remote_copy(
            src_ref=out.at[part, origin] if source is None else source,
            dst_ref=out.at[part, origin],
            send_sem=send.at[slot],
            recv_sem=recv.at[slot],
            device_id=to,
            device_id_type=MESH,
        )
        copy.start()
        started.append(copy)
        return copy

    keep = pltpu.make_async_copy(own, out.at[:, d], local_sem)
    near = {}
    turned = []

    def begin():
        for way, part in ((0, 0), (1, 1), (0, 1), (1, 0)):
            near[way, part] = push(
                2 * way + part, d, parts[part], ((near_x, near_y)[way], z), own.at[parts[part]]
            )
        keep.start()
        last.extend([push(4 + i, d, parts[i], (sib, z), own.at[parts[i]]) for i in (0, 1)])

    def forward():
        near[0, 0].wait_recv()
        turned.append(push(6, near_x, parts[0], (near_y, z)))
        last.append(push(7, near_x, parts[0], (sib, z)))
        near[1, 1].wait_recv()
        turned.append(push(8, near_y, parts[1], (near_x, z)))
        last.append(push(9, near_y, parts[1], (sib, z)))

    def collect():
        near[1, 0].wait_recv()
        last.append(push(10, near_y, parts[0], (sib, z)))
        near[0, 1].wait_recv()
        last.append(push(11, near_x, parts[1], (sib, z)))
        for i in (0, 1):
            turned[i].wait_recv()
            last.append(push(12 + i, diagonal, parts[i], (sib, z)))

    def finish():
        for copy in last:
            copy.wait_recv()
        for copy in started:
            copy.wait_send()
        keep.wait()

    return (begin, forward, collect, finish)


def spread_kernel(own, out, local_sem, send, recv):
    d, z, _ = places()
    greet([(flip(d, 1), z), (flip(d, 2), z), (flip(d, 4), z)])
    for stage in spread_stages(own, out, local_sem, send, recv):
        stage()


def spread(own, collective):
    lanes = lax.axis_size("dp")
    if lax.axis_size("fsdp") != 4 or lanes != 8:
        return lax.all_gather(own, "dp", axis=1)
    return pl.pallas_call(
        spread_kernel,
        out_shape=jax.ShapeDtypeStruct(own.shape[:1] + (lanes,) + own.shape[1:], own.dtype),
        in_specs=[pl.BlockSpec(memory_space=pltpu.VMEM)],
        out_specs=pl.BlockSpec(memory_space=pl.ANY),
        scratch_shapes=[
            pltpu.SemaphoreType.DMA,
            pltpu.SemaphoreType.DMA((14,)),
            pltpu.SemaphoreType.DMA((14,)),
        ],
        compiler_params=pltpu.CompilerParams(
            collective_id=collective, has_side_effects=True, vmem_limit_bytes=VMEM_LIMIT
        ),
        name=f"spread_{collective}",
    )(own)


def meet_kernel(own, parts, out, mine, local_sem, send, recv, part_send, part_recv):
    d, z, zs = places()
    sib, near_x, near_y = flip(d, 1), flip(d, 2), flip(d, 4)
    diagonal = flip(near_x, 4)
    others = [near_x, near_y, diagonal, sib, flip(near_x, 1), flip(near_y, 1), flip(diagonal, 1)]
    greet([(d, zs[1]), (d, zs[2]), (d, zs[3])] + [(other, z) for other in others])
    out[d, z] = own[...]

    def push(slot, source, target, to, sems=(send, recv)):
        copy = pltpu.make_async_remote_copy(
            src_ref=source,
            dst_ref=target,
            send_sem=sems[0].at[slot],
            recv_sem=sems[1].at[slot],
            device_id=to,
            device_id_type=MESH,
        )
        copy.start()
        return copy

    first = [push(o - 1, own, out.at[d, z], (d, zs[o])) for o in (1, 2, 3)]
    moved = [
        push(i, parts.at[other], mine.at[:, d], (other, z), (part_send, part_recv))
        for i, other in enumerate(others)
    ]
    keep = pltpu.make_async_copy(parts.at[d], mine.at[:, d], local_sem)
    keep.start()
    for copy in first:
        copy.wait_recv()
    second = [push(3 + i, out.at[d], out.at[d], (to, z)) for i, to in enumerate(others[:3])]
    last = [push(6, out.at[d], out.at[d], (sib, z))]
    for i, origin in enumerate(others[:3]):
        second[i].wait_recv()
        last.append(push(7 + i, out.at[origin], out.at[origin], (sib, z)))
    for copy in last + moved:
        copy.wait_recv()
    for copy in first + second + last + moved:
        copy.wait_send()
    keep.wait()


def meet(own, parts, collective):
    lanes, depth = lax.axis_size("dp"), lax.axis_size("fsdp")
    rest = parts.shape[1:]
    return pl.pallas_call(
        meet_kernel,
        out_shape=[
            jax.ShapeDtypeStruct((lanes, depth) + own.shape, own.dtype),
            jax.ShapeDtypeStruct(rest[:1] + (lanes,) + rest[1:], parts.dtype),
        ],
        in_specs=[pl.BlockSpec(memory_space=pltpu.VMEM)] * 2,
        out_specs=[pl.BlockSpec(memory_space=pltpu.VMEM)] * 2,
        scratch_shapes=[
            pltpu.SemaphoreType.DMA,
            pltpu.SemaphoreType.DMA((10,)),
            pltpu.SemaphoreType.DMA((10,)),
            pltpu.SemaphoreType.DMA((7,)),
            pltpu.SemaphoreType.DMA((7,)),
        ],
        compiler_params=pltpu.CompilerParams(
            collective_id=collective, has_side_effects=True, vmem_limit_bytes=VMEM_LIMIT
        ),
        name=f"meet_{collective}",
    )(own, parts)


GRAM_TILE = 128


def gram_kernel(gram, own, total, shards, left, right, onward, back, sems, local_sem, send, recv):
    d, z, _ = places()
    up, down = (z + 1, z - 1)
    two = jnp.logical_and(lax.rem(d, 2) == 1, d // 4 == 1)
    sib, near_x, near_y = flip(d, 1), flip(d, 2), flip(d, 4)
    greet([(d, lax.rem(z + step, 4)) for step in (1, 2, 3)] + [(sib, z), (near_x, z), (near_y, z)])
    stages = spread_stages(own, shards, local_sem, send, recv)
    stages[0]()
    count = D // GRAM_TILE

    def at(ref, slot, j):
        return ref.at[slot, pl.ds(j * GRAM_TILE, GRAM_TILE), pl.ds(j * GRAM_TILE, D - j * GRAM_TILE)]

    def copy(source, target, slot, j, way, to):
        return pltpu.make_async_remote_copy(
            src_ref=at(source, slot, j),
            dst_ref=at(target, slot, j),
            send_sem=sems.at[2 * way, slot, j],
            recv_sem=sems.at[2 * way + 1, slot, j],
            device_id=(d, to),
            device_id_type=MESH,
        )

    def add(target, slot, j, *terms):
        @pl.loop(0, GRAM_TILE // 16)
        def _(i):
            rows = pl.ds(pl.multiple_of(j * GRAM_TILE + i * 16, 16), 16)
            columns = pl.ds(j * GRAM_TILE, D - j * GRAM_TILE)
            value = terms[0][slot, rows, columns]
            for term in terms[1:]:
                value = value + term[slot, rows, columns]
            target[slot, rows, columns] = value

    def ends(slot):
        @pl.when(z == 0)
        def _():
            for j in range(count):
                copy(gram, left, slot, j, 0, up).start()

        @pl.when(z == 3)
        def _():
            for j in range(count):
                copy(gram, right, slot, j, 1, down).start()

    def near(slot, j):
        @pl.when(z == 1)
        def _():
            copy(onward, left, slot, j, 0, up).wait_recv()
            add(onward, slot, j, gram, left)
            copy(onward, left, slot, j, 0, up).start()

        @pl.when(z == 2)
        def _():
            copy(back, right, slot, j, 1, down).wait_recv()
            add(back, slot, j, gram, right)
            copy(back, right, slot, j, 1, down).start()

    def far(slot, j):
        @pl.when(z == 1)
        def _():
            copy(back, right, slot, j, 1, down).wait_recv()
            add(back, slot, j, gram, right)
            copy(back, right, slot, j, 1, down).start()
            add(total, slot, j, onward, right)

        @pl.when(z == 2)
        def _():
            copy(onward, left, slot, j, 0, up).wait_recv()
            add(onward, slot, j, gram, left)
            copy(onward, left, slot, j, 0, up).start()
            add(total, slot, j, onward, right)

    def close(slot, j):
        @pl.when(z == 3)
        def _():
            copy(gram, left, slot, j, 0, up).wait_recv()
            add(total, slot, j, left, gram)

        @pl.when(z == 0)
        def _():
            copy(gram, right, slot, j, 1, down).wait_recv()
            add(total, slot, j, gram, right)

    def finish(slot):
        for j in range(count):
            @pl.when(z == 0)
            def _():
                copy(gram, left, slot, j, 0, up).wait_send()

            @pl.when(z == 3)
            def _():
                copy(gram, right, slot, j, 1, down).wait_send()

            @pl.when(jnp.logical_and(z > 0, z < 3))
            def _():
                copy(onward, left, slot, j, 0, up).wait_send()
                copy(back, right, slot, j, 1, down).wait_send()

    def mirror(slot):
        for i in range(count):
            for j in range(i + 1, count):
                block = total[slot, i * GRAM_TILE : (i + 1) * GRAM_TILE, j * GRAM_TILE : (j + 1) * GRAM_TILE]
                total[slot, j * GRAM_TILE : (j + 1) * GRAM_TILE, i * GRAM_TILE : (i + 1) * GRAM_TILE] = block.T

    ends(0)

    @pl.when(two)
    def _():
        ends(1)

    def guarded(action, item):
        if item[0] == 0:
            action(*item)
        else:
            pl.when(two)(lambda: action(*item))

    skew = 2
    items = [(slot, j) for slot in (0, 1) for j in range(count)]
    for step in range(len(items) + skew):
        if step < len(items):
            guarded(near, items[step])
        if step >= skew:
            guarded(far, items[step - skew])
            guarded(close, items[step - skew])
        if step == 3:
            stages[1]()
        if step == count + 1:
            stages[2]()

    mirror(0)

    @pl.when(two)
    def _():
        mirror(1)

    finish(0)

    @pl.when(two)
    def _():
        finish(1)

    stages[3]()


def sum_grams(grams, own, collective):
    lanes = lax.axis_size("dp")
    whole = pltpu.VMEM(grams.shape, jnp.float32)
    return pl.pallas_call(
        gram_kernel,
        out_shape=[
            jax.ShapeDtypeStruct(grams.shape, jnp.float32),
            jax.ShapeDtypeStruct(own.shape[:1] + (lanes,) + own.shape[1:], own.dtype),
        ],
        in_specs=[pl.BlockSpec(memory_space=pltpu.VMEM)] * 2,
        out_specs=[
            pl.BlockSpec(memory_space=pltpu.VMEM),
            pl.BlockSpec(memory_space=pl.ANY),
        ],
        scratch_shapes=[
            whole,
            whole,
            whole,
            whole,
            pltpu.SemaphoreType.DMA((4, grams.shape[0], D // GRAM_TILE)),
            pltpu.SemaphoreType.DMA,
            pltpu.SemaphoreType.DMA((14,)),
            pltpu.SemaphoreType.DMA((14,)),
        ],
        compiler_params=pltpu.CompilerParams(
            collective_id=collective, has_side_effects=True, vmem_limit_bytes=VMEM_LIMIT
        ),
        name=f"gram_{collective}",
    )(grams, own)


def schulz_kernel(two, gram, rows, out, state, state_low, change, current):
    tile = 256

    def chain(slot, first, places_here, step):
        total = jnp.zeros((1, 1), jnp.float32)
        for t in range(0, D, tile):
            value = gram[slot, t : t + tile, :]
            line = lax.broadcasted_iota(jnp.int32, value.shape, 0) + t
            column = lax.broadcasted_iota(jnp.int32, value.shape, 1)
            total = total + jnp.sum(
                jnp.where(line == column, value, 0.0), axis=(0, 1), keepdims=True
            )
        inverse = 1.0 / (jnp.sqrt(total) + 1e-07)

        @pl.loop(0, D // tile)
        def _(t):
            part = pl.ds(pl.multiple_of(t * tile, tile), tile)
            value = gram[slot, part, :] * (inverse * inverse)
            state[part, :] = value
            state_low[part, :] = value.astype(jnp.bfloat16)

        for place in range(places_here):
            current[first + place] = rows[first + place] * inverse

        @pl.loop(0, NS_ITERS)
        def _(turn):
            @pl.loop(0, D // tile)
            def _(t):
                part = pl.ds(pl.multiple_of(t * tile, tile), tile)
                square = jnp.dot(
                    state_low[part, :], state_low[...], preferred_element_type=jnp.float32
                )
                change[part, :] = (COEF_B * state[part, :] + COEF_C * square).astype(jnp.bfloat16)

            @pl.loop(first, first + places_here)
            def _(place):
                value = current[place]
                current[place] = COEF_A * value + jnp.dot(
                    value.astype(jnp.bfloat16), change[...], preferred_element_type=jnp.float32
                )

            @pl.when(turn < NS_ITERS - 1)
            def _():
                @pl.loop(0, D // tile)
                def _(t):
                    part = pl.ds(pl.multiple_of(t * tile, tile), tile)
                    value = state[part, :]
                    for _ in range(2):
                        value = COEF_A * value + jnp.dot(
                            value.astype(jnp.bfloat16),
                            change[...],
                            preferred_element_type=jnp.float32,
                        )
                    state[part, :] = value
                    state_low[part, :] = value.astype(jnp.bfloat16)

        for place in range(places_here):
            out[first + place] = current[first + place].astype(jnp.bfloat16)

    @pl.when(two[0] == 0)
    def _():
        chain(0, 0, 4, 0)

    @pl.when(two[0] == 1)
    def _():
        chain(0, 0, 1, 0)
        chain(1, 1, 1, 0)
        for place in (2, 3):
            out[place] = jnp.zeros(out.shape[1:], jnp.bfloat16)


def schulz(two, grams, rows):
    return pl.pallas_call(
        schulz_kernel,
        out_shape=jax.ShapeDtypeStruct(rows.shape, jnp.bfloat16),
        in_specs=[
            pl.BlockSpec(memory_space=pltpu.SMEM),
            pl.BlockSpec(memory_space=pltpu.VMEM),
            pl.BlockSpec(memory_space=pltpu.VMEM),
        ],
        out_specs=pl.BlockSpec(memory_space=pltpu.VMEM),
        scratch_shapes=[
            pltpu.VMEM((D, D), jnp.float32),
            pltpu.VMEM((D, D), jnp.bfloat16),
            pltpu.VMEM((D, D), jnp.bfloat16),
            pltpu.VMEM(rows.shape, jnp.float32),
        ],
        compiler_params=pltpu.CompilerParams(vmem_limit_bytes=VMEM_LIMIT),
        name="schulz",
    )(two, grams, rows)


def update_kernel(table, scale, clip, momenta, grads, weights, turned, momenta_new, weights_new, weights_low):
    b = pl.program_id(0)
    momenta_new[...] = MOMENT * momenta[...] + clip[0] * grads[...].astype(jnp.float32)
    value = weights[...] * (1.0 - MUON_RATE * MUON_DECAY) - scale[b] * turned[0].astype(jnp.float32)
    weights_new[...] = value
    weights_low[...] = value.astype(jnp.bfloat16)


def update(home, scale, clip, momenta, grads, weights, turned):
    blocks, rows, width = weights.shape
    table = np.array([home[block][1] for block in range(blocks)] + [home[block][0] for block in range(blocks)], np.int32)
    block = pl.BlockSpec((1, rows, width), lambda b, *_: (b, 0, 0))
    return pl.pallas_call(
        update_kernel,
        grid_spec=pltpu.PrefetchScalarGridSpec(
            num_scalar_prefetch=3,
            grid=(blocks,),
            in_specs=[
                block,
                block,
                block,
                pl.BlockSpec(
                    (1, 1, rows, width),
                    lambda b, table, *_: (table[b], table[blocks + b], 0, 0),
                ),
            ],
            out_specs=[block, block, block],
        ),
        out_shape=[
            jax.ShapeDtypeStruct(weights.shape, jnp.float32),
            jax.ShapeDtypeStruct(weights.shape, jnp.float32),
            jax.ShapeDtypeStruct(weights.shape, jnp.bfloat16),
        ],
        compiler_params=pltpu.CompilerParams(vmem_limit_bytes=VMEM_LIMIT),
        name="update",
    )(jnp.asarray(table), jnp.asarray(scale), clip.reshape(1), momenta, grads, weights, turned)


GROUP = 4 * HD


def normed_head(value, gain):
    centred = value - jnp.mean(value, 0, keepdims=True)
    scale = lax.rsqrt(jnp.mean(centred * centred, 0, keepdims=True) + 1e-06)
    centred = centred * scale
    return (centred * gain, centred, scale)


def contract_first(left, right):
    return lax.dot_general(
        left, right, (((0,), (0,)), ((), ())), preferred_element_type=jnp.float32
    )


def contract_last(left, right):
    return lax.dot_general(
        left, right, (((1,), (1,)), ((), ())), preferred_element_type=jnp.float32
    )


def head_shares(query_low, key_low, same):
    scores = contract_first(key_low, query_low) * (1.0 / math.sqrt(HD))
    scores = jnp.where(same, scores, -1e30)
    exponent = jnp.exp(scores - jnp.max(scores, 0, keepdims=True))
    return exponent * (1.0 / jnp.sum(exponent, 0, keepdims=True))


def attend_kernel(query, key, value, gain_query, gain_key, rows, columns, out):
    same = rows[0] == columns[0]
    for head in range(GROUP // HD):
        part = slice(head * HD, (head + 1) * HD)
        query_low = normed_head(query[part], gain_query[part])[0].astype(jnp.bfloat16)
        key_low = normed_head(key[part], gain_key[part])[0].astype(jnp.bfloat16)
        share = head_shares(query_low, key_low, same).astype(jnp.bfloat16)
        out[part] = jnp.dot(
            value[part].astype(jnp.bfloat16), share, preferred_element_type=jnp.float32
        ).astype(jnp.bfloat16)


def attend_back_kernel(
    query, key, value, gain_query, gain_key, rows, columns, grad, out, gain_out
):
    same = rows[0] == columns[0]
    for head in range(GROUP // HD):
        part = slice(head * HD, (head + 1) * HD)
        query_value, query_unit, query_scale = normed_head(query[part], gain_query[part])
        key_value, key_unit, key_scale = normed_head(key[part], gain_key[part])
        query_low = query_value.astype(jnp.bfloat16)
        key_low = key_value.astype(jnp.bfloat16)
        value_low = value[part].astype(jnp.bfloat16)
        grad_low = grad[part]
        share = head_shares(query_low, key_low, same)
        out[2, part] = contract_last(grad_low, share.astype(jnp.bfloat16)).astype(jnp.bfloat16)
        share_grad = contract_first(value_low, grad_low)
        total = jnp.sum(share * share_grad, 0, keepdims=True)
        score_low = (share * (share_grad - total) * (1.0 / math.sqrt(HD))).astype(jnp.bfloat16)
        query_grad = jnp.dot(key_low, score_low, preferred_element_type=jnp.float32)
        key_grad = contract_last(query_low, score_low)
        for place, (delta, unit, scale, gain) in enumerate(
            (
                (query_grad, query_unit, query_scale, gain_query[part]),
                (key_grad, key_unit, key_scale, gain_key[part]),
            )
        ):
            gain_out[0, place, part] = jnp.sum(delta * unit, 1, keepdims=True)
            delta = delta * gain
            delta = delta - jnp.mean(delta, 0, keepdims=True) - unit * jnp.mean(
                delta * unit, 0, keepdims=True
            )
            out[place, part] = (delta * scale).astype(jnp.bfloat16)


def attention_specs(length):
    def rows_of(first):
        return pl.BlockSpec((GROUP, length), lambda b, group: (first + group, b))

    count = D // GROUP
    gain = pl.BlockSpec((GROUP, 1), lambda b, group: (group, 0))
    return [rows_of(0), rows_of(count), rows_of(2 * count), gain, gain] + [
        pl.BlockSpec((1, length, 1), lambda b, group: (b, 0, 0)),
        pl.BlockSpec((1, 1, length), lambda b, group: (b, 0, 0)),
    ]


def attention_operands(mixed, gains, segment):
    return (
        mixed,
        mixed,
        mixed,
        gains[4][:, None],
        gains[5][:, None],
        segment[:, :, None],
        segment[:, None, :],
    )


def attend(mixed, gains, segment):
    parts, length = segment.shape
    return pl.pallas_call(
        attend_kernel,
        grid=(parts, D // GROUP),
        in_specs=attention_specs(length),
        out_specs=pl.BlockSpec((GROUP, length), lambda b, group: (group, b)),
        out_shape=jax.ShapeDtypeStruct((D, parts * length), jnp.bfloat16),
        name="attend",
    )(*attention_operands(mixed, gains, segment))


def attend_back(mixed, gains, segment, grad):
    parts, length = segment.shape
    return pl.pallas_call(
        attend_back_kernel,
        grid=(parts, D // GROUP),
        in_specs=attention_specs(length)
        + [pl.BlockSpec((GROUP, length), lambda b, group: (group, b))],
        out_specs=[
            pl.BlockSpec((3, GROUP, length), lambda b, group: (0, group, b)),
            pl.BlockSpec((1, 2, GROUP, 1), lambda b, group: (b, 0, group, 0)),
        ],
        out_shape=[
            jax.ShapeDtypeStruct((3, D, parts * length), jnp.bfloat16),
            jax.ShapeDtypeStruct((parts, 2, D, 1), jnp.float32),
        ],
        name="attend_back",
    )(*attention_operands(mixed, gains, segment), grad)


def layer_forward(state, blocks, gains, segment):
    heads_in, norm_one = jax.vjp(layer_norm, state, gains[0], gains[1])
    heads_low = rounded(heads_in)
    mixed = product(blocks[0].reshape(3 * D, D), heads_low, "rd,sd->rs")
    attended_low = attend(mixed, gains, segment)
    state = state + product(attended_low, blocks[1].reshape(D, D), "rs,rd->sd")
    normed, norm_two = jax.vjp(layer_norm, state, gains[2], gains[3])
    normed_low = rounded(normed)
    hidden, gelu_back = jax.vjp(
        jax.nn.gelu, product(normed_low, blocks[2].reshape(FF, D), "sd,rd->sr")
    )
    hidden_low = rounded(hidden)
    state = state + product(hidden_low, blocks[3].reshape(FF, D), "sr,rd->sd")
    kept = (
        norm_one,
        heads_low,
        mixed,
        attended_low,
        norm_two,
        normed_low,
        gelu_back,
        hidden_low,
    )
    return (state, kept)


def layer_backward(grad, kept, blocks, gains, segment):
    norm_one, heads_low, mixed, attended_low, norm_two, normed_low, gelu_back, hidden_low = kept
    down = blocks[3].reshape(FF, D)
    upward = blocks[2].reshape(FF, D)
    grad_low = rounded(grad)
    grad_down = rounded(product(hidden_low, grad_low, "sr,sd->rd"))
    (grad_hidden,) = gelu_back(product(grad_low, down, "sd,rd->sr"))
    hidden_grad = rounded(grad_hidden)
    grad_up = rounded(product(hidden_grad, normed_low, "sr,sd->rd"))
    inner, gain_two, shift_two = norm_two(product(hidden_grad, upward, "sr,rd->sd"))
    grad = grad + inner
    grad_low = rounded(grad)
    grad_out = rounded(product(attended_low, grad_low, "rs,sd->rd"))
    attended_grad = rounded(product(blocks[1].reshape(D, D), grad_low, "rd,sd->rs"))
    mixed_low, head_gains = attend_back(mixed, gains, segment, attended_grad)
    head_gains = jnp.sum(head_gains[..., 0], 0)
    grad_mixed = rounded(product(mixed_low, heads_low, "krs,sd->krd"))
    inner, gain_one, shift_one = norm_one(
        product(
            mixed_low.reshape(3 * D, -1), blocks[0].reshape(3 * D, D), "rs,rd->sd"
        )
    )
    grad = grad + inner
    block_grads = [grad_mixed, grad_out, grad_up, grad_down]
    gain_grads = jnp.concatenate(
        [jnp.stack([gain_one, shift_one, gain_two, shift_two]), head_gains], 0
    )
    return (grad, block_grads, gain_grads)


def contrast_rows(scores, alive, own_live, rows):
    masked = jnp.where(alive[None, :] > 0, scores, -1e30)
    top = jax.scipy.special.logsumexp(masked, axis=1, keepdims=True)
    share = jnp.exp(masked - top)
    columns = jnp.arange(scores.shape[1], dtype=jnp.int32)
    target = (columns[None, :] == rows[:, None]).astype(jnp.float32)
    diagonal = jnp.sum(scores * target, 1)
    return ((top[:, 0] - diagonal) * own_live, (share - target) * own_live[:, None])


def muon_groups():
    found = [(0, 1), (1, 1)]
    for index in range(LAYERS):
        base = 2 + 12 * index
        found = found + [(base, 3), (base + 3, 1), (base + 4, 4), (base + 8, 4)]
    return found


def lane_plan(lanes):
    plan = [[] for _ in range(lanes)]
    for start, number in sorted(muon_groups(), key=lambda group: -group[1]):
        lane = min(range(lanes), key=lambda i: (sum(n for _, n in plan[i]), len(plan[i]), i))
        plan[lane].append((start, number))
    plan.sort(key=lambda entry: (-entry[0][1] if entry else 0))
    if lanes == 8:
        plan = [plan[i] for i in (0, 1, 2, 3, 4, 6, 5, 7)]
    depth = max(len(entry) for entry in plan)
    widths = [
        max([entry[slot][1] for entry in plan if slot < len(entry)]) for slot in range(depth)
    ]
    return (plan, widths)


def lane_blocks(plan):
    rows = [[start + i for start, number in entry for i in range(number)] for entry in plan]
    most = max(len(row) for row in rows)
    return np.array([row + [-1] * (most - len(row)) for row in rows], np.int32)


def lane_tables(plan, widths):
    index = np.zeros((len(plan), sum(widths)), np.int32)
    mask = np.zeros((len(plan), sum(widths)), np.float32)
    number = np.ones((len(plan), sum(widths)), np.float32)
    home = {}
    for lane, entry in enumerate(plan):
        first = 0
        for slot, width in enumerate(widths):
            if slot < len(entry):
                start, count = entry[slot]
                for place in range(count):
                    index[lane, first + place] = start + place
                    mask[lane, first + place] = 1.0
                    number[lane, first + place] = count
                    home[start + place] = (lane, first + place)
            first += width
    return (index, mask, number, home)


def orthogonal_factor(gram):
    size = jnp.sqrt(jnp.trace(gram)) + 1e-07
    state = gram / (size * size)
    total = None
    for turn in range(NS_ITERS):
        low = rounded(state)
        change = COEF_B * state + COEF_C * jnp.dot(low, low, preferred_element_type=jnp.float32)
        change_low = rounded(change)
        if total is None:
            total = COEF_A * jnp.eye(D, dtype=jnp.float32) + change
        else:
            total = COEF_A * total + jnp.dot(
                rounded(total), change_low, preferred_element_type=jnp.float32
            )
        if turn < NS_ITERS - 1:
            for _ in range(2):
                state = COEF_A * state + jnp.dot(
                    rounded(state), change_low, preferred_element_type=jnp.float32
                )
    return total / size


def per_device(
    patches, grid, segments, text_ids, table, weights, momenta, gains, gains_m, gains_v, step
):
    fin = 6 * LAYERS
    base = fin + 3
    lanes = lax.axis_size("dp")
    slots = jnp.arange(IMGS, dtype=jnp.int32)
    live = jnp.any(segments[:, 0, None, :] == slots[None, :, None], -1).astype(jnp.float32)
    depth = lax.axis_size("fsdp")
    captions = MB * IMGS
    ids = jnp.broadcast_to(text_ids.reshape(1, captions, -1), (depth, captions, text_ids.shape[3]))
    ids = swap(ids, 10)
    stem, *first_blocks = fetch(weights, [(0, 1), (2, 3), (5, 1), (6, 4), (10, 4)], 1)
    flat_ids = ids.reshape(depth * captions, -1)
    share_rows = table.shape[0]
    picked = flat_ids - lax.axis_index("fsdp") * share_rows
    hits = jnp.sum(
        (picked[:, :, None] == jnp.arange(share_rows, dtype=jnp.int32)[None, None, :]).astype(
            jnp.int32
        ),
        1,
    )
    parts = jnp.dot(rounded(hits.astype(jnp.float32)), table, preferred_element_type=jnp.float32)
    text_sum = jnp.sum(swap(parts.reshape(depth, captions, D), 11), 0)
    text_low = rounded(unit_rows(text_sum / text_ids.shape[-1]))
    me = lax.axis_index(("dp", "fsdp"))
    segment = segments[:, 0]
    rows_hot, cols_hot = jax.vmap(positions)(grid[:, 0])
    rows_hot = rows_hot.reshape(-1, POS)
    cols_hot = cols_hot.reshape(-1, POS)
    patch_low = patches.reshape(-1, D)
    state = product(patch_low, stem[0], "sd,rd->sr")
    state = state + jnp.dot(rows_hot, gains[base : base + POS], precision=HIGH)
    state = state + jnp.dot(cols_hot, gains[base + POS : base + 2 * POS], precision=HIGH)
    saved = []
    for index in range(LAYERS):
        if index == 0:
            blocks = first_blocks
        else:
            start = 2 + 12 * index
            pieces = [(start, 3), (start + 3, 1), (start + 4, 4), (start + 8, 4)]
            if index == 1:
                pieces = pieces + [(1, 1)]
            blocks = fetch(weights, pieces, 2 + index)
            if index == 1:
                pooling_matrix = blocks.pop()[0]
        state, kept = layer_forward(state, blocks, gains[6 * index : 6 * index + 6], segment)
        saved.append((kept, blocks))
    final, norm_final = jax.vjp(layer_norm, state, gains[fin], gains[fin + 1])

    def pool_all(values, query):
        split = values.reshape(MB, -1, D)
        return jnp.concatenate([pooling(segment[part])(split[part], query) for part in range(MB)])

    pooled, pool_back = jax.vjp(pool_all, final, gains[fin + 2])
    pooled_low = rounded(pooled)
    embedded, unit_back = jax.vjp(unit_rows, product(pooled_low, pooling_matrix, "kr,rd->kd"))
    image_low = rounded(embedded)
    flags = jnp.broadcast_to(live.reshape(1, captions, 1), (1, captions, D)).astype(jnp.bfloat16)
    both = jnp.concatenate([image_low[None], text_low[None], flags], 0).reshape(3 * captions, D)
    whole = share(both, 8).reshape(-1, 3, MB, IMGS, D)
    flags = whole[:, 2, :, :, 0].astype(jnp.float32)
    count = jnp.sum(flags)
    factor = 1.0 / (2.0 * count)
    loss_part = jnp.float32(0.0)
    image_grads = []
    for part in range(MB):
        images = whole[:, 0, part].reshape(-1, D)
        texts = whole[:, 1, part].reshape(-1, D)
        alive = flags[:, part].reshape(-1)
        own_image = image_low[part * IMGS : (part + 1) * IMGS]
        forward = LOGIT_SCALE * product(own_image, texts, "kd,nd->kn")
        backward = LOGIT_SCALE * product(texts, images, "kd,nd->kn")
        own = me * IMGS + jnp.arange(IMGS, dtype=jnp.int32)
        everyone = jnp.arange(alive.shape[0], dtype=jnp.int32)
        term_f, grad_f = contrast_rows(forward, alive, live[part], own)
        term_b, grad_b = contrast_rows(backward, alive, alive, everyone)
        own_terms = jnp.sum(jnp.where((everyone // IMGS) == me, term_b, 0.0))
        loss_part = loss_part + (jnp.sum(term_f) + own_terms) * factor
        forward_low = rounded(grad_f * factor * LOGIT_SCALE)
        backward_low = rounded(
            lax.dynamic_slice_in_dim(grad_b, me * IMGS, IMGS, 1) * factor * LOGIT_SCALE
        )
        image_grads.append(
            product(forward_low, texts, "kn,nd->kd") + product(backward_low, texts, "nk,nd->kd")
        )
    image_grad = jnp.concatenate(image_grads, 0)
    (embed_grad,) = unit_back(image_grad)
    embed_low = rounded(embed_grad)
    grad_pool = rounded(product(pooled_low, embed_low, "kr,kd->rd"))
    final_grad, query_grad = pool_back(product(embed_low, pooling_matrix, "kd,rd->kr"))
    grad, gain_final, shift_final = norm_final(final_grad)
    gain_parts = [None] * LAYERS
    block_grads = [None] * LAYERS
    fast = depth == 4 and lanes == 8
    slices = [None] * LAYERS
    for index in reversed(range(LAYERS)):
        kept, blocks = saved[index]
        grad, block_grads[index], gain_parts[index] = layer_backward(
            grad, kept, blocks, gains[6 * index : 6 * index + 6], segment
        )
        if index == 1:
            block_grads[index].append(grad_pool)
        if fast and index > 0:
            slices[index], _ = reduce_grads(block_grads[index], None, 4 + index)
    grad_low = rounded(grad)
    grad_patch = rounded(product(grad_low, patch_low, "sr,sd->rd"))
    block_grads[0].append(grad_patch)
    grad_rows = jnp.dot(rows_hot.T, grad, precision=HIGH)
    grad_cols = jnp.dot(cols_hot.T, grad, precision=HIGH)
    gains_grad = jnp.concatenate(
        gain_parts
        + [jnp.stack([gain_final, shift_final, query_grad]), grad_rows, grad_cols],
        0,
    )
    plan, widths = lane_plan(lanes)
    index, mask, number, home = lane_tables(plan, widths)
    lane = lax.axis_index("dp")
    scale = np.ones((weights.shape[0],), np.float32)
    for start, count_blocks in muon_groups():
        scale[start : start + count_blocks] = MUON_RATE * math.sqrt(count_blocks)
    if fast:
        width = 256
        small = jnp.concatenate([gains_grad.reshape(-1), loss_part[None]])
        small = jnp.pad(small, (0, lanes * depth * 8 * width - small.shape[0]))
        slices[0], small = reduce_grads(
            block_grads[0], small.reshape(lanes * depth, 8, width), 4
        )
        squares = jnp.sum(slices[0] * slices[0]) + jnp.sum(slices[1] * slices[1])
        slices = [rounded(value) for value in slices]
        slices = jnp.concatenate(
            [slices[0][12:], slices[1][12:]] + [values[:12] for values in slices], 0
        )
        empty = jnp.zeros((1,) + slices.shape[1:], slices.dtype)
        parts = jnp.concatenate(
            [
                slices[block : block + 1] if block >= 0 else empty
                for block in lane_blocks(plan).reshape(-1)
            ],
            0,
        ).reshape((lanes, -1) + slices.shape[1:])
        squares = jnp.broadcast_to(squares, (8, width))
        shared, mine = meet(jnp.concatenate([small[0], squares], 0), parts, 9)
        flat = jnp.transpose(shared[:, :, :8], (1, 0, 2, 3)).reshape(-1)
        gains_grad, loss = (flat[: gains.size].reshape(gains.shape), flat[gains.size])
        squares = jnp.sum(shared[:, :, 8, 0])
        norm = jnp.sqrt(squares + jnp.sum(gains_grad * gains_grad))
        clip = jnp.minimum(1.0, CLIP_LIMIT / (norm + 1e-06))
        blocks_here = lane_blocks(plan)
        own_momenta = jnp.stack(
            [
                jnp.where(
                    jnp.asarray(blocks_here >= 0)[lane, place],
                    lax.dynamic_index_in_dim(
                        momenta, jnp.maximum(jnp.asarray(blocks_here)[lane, place], 0), 0, False
                    ),
                    0.0,
                )
                for place in range(blocks_here.shape[1])
            ]
        )
        own = MOMENT * own_momenta + clip * mine.reshape(own_momenta.shape).astype(jnp.float32)
        two = jnp.asarray(np.array([len(entry) > 1 for entry in plan], np.int32))[lane]
        own_low = rounded(own)
        first_low = jnp.concatenate(
            [own_low[:1], jnp.where(two > 0, jnp.bfloat16(0), own_low[1:])], 0
        )
        grams = jnp.stack(
            [
                product(first_low, first_low, "brd,bre->de"),
                product(own_low[1], own_low[1], "rd,re->de"),
            ]
        )
        grams, shard_grads = sum_grams(grams, slices, 12)
        turned = spread(schulz(two.reshape(1), grams, own), 13)
        homes = {
            int(block): (lane_of, place)
            for lane_of, entry in enumerate(blocks_here)
            for place, block in enumerate(entry)
            if block >= 0
        }
        momenta_new, weights_new, weights_low = update(
            homes, scale, clip, momenta, shard_grads.reshape(weights.shape), weights, turned
        )
    else:
        stack = jnp.concatenate(
            [block_grads[index].pop().reshape(1, D, D) for index in range(LAYERS)]
            + [value.reshape(-1, D, D) for values in block_grads for value in values],
            0,
        )
        shard_grads = lax.psum(
            lax.psum_scatter(stack, "fsdp", scatter_dimension=1, tiled=True), "dp"
        ).astype(jnp.float32)
        gains_grad, loss = lax.psum((gains_grad, loss_part), ("dp", "fsdp"))
        squares = lax.psum(jnp.sum(shard_grads * shard_grads), "fsdp")
        norm = jnp.sqrt(squares + jnp.sum(gains_grad * gains_grad))
        clip = jnp.minimum(1.0, CLIP_LIMIT / (norm + 1e-06))
        momenta_new = MOMENT * momenta + clip * shard_grads
        own = jnp.stack(
            [
                lax.dynamic_index_in_dim(momenta_new, jnp.asarray(index)[lane, place], 0, False)
                * jnp.asarray(mask)[lane, place]
                for place in range(index.shape[1])
            ]
        )
        own_low = rounded(own)
        bounds = np.cumsum([0] + widths)
        grams = jnp.stack(
            [
                product(own_low[a:b], own_low[a:b], "brd,bre->de")
                for a, b in zip(bounds[:-1], bounds[1:])
            ]
        )
        grams = lax.psum(grams, "fsdp")
        turned = jnp.concatenate(
            [
                product(
                    own_low[bounds[slot] : bounds[slot + 1]],
                    rounded(orthogonal_factor(grams[slot])),
                    "brd,de->bre",
                )
                for slot in range(len(widths))
            ],
            0,
        )
        spread_rows = lax.all_gather(rounded(turned), "dp", axis=0)
        current = jnp.stack(
            [spread_rows[home[block][0], home[block][1]] for block in range(weights.shape[0])]
        ).astype(jnp.float32)
        weights_new = weights * (1.0 - MUON_RATE * MUON_DECAY) - jnp.asarray(scale)[:, None, None] * current
        weights_low = rounded(weights_new)
    grad_small = clip * gains_grad
    moment_one = BETA_ONE * gains_m + (1.0 - BETA_ONE) * grad_small
    moment_two = BETA_TWO * gains_v + (1.0 - BETA_TWO) * grad_small * grad_small
    count_steps = step[0].astype(jnp.float32)
    corrected_one = moment_one / (1.0 - jnp.power(BETA_ONE, count_steps))
    corrected_two = moment_two / (1.0 - jnp.power(BETA_TWO, count_steps))
    gains_new = gains - ADAM_RATE * (
        corrected_one / (jnp.sqrt(corrected_two) + ADAM_EPS) + ADAM_DECAY * gains
    )
    shift_grad = grad_small[fin + 1]
    return (
        loss,
        norm,
        weights_new,
        weights_low,
        momenta_new,
        gains_new,
        moment_one,
        moment_two,
        shift_grad,
    )


def solution(mesh):
    placed = (
        P(None, ("dp", "fsdp"), None, None),
        P(None, ("dp", "fsdp"), None, None),
        P(None, ("dp", "fsdp"), None),
        P(None, ("dp", "fsdp"), None, None),
        P("fsdp", None),
        P(None, "fsdp", None),
        P(None, "fsdp", None),
        P(),
        P(),
        P(),
        P(),
    )
    return jax.shard_map(
        per_device,
        mesh=mesh,
        in_specs=placed,
        out_specs=(
            P(),
            P(),
            P(None, "fsdp", None),
            P(None, "fsdp", None),
            P(None, "fsdp", None),
            P(),
            P(),
            P(),
            P(),
        ),
        check_vma=False,
    )
```

```python
import functools
import math

import jax
import jax.numpy as jnp
import numpy as np
from jax import lax
from jax.experimental import pallas as pl
from jax.experimental.pallas import tpu as pltpu
from jax.sharding import PartitionSpec as P

D = 768
HEADS = 12
FF = 3072
LAYERS = 2
IMGS = 8
POS = 32
MB = 2
NS_ITERS = 5
HD = 64


MESH = pl.DeviceIdType.MESH
VMEM_LIMIT = 56 * 1024 * 1024
HIGH = lax.Precision.HIGHEST
LOGIT_SCALE = 50.0
CLIP_LIMIT = 0.005
MOMENT = 0.95
MUON_RATE = 0.5
MUON_DECAY = 0.01
ADAM_RATE = 0.4
BETA_ONE = 0.9
BETA_TWO = 0.999
ADAM_EPS = 1e-08
ADAM_DECAY = 0.01
COEF_A = 3.4445
COEF_B = -4.775
COEF_C = 2.0315


def rounded(value):
    return value.astype(jnp.bfloat16)


def product(left, right, form):
    return jnp.einsum(form, left, right, preferred_element_type=jnp.float32)


def unit_rows(value):
    return (
        value
        * lax.rsqrt(jnp.mean(value * value, -1, keepdims=True) + 1e-06)
        * (1.0 / math.sqrt(value.shape[-1]))
    )


def positions(grid):
    slots = jnp.arange(POS, dtype=jnp.int32)
    row_index = grid[0] * POS // grid[2]
    col_index = grid[1] * POS // grid[3]
    return (
        (row_index[:, None] == slots[None]).astype(jnp.float32),
        (col_index[:, None] == slots[None]).astype(jnp.float32),
    )


def flip(index, bit):
    return index + bit - 2 * bit * lax.rem(index // bit, 2)


def greet(peers):
    barrier = pltpu.get_barrier_semaphore()
    for peer in peers:
        pl.semaphore_signal(barrier, inc=1, device_id=peer, device_id_type=MESH)
    pl.semaphore_wait(barrier, len(peers))


def places():
    d = lax.axis_index("dp")
    z = lax.axis_index("fsdp")
    return (d, z, [lax.rem(z + step, 4) for step in range(4)])


def fetch_kernel(chunks, sizes, later, weights, ids, *refs):
    outs = refs[: len(sizes)]
    all_ids, slices = refs[len(sizes) : len(sizes) + 2]
    full, low, held, load_sem, store_sem, send, recv, later_sem, id_send, id_recv = refs[
        len(sizes) + 2 :
    ]
    d, z, zs = places()
    sib, near_x, near_y = flip(d, 1), flip(d, 2), flip(d, 4)
    diagonal = flip(near_x, 4)
    starts = [sum(chunk[3] for chunk in chunks[:k]) for k in range(len(chunks))]
    loads = []
    for k, (source, _, _, n) in enumerate(chunks):
        loads.append(
            pltpu.make_async_copy(
                weights.at[pl.ds(source, n)], full.at[pl.ds(starts[k], n)], load_sem.at[k]
            )
        )
        loads[k].start()
    later_loads = [
        pltpu.make_async_copy(
            weights.at[pl.ds(first, n), d], held.at[pl.ds(place, n)], later_sem.at[i]
        )
        for i, (first, place, n) in enumerate(later)
    ]
    for copy in later_loads:
        copy.start()
    greet([(d, zs[1]), (d, zs[2]), (d, zs[3]), (sib, z), (near_x, z), (near_y, z)])
    pending = []
    all_ids[z] = ids[...]
    id_copies = []
    for o in (1, 2, 3):
        id_copies.append(
            pltpu.make_async_remote_copy(
                src_ref=ids,
                dst_ref=all_ids.at[z],
                send_sem=id_send.at[o - 1],
                recv_sem=id_recv.at[o - 1],
                device_id=(d, zs[o]),
                device_id_type=MESH,
            )
        )
        id_copies[-1].start()

    def push(k, slot, first, n, zz, dd, to, source=None):
        out = outs[chunks[k][1]]
        rows = pl.ds(chunks[k][2] + first, n)
        copy = pltpu.make_async_remote_copy(
            src_ref=out.at[rows, zz, dd] if source is None else source,
            dst_ref=out.at[rows, zz, dd],
            send_sem=send.at[k, slot],
            recv_sem=recv.at[k, slot],
            device_id=to,
            device_id_type=MESH,
        )
        copy.start()
        pending.append(copy)
        return copy

    along_z = []
    stores = []
    for k, (_, out, offset, n) in enumerate(chunks):
        loads[k].wait()

        @pl.loop(starts[k], starts[k] + n)
        def _(i):
            low[i] = full[i].astype(low.dtype)

        along_z.append(
            [
                push(k, o - 1, 0, n, z, d, (d, zs[o]), low.at[pl.ds(starts[k], n), d])
                for o in (1, 2, 3)
            ]
        )
        stores.append(
            pltpu.make_async_copy(
                low.at[pl.ds(starts[k], n)],
                outs[out].at[pl.ds(offset, n), z],
                store_sem.at[k],
            )
        )
        stores[k].start()
    for copy in later_loads:
        copy.wait()

    @pl.loop(0, held.shape[0])
    def _(i):
        slices[i] = held[i].astype(slices.dtype)

    along_x, along_y, turn_y, turn_x, last = {}, {}, {}, {}, []
    count = len(chunks)
    for step in range(count + 2):
        if step < count:
            k, n = step, chunks[step][3]
            along_x[k], along_y[k] = [], []
            for o in (1, 2, 3):
                zz = zs[4 - o]
                along_z[k][o - 1].wait_recv()
                along_x[k].append(push(k, 2 + o, 0, n, zz, d, (near_x, z)))
                along_y[k].append(push(k, 5 + o, 0, n, zz, d, (near_y, z)))
                last.append(push(k, 14 + o, 0, n, zz, d, (sib, z)))
        if 1 <= step <= count:
            k, n = step - 1, chunks[step - 1][3]
            half = n // 2
            turn_y[k], turn_x[k] = [], []
            for o in (1, 2, 3):
                zz = zs[4 - o]
                along_x[k][o - 1].wait_recv()
                if half:
                    turn_y[k].append(push(k, 8 + o, 0, half, zz, near_x, (near_y, z)))
                last.append(push(k, 17 + o, 0, n, zz, near_x, (sib, z)))
                along_y[k][o - 1].wait_recv()
                turn_x[k].append(push(k, 11 + o, half, n - half, zz, near_y, (near_x, z)))
                last.append(push(k, 20 + o, 0, n, zz, near_y, (sib, z)))
        if step >= 2:
            k, n = step - 2, chunks[step - 2][3]
            for o in (1, 2, 3):
                for copies in (turn_y[k], turn_x[k]):
                    if copies:
                        copies[o - 1].wait_recv()
                last.append(push(k, 23 + o, 0, n, zs[4 - o], diagonal, (sib, z)))
    for copy in last:
        copy.wait_recv()
    for copy in pending:
        copy.wait_send()
    for copy in stores:
        copy.wait()
    for copy in id_copies:
        copy.wait()


def fetch(weights, pieces, later, ids, collective):
    depth, eighths = lax.axis_size("fsdp"), lax.axis_size("dp")
    if depth != 4 or eighths != 8:
        return (
            [
                lax.all_gather(rounded(weights[a : a + n]), "fsdp", axis=1, tiled=True)
                for a, n in pieces
            ],
            lax.all_gather(ids, "fsdp", axis=0),
            jnp.concatenate([rounded(weights[a : a + n]) for a, n in later], 0),
        )
    blocks, rows, width = weights.shape
    part = (eighths, rows // eighths, width)
    chunks = []
    for out, (a, n) in enumerate(pieces):
        for first in range(0, n, 2):
            chunks.append((a + first, out, first, min(2, n - first)))
    total = sum(n for _, n in pieces)
    later_places = []
    for a, n in later:
        later_places.append((a, sum(m for _, _, m in later_places), n))
    later_total = sum(n for _, n in later)
    outs = pl.pallas_call(
        functools.partial(fetch_kernel, chunks, [n for _, n in pieces], later_places),
        out_shape=[
            jax.ShapeDtypeStruct((n, depth) + part, jnp.bfloat16) for _, n in pieces
        ]
        + [
            jax.ShapeDtypeStruct((depth,) + ids.shape, ids.dtype),
            jax.ShapeDtypeStruct((later_total,) + part[1:], jnp.bfloat16),
        ],
        in_specs=[pl.BlockSpec(memory_space=pl.ANY), pl.BlockSpec(memory_space=pltpu.VMEM)],
        out_specs=[pl.BlockSpec(memory_space=pl.ANY)] * len(pieces)
        + [pl.BlockSpec(memory_space=pltpu.VMEM)] * 2,
        scratch_shapes=[
            pltpu.VMEM((total,) + part, jnp.float32),
            pltpu.VMEM((total,) + part, jnp.bfloat16),
            pltpu.VMEM((later_total,) + part[1:], jnp.float32),
            pltpu.SemaphoreType.DMA((len(chunks),)),
            pltpu.SemaphoreType.DMA((len(chunks),)),
            pltpu.SemaphoreType.DMA((len(chunks), 27)),
            pltpu.SemaphoreType.DMA((len(chunks), 27)),
            pltpu.SemaphoreType.DMA((len(later),)),
            pltpu.SemaphoreType.DMA((3,)),
            pltpu.SemaphoreType.DMA((3,)),
        ],
        compiler_params=pltpu.CompilerParams(
            collective_id=collective, has_side_effects=True, vmem_limit_bytes=VMEM_LIMIT
        ),
        name=f"fetch_{collective}",
    )(weights.reshape((blocks,) + part), ids)
    return ([out.reshape(-1, width, width) for out in outs[:-2]], outs[-2], outs[-1])


def gather_later(own):
    depth, eighths = lax.axis_size("fsdp"), lax.axis_size("dp")
    if depth != 4 or eighths != 8:
        return lax.all_gather(own, "fsdp", axis=1, tiled=True)
    return lax.all_gather(own, ("fsdp", "dp"), axis=1).reshape(-1, D, D)


def share_kernel(count, *refs):
    owns, outs, (send, recv) = (refs[:count], refs[count : 2 * count], refs[2 * count :])
    d, z, zs = places()
    sib, near_x, near_y = flip(d, 1), flip(d, 2), flip(d, 4)
    diagonal = flip(near_x, 4)
    greet(
        [(d, zs[1]), (d, zs[2]), (d, zs[3]), (sib, z), (near_x, z), (near_y, z), (diagonal, z)]
    )
    for own, out in zip(owns, outs):
        out[d, z] = own[...]
    started = []

    def push(slot, origin, to, first=False):
        copies = []
        for i in range(count):
            copies.append(
                pltpu.make_async_remote_copy(
                    src_ref=owns[i] if first else outs[i].at[origin],
                    dst_ref=outs[i].at[origin, z] if first else outs[i].at[origin],
                    send_sem=send.at[i, slot],
                    recv_sem=recv.at[i, slot],
                    device_id=to,
                    device_id_type=MESH,
                )
            )
            copies[-1].start()
        started.extend(copies)
        return copies

    def arrive(copies):
        for copy in copies:
            copy.wait_recv()

    first = [push(o - 1, d, (d, zs[o]), True) for o in (1, 2, 3)]
    for copies in first:
        arrive(copies)
    second = [push(3 + i, d, (to, z)) for i, to in enumerate((near_x, near_y, diagonal))]
    last = [push(6, d, (sib, z))]
    for i, origin in enumerate((near_x, near_y, diagonal)):
        arrive(second[i])
        last.append(push(7 + i, origin, (sib, z)))
    for copies in last:
        arrive(copies)
    for copy in started:
        copy.wait_send()


def share(owns, collective):
    lanes, depth = lax.axis_size("dp"), lax.axis_size("fsdp")
    if depth != 4 or lanes != 8:
        return [
            lax.all_gather(own, ("dp", "fsdp"), axis=0).reshape((lanes, depth) + own.shape)
            for own in owns
        ]
    count = len(owns)
    return pl.pallas_call(
        functools.partial(share_kernel, count),
        out_shape=[jax.ShapeDtypeStruct((lanes, depth) + own.shape, own.dtype) for own in owns],
        in_specs=[pl.BlockSpec(memory_space=pltpu.VMEM)] * count,
        out_specs=[pl.BlockSpec(memory_space=pltpu.VMEM)] * count,
        scratch_shapes=[
            pltpu.SemaphoreType.DMA((count, 10)),
            pltpu.SemaphoreType.DMA((count, 10)),
        ],
        compiler_params=pltpu.CompilerParams(collective_id=collective, has_side_effects=True),
        name=f"share_{collective}",
    )(*owns)


def swap_kernel(parts, out, send, recv):
    d, z, zs = places()
    greet([(d, zs[1]), (d, zs[2]), (d, zs[3])])
    out[z] = parts[z]
    copies = []
    for o in (1, 2, 3):
        copies.append(
            pltpu.make_async_remote_copy(
                src_ref=parts.at[zs[o]],
                dst_ref=out.at[z],
                send_sem=send.at[o - 1],
                recv_sem=recv.at[o - 1],
                device_id=(d, zs[o]),
                device_id_type=MESH,
            )
        )
        copies[-1].start()
    for copy in copies:
        copy.wait()


def swap(parts, collective):
    depth = lax.axis_size("fsdp")
    if depth != 4 or lax.axis_size("dp") != 8:
        return lax.all_to_all(parts, "fsdp", 0, 0)
    return pl.pallas_call(
        swap_kernel,
        out_shape=jax.ShapeDtypeStruct(parts.shape, parts.dtype),
        in_specs=[pl.BlockSpec(memory_space=pltpu.VMEM)],
        out_specs=pl.BlockSpec(memory_space=pltpu.VMEM),
        scratch_shapes=[pltpu.SemaphoreType.DMA((3,)), pltpu.SemaphoreType.DMA((3,))],
        compiler_params=pltpu.CompilerParams(collective_id=collective, has_side_effects=True),
        name=f"swap_{collective}",
    )(parts)


class Reduction:
    def __init__(self, source, start, first, n, buffers, k, semaphores, spots):
        self.source, self.start, self.first, self.n, self.k = (source, start, first, n, k)
        self.held, self.from_core, self.from_near, self.from_turn, self.ready, self.from_z = buffers
        self.local_sem, self.send, self.recv = semaphores
        self.spots = spots
        self.rows = pl.ds(first, n)
        self.started = []

    def push(self, slot, source, target, to):
        copy = pltpu.make_async_remote_copy(
            src_ref=source,
            dst_ref=target,
            send_sem=self.send.at[self.k, slot],
            recv_sem=self.recv.at[self.k, slot],
            device_id=to,
            device_id_type=MESH,
        )
        copy.start()
        self.started.append(copy)
        return copy

    def begin(self):
        d, z, zs, x, y, c = self.spots
        blocks = pl.ds(self.start, self.n)
        self.local = pltpu.make_async_copy(
            self.source.at[blocks, :, :, :, c], self.held.at[self.rows], self.local_sem.at[self.k]
        )
        self.local.start()
        self.core = self.push(
            0,
            self.source.at[blocks, :, :, :, 1 - c],
            self.from_core.at[self.rows],
            (flip(d, 1), z),
        )

    def add(self, count, place):
        @pl.loop(0, self.n * count)
        def _(i):
            target, other = place(self.first + i // count, lax.rem(i, count))
            self.held[target] = self.held[target] + other

    def across_plane(self):
        d, z, zs, x, y, c = self.spots
        self.local.wait()
        self.core.wait_recv()

        def place(b, i):
            target = (b, i // 4, lax.rem(i // 2, 2), lax.rem(i, 2))
            return (target, self.from_core[target])

        self.add(16, place)
        self.near = [
            self.push(
                1,
                self.held.at[self.rows, 0:2, :, 1 - x],
                self.from_near.at[self.rows, 0:2],
                (flip(d, 2), z),
            ),
            self.push(
                2,
                self.held.at[self.rows, 2:4, 1 - y],
                self.from_near.at[self.rows, 2:4],
                (flip(d, 4), z),
            ),
        ]

    def turn(self):
        d, z, zs, x, y, c = self.spots

        def place_a(b, i):
            return ((b, i // 2, lax.rem(i, 2), x), self.from_near[b, i // 2, lax.rem(i, 2)])

        def place_b(b, i):
            return ((b, 2 + i // 2, y, lax.rem(i, 2)), self.from_near[b, 2 + i // 2, lax.rem(i, 2)])

        self.near[0].wait_recv()
        self.add(4, place_a)
        a = self.push(
            3,
            self.held.at[self.rows, 0:2, 1 - y, x],
            self.from_turn.at[self.rows, 0:2],
            (flip(d, 4), z),
        )
        self.near[1].wait_recv()
        self.add(4, place_b)
        b = self.push(
            4,
            self.held.at[self.rows, 2:4, y, 1 - x],
            self.from_turn.at[self.rows, 2:4],
            (flip(d, 2), z),
        )
        self.turned = [a, b]

    def along_z(self):
        d, z, zs, x, y, c = self.spots
        for copy in self.turned:
            copy.wait_recv()

        @pl.loop(0, self.n * 4)
        def _(i):
            b, zz = (self.first + i // 4, lax.rem(i, 4))
            self.ready[b, zz] = self.held[b, zz, y, x] + self.from_turn[b, zz]

        self.spread = [
            self.push(
                4 + o,
                self.ready.at[self.rows, zs[o]],
                self.from_z.at[self.rows, o - 1],
                (d, zs[o]),
            )
            for o in (1, 2, 3)
        ]

    def finish(self, out):
        d, z, zs, x, y, c = self.spots
        for copy in self.spread:
            copy.wait_recv()

        @pl.loop(self.first, self.first + self.n)
        def _(b):
            total = self.held[b, z, y, x].astype(jnp.float32) + self.from_turn[b, z].astype(
                jnp.float32
            )
            for o in range(3):
                total = total + self.from_z[b, o].astype(jnp.float32)
            out[b] = total

        for copy in self.started:
            copy.wait_send()


def reduce_kernel(chunks, sources, sets, *refs):
    ins = refs[:sources]
    outs = refs[sources : sources + sets]
    buffers = [refs[sources + sets + 6 * i : sources + sets + 6 * i + 6] for i in range(sets)]
    semaphores = refs[sources + 7 * sets :]
    d, z, zs = places()
    spots = (d, z, zs, lax.rem(d // 2, 2), d // 4, lax.rem(d, 2))
    greet([(d, zs[1]), (d, zs[2]), (d, zs[3]), (flip(d, 1), z), (flip(d, 2), z), (flip(d, 4), z)])
    work = []
    for k, (source, start, first, n, which) in enumerate(chunks):
        work.append(
            Reduction(ins[source], start, first, n, buffers[which], k, semaphores, spots)
        )
        work[k].begin()
    count = len(chunks)
    for step in range(count + 3):
        if step < count:
            work[step].across_plane()
        if 1 <= step <= count:
            work[step - 1].turn()
        if 2 <= step <= count + 1:
            work[step - 2].along_z()
        if step >= 3:
            work[step - 3].finish(outs[chunks[step - 3][4]])


def reduce_grads(grads, small, collective):
    lanes, depth = lax.axis_size("dp"), lax.axis_size("fsdp")
    rows = D // (lanes * depth)
    tail = (depth, 2, 2, 2)
    sources = [grad.reshape((-1,) + tail + (rows, D)) for grad in grads]
    chunks = []
    first = 0
    for i, source in enumerate(sources):
        for start in range(0, source.shape[0], 2):
            n = min(2, source.shape[0] - start)
            chunks.append((i, start, first, n, 0))
            first += n
    sets = [(first, (rows, D), jnp.bfloat16)]
    if small is not None:
        sources.append(small.reshape((1,) + tail + small.shape[1:]))
        chunks.insert(1, (len(sources) - 1, 0, 0, 1, 1))
        sets.append((1, small.shape[1:], jnp.float32))
    scratch = []
    for n, shape, kind in sets:
        scratch += [
            pltpu.VMEM((n, depth, 2, 2) + shape, kind),
            pltpu.VMEM((n, depth, 2, 2) + shape, kind),
            pltpu.VMEM((n, depth, 2) + shape, kind),
            pltpu.VMEM((n, depth) + shape, kind),
            pltpu.VMEM((n, depth) + shape, kind),
            pltpu.VMEM((n, 3) + shape, kind),
        ]
    outs = pl.pallas_call(
        functools.partial(reduce_kernel, chunks, len(sources), len(sets)),
        out_shape=[jax.ShapeDtypeStruct((n,) + shape, jnp.float32) for n, shape, _ in sets],
        in_specs=[pl.BlockSpec(memory_space=pl.ANY)] * len(sources),
        out_specs=[pl.BlockSpec(memory_space=pltpu.VMEM)] * len(sets),
        scratch_shapes=scratch
        + [
            pltpu.SemaphoreType.DMA((len(chunks),)),
            pltpu.SemaphoreType.DMA((len(chunks), 8)),
            pltpu.SemaphoreType.DMA((len(chunks), 8)),
        ],
        compiler_params=pltpu.CompilerParams(
            collective_id=collective, has_side_effects=True, vmem_limit_bytes=VMEM_LIMIT
        ),
        name=f"reduce_{collective}",
    )(*sources)
    return (outs[0], outs[1] if small is not None else None)


def spread_stages(own, out, local_sem, send, recv):
    d, z, _ = places()
    sib, near_x, near_y = flip(d, 1), flip(d, 2), flip(d, 4)
    diagonal = flip(near_x, 4)
    half = own.shape[0] // 2
    parts = (pl.ds(0, half), pl.ds(half, own.shape[0] - half))
    started = []
    last = []

    def push(slot, origin, part, to, source=None):
        copy = pltpu.make_async_remote_copy(
            src_ref=out.at[part, origin] if source is None else source,
            dst_ref=out.at[part, origin],
            send_sem=send.at[slot],
            recv_sem=recv.at[slot],
            device_id=to,
            device_id_type=MESH,
        )
        copy.start()
        started.append(copy)
        return copy

    keep = pltpu.make_async_copy(own, out.at[:, d], local_sem)
    near = {}
    turned = []

    def begin():
        for way, part in ((0, 0), (1, 1), (0, 1), (1, 0)):
            near[way, part] = push(
                2 * way + part, d, parts[part], ((near_x, near_y)[way], z), own.at[parts[part]]
            )
        keep.start()
        last.extend([push(4 + i, d, parts[i], (sib, z), own.at[parts[i]]) for i in (0, 1)])

    def forward():
        near[0, 0].wait_recv()
        turned.append(push(6, near_x, parts[0], (near_y, z)))
        last.append(push(7, near_x, parts[0], (sib, z)))
        near[1, 1].wait_recv()
        turned.append(push(8, near_y, parts[1], (near_x, z)))
        last.append(push(9, near_y, parts[1], (sib, z)))

    def collect():
        near[1, 0].wait_recv()
        last.append(push(10, near_y, parts[0], (sib, z)))
        near[0, 1].wait_recv()
        last.append(push(11, near_x, parts[1], (sib, z)))
        for i in (0, 1):
            turned[i].wait_recv()
            last.append(push(12 + i, diagonal, parts[i], (sib, z)))

    def finish():
        for copy in last:
            copy.wait_recv()
        for copy in started:
            copy.wait_send()
        keep.wait()

    return (begin, forward, collect, finish)


def meet_kernel(own, parts, out, mine, local_sem, send, recv, part_send, part_recv):
    d, z, zs = places()
    sib, near_x, near_y = flip(d, 1), flip(d, 2), flip(d, 4)
    diagonal = flip(near_x, 4)
    others = [near_x, near_y, diagonal, sib, flip(near_x, 1), flip(near_y, 1), flip(diagonal, 1)]
    greet([(d, zs[1]), (d, zs[2]), (d, zs[3])] + [(other, z) for other in others])
    out[d, z] = own[...]

    def push(slot, source, target, to, sems=(send, recv)):
        copy = pltpu.make_async_remote_copy(
            src_ref=source,
            dst_ref=target,
            send_sem=sems[0].at[slot],
            recv_sem=sems[1].at[slot],
            device_id=to,
            device_id_type=MESH,
        )
        copy.start()
        return copy

    first = [push(o - 1, own, out.at[d, z], (d, zs[o])) for o in (1, 2, 3)]
    moved = [
        push(i, parts.at[other], mine.at[:, d], (other, z), (part_send, part_recv))
        for i, other in enumerate(others)
    ]
    keep = pltpu.make_async_copy(parts.at[d], mine.at[:, d], local_sem)
    keep.start()
    for copy in first:
        copy.wait_recv()
    second = [push(3 + i, out.at[d], out.at[d], (to, z)) for i, to in enumerate(others[:3])]
    last = [push(6, out.at[d], out.at[d], (sib, z))]
    for i, origin in enumerate(others[:3]):
        second[i].wait_recv()
        last.append(push(7 + i, out.at[origin], out.at[origin], (sib, z)))
    for copy in last + moved:
        copy.wait_recv()
    for copy in first + second + last + moved:
        copy.wait_send()
    keep.wait()


def meet(own, parts, collective):
    lanes, depth = lax.axis_size("dp"), lax.axis_size("fsdp")
    rest = parts.shape[1:]
    return pl.pallas_call(
        meet_kernel,
        out_shape=[
            jax.ShapeDtypeStruct((lanes, depth) + own.shape, own.dtype),
            jax.ShapeDtypeStruct(rest[:1] + (lanes,) + rest[1:], parts.dtype),
        ],
        in_specs=[pl.BlockSpec(memory_space=pltpu.VMEM)] * 2,
        out_specs=[pl.BlockSpec(memory_space=pltpu.VMEM)] * 2,
        scratch_shapes=[
            pltpu.SemaphoreType.DMA,
            pltpu.SemaphoreType.DMA((10,)),
            pltpu.SemaphoreType.DMA((10,)),
            pltpu.SemaphoreType.DMA((7,)),
            pltpu.SemaphoreType.DMA((7,)),
        ],
        compiler_params=pltpu.CompilerParams(
            collective_id=collective, has_side_effects=True, vmem_limit_bytes=VMEM_LIMIT
        ),
        name=f"meet_{collective}",
    )(own, parts)


GRAM_TILE = 128


def gram_kernel(gram, own, total, shards, left, right, onward, back, sems, local_sem, send, recv):
    d, z, _ = places()
    up, down = (z + 1, z - 1)
    two = jnp.logical_and(lax.rem(d, 2) == 1, d // 4 == 1)
    sib, near_x, near_y = flip(d, 1), flip(d, 2), flip(d, 4)
    greet([(d, lax.rem(z + step, 4)) for step in (1, 2, 3)] + [(sib, z), (near_x, z), (near_y, z)])
    stages = spread_stages(own, shards, local_sem, send, recv)
    stages[0]()
    count = D // GRAM_TILE

    def at(ref, slot, j):
        return ref.at[slot, pl.ds(j * GRAM_TILE, GRAM_TILE), pl.ds(j * GRAM_TILE, D - j * GRAM_TILE)]

    def copy(source, target, slot, j, way, to):
        return pltpu.make_async_remote_copy(
            src_ref=at(source, slot, j),
            dst_ref=at(target, slot, j),
            send_sem=sems.at[2 * way, slot, j],
            recv_sem=sems.at[2 * way + 1, slot, j],
            device_id=(d, to),
            device_id_type=MESH,
        )

    def add(target, slot, j, *terms):
        @pl.loop(0, GRAM_TILE // 16)
        def _(i):
            rows = pl.ds(pl.multiple_of(j * GRAM_TILE + i * 16, 16), 16)
            columns = pl.ds(j * GRAM_TILE, D - j * GRAM_TILE)
            value = terms[0][slot, rows, columns]
            for term in terms[1:]:
                value = value + term[slot, rows, columns]
            target[slot, rows, columns] = value

    def ends(slot):
        @pl.when(z == 0)
        def _():
            for j in range(count):
                copy(gram, left, slot, j, 0, up).start()

        @pl.when(z == 3)
        def _():
            for j in range(count):
                copy(gram, right, slot, j, 1, down).start()

    def near(slot, j):
        @pl.when(z == 1)
        def _():
            copy(onward, left, slot, j, 0, up).wait_recv()
            add(onward, slot, j, gram, left)
            copy(onward, left, slot, j, 0, up).start()

        @pl.when(z == 2)
        def _():
            copy(back, right, slot, j, 1, down).wait_recv()
            add(back, slot, j, gram, right)
            copy(back, right, slot, j, 1, down).start()

    def far(slot, j):
        @pl.when(z == 1)
        def _():
            copy(back, right, slot, j, 1, down).wait_recv()
            add(back, slot, j, gram, right)
            copy(back, right, slot, j, 1, down).start()
            add(total, slot, j, onward, right)

        @pl.when(z == 2)
        def _():
            copy(onward, left, slot, j, 0, up).wait_recv()
            add(onward, slot, j, gram, left)
            copy(onward, left, slot, j, 0, up).start()
            add(total, slot, j, onward, right)

    def close(slot, j):
        @pl.when(z == 3)
        def _():
            copy(gram, left, slot, j, 0, up).wait_recv()
            add(total, slot, j, left, gram)

        @pl.when(z == 0)
        def _():
            copy(gram, right, slot, j, 1, down).wait_recv()
            add(total, slot, j, gram, right)

    def finish(slot):
        for j in range(count):
            @pl.when(z == 0)
            def _():
                copy(gram, left, slot, j, 0, up).wait_send()

            @pl.when(z == 3)
            def _():
                copy(gram, right, slot, j, 1, down).wait_send()

            @pl.when(jnp.logical_and(z > 0, z < 3))
            def _():
                copy(onward, left, slot, j, 0, up).wait_send()
                copy(back, right, slot, j, 1, down).wait_send()

    def mirror(slot):
        for i in range(count):
            for j in range(i + 1, count):
                block = total[slot, i * GRAM_TILE : (i + 1) * GRAM_TILE, j * GRAM_TILE : (j + 1) * GRAM_TILE]
                total[slot, j * GRAM_TILE : (j + 1) * GRAM_TILE, i * GRAM_TILE : (i + 1) * GRAM_TILE] = block.T

    ends(0)

    @pl.when(two)
    def _():
        ends(1)

    def guarded(action, item):
        if item[0] == 0:
            action(*item)
        else:
            pl.when(two)(lambda: action(*item))

    skew = 2
    items = [(slot, j) for slot in (0, 1) for j in range(count)]
    for step in range(len(items) + skew):
        if step < len(items):
            guarded(near, items[step])
        if step >= skew:
            guarded(far, items[step - skew])
            guarded(close, items[step - skew])
        if step == 3:
            stages[1]()
        if step == count + 1:
            stages[2]()

    mirror(0)

    @pl.when(two)
    def _():
        mirror(1)

    finish(0)

    @pl.when(two)
    def _():
        finish(1)

    stages[3]()


def sum_grams(grams, own, collective):
    lanes = lax.axis_size("dp")
    whole = pltpu.VMEM(grams.shape, jnp.float32)
    return pl.pallas_call(
        gram_kernel,
        out_shape=[
            jax.ShapeDtypeStruct(grams.shape, jnp.float32),
            jax.ShapeDtypeStruct(own.shape[:1] + (lanes,) + own.shape[1:], own.dtype),
        ],
        in_specs=[pl.BlockSpec(memory_space=pltpu.VMEM)] * 2,
        out_specs=[
            pl.BlockSpec(memory_space=pltpu.VMEM),
            pl.BlockSpec(memory_space=pl.ANY),
        ],
        scratch_shapes=[
            whole,
            whole,
            whole,
            whole,
            pltpu.SemaphoreType.DMA((4, grams.shape[0], D // GRAM_TILE)),
            pltpu.SemaphoreType.DMA,
            pltpu.SemaphoreType.DMA((14,)),
            pltpu.SemaphoreType.DMA((14,)),
        ],
        compiler_params=pltpu.CompilerParams(
            collective_id=collective, has_side_effects=True, vmem_limit_bytes=VMEM_LIMIT
        ),
        name=f"gram_{collective}",
    )(grams, own)


def schulz_kernel(two, gram, rows, out, state, state_low, change, current):
    tile = 256

    def chain(slot, first, places_here, step):
        total = jnp.zeros((1, 1), jnp.float32)
        for t in range(0, D, tile):
            value = gram[slot, t : t + tile, :]
            line = lax.broadcasted_iota(jnp.int32, value.shape, 0) + t
            column = lax.broadcasted_iota(jnp.int32, value.shape, 1)
            total = total + jnp.sum(
                jnp.where(line == column, value, 0.0), axis=(0, 1), keepdims=True
            )
        inverse = 1.0 / (jnp.sqrt(total) + 1e-07)

        @pl.loop(0, D // tile)
        def _(t):
            part = pl.ds(pl.multiple_of(t * tile, tile), tile)
            value = gram[slot, part, :] * (inverse * inverse)
            state[part, :] = value
            state_low[part, :] = value.astype(jnp.bfloat16)

        for place in range(places_here):
            current[first + place] = rows[first + place] * inverse

        @pl.loop(0, NS_ITERS)
        def _(turn):
            @pl.loop(0, D // tile)
            def _(t):
                part = pl.ds(pl.multiple_of(t * tile, tile), tile)
                square = jnp.dot(
                    state_low[part, :], state_low[...], preferred_element_type=jnp.float32
                )
                change[part, :] = (COEF_B * state[part, :] + COEF_C * square).astype(jnp.bfloat16)

            @pl.loop(first, first + places_here)
            def _(place):
                value = current[place]
                current[place] = COEF_A * value + jnp.dot(
                    value.astype(jnp.bfloat16), change[...], preferred_element_type=jnp.float32
                )

            @pl.when(turn < NS_ITERS - 1)
            def _():
                @pl.loop(0, D // tile)
                def _(t):
                    part = pl.ds(pl.multiple_of(t * tile, tile), tile)
                    value = state[part, :]
                    for _ in range(2):
                        value = COEF_A * value + jnp.dot(
                            value.astype(jnp.bfloat16),
                            change[...],
                            preferred_element_type=jnp.float32,
                        )
                    state[part, :] = value
                    state_low[part, :] = value.astype(jnp.bfloat16)

        for place in range(places_here):
            out[first + place] = current[first + place].astype(jnp.bfloat16)

    @pl.when(two[0] == 0)
    def _():
        chain(0, 0, 4, 0)

    @pl.when(two[0] == 1)
    def _():
        chain(0, 0, 1, 0)
        chain(1, 1, 1, 0)
        for place in (2, 3):
            out[place] = jnp.zeros(out.shape[1:], jnp.bfloat16)


def schulz(two, grams, rows):
    return pl.pallas_call(
        schulz_kernel,
        out_shape=jax.ShapeDtypeStruct(rows.shape, jnp.bfloat16),
        in_specs=[
            pl.BlockSpec(memory_space=pltpu.SMEM),
            pl.BlockSpec(memory_space=pltpu.VMEM),
            pl.BlockSpec(memory_space=pltpu.VMEM),
        ],
        out_specs=pl.BlockSpec(memory_space=pltpu.VMEM),
        scratch_shapes=[
            pltpu.VMEM((D, D), jnp.float32),
            pltpu.VMEM((D, D), jnp.bfloat16),
            pltpu.VMEM((D, D), jnp.bfloat16),
            pltpu.VMEM(rows.shape, jnp.float32),
        ],
        compiler_params=pltpu.CompilerParams(vmem_limit_bytes=VMEM_LIMIT),
        name="schulz",
    )(two, grams, rows)


def spread_kernel(own, out, local_sem, send, recv):
    d, z, _ = places()
    greet([(flip(d, 1), z), (flip(d, 2), z), (flip(d, 4), z)])
    for stage in spread_stages(own, out, local_sem, send, recv):
        stage()


def spread(own, collective):
    lanes = lax.axis_size("dp")
    return pl.pallas_call(
        spread_kernel,
        out_shape=jax.ShapeDtypeStruct(own.shape[:1] + (lanes,) + own.shape[1:], own.dtype),
        in_specs=[pl.BlockSpec(memory_space=pltpu.VMEM)],
        out_specs=pl.BlockSpec(memory_space=pl.ANY),
        scratch_shapes=[
            pltpu.SemaphoreType.DMA,
            pltpu.SemaphoreType.DMA((14,)),
            pltpu.SemaphoreType.DMA((14,)),
        ],
        compiler_params=pltpu.CompilerParams(
            collective_id=collective, has_side_effects=True, vmem_limit_bytes=VMEM_LIMIT
        ),
        name=f"spread_{collective}",
    )(own)


def update_kernel(table, scale, clip, momenta, grads, weights, turned, momenta_new, weights_new, weights_low):
    b = pl.program_id(0)
    momenta_new[...] = MOMENT * momenta[...] + clip[0] * grads[...].astype(jnp.float32)
    value = weights[...] * (1.0 - MUON_RATE * MUON_DECAY) - scale[b] * turned[0].astype(jnp.float32)
    weights_new[...] = value
    weights_low[...] = value.astype(jnp.bfloat16)


def update(home, scale, clip, momenta, grads, weights, turned):
    blocks, rows, width = weights.shape
    table = np.array([home[block][1] for block in range(blocks)] + [home[block][0] for block in range(blocks)], np.int32)
    block = pl.BlockSpec((1, rows, width), lambda b, *_: (b, 0, 0))
    return pl.pallas_call(
        update_kernel,
        grid_spec=pltpu.PrefetchScalarGridSpec(
            num_scalar_prefetch=3,
            grid=(blocks,),
            in_specs=[
                block,
                block,
                block,
                pl.BlockSpec(
                    (1, 1, rows, width),
                    lambda b, table, *_: (table[b], table[blocks + b], 0, 0),
                ),
            ],
            out_specs=[block, block, block],
        ),
        out_shape=[
            jax.ShapeDtypeStruct(weights.shape, jnp.float32),
            jax.ShapeDtypeStruct(weights.shape, jnp.float32),
            jax.ShapeDtypeStruct(weights.shape, jnp.bfloat16),
        ],
        compiler_params=pltpu.CompilerParams(vmem_limit_bytes=VMEM_LIMIT),
        name="update",
    )(jnp.asarray(table), jnp.asarray(scale), clip.reshape(1), momenta, grads, weights, turned)


GROUP = 4 * HD


def normed_head(value, gain):
    centred = value - jnp.mean(value, 0, keepdims=True)
    scale = lax.rsqrt(jnp.mean(centred * centred, 0, keepdims=True) + 1e-06)
    centred = centred * scale
    return (centred * gain, centred, scale)


def contract_first(left, right):
    return lax.dot_general(
        left, right, (((0,), (0,)), ((), ())), preferred_element_type=jnp.float32
    )


def contract_last(left, right):
    return lax.dot_general(
        left, right, (((1,), (1,)), ((), ())), preferred_element_type=jnp.float32
    )


def head_shares(query_low, key_low, same):
    scores = contract_first(key_low, query_low) * (1.0 / math.sqrt(HD))
    scores = jnp.where(same, scores, -1e30)
    exponent = jnp.exp(scores - jnp.max(scores, 0, keepdims=True))
    return exponent * (1.0 / jnp.sum(exponent, 0, keepdims=True))


TILE = 256
SLOPE = math.sqrt(2.0 / math.pi)
CUBIC = 0.044715


def tile_of(t, size=TILE):
    return pl.ds(pl.multiple_of(t * size, size), size)


def row_norm(value):
    centred = value - jnp.mean(value, -1, keepdims=True)
    scale = lax.rsqrt(jnp.mean(centred * centred, -1, keepdims=True) + 1e-06)
    return (centred * scale, scale)


def gelu_parts(value):
    square = value * value
    bend = jnp.tanh(SLOPE * value * (1.0 + CUBIC * square))
    half = 0.5 + 0.5 * bend
    slope = half + 0.5 * value * (1.0 - bend * bend) * SLOPE * (1.0 + 3.0 * CUBIC * square)
    return (value * half, slope)


def load_all(pairs, sem):
    copies = [
        pltpu.make_async_copy(source, target, sem.at[i])
        for i, (source, target) in enumerate(pairs)
    ]
    for copy in copies:
        copy.start()
    return copies


def norm_rows(source, gains, first, target):
    gain, shift = (gains[first : first + 1], gains[first + 1 : first + 2])

    @pl.loop(0, source.shape[0] // 64)
    def _(t):
        part = tile_of(t, 64)
        target[part] = (row_norm(source[part])[0] * gain + shift).astype(target.dtype)


def forward_kernel(
    state,
    gains,
    gain_query,
    gain_key,
    rows,
    columns,
    mixing,
    mixing_out,
    upward,
    down,
    state_out,
    middle,
    mixed,
    heads_low,
    attended,
    normed_low,
    mixing_held,
    out_held,
    up_held,
    down_held,
    hidden,
    sem,
):
    loads = load_all(
        [(mixing, mixing_held), (mixing_out, out_held), (upward, up_held), (down, down_held)], sem
    )
    norm_rows(state, gains, 0, heads_low)
    loads[0].wait()

    @pl.loop(0, 3 * D // TILE)
    def _(t):
        mixed[tile_of(t)] = contract_last(mixing_held[tile_of(t)], heads_low[...])

    parts, length = (rows.shape[0], rows.shape[1])
    for b in range(parts):
        same = rows[b] == columns[b]
        tokens = slice(b * length, (b + 1) * length)

        @pl.loop(0, D // GROUP)
        def _(group):
            for head in range(GROUP // HD):
                first = group * GROUP + head * HD
                part = pl.ds(pl.multiple_of(first, HD), HD)
                query, key, value = [
                    mixed[pl.ds(pl.multiple_of(place * D + first, HD), HD), tokens]
                    for place in range(3)
                ]
                query_low = normed_head(query, gain_query[part])[0].astype(jnp.bfloat16)
                key_low = normed_head(key, gain_key[part])[0].astype(jnp.bfloat16)
                share = head_shares(query_low, key_low, same).astype(jnp.bfloat16)
                attended[part, tokens] = jnp.dot(
                    value.astype(jnp.bfloat16), share, preferred_element_type=jnp.float32
                ).astype(jnp.bfloat16)

    loads[1].wait()
    for t in range(state.shape[0] // TILE):
        part = slice(t * TILE, (t + 1) * TILE)
        middle[part] = state[part] + contract_first(attended[:, part], out_held[...])
    norm_rows(middle, gains, 2, normed_low)
    loads[2].wait()

    @pl.loop(0, FF // TILE)
    def _(t):
        value = contract_last(up_held[tile_of(t)], normed_low[...])
        hidden[tile_of(t)] = gelu_parts(value)[0].astype(jnp.bfloat16)

    loads[3].wait()
    for t in range(state.shape[0] // TILE):
        part = slice(t * TILE, (t + 1) * TILE)
        state_out[part] = middle[part] + contract_first(hidden[:, part], down_held[...])


def attention_operands(gains, segment):
    return (
        jnp.pad(gains[:4], ((0, 4), (0, 0))),
        gains[4][:, None],
        gains[5][:, None],
        segment[:, :, None],
        segment[:, None, :],
    )


def whole(*memory):
    kinds = {"v": pltpu.VMEM, "a": pl.ANY}
    return [pl.BlockSpec(memory_space=kinds[kind]) for kind in memory[0]]


def layer_forward(state, blocks, gains, segment):
    tokens = state.shape[0]
    weights = [block.reshape(-1, D) for block in blocks]
    state_out, middle, mixed, heads_low, attended, normed_low = pl.pallas_call(
        forward_kernel,
        out_shape=[
            jax.ShapeDtypeStruct((tokens, D), jnp.float32),
            jax.ShapeDtypeStruct((tokens, D), jnp.float32),
            jax.ShapeDtypeStruct((3 * D, tokens), jnp.float32),
            jax.ShapeDtypeStruct((tokens, D), jnp.bfloat16),
            jax.ShapeDtypeStruct((D, tokens), jnp.bfloat16),
            jax.ShapeDtypeStruct((tokens, D), jnp.bfloat16),
        ],
        in_specs=whole("vvvvvvaaaa"),
        out_specs=whole("vvvvvv"),
        scratch_shapes=[pltpu.VMEM(weight.shape, jnp.bfloat16) for weight in weights]
        + [pltpu.VMEM((FF, tokens), jnp.bfloat16), pltpu.SemaphoreType.DMA((4,))],
        compiler_params=pltpu.CompilerParams(vmem_limit_bytes=VMEM_LIMIT),
        name="layer_forward",
    )(state, *attention_operands(gains, segment), *weights)
    return (state_out, (state, middle, mixed, heads_low, attended, normed_low))


def backward_kernel(
    grad,
    middle,
    normed_low,
    gains,
    gain_query,
    gain_key,
    rows,
    columns,
    state,
    mixed,
    heads_low,
    attended,
    mixing,
    mixing_out,
    upward,
    down,
    grad_out,
    gain_out,
    head_gain_out,
    grad_mixing,
    grad_mixing_out,
    grad_up,
    grad_down,
    state_held,
    mixed_held,
    heads_held,
    attended_held,
    mixing_held,
    out_held,
    up_held,
    down_held,
    low,
    inner,
    hidden_grad,
    mixed_low,
    attended_grad,
    made_up,
    made_down,
    made_mixing,
    made_out,
    sem,
    store_sem,
):
    loads = load_all(
        [
            (upward, up_held),
            (down, down_held),
            (mixing_out, out_held),
            (attended, attended_held),
            (mixed, mixed_held),
            (heads_low, heads_held),
            (mixing, mixing_held),
            (state, state_held),
        ],
        sem,
    )
    stores = [
        pltpu.make_async_copy(made_up, grad_up, store_sem.at[0]),
        pltpu.make_async_copy(made_down, grad_down, store_sem.at[1]),
        pltpu.make_async_copy(made_out, grad_mixing_out, store_sem.at[2]),
        pltpu.make_async_copy(made_mixing, grad_mixing, store_sem.at[3]),
    ]
    tokens = grad.shape[0]
    gain_out[...] = jnp.zeros_like(gain_out)

    @pl.loop(0, tokens // 64)
    def _(t):
        low[tile_of(t, 64)] = grad[tile_of(t, 64)].astype(jnp.bfloat16)

    loads[0].wait()
    loads[1].wait()

    @pl.loop(0, FF // TILE)
    def _(t):
        part = tile_of(t)
        value, slope = gelu_parts(contract_last(up_held[part], normed_low[...]))
        delta = (contract_last(down_held[part], low[...]) * slope).astype(jnp.bfloat16)
        hidden_grad[part] = delta
        made_down[part] = jnp.dot(
            value.astype(jnp.bfloat16), low[...], preferred_element_type=jnp.float32
        ).astype(jnp.bfloat16)
        made_up[part] = jnp.dot(
            delta, normed_low[...], preferred_element_type=jnp.float32
        ).astype(jnp.bfloat16)

    stores[0].start()
    stores[1].start()
    for t in range(tokens // TILE):
        part = slice(t * TILE, (t + 1) * TILE)
        inner[part] = contract_first(hidden_grad[:, part], up_held[...])

    def norm_back(source, first, previous, target, target_low):
        gain = gains[first : first + 1]

        @pl.loop(0, tokens // 64)
        def _(t):
            part = tile_of(t, 64)
            unit, scale = row_norm(source[part])
            delta = inner[part]
            gain_out[first : first + 1] += jnp.sum(delta * unit, 0, keepdims=True)
            gain_out[first + 1 : first + 2] += jnp.sum(delta, 0, keepdims=True)
            delta = delta * gain
            delta = delta - jnp.mean(delta, -1, keepdims=True) - unit * jnp.mean(
                delta * unit, -1, keepdims=True
            )
            value = previous[part] + delta * scale
            target[part] = value
            if target_low is not None:
                target_low[part] = value.astype(jnp.bfloat16)

    norm_back(middle, 2, grad, grad_out, low)
    loads[2].wait()
    loads[3].wait()

    @pl.loop(0, D // TILE)
    def _(t):
        part = tile_of(t)
        made_out[part] = jnp.dot(
            attended_held[part], low[...], preferred_element_type=jnp.float32
        ).astype(jnp.bfloat16)
        attended_grad[part] = contract_last(out_held[part], low[...]).astype(jnp.bfloat16)

    stores[2].start()
    loads[4].wait()
    parts, length = (rows.shape[0], rows.shape[1])
    for b in range(parts):
        same = rows[b] == columns[b]
        span = slice(b * length, (b + 1) * length)

        @pl.loop(0, D // GROUP)
        def _(group):
            for head in range(GROUP // HD):
                first = group * GROUP + head * HD
                part = pl.ds(pl.multiple_of(first, HD), HD)
                where = [pl.ds(pl.multiple_of(place * D + first, HD), HD) for place in range(3)]
                query, key, value = [mixed_held[at, span] for at in where]
                query_value, query_unit, query_scale = normed_head(query, gain_query[part])
                key_value, key_unit, key_scale = normed_head(key, gain_key[part])
                query_low = query_value.astype(jnp.bfloat16)
                key_low = key_value.astype(jnp.bfloat16)
                value_low = value.astype(jnp.bfloat16)
                out_low = attended_grad[part, span]
                share = head_shares(query_low, key_low, same)
                mixed_low[where[2], span] = contract_last(
                    out_low, share.astype(jnp.bfloat16)
                ).astype(jnp.bfloat16)
                share_grad = contract_first(value_low, out_low)
                total = jnp.sum(share * share_grad, 0, keepdims=True)
                score_low = (share * (share_grad - total) * (1.0 / math.sqrt(HD))).astype(
                    jnp.bfloat16
                )
                query_grad = jnp.dot(key_low, score_low, preferred_element_type=jnp.float32)
                key_grad = contract_last(query_low, score_low)
                for place, (delta, unit, scale, gain) in enumerate(
                    (
                        (query_grad, query_unit, query_scale, gain_query[part]),
                        (key_grad, key_unit, key_scale, gain_key[part]),
                    )
                ):
                    head_gain_out[b, place, part] = jnp.sum(delta * unit, 1, keepdims=True)
                    delta = delta * gain
                    delta = delta - jnp.mean(delta, 0, keepdims=True) - unit * jnp.mean(
                        delta * unit, 0, keepdims=True
                    )
                    mixed_low[where[place], span] = (delta * scale).astype(jnp.bfloat16)

    loads[5].wait()

    @pl.loop(0, 3 * D // TILE)
    def _(t):
        part = tile_of(t)
        made_mixing[part] = jnp.dot(
            mixed_low[part], heads_held[...], preferred_element_type=jnp.float32
        ).astype(jnp.bfloat16)

    stores[3].start()
    loads[6].wait()
    for t in range(tokens // TILE):
        part = slice(t * TILE, (t + 1) * TILE)
        inner[part] = contract_first(mixed_low[:, part], mixing_held[...])
    loads[7].wait()
    norm_back(state_held, 0, grad_out, grad_out, None)
    for copy in stores:
        copy.wait()


def layer_backward(grad, kept, blocks, gains, segment):
    state, middle, mixed, heads_low, attended, normed_low = kept
    tokens = grad.shape[0]
    weights = [block.reshape(-1, D) for block in blocks]
    low = jnp.bfloat16
    grad, gain_grads, head_gains, *block_grads = pl.pallas_call(
        backward_kernel,
        out_shape=[
            jax.ShapeDtypeStruct((tokens, D), jnp.float32),
            jax.ShapeDtypeStruct((8, D), jnp.float32),
            jax.ShapeDtypeStruct((segment.shape[0], 2, D, 1), jnp.float32),
        ]
        + [jax.ShapeDtypeStruct(weight.shape, low) for weight in weights],
        in_specs=whole("vvvvvvvvaaaaaaaa"),
        out_specs=whole("vvvaaaa"),
        scratch_shapes=[
            pltpu.VMEM(state.shape, jnp.float32),
            pltpu.VMEM(mixed.shape, jnp.float32),
            pltpu.VMEM(heads_low.shape, low),
            pltpu.VMEM(attended.shape, low),
        ]
        + [pltpu.VMEM(weight.shape, low) for weight in weights]
        + [
            pltpu.VMEM((tokens, D), low),
            pltpu.VMEM((tokens, D), jnp.float32),
            pltpu.VMEM((FF, tokens), low),
            pltpu.VMEM((3 * D, tokens), low),
            pltpu.VMEM((D, tokens), low),
            pltpu.VMEM((FF, D), low),
            pltpu.VMEM((FF, D), low),
            pltpu.VMEM((3 * D, D), low),
            pltpu.VMEM((D, D), low),
            pltpu.SemaphoreType.DMA((8,)),
            pltpu.SemaphoreType.DMA((4,)),
        ],
        compiler_params=pltpu.CompilerParams(vmem_limit_bytes=60 * 1024 * 1024),
        name="layer_backward",
    )(grad, middle, normed_low, *attention_operands(gains, segment), state, mixed, heads_low, attended, *weights)
    gain_grads = jnp.concatenate([gain_grads[:4], jnp.sum(head_gains[..., 0], 0)], 0)
    return (grad, block_grads, gain_grads)


HEAD_LANES = 128


def full_dot(left, right):
    return jnp.dot(left, right, preferred_element_type=jnp.float32, precision=HIGH)


def head_marks():
    entry = lax.broadcasted_iota(jnp.int32, (D, HEAD_LANES), 0)
    lane = lax.broadcasted_iota(jnp.int32, (D, HEAD_LANES), 1)
    return (entry // HD == lane).astype(jnp.float32)


def full_dot_last(left, right):
    return lax.dot_general(
        left,
        right,
        (((1,), (1,)), ((), ())),
        preferred_element_type=jnp.float32,
        precision=HIGH,
    )


def pool_sequence(state, gains, rows, columns):
    unit, scale = row_norm(state)
    final = unit * gains[0:1] + gains[1:2]
    marks = head_marks()
    logits = full_dot(final * gains[2:3], marks) * (1.0 / math.sqrt(HD))
    slot = lax.broadcasted_iota(jnp.int32, (rows.shape[0], IMGS), 1)
    member = (rows == slot).astype(jnp.float32)
    slot = lax.broadcasted_iota(jnp.int32, (IMGS, columns.shape[1]), 0)
    member_rows = (columns == slot).astype(jnp.float32)
    tops = jnp.zeros_like(logits)
    for k in range(IMGS):
        here = rows == k
        top = jnp.max(jnp.where(here, logits, -1e30), 0, keepdims=True)
        tops = jnp.where(here, top, tops)
    exponent = jnp.exp(logits - tops)
    share = exponent / full_dot(member, full_dot(member_rows, exponent))
    spread_share = full_dot_last(share, marks)
    dead = (jnp.sum(member_rows, 1, keepdims=True) == 0.0).astype(jnp.float32)
    pooled = full_dot(member_rows, spread_share * final) + dead * jnp.mean(
        final, 0, keepdims=True
    )
    return (unit, scale, final, marks, member, member_rows, share, spread_share, dead, pooled)


def unit_scale(value):
    return lax.rsqrt(jnp.mean(value * value, -1, keepdims=True) + 1e-06)


def pool_kernel(state, gains, rows, columns, matrix, pooled_low, embedded, image_low):
    parts, length = (rows.shape[0], rows.shape[1])
    for b in range(parts):
        pooled = pool_sequence(
            state[b * length : (b + 1) * length], gains[...], rows[b], columns[b]
        )[-1]
        pooled_low[b] = pooled.astype(jnp.bfloat16)
        value = jnp.dot(
            pooled.astype(jnp.bfloat16), matrix[...], preferred_element_type=jnp.float32
        )
        embedded[b] = value
        image_low[b] = (value * unit_scale(value) * (1.0 / math.sqrt(D))).astype(jnp.bfloat16)


def pool_forward(state, gains, segment, matrix):
    parts = segment.shape[0]
    shape = (parts, IMGS, D)
    return pl.pallas_call(
        pool_kernel,
        out_shape=[
            jax.ShapeDtypeStruct(shape, jnp.bfloat16),
            jax.ShapeDtypeStruct(shape, jnp.float32),
            jax.ShapeDtypeStruct(shape, jnp.bfloat16),
        ],
        in_specs=whole("vvvvv"),
        out_specs=whole("vvv"),
        compiler_params=pltpu.CompilerParams(vmem_limit_bytes=VMEM_LIMIT),
        name="pool_forward",
    )(state, gains, segment[:, :, None], segment[:, None, :], matrix)


def contrast_kernel(
    me,
    images,
    texts,
    alive_columns,
    alive_rows,
    own_images,
    own_live,
    state,
    gains,
    rows,
    columns,
    matrix,
    pooled_low,
    embedded,
    loss,
    grad,
    grad_matrix,
    gain_out,
    text_side,
):
    parts, length = (rows.shape[0], rows.shape[1])
    everyone = images.shape[1]
    count = jnp.zeros((1, 1), jnp.float32)
    for b in range(parts):
        count = count + jnp.sum(alive_columns[b], -1, keepdims=True)
    factor = 1.0 / (2.0 * count)
    first = me[0] * IMGS

    def rows_of(scores, alive, live, start):
        masked = jnp.where(alive > 0, scores, -1e30)
        top = jnp.max(masked, -1, keepdims=True)
        exponent = jnp.exp(masked - top)
        total = jnp.sum(exponent, -1, keepdims=True)
        line = lax.broadcasted_iota(jnp.int32, scores.shape, 0) + start
        column = lax.broadcasted_iota(jnp.int32, scores.shape, 1)
        target = (line == column).astype(jnp.float32)
        diagonal = jnp.sum(scores * target, -1, keepdims=True)
        term = (top + jnp.log(total) - diagonal) * live
        delta = (exponent * (1.0 / total) - target) * live
        return (term, (delta * factor * LOGIT_SCALE).astype(jnp.bfloat16))

    loss[...] = jnp.zeros_like(loss)
    grad_sum = jnp.zeros((D, D), jnp.float32)
    gain_out[...] = jnp.zeros_like(gain_out)
    for b in range(parts):
        forward = LOGIT_SCALE * contract_last(own_images[b], texts[b])
        term, forward_low = rows_of(forward, alive_columns[b], own_live[b], first)
        loss[...] += jnp.sum(term, 0, keepdims=True) * factor
        text_side[...] = jnp.zeros_like(text_side)

        @pl.loop(0, everyone // TILE)
        def _(t):
            part = tile_of(t)
            backward = LOGIT_SCALE * contract_last(texts[b, part], images[b])
            term, backward_low = rows_of(
                backward, alive_columns[b], alive_rows[b, part], t * TILE
            )
            line = lax.broadcasted_iota(jnp.int32, term.shape, 0) + t * TILE
            here = jnp.logical_and(line >= first, line < first + IMGS)
            loss[...] += jnp.sum(jnp.where(here, term, 0.0), 0, keepdims=True) * factor
            text_side[...] += contract_first(backward_low, texts[b, part])

        image_grad = jnp.dot(forward_low, texts[b], preferred_element_type=jnp.float32)
        image_grad = image_grad + text_side[pl.ds(pl.multiple_of(first, IMGS), IMGS)]
        value = embedded[b]
        scale = unit_scale(value)
        embed_low = (
            (
                image_grad * scale
                - value * (scale * scale * scale) * jnp.mean(value * image_grad, -1, keepdims=True)
            )
            * (1.0 / math.sqrt(D))
        ).astype(jnp.bfloat16)
        grad_sum = grad_sum + contract_first(pooled_low[b], embed_low)
        pooled_grad = contract_last(embed_low, matrix[...])
        unit, norm_scale, final, marks, member, member_rows, share, spread_share, dead, _ = (
            pool_sequence(
                state[b * length : (b + 1) * length], gains[...], rows[b], columns[b]
            )
        )
        token_grad = full_dot(member, pooled_grad)
        share_grad = full_dot(final * token_grad, marks)
        inside = full_dot(member, full_dot(member_rows, share * share_grad))
        logit_grad = share * (share_grad - inside) * (1.0 / math.sqrt(HD))
        spread_logit = full_dot_last(logit_grad, marks)
        final_grad = (
            spread_share * token_grad
            + spread_logit * gains[2:3]
            + jnp.sum(dead * pooled_grad, 0, keepdims=True) * (1.0 / length)
        )
        gain_out[0:1] += jnp.sum(final_grad * unit, 0, keepdims=True)
        gain_out[1:2] += jnp.sum(final_grad, 0, keepdims=True)
        gain_out[2:3] += jnp.sum(spread_logit * final, 0, keepdims=True)
        delta = final_grad * gains[0:1]
        delta = delta - jnp.mean(delta, -1, keepdims=True) - unit * jnp.mean(
            delta * unit, -1, keepdims=True
        )
        grad[b * length : (b + 1) * length] = delta * norm_scale
    grad_matrix[...] = grad_sum.astype(jnp.bfloat16)


def contrast(me, images, texts, alive, own_images, live, state, gains, segment, matrix, pooled_low, embedded):
    parts, everyone = alive.shape
    loss, grad, grad_matrix, gain_grads = pl.pallas_call(
        contrast_kernel,
        out_shape=[
            jax.ShapeDtypeStruct((8, 128), jnp.float32),
            jax.ShapeDtypeStruct(state.shape, jnp.float32),
            jax.ShapeDtypeStruct((D, D), jnp.bfloat16),
            jax.ShapeDtypeStruct((8, D), jnp.float32),
        ],
        in_specs=[pl.BlockSpec(memory_space=pltpu.SMEM)] + whole("vvvvvvvvvvvvv"),
        out_specs=whole("vvvv"),
        scratch_shapes=[pltpu.VMEM((everyone, D), jnp.float32)],
        compiler_params=pltpu.CompilerParams(vmem_limit_bytes=VMEM_LIMIT),
        name="contrast",
    )(
        me.reshape(1),
        images,
        texts,
        alive[:, None, :],
        alive[:, :, None],
        own_images,
        live[:, :, None],
        state,
        gains,
        segment[:, :, None],
        segment[:, None, :],
        matrix,
        pooled_low,
        embedded,
    )
    return (loss[0, 0], grad, grad_matrix, gain_grads[:3])


def muon_groups():
    found = [(0, 1), (1, 1)]
    for index in range(LAYERS):
        base = 2 + 12 * index
        found = found + [(base, 3), (base + 3, 1), (base + 4, 4), (base + 8, 4)]
    return found


def lane_plan(lanes):
    plan = [[] for _ in range(lanes)]
    for start, number in sorted(muon_groups(), key=lambda group: -group[1]):
        lane = min(range(lanes), key=lambda i: (sum(n for _, n in plan[i]), len(plan[i]), i))
        plan[lane].append((start, number))
    plan.sort(key=lambda entry: (-entry[0][1] if entry else 0))
    if lanes == 8:
        plan = [plan[i] for i in (0, 1, 2, 3, 4, 6, 5, 7)]
    depth = max(len(entry) for entry in plan)
    widths = [
        max([entry[slot][1] for entry in plan if slot < len(entry)]) for slot in range(depth)
    ]
    return (plan, widths)


def lane_blocks(plan):
    rows = [[start + i for start, number in entry for i in range(number)] for entry in plan]
    most = max(len(row) for row in rows)
    return np.array([row + [-1] * (most - len(row)) for row in rows], np.int32)


def lane_tables(plan, widths):
    index = np.zeros((len(plan), sum(widths)), np.int32)
    mask = np.zeros((len(plan), sum(widths)), np.float32)
    number = np.ones((len(plan), sum(widths)), np.float32)
    home = {}
    for lane, entry in enumerate(plan):
        first = 0
        for slot, width in enumerate(widths):
            if slot < len(entry):
                start, count = entry[slot]
                for place in range(count):
                    index[lane, first + place] = start + place
                    mask[lane, first + place] = 1.0
                    number[lane, first + place] = count
                    home[start + place] = (lane, first + place)
            first += width
    return (index, mask, number, home)


def orthogonal_factor(gram):
    size = jnp.sqrt(jnp.trace(gram)) + 1e-07
    state = gram / (size * size)
    total = None
    for turn in range(NS_ITERS):
        low = rounded(state)
        change = COEF_B * state + COEF_C * jnp.dot(low, low, preferred_element_type=jnp.float32)
        change_low = rounded(change)
        if total is None:
            total = COEF_A * jnp.eye(D, dtype=jnp.float32) + change
        else:
            total = COEF_A * total + jnp.dot(
                rounded(total), change_low, preferred_element_type=jnp.float32
            )
        if turn < NS_ITERS - 1:
            for _ in range(2):
                state = COEF_A * state + jnp.dot(
                    rounded(state), change_low, preferred_element_type=jnp.float32
                )
    return total / size


def per_device(
    patches, grid, segments, text_ids, table, weights, momenta, gains, gains_m, gains_v, step
):
    fin = 6 * LAYERS
    base = fin + 3
    lanes = lax.axis_size("dp")
    slots = jnp.arange(IMGS, dtype=jnp.int32)
    live = jnp.any(segments[:, 0, None, :] == slots[None, :, None], -1).astype(jnp.float32)
    depth = lax.axis_size("fsdp")
    captions = MB * IMGS
    tokens = text_ids.shape[3]
    own_ids = jnp.pad(text_ids.reshape(captions, tokens), ((0, 0), (0, 128 - tokens)))
    early = [(0, 1), (2, 3), (5, 1), (6, 4), (10, 4), (1, 1)]
    later = []
    for index in range(1, LAYERS):
        start = 2 + 12 * index
        early = early + [(start, 3), (start + 3, 1)]
        later = later + [(start + 4, 4), (start + 8, 4)]
    (stem, *first_blocks), ids, later_part = fetch(weights, early, later, own_ids, 1)
    early_blocks = first_blocks[5:]
    pooling_matrix = first_blocks[4][0]
    first_blocks = first_blocks[:4]
    later_blocks = gather_later(later_part)
    ids = ids[:, :, :tokens]
    flat_ids = ids.reshape(depth * captions, -1)
    share_rows = table.shape[0]
    picked = flat_ids - lax.axis_index("fsdp") * share_rows
    hits = jnp.sum(
        (picked[:, :, None] == jnp.arange(share_rows, dtype=jnp.int32)[None, None, :]).astype(
            jnp.int32
        ),
        1,
    )
    parts = jnp.dot(rounded(hits.astype(jnp.float32)), table, preferred_element_type=jnp.float32)
    text_sum = jnp.sum(swap(parts.reshape(depth, captions, D), 11), 0)
    text_low = rounded(unit_rows(text_sum / text_ids.shape[-1]))
    me = lax.axis_index(("dp", "fsdp"))
    segment = segments[:, 0]
    rows_hot, cols_hot = jax.vmap(positions)(grid[:, 0])
    rows_hot = rows_hot.reshape(-1, POS)
    cols_hot = cols_hot.reshape(-1, POS)
    patch_low = patches.reshape(-1, D)
    state = product(patch_low, stem[0], "sd,rd->sr")
    state = state + jnp.dot(rows_hot, gains[base : base + POS], precision=HIGH)
    state = state + jnp.dot(cols_hot, gains[base + POS : base + 2 * POS], precision=HIGH)
    saved = []
    for index in range(LAYERS):
        if index == 0:
            blocks = first_blocks
        else:
            first = 8 * index - 8
            blocks = early_blocks[2 * index - 2 : 2 * index] + [
                later_blocks[first : first + 4],
                later_blocks[first + 4 : first + 8],
            ]
        state, kept = layer_forward(state, blocks, gains[6 * index : 6 * index + 6], segment)
        saved.append((kept, blocks))
    pool_gains = jnp.pad(gains[fin : fin + 3], ((0, 5), (0, 0)))
    pooled_low, embedded, image_low = pool_forward(state, pool_gains, segment, pooling_matrix)
    own_flags = jnp.broadcast_to(live.reshape(captions, 1), (captions, 128)).astype(jnp.bfloat16)
    both = jnp.stack([image_low.reshape(captions, D), text_low]).reshape(2 * captions, D)
    gathered, flags = share([both, own_flags], 8)
    gathered = gathered.reshape(-1, 2, MB, IMGS, D)
    flags = flags.reshape(-1, MB, IMGS, 128)[..., 0].astype(jnp.float32)
    images, texts = [
        jnp.moveaxis(gathered[:, i], 0, 1).reshape(MB, -1, D) for i in range(2)
    ]
    loss_part, grad, grad_pool, pool_gain_grads = contrast(
        me,
        images,
        texts,
        jnp.moveaxis(flags, 0, 1).reshape(MB, -1),
        image_low,
        live,
        state,
        pool_gains,
        segment,
        pooling_matrix,
        pooled_low,
        embedded,
    )
    gain_parts = [None] * LAYERS
    block_grads = [None] * LAYERS
    fast = depth == 4 and lanes == 8
    slices = [None] * LAYERS
    for index in reversed(range(LAYERS)):
        kept, blocks = saved[index]
        grad, block_grads[index], gain_parts[index] = layer_backward(
            grad, kept, blocks, gains[6 * index : 6 * index + 6], segment
        )
        if index == 1:
            block_grads[index].append(grad_pool)
        if fast and index > 0:
            slices[index], _ = reduce_grads(block_grads[index], None, 4 + index)
    grad_low = rounded(grad)
    grad_patch = rounded(product(grad_low, patch_low, "sr,sd->rd"))
    block_grads[0].append(grad_patch)
    grad_rows = jnp.dot(rows_hot.T, grad, precision=HIGH)
    grad_cols = jnp.dot(cols_hot.T, grad, precision=HIGH)
    gains_grad = jnp.concatenate(
        gain_parts
        + [pool_gain_grads, grad_rows, grad_cols],
        0,
    )
    plan, widths = lane_plan(lanes)
    index, mask, number, home = lane_tables(plan, widths)
    lane = lax.axis_index("dp")
    scale = np.ones((weights.shape[0],), np.float32)
    for start, count_blocks in muon_groups():
        scale[start : start + count_blocks] = MUON_RATE * math.sqrt(count_blocks)
    if fast:
        width = 256
        small = jnp.concatenate([gains_grad.reshape(-1), loss_part[None]])
        small = jnp.pad(small, (0, lanes * depth * 8 * width - small.shape[0]))
        slices[0], small = reduce_grads(
            block_grads[0], small.reshape(lanes * depth, 8, width), 4
        )
        squares = jnp.sum(slices[0] * slices[0]) + jnp.sum(slices[1] * slices[1])
        slices = [rounded(value) for value in slices]
        slices = jnp.concatenate(
            [slices[0][12:], slices[1][12:]] + [values[:12] for values in slices], 0
        )
        empty = jnp.zeros((1,) + slices.shape[1:], slices.dtype)
        parts = jnp.concatenate(
            [
                slices[block : block + 1] if block >= 0 else empty
                for block in lane_blocks(plan).reshape(-1)
            ],
            0,
        ).reshape((lanes, -1) + slices.shape[1:])
        squares = jnp.broadcast_to(squares, (8, width))
        shared, mine = meet(jnp.concatenate([small[0], squares], 0), parts, 9)
        flat = jnp.transpose(shared[:, :, :8], (1, 0, 2, 3)).reshape(-1)
        gains_grad, loss = (flat[: gains.size].reshape(gains.shape), flat[gains.size])
        squares = jnp.sum(shared[:, :, 8, 0])
        norm = jnp.sqrt(squares + jnp.sum(gains_grad * gains_grad))
        clip = jnp.minimum(1.0, CLIP_LIMIT / (norm + 1e-06))
        blocks_here = lane_blocks(plan)
        own_momenta = jnp.stack(
            [
                jnp.where(
                    jnp.asarray(blocks_here >= 0)[lane, place],
                    lax.dynamic_index_in_dim(
                        momenta, jnp.maximum(jnp.asarray(blocks_here)[lane, place], 0), 0, False
                    ),
                    0.0,
                )
                for place in range(blocks_here.shape[1])
            ]
        )
        own = MOMENT * own_momenta + clip * mine.reshape(own_momenta.shape).astype(jnp.float32)
        two = jnp.asarray(np.array([len(entry) > 1 for entry in plan], np.int32))[lane]
        own_low = rounded(own)
        first_low = jnp.concatenate(
            [own_low[:1], jnp.where(two > 0, jnp.bfloat16(0), own_low[1:])], 0
        )
        grams = jnp.stack(
            [
                product(first_low, first_low, "brd,bre->de"),
                product(own_low[1], own_low[1], "rd,re->de"),
            ]
        )
        grams, shard_grads = sum_grams(grams, slices, 12)
        turned = spread(schulz(two.reshape(1), grams, own), 13)
        homes = {
            int(block): (lane_of, place)
            for lane_of, entry in enumerate(blocks_here)
            for place, block in enumerate(entry)
            if block >= 0
        }
        momenta_new, weights_new, weights_low = update(
            homes, scale, clip, momenta, shard_grads.reshape(weights.shape), weights, turned
        )
    else:
        stack = jnp.concatenate(
            [block_grads[index].pop().reshape(1, D, D) for index in range(LAYERS)]
            + [value.reshape(-1, D, D) for values in block_grads for value in values],
            0,
        )
        shard_grads = lax.psum(
            lax.psum_scatter(stack, "fsdp", scatter_dimension=1, tiled=True), "dp"
        ).astype(jnp.float32)
        gains_grad, loss = lax.psum((gains_grad, loss_part), ("dp", "fsdp"))
        squares = lax.psum(jnp.sum(shard_grads * shard_grads), "fsdp")
        norm = jnp.sqrt(squares + jnp.sum(gains_grad * gains_grad))
        clip = jnp.minimum(1.0, CLIP_LIMIT / (norm + 1e-06))
        momenta_new = MOMENT * momenta + clip * shard_grads
        own = jnp.stack(
            [
                lax.dynamic_index_in_dim(momenta_new, jnp.asarray(index)[lane, place], 0, False)
                * jnp.asarray(mask)[lane, place]
                for place in range(index.shape[1])
            ]
        )
        own_low = rounded(own)
        bounds = np.cumsum([0] + widths)
        grams = jnp.stack(
            [
                product(own_low[a:b], own_low[a:b], "brd,bre->de")
                for a, b in zip(bounds[:-1], bounds[1:])
            ]
        )
        grams = lax.psum(grams, "fsdp")
        turned = jnp.concatenate(
            [
                product(
                    own_low[bounds[slot] : bounds[slot + 1]],
                    rounded(orthogonal_factor(grams[slot])),
                    "brd,de->bre",
                )
                for slot in range(len(widths))
            ],
            0,
        )
        spread_rows = lax.all_gather(rounded(turned), "dp", axis=0)
        current = jnp.stack(
            [spread_rows[home[block][0], home[block][1]] for block in range(weights.shape[0])]
        ).astype(jnp.float32)
        weights_new = weights * (1.0 - MUON_RATE * MUON_DECAY) - jnp.asarray(scale)[:, None, None] * current
        weights_low = rounded(weights_new)
    grad_small = clip * gains_grad
    moment_one = BETA_ONE * gains_m + (1.0 - BETA_ONE) * grad_small
    moment_two = BETA_TWO * gains_v + (1.0 - BETA_TWO) * grad_small * grad_small
    count_steps = step[0].astype(jnp.float32)
    corrected_one = moment_one / (1.0 - jnp.power(BETA_ONE, count_steps))
    corrected_two = moment_two / (1.0 - jnp.power(BETA_TWO, count_steps))
    gains_new = gains - ADAM_RATE * (
        corrected_one / (jnp.sqrt(corrected_two) + ADAM_EPS) + ADAM_DECAY * gains
    )
    shift_grad = grad_small[fin + 1]
    return (
        loss,
        norm,
        weights_new,
        weights_low,
        momenta_new,
        gains_new,
        moment_one,
        moment_two,
        shift_grad,
    )


def solution(mesh):
    placed = (
        P(None, ("dp", "fsdp"), None, None),
        P(None, ("dp", "fsdp"), None, None),
        P(None, ("dp", "fsdp"), None),
        P(None, ("dp", "fsdp"), None, None),
        P("fsdp", None),
        P(None, "fsdp", None),
        P(None, "fsdp", None),
        P(),
        P(),
        P(),
        P(),
    )
    return jax.shard_map(
        per_device,
        mesh=mesh,
        in_specs=placed,
        out_specs=(
            P(),
            P(),
            P(None, "fsdp", None),
            P(None, "fsdp", None),
            P(None, "fsdp", None),
            P(),
            P(),
            P(),
            P(),
        ),
        check_vma=False,
    )
```

```python
import functools
import math

import jax
import jax.numpy as jnp
import numpy as np
from jax import lax
from jax.experimental import pallas as pl
from jax.experimental.pallas import tpu as pltpu
from jax.sharding import PartitionSpec as P

D = 768
HEADS = 12
FF = 3072
LAYERS = 2
IMGS = 8
POS = 32
MB = 2
NS_ITERS = 5
HD = 64


MESH = pl.DeviceIdType.MESH
VMEM_LIMIT = 56 * 1024 * 1024
HIGH = lax.Precision.HIGHEST
LOGIT_SCALE = 50.0
CLIP_LIMIT = 0.005
MOMENT = 0.95
MUON_RATE = 0.5
MUON_DECAY = 0.01
ADAM_RATE = 0.4
BETA_ONE = 0.9
BETA_TWO = 0.999
ADAM_EPS = 1e-08
ADAM_DECAY = 0.01
COEF_A = 3.4445
COEF_B = -4.775
COEF_C = 2.0315


def rounded(value):
    return value.astype(jnp.bfloat16)


def product(left, right, form):
    return jnp.einsum(form, left, right, preferred_element_type=jnp.float32)


def unit_rows(value):
    return (
        value
        * lax.rsqrt(jnp.mean(value * value, -1, keepdims=True) + 1e-06)
        * (1.0 / math.sqrt(value.shape[-1]))
    )


def positions(grid):
    slots = jnp.arange(POS, dtype=jnp.int32)
    row_index = grid[0] * POS // grid[2]
    col_index = grid[1] * POS // grid[3]
    return (
        (row_index[:, None] == slots[None]).astype(jnp.float32),
        (col_index[:, None] == slots[None]).astype(jnp.float32),
    )


def whole(kinds):
    memory = {"v": pltpu.VMEM, "a": pl.ANY}
    return [pl.BlockSpec(memory_space=memory[kind]) for kind in kinds]


def flip(index, bit):
    return index + bit - 2 * bit * lax.rem(index // bit, 2)


def greet(peers):
    barrier = pltpu.get_barrier_semaphore()
    for peer in peers:
        pl.semaphore_signal(barrier, inc=1, device_id=peer, device_id_type=MESH)
    pl.semaphore_wait(barrier, len(peers))


def places():
    d = lax.axis_index("dp")
    z = lax.axis_index("fsdp")
    return (d, z, [lax.rem(z + step, 4) for step in range(4)])


CAPTION_TILE = 400


def fetch_kernel(chunks, sizes, weights, ids, table, *refs):
    outs = refs[: len(sizes)]
    text_sum = refs[len(sizes)]
    (
        full,
        low,
        all_ids,
        pages,
        found,
        found_parts,
        from_z,
        load_sem,
        store_sem,
        send,
        recv,
        page_sem,
        id_send,
        id_recv,
        part_send,
        part_recv,
    ) = refs[len(sizes) + 1 :]
    d, z, zs = places()
    sib, near_x, near_y = flip(d, 1), flip(d, 2), flip(d, 4)
    diagonal = flip(near_x, 4)
    starts = [sum(chunk[3] for chunk in chunks[:k]) for k in range(len(chunks))]
    loads = []
    for k, (source, _, _, n) in enumerate(chunks):
        loads.append(
            pltpu.make_async_copy(
                weights.at[pl.ds(source, n)], full.at[pl.ds(starts[k], n)], load_sem.at[k]
            )
        )
        loads[k].start()
    page_count = table.shape[0] // CAPTION_TILE

    def page(t):
        return pltpu.make_async_copy(
            table.at[tile_of(t, CAPTION_TILE)], pages.at[lax.rem(t, 2)], page_sem.at[lax.rem(t, 2)]
        )

    page(0).start()
    greet([(d, zs[1]), (d, zs[2]), (d, zs[3]), (sib, z), (near_x, z), (near_y, z)])
    pending = []
    all_ids[z] = ids[...]
    id_copies = []
    for o in (1, 2, 3):
        id_copies.append(
            pltpu.make_async_remote_copy(
                src_ref=ids,
                dst_ref=all_ids.at[z],
                send_sem=id_send.at[o - 1],
                recv_sem=id_recv.at[o - 1],
                device_id=(d, zs[o]),
                device_id_type=MESH,
            )
        )
        id_copies[-1].start()

    def push(k, slot, first, n, zz, dd, to, source=None):
        out = outs[chunks[k][1]]
        rows = pl.ds(chunks[k][2] + first, n)
        copy = pltpu.make_async_remote_copy(
            src_ref=out.at[rows, zz, dd] if source is None else source,
            dst_ref=out.at[rows, zz, dd],
            send_sem=send.at[k, slot],
            recv_sem=recv.at[k, slot],
            device_id=to,
            device_id_type=MESH,
        )
        copy.start()
        pending.append(copy)
        return copy

    along_z = []
    stores = []
    for k, (_, out, offset, n) in enumerate(chunks):
        loads[k].wait()

        @pl.loop(starts[k], starts[k] + n)
        def _(i):
            low[i] = full[i].astype(low.dtype)

        along_z.append(
            [
                push(k, o - 1, 0, n, z, d, (d, zs[o]), low.at[pl.ds(starts[k], n), d])
                for o in (1, 2, 3)
            ]
        )
        stores.append(
            pltpu.make_async_copy(
                low.at[pl.ds(starts[k], n)],
                outs[out].at[pl.ds(offset, n), z],
                store_sem.at[k],
            )
        )
        stores[k].start()
    for copy in id_copies:
        copy.wait_recv()
    marks = all_ids[0] + all_ids[1] + all_ids[2] + all_ids[3]
    found[...] = jnp.zeros_like(found)

    def look_up(t):
        @pl.when(t + 1 < page_count)
        def _():
            page(t + 1).start()

        page(t).wait()
        row = lax.broadcasted_iota(jnp.int32, (CAPTION_TILE, marks.shape[1]), 0)
        row = row + (z * table.shape[0] + t * CAPTION_TILE)
        hits = jnp.zeros(row.shape, jnp.float32)
        for token in range(marks.shape[0]):
            hits = hits + jnp.where(row == marks[token : token + 1], 1.0, 0.0)
        found[...] += contract_first(hits.astype(jnp.bfloat16), pages[lax.rem(t, 2)])

    def look_up_span(first, last):
        @pl.loop(first, last)
        def _(t):
            look_up(t)

    share_of = -(-page_count // (len(chunks) - 1))
    part_copies = []

    def send_parts():
        captions = found_parts.shape[1]
        for owner in range(4):
            found_parts[owner] = (
                found[2 * owner * captions : (2 * owner + 1) * captions]
                + found[(2 * owner + 1) * captions : (2 * owner + 2) * captions]
            )
        for o in (1, 2, 3):
            part_copies.append(
                pltpu.make_async_remote_copy(
                    src_ref=found_parts.at[zs[o]],
                    dst_ref=from_z.at[o - 1],
                    send_sem=part_send.at[o - 1],
                    recv_sem=part_recv.at[o - 1],
                    device_id=(d, zs[o]),
                    device_id_type=MESH,
                )
            )
            part_copies[-1].start()

    along_x, along_y, turn_y, turn_x, last = {}, {}, {}, {}, []
    count = len(chunks)
    for step in range(count + 2):
        if step < count:
            k, n = step, chunks[step][3]
            along_x[k], along_y[k] = [], []
            for o in (1, 2, 3):
                zz = zs[4 - o]
                along_z[k][o - 1].wait_recv()
                along_x[k].append(push(k, 2 + o, 0, n, zz, d, (near_x, z)))
                along_y[k].append(push(k, 5 + o, 0, n, zz, d, (near_y, z)))
                last.append(push(k, 14 + o, 0, n, zz, d, (sib, z)))
        if 1 <= step <= count:
            k, n = step - 1, chunks[step - 1][3]
            half = n // 2
            turn_y[k], turn_x[k] = [], []
            for o in (1, 2, 3):
                zz = zs[4 - o]
                along_x[k][o - 1].wait_recv()
                if half:
                    turn_y[k].append(push(k, 8 + o, 0, half, zz, near_x, (near_y, z)))
                last.append(push(k, 17 + o, 0, n, zz, near_x, (sib, z)))
                along_y[k][o - 1].wait_recv()
                turn_x[k].append(push(k, 11 + o, half, n - half, zz, near_y, (near_x, z)))
                last.append(push(k, 20 + o, 0, n, zz, near_y, (sib, z)))
        if step * share_of < page_count:
            look_up_span(step * share_of, min((step + 1) * share_of, page_count))
        if step == count - 1:
            send_parts()
        if step >= 2:
            k, n = step - 2, chunks[step - 2][3]
            for o in (1, 2, 3):
                for copies in (turn_y[k], turn_x[k]):
                    if copies:
                        copies[o - 1].wait_recv()
                last.append(push(k, 23 + o, 0, n, zs[4 - o], diagonal, (sib, z)))
    for copy in last:
        copy.wait_recv()
    for copy in pending:
        copy.wait_send()
    for copy in stores:
        copy.wait()
    for copy in id_copies:
        copy.wait_send()
    for copy in part_copies:
        copy.wait()
    text_sum[...] = found_parts[z] + from_z[0] + from_z[1] + from_z[2]


def fetch(weights, pieces, ids, table, captions, collective):
    depth, eighths = lax.axis_size("fsdp"), lax.axis_size("dp")
    blocks, rows, width = weights.shape
    part = (eighths, rows // eighths, width)
    chunks = []
    for out, (a, n) in enumerate(pieces):
        for first in range(0, n, 2):
            chunks.append((a + first, out, first, min(2, n - first)))
    total = sum(n for _, n in pieces)
    outs = pl.pallas_call(
        functools.partial(fetch_kernel, chunks, [n for _, n in pieces]),
        out_shape=[
            jax.ShapeDtypeStruct((n, depth) + part, jnp.bfloat16) for _, n in pieces
        ]
        + [jax.ShapeDtypeStruct((captions, width), jnp.float32)],
        in_specs=whole("ava"),
        out_specs=whole("a" * len(pieces) + "v"),
        scratch_shapes=[
            pltpu.VMEM((total,) + part, jnp.float32),
            pltpu.VMEM((total,) + part, jnp.bfloat16),
            pltpu.VMEM((depth,) + ids.shape, jnp.int32),
            pltpu.VMEM((2, CAPTION_TILE, width), jnp.bfloat16),
            pltpu.VMEM((2 * depth * captions, width), jnp.float32),
            pltpu.VMEM((depth, captions, width), jnp.float32),
            pltpu.VMEM((3, captions, width), jnp.float32),
            pltpu.SemaphoreType.DMA((len(chunks),)),
            pltpu.SemaphoreType.DMA((len(chunks),)),
            pltpu.SemaphoreType.DMA((len(chunks), 27)),
            pltpu.SemaphoreType.DMA((len(chunks), 27)),
            pltpu.SemaphoreType.DMA((2,)),
            pltpu.SemaphoreType.DMA((3,)),
            pltpu.SemaphoreType.DMA((3,)),
            pltpu.SemaphoreType.DMA((3,)),
            pltpu.SemaphoreType.DMA((3,)),
        ],
        compiler_params=pltpu.CompilerParams(
            collective_id=collective, has_side_effects=True, vmem_limit_bytes=VMEM_LIMIT
        ),
        name=f"fetch_{collective}",
    )(weights.reshape((blocks,) + part), ids, table)
    return ([out.reshape(-1, width, width) for out in outs[:-1]], outs[-1])


def gather_later(own):
    depth, eighths = lax.axis_size("fsdp"), lax.axis_size("dp")
    if depth != 4 or eighths != 8:
        return lax.all_gather(own, "fsdp", axis=1, tiled=True)
    return lax.all_gather(own, ("fsdp", "dp"), axis=1).reshape(-1, D, D)


def share_kernel(count, *refs):
    owns, outs, (send, recv) = (refs[:count], refs[count : 2 * count], refs[2 * count :])
    d, z, zs = places()
    sib, near_x, near_y = flip(d, 1), flip(d, 2), flip(d, 4)
    diagonal = flip(near_x, 4)
    greet(
        [(d, zs[1]), (d, zs[2]), (d, zs[3]), (sib, z), (near_x, z), (near_y, z), (diagonal, z)]
    )
    for own, out in zip(owns, outs):
        out[d, z] = own[...]
    started = []

    def push(slot, origin, to, first=False):
        copies = []
        for i in range(count):
            copies.append(
                pltpu.make_async_remote_copy(
                    src_ref=owns[i] if first else outs[i].at[origin],
                    dst_ref=outs[i].at[origin, z] if first else outs[i].at[origin],
                    send_sem=send.at[i, slot],
                    recv_sem=recv.at[i, slot],
                    device_id=to,
                    device_id_type=MESH,
                )
            )
            copies[-1].start()
        started.extend(copies)
        return copies

    def arrive(copies):
        for copy in copies:
            copy.wait_recv()

    first = [push(o - 1, d, (d, zs[o]), True) for o in (1, 2, 3)]
    for copies in first:
        arrive(copies)
    second = [push(3 + i, d, (to, z)) for i, to in enumerate((near_x, near_y, diagonal))]
    last = [push(6, d, (sib, z))]
    for i, origin in enumerate((near_x, near_y, diagonal)):
        arrive(second[i])
        last.append(push(7 + i, origin, (sib, z)))
    for copies in last:
        arrive(copies)
    for copy in started:
        copy.wait_send()


def share(owns, collective):
    lanes, depth = lax.axis_size("dp"), lax.axis_size("fsdp")
    if depth != 4 or lanes != 8:
        return [
            lax.all_gather(own, ("dp", "fsdp"), axis=0).reshape((lanes, depth) + own.shape)
            for own in owns
        ]
    count = len(owns)
    return pl.pallas_call(
        functools.partial(share_kernel, count),
        out_shape=[jax.ShapeDtypeStruct((lanes, depth) + own.shape, own.dtype) for own in owns],
        in_specs=[pl.BlockSpec(memory_space=pltpu.VMEM)] * count,
        out_specs=[pl.BlockSpec(memory_space=pltpu.VMEM)] * count,
        scratch_shapes=[
            pltpu.SemaphoreType.DMA((count, 10)),
            pltpu.SemaphoreType.DMA((count, 10)),
        ],
        compiler_params=pltpu.CompilerParams(collective_id=collective, has_side_effects=True),
        name=f"share_{collective}",
    )(*owns)


class Reduction:
    def __init__(self, source, start, first, n, buffers, k, semaphores, spots):
        self.source, self.start, self.first, self.n, self.k = (source, start, first, n, k)
        self.held, self.from_core, self.from_near, self.from_turn, self.ready, self.from_z = buffers
        self.local_sem, self.send, self.recv = semaphores
        self.spots = spots
        self.rows = pl.ds(first, n)
        self.started = []

    def push(self, slot, source, target, to):
        copy = pltpu.make_async_remote_copy(
            src_ref=source,
            dst_ref=target,
            send_sem=self.send.at[self.k, slot],
            recv_sem=self.recv.at[self.k, slot],
            device_id=to,
            device_id_type=MESH,
        )
        copy.start()
        self.started.append(copy)
        return copy

    def begin(self):
        d, z, zs, x, y, c = self.spots
        blocks = pl.ds(self.start, self.n)
        self.local = pltpu.make_async_copy(
            self.source.at[blocks, :, :, :, c], self.held.at[self.rows], self.local_sem.at[self.k]
        )
        self.local.start()
        self.core = self.push(
            0,
            self.source.at[blocks, :, :, :, 1 - c],
            self.from_core.at[self.rows],
            (flip(d, 1), z),
        )

    def add(self, count, place):
        @pl.loop(0, self.n * count)
        def _(i):
            target, other = place(self.first + i // count, lax.rem(i, count))
            self.held[target] = self.held[target] + other

    def across_plane(self):
        d, z, zs, x, y, c = self.spots
        self.local.wait()
        self.core.wait_recv()

        def place(b, i):
            target = (b, i // 4, lax.rem(i // 2, 2), lax.rem(i, 2))
            return (target, self.from_core[target])

        self.add(16, place)
        self.near = [
            self.push(
                1,
                self.held.at[self.rows, 0:2, :, 1 - x],
                self.from_near.at[self.rows, 0:2],
                (flip(d, 2), z),
            ),
            self.push(
                2,
                self.held.at[self.rows, 2:4, 1 - y],
                self.from_near.at[self.rows, 2:4],
                (flip(d, 4), z),
            ),
        ]

    def turn(self):
        d, z, zs, x, y, c = self.spots

        def place_a(b, i):
            return ((b, i // 2, lax.rem(i, 2), x), self.from_near[b, i // 2, lax.rem(i, 2)])

        def place_b(b, i):
            return ((b, 2 + i // 2, y, lax.rem(i, 2)), self.from_near[b, 2 + i // 2, lax.rem(i, 2)])

        self.near[0].wait_recv()
        self.add(4, place_a)
        a = self.push(
            3,
            self.held.at[self.rows, 0:2, 1 - y, x],
            self.from_turn.at[self.rows, 0:2],
            (flip(d, 4), z),
        )
        self.near[1].wait_recv()
        self.add(4, place_b)
        b = self.push(
            4,
            self.held.at[self.rows, 2:4, y, 1 - x],
            self.from_turn.at[self.rows, 2:4],
            (flip(d, 2), z),
        )
        self.turned = [a, b]

    def along_z(self):
        d, z, zs, x, y, c = self.spots
        for copy in self.turned:
            copy.wait_recv()

        @pl.loop(0, self.n * 4)
        def _(i):
            b, zz = (self.first + i // 4, lax.rem(i, 4))
            self.ready[b, zz] = self.held[b, zz, y, x] + self.from_turn[b, zz]

        self.spread = [
            self.push(
                4 + o,
                self.ready.at[self.rows, zs[o]],
                self.from_z.at[self.rows, o - 1],
                (d, zs[o]),
            )
            for o in (1, 2, 3)
        ]

    def finish(self, out):
        d, z, zs, x, y, c = self.spots
        for copy in self.spread:
            copy.wait_recv()

        @pl.loop(self.first, self.first + self.n)
        def _(b):
            total = self.held[b, z, y, x].astype(jnp.float32) + self.from_turn[b, z].astype(
                jnp.float32
            )
            for o in range(3):
                total = total + self.from_z[b, o].astype(jnp.float32)
            out[b] = total

        for copy in self.started:
            copy.wait_send()


class Meeting:
    def __init__(self, blocks_of, sources, refs):
        self.blocks_of, self.sources = (blocks_of, sources)
        self.small_out, self.stats_out, self.mine, self.low = refs[:4]
        self.parts, self.stats, self.local_sem, self.send, self.recv = refs[4:9]
        self.part_send, self.part_recv = refs[9:]

    def push(self, slot, source, target, to, sems):
        copy = pltpu.make_async_remote_copy(
            src_ref=source,
            dst_ref=target,
            send_sem=sems[0].at[slot],
            recv_sem=sems[1].at[slot],
            device_id=to,
            device_id_type=MESH,
        )
        copy.start()
        return copy

    def run(self, small, results, spots, others):
        d, z, zs = spots[:3]
        total = jnp.zeros(results[0].shape[1:], jnp.float32)
        homes = {
            int(block): (lane, place)
            for lane, entry in enumerate(self.blocks_of)
            for place, block in enumerate(entry)
        }
        for block, (source, index) in enumerate(self.sources):
            value = results[source][index]
            total = total + value * value
            value = value.astype(self.low.dtype)
            self.low[block] = value
            lane, place = homes[block]
            self.parts[lane, place] = value
        for lane, entry in enumerate(self.blocks_of):
            for place, block in enumerate(entry):
                if block < 0:
                    self.parts[lane, place] = jnp.zeros_like(self.parts[lane, place])
        squares = jnp.sum(total, axis=(0, 1), keepdims=True)
        self.stats[...] = jnp.broadcast_to(squares, self.stats.shape)
        moved = [
            self.push(
                i,
                self.parts.at[other],
                self.mine.at[:, d],
                (other, z),
                (self.part_send, self.part_recv),
            )
            for i, other in enumerate(others)
        ]
        keep = pltpu.make_async_copy(self.parts.at[d], self.mine.at[:, d], self.local_sem)
        keep.start()
        pairs = [(small, self.small_out), (self.stats, self.stats_out)]
        for own, out in pairs:
            out[z, d] = own[...]
        started = []

        def push_all(slot, origin, to, first=False):
            copies = []
            for i, (own, out) in enumerate(pairs):
                copies.append(
                    self.push(
                        slot,
                        own if first else out.at[:, origin],
                        out.at[z, origin] if first else out.at[:, origin],
                        to,
                        (self.send.at[i], self.recv.at[i]),
                    )
                )
            started.extend(copies)
            return copies

        def arrive(copies):
            for copy in copies:
                copy.wait_recv()

        first = [push_all(o - 1, d, (d, zs[o]), True) for o in (1, 2, 3)]
        for copies in first:
            arrive(copies)
        second = [push_all(3 + i, d, (to, z)) for i, to in enumerate(others[:3])]
        last = [push_all(6, d, (others[3], z))]
        for i, origin in enumerate(others[:3]):
            arrive(second[i])
            last.append(push_all(7 + i, origin, (others[3], z)))
        for copies in last:
            arrive(copies)
        arrive(moved)
        for copy in started + moved:
            copy.wait_send()
        keep.wait()


def reduce_kernel(chunks, sources, sets, meeting, *refs):
    ins = refs[:sources]
    refs = refs[sources:]
    if meeting is not None:
        earlier, refs = (refs[0], refs[1:])
    outs = refs[:sets]
    refs = refs[sets:]
    if meeting is not None:
        outside, refs = (refs[:4], refs[4:])
    buffers = [refs[6 * i : 6 * i + 6] for i in range(sets)]
    semaphores = refs[6 * sets : 6 * sets + 3]
    d, z, zs = places()
    spots = (d, z, zs, lax.rem(d // 2, 2), d // 4, lax.rem(d, 2))
    sib, near_x, near_y = (flip(d, 1), flip(d, 2), flip(d, 4))
    diagonal = flip(near_x, 4)
    others = [near_x, near_y, diagonal, sib, flip(near_x, 1), flip(near_y, 1), flip(diagonal, 1)]
    if meeting is None:
        others = [near_x, near_y, sib]
    greet([(d, zs[1]), (d, zs[2]), (d, zs[3])] + [(other, z) for other in others])
    work = []
    for k, (source, start, first, n, which) in enumerate(chunks):
        work.append(
            Reduction(ins[source], start, first, n, buffers[which], k, semaphores, spots)
        )
        work[k].begin()
    count = len(chunks)
    for step in range(count + 3):
        if step < count:
            work[step].across_plane()
        if 1 <= step <= count:
            work[step - 1].turn()
        if 2 <= step <= count + 1:
            work[step - 2].along_z()
        if step >= 3:
            work[step - 3].finish(outs[chunks[step - 3][4]])
    if meeting is not None:
        tail = Meeting(*meeting, tuple(outside) + tuple(refs[6 * sets + 3 :]))
        tail.run(outs[1].at[0], (outs[0], earlier), spots, others)


def reduce_grads(grads, collective, small=None, meeting=None, earlier=None):
    lanes, depth = lax.axis_size("dp"), lax.axis_size("fsdp")
    rows = D // (lanes * depth)
    tail = (depth, 2, 2, 2)
    sources = [grad.reshape((-1,) + tail + (rows, D)) for grad in grads]
    chunks = []
    first = 0
    for i, source in enumerate(sources):
        for start in range(0, source.shape[0], 2):
            n = min(2, source.shape[0] - start)
            chunks.append((i, start, first, n, 0))
            first += n
    sets = [(first, (rows, D), jnp.bfloat16)]
    if small is not None:
        sources.append(small.reshape((1,) + tail + small.shape[1:]))
        chunks.insert(1, (len(sources) - 1, 0, 0, 1, 1))
        sets.append((1, small.shape[1:], jnp.float32))
    scratch = []
    for n, shape, kind in sets:
        scratch += [
            pltpu.VMEM((n, depth, 2, 2) + shape, kind),
            pltpu.VMEM((n, depth, 2, 2) + shape, kind),
            pltpu.VMEM((n, depth, 2) + shape, kind),
            pltpu.VMEM((n, depth) + shape, kind),
            pltpu.VMEM((n, depth) + shape, kind),
            pltpu.VMEM((n, 3) + shape, kind),
        ]
    scratch += [
        pltpu.SemaphoreType.DMA((len(chunks),)),
        pltpu.SemaphoreType.DMA((len(chunks), 8)),
        pltpu.SemaphoreType.DMA((len(chunks), 8)),
    ]
    out_shape = [jax.ShapeDtypeStruct((n,) + shape, jnp.float32) for n, shape, _ in sets]
    count = len(sources)
    if meeting is not None:
        blocks_of, origins = meeting
        most = len(blocks_of[0])
        out_shape += [
            jax.ShapeDtypeStruct((depth, lanes) + small.shape[1:], jnp.float32),
            jax.ShapeDtypeStruct((depth, lanes, 8, 128), jnp.float32),
            jax.ShapeDtypeStruct((most, lanes, rows, D), jnp.bfloat16),
            jax.ShapeDtypeStruct((len(origins), rows, D), jnp.bfloat16),
        ]
        scratch += [
            pltpu.VMEM((lanes, most, rows, D), jnp.bfloat16),
            pltpu.VMEM((8, 128), jnp.float32),
            pltpu.SemaphoreType.DMA,
            pltpu.SemaphoreType.DMA((2, 10)),
            pltpu.SemaphoreType.DMA((2, 10)),
            pltpu.SemaphoreType.DMA((7,)),
            pltpu.SemaphoreType.DMA((7,)),
        ]
        sources.append(earlier)
    return pl.pallas_call(
        functools.partial(reduce_kernel, chunks, count, len(sets), meeting),
        out_shape=out_shape,
        in_specs=whole("a" * count + "v" * (len(sources) - count)),
        out_specs=whole("v" * len(out_shape)),
        scratch_shapes=scratch,
        compiler_params=pltpu.CompilerParams(
            collective_id=collective, has_side_effects=True, vmem_limit_bytes=VMEM_LIMIT
        ),
        name=f"reduce_{collective}",
    )(*sources)


def spread_stages(own, out, local_sem, send, recv):
    d, z, _ = places()
    sib, near_x, near_y = flip(d, 1), flip(d, 2), flip(d, 4)
    diagonal = flip(near_x, 4)
    half = own.shape[0] // 2
    parts = (pl.ds(0, half), pl.ds(half, own.shape[0] - half))
    started = []
    last = []

    def push(slot, origin, part, to, source=None):
        copy = pltpu.make_async_remote_copy(
            src_ref=out.at[part, origin] if source is None else source,
            dst_ref=out.at[part, origin],
            send_sem=send.at[slot],
            recv_sem=recv.at[slot],
            device_id=to,
            device_id_type=MESH,
        )
        copy.start()
        started.append(copy)
        return copy

    keep = pltpu.make_async_copy(own, out.at[:, d], local_sem)
    near = {}
    turned = []

    def begin():
        for way, part in ((0, 0), (1, 1), (0, 1), (1, 0)):
            near[way, part] = push(
                2 * way + part, d, parts[part], ((near_x, near_y)[way], z), own.at[parts[part]]
            )
        keep.start()
        last.extend([push(4 + i, d, parts[i], (sib, z), own.at[parts[i]]) for i in (0, 1)])

    def forward():
        near[0, 0].wait_recv()
        turned.append(push(6, near_x, parts[0], (near_y, z)))
        last.append(push(7, near_x, parts[0], (sib, z)))
        near[1, 1].wait_recv()
        turned.append(push(8, near_y, parts[1], (near_x, z)))
        last.append(push(9, near_y, parts[1], (sib, z)))

    def collect():
        near[1, 0].wait_recv()
        last.append(push(10, near_y, parts[0], (sib, z)))
        near[0, 1].wait_recv()
        last.append(push(11, near_x, parts[1], (sib, z)))
        for i in (0, 1):
            turned[i].wait_recv()
            last.append(push(12 + i, diagonal, parts[i], (sib, z)))

    def finish():
        for copy in last:
            copy.wait_recv()
        for copy in started:
            copy.wait_send()
        keep.wait()

    return (begin, forward, collect, finish)


GRAM_TILE = 128


def gram_kernel(gram, own, total, shards, left, right, onward, back, sems, local_sem, send, recv):
    d, z, _ = places()
    up, down = (z + 1, z - 1)
    two = jnp.logical_and(lax.rem(d, 2) == 1, d // 4 == 1)
    sib, near_x, near_y = flip(d, 1), flip(d, 2), flip(d, 4)
    greet([(d, lax.rem(z + step, 4)) for step in (1, 2, 3)] + [(sib, z), (near_x, z), (near_y, z)])
    stages = spread_stages(own, shards, local_sem, send, recv)
    stages[0]()
    count = D // GRAM_TILE

    def at(ref, slot, j):
        return ref.at[slot, pl.ds(j * GRAM_TILE, GRAM_TILE), pl.ds(j * GRAM_TILE, D - j * GRAM_TILE)]

    def copy(source, target, slot, j, way, to):
        return pltpu.make_async_remote_copy(
            src_ref=at(source, slot, j),
            dst_ref=at(target, slot, j),
            send_sem=sems.at[2 * way, slot, j],
            recv_sem=sems.at[2 * way + 1, slot, j],
            device_id=(d, to),
            device_id_type=MESH,
        )

    def add(target, slot, j, *terms):
        @pl.loop(0, GRAM_TILE // 16)
        def _(i):
            rows = pl.ds(pl.multiple_of(j * GRAM_TILE + i * 16, 16), 16)
            columns = pl.ds(j * GRAM_TILE, D - j * GRAM_TILE)
            value = terms[0][slot, rows, columns]
            for term in terms[1:]:
                value = value + term[slot, rows, columns]
            target[slot, rows, columns] = value

    def ends(slot):
        @pl.when(z == 0)
        def _():
            for j in range(count):
                copy(gram, left, slot, j, 0, up).start()

        @pl.when(z == 3)
        def _():
            for j in range(count):
                copy(gram, right, slot, j, 1, down).start()

    def near(slot, j):
        @pl.when(z == 1)
        def _():
            copy(onward, left, slot, j, 0, up).wait_recv()
            add(onward, slot, j, gram, left)
            copy(onward, left, slot, j, 0, up).start()

        @pl.when(z == 2)
        def _():
            copy(back, right, slot, j, 1, down).wait_recv()
            add(back, slot, j, gram, right)
            copy(back, right, slot, j, 1, down).start()

    def far(slot, j):
        @pl.when(z == 1)
        def _():
            copy(back, right, slot, j, 1, down).wait_recv()
            add(back, slot, j, gram, right)
            copy(back, right, slot, j, 1, down).start()
            add(total, slot, j, onward, right)

        @pl.when(z == 2)
        def _():
            copy(onward, left, slot, j, 0, up).wait_recv()
            add(onward, slot, j, gram, left)
            copy(onward, left, slot, j, 0, up).start()
            add(total, slot, j, onward, right)

    def close(slot, j):
        @pl.when(z == 3)
        def _():
            copy(gram, left, slot, j, 0, up).wait_recv()
            add(total, slot, j, left, gram)

        @pl.when(z == 0)
        def _():
            copy(gram, right, slot, j, 1, down).wait_recv()
            add(total, slot, j, gram, right)

    def finish(slot):
        for j in range(count):
            @pl.when(z == 0)
            def _():
                copy(gram, left, slot, j, 0, up).wait_send()

            @pl.when(z == 3)
            def _():
                copy(gram, right, slot, j, 1, down).wait_send()

            @pl.when(jnp.logical_and(z > 0, z < 3))
            def _():
                copy(onward, left, slot, j, 0, up).wait_send()
                copy(back, right, slot, j, 1, down).wait_send()

    def mirror(slot):
        for i in range(count):
            for j in range(i + 1, count):
                block = total[slot, i * GRAM_TILE : (i + 1) * GRAM_TILE, j * GRAM_TILE : (j + 1) * GRAM_TILE]
                total[slot, j * GRAM_TILE : (j + 1) * GRAM_TILE, i * GRAM_TILE : (i + 1) * GRAM_TILE] = block.T

    ends(0)

    @pl.when(two)
    def _():
        ends(1)

    def guarded(action, item):
        if item[0] == 0:
            action(*item)
        else:
            pl.when(two)(lambda: action(*item))

    skew = 2
    items = [(slot, j) for slot in (0, 1) for j in range(count)]
    for step in range(len(items) + skew):
        if step < len(items):
            guarded(near, items[step])
        if step >= skew:
            guarded(far, items[step - skew])
            guarded(close, items[step - skew])
        if step == 3:
            stages[1]()
        if step == count + 1:
            stages[2]()

    mirror(0)

    @pl.when(two)
    def _():
        mirror(1)

    finish(0)

    @pl.when(two)
    def _():
        finish(1)

    stages[3]()


def sum_grams(grams, own, collective):
    lanes = lax.axis_size("dp")
    whole = pltpu.VMEM(grams.shape, jnp.float32)
    return pl.pallas_call(
        gram_kernel,
        out_shape=[
            jax.ShapeDtypeStruct(grams.shape, jnp.float32),
            jax.ShapeDtypeStruct(own.shape[:1] + (lanes,) + own.shape[1:], own.dtype),
        ],
        in_specs=[pl.BlockSpec(memory_space=pltpu.VMEM)] * 2,
        out_specs=[
            pl.BlockSpec(memory_space=pltpu.VMEM),
            pl.BlockSpec(memory_space=pl.ANY),
        ],
        scratch_shapes=[
            whole,
            whole,
            whole,
            whole,
            pltpu.SemaphoreType.DMA((4, grams.shape[0], D // GRAM_TILE)),
            pltpu.SemaphoreType.DMA,
            pltpu.SemaphoreType.DMA((14,)),
            pltpu.SemaphoreType.DMA((14,)),
        ],
        compiler_params=pltpu.CompilerParams(
            collective_id=collective, has_side_effects=True, vmem_limit_bytes=VMEM_LIMIT
        ),
        name=f"gram_{collective}",
    )(grams, own)


def schulz_kernel(two, gram, rows, out, state, state_low, change, current):
    tile = 256

    def chain(slot, first, places_here, step):
        total = jnp.zeros((1, 1), jnp.float32)
        for t in range(0, D, tile):
            value = gram[slot, t : t + tile, :]
            line = lax.broadcasted_iota(jnp.int32, value.shape, 0) + t
            column = lax.broadcasted_iota(jnp.int32, value.shape, 1)
            total = total + jnp.sum(
                jnp.where(line == column, value, 0.0), axis=(0, 1), keepdims=True
            )
        inverse = 1.0 / (jnp.sqrt(total) + 1e-07)

        @pl.loop(0, D // tile)
        def _(t):
            part = pl.ds(pl.multiple_of(t * tile, tile), tile)
            value = gram[slot, part, :] * (inverse * inverse)
            state[part, :] = value
            state_low[part, :] = value.astype(jnp.bfloat16)

        for place in range(places_here):
            current[first + place] = rows[first + place] * inverse

        @pl.loop(0, NS_ITERS)
        def _(turn):
            @pl.loop(0, D // tile)
            def _(t):
                part = pl.ds(pl.multiple_of(t * tile, tile), tile)
                square = jnp.dot(
                    state_low[part, :], state_low[...], preferred_element_type=jnp.float32
                )
                change[part, :] = (COEF_B * state[part, :] + COEF_C * square).astype(jnp.bfloat16)

            @pl.loop(first, first + places_here)
            def _(place):
                value = current[place]
                current[place] = COEF_A * value + jnp.dot(
                    value.astype(jnp.bfloat16), change[...], preferred_element_type=jnp.float32
                )

            @pl.when(turn < NS_ITERS - 1)
            def _():
                @pl.loop(0, D // tile)
                def _(t):
                    part = pl.ds(pl.multiple_of(t * tile, tile), tile)
                    value = state[part, :]
                    for _ in range(2):
                        value = COEF_A * value + jnp.dot(
                            value.astype(jnp.bfloat16),
                            change[...],
                            preferred_element_type=jnp.float32,
                        )
                    state[part, :] = value
                    state_low[part, :] = value.astype(jnp.bfloat16)

        for place in range(places_here):
            out[first + place] = current[first + place].astype(jnp.bfloat16)

    @pl.when(two[0] == 0)
    def _():
        chain(0, 0, 4, 0)

    @pl.when(two[0] == 1)
    def _():
        chain(0, 0, 1, 0)
        chain(1, 1, 1, 0)
        for place in (2, 3):
            out[place] = jnp.zeros(out.shape[1:], jnp.bfloat16)


def schulz(two, grams, rows):
    return pl.pallas_call(
        schulz_kernel,
        out_shape=jax.ShapeDtypeStruct(rows.shape, jnp.bfloat16),
        in_specs=[
            pl.BlockSpec(memory_space=pltpu.SMEM),
            pl.BlockSpec(memory_space=pltpu.VMEM),
            pl.BlockSpec(memory_space=pltpu.VMEM),
        ],
        out_specs=pl.BlockSpec(memory_space=pltpu.VMEM),
        scratch_shapes=[
            pltpu.VMEM((D, D), jnp.float32),
            pltpu.VMEM((D, D), jnp.bfloat16),
            pltpu.VMEM((D, D), jnp.bfloat16),
            pltpu.VMEM(rows.shape, jnp.float32),
        ],
        compiler_params=pltpu.CompilerParams(vmem_limit_bytes=VMEM_LIMIT),
        name="schulz",
    )(two, grams, rows)


def spread_kernel(own, out, local_sem, send, recv):
    d, z, _ = places()
    greet([(flip(d, 1), z), (flip(d, 2), z), (flip(d, 4), z)])
    for stage in spread_stages(own, out, local_sem, send, recv):
        stage()


def spread(own, collective):
    lanes = lax.axis_size("dp")
    return pl.pallas_call(
        spread_kernel,
        out_shape=jax.ShapeDtypeStruct(own.shape[:1] + (lanes,) + own.shape[1:], own.dtype),
        in_specs=[pl.BlockSpec(memory_space=pltpu.VMEM)],
        out_specs=pl.BlockSpec(memory_space=pl.ANY),
        scratch_shapes=[
            pltpu.SemaphoreType.DMA,
            pltpu.SemaphoreType.DMA((14,)),
            pltpu.SemaphoreType.DMA((14,)),
        ],
        compiler_params=pltpu.CompilerParams(
            collective_id=collective, has_side_effects=True, vmem_limit_bytes=VMEM_LIMIT
        ),
        name=f"spread_{collective}",
    )(own)


def update_kernel(table, scale, clip, momenta, grads, weights, turned, momenta_new, weights_new, weights_low):
    b = pl.program_id(0)
    momenta_new[...] = MOMENT * momenta[...] + clip[0] * grads[...].astype(jnp.float32)
    value = weights[...] * (1.0 - MUON_RATE * MUON_DECAY) - scale[b] * turned[0].astype(jnp.float32)
    weights_new[...] = value
    weights_low[...] = value.astype(jnp.bfloat16)


def update(home, scale, clip, momenta, grads, weights, turned):
    blocks, rows, width = weights.shape
    table = np.array([home[block][1] for block in range(blocks)] + [home[block][0] for block in range(blocks)], np.int32)
    block = pl.BlockSpec((1, rows, width), lambda b, *_: (b, 0, 0))
    return pl.pallas_call(
        update_kernel,
        grid_spec=pltpu.PrefetchScalarGridSpec(
            num_scalar_prefetch=3,
            grid=(blocks,),
            in_specs=[
                block,
                block,
                block,
                pl.BlockSpec(
                    (1, 1, rows, width),
                    lambda b, table, *_: (table[b], table[blocks + b], 0, 0),
                ),
            ],
            out_specs=[block, block, block],
        ),
        out_shape=[
            jax.ShapeDtypeStruct(weights.shape, jnp.float32),
            jax.ShapeDtypeStruct(weights.shape, jnp.float32),
            jax.ShapeDtypeStruct(weights.shape, jnp.bfloat16),
        ],
        compiler_params=pltpu.CompilerParams(vmem_limit_bytes=VMEM_LIMIT),
        name="update",
    )(jnp.asarray(table), jnp.asarray(scale), clip.reshape(1), momenta, grads, weights, turned)


GROUP = 4 * HD


def normed_head(value, gain):
    centred = value - jnp.mean(value, 0, keepdims=True)
    scale = lax.rsqrt(jnp.mean(centred * centred, 0, keepdims=True) + 1e-06)
    centred = centred * scale
    return (centred * gain, centred, scale)


def contract_first(left, right):
    return lax.dot_general(
        left, right, (((0,), (0,)), ((), ())), preferred_element_type=jnp.float32
    )


def contract_last(left, right):
    return lax.dot_general(
        left, right, (((1,), (1,)), ((), ())), preferred_element_type=jnp.float32
    )


def head_shares(query_low, key_low, same):
    scores = contract_first(key_low, query_low) * (1.0 / math.sqrt(HD))
    scores = jnp.where(same, scores, -1e30)
    exponent = jnp.exp(scores - jnp.max(scores, 0, keepdims=True))
    return exponent * (1.0 / jnp.sum(exponent, 0, keepdims=True))


TILE = 256
SLOPE = math.sqrt(2.0 / math.pi)
CUBIC = 0.044715


def tile_of(t, size=TILE):
    return pl.ds(pl.multiple_of(t * size, size), size)


def row_norm(value):
    centred = value - jnp.mean(value, -1, keepdims=True)
    scale = lax.rsqrt(jnp.mean(centred * centred, -1, keepdims=True) + 1e-06)
    return (centred * scale, scale)


def gelu_parts(value):
    square = value * value
    bend = jnp.tanh(SLOPE * value * (1.0 + CUBIC * square))
    half = 0.5 + 0.5 * bend
    slope = half + 0.5 * value * (1.0 - bend * bend) * SLOPE * (1.0 + 3.0 * CUBIC * square)
    return (value * half, slope)


def load_all(pairs, sem):
    copies = [
        pltpu.make_async_copy(source, target, sem.at[i])
        for i, (source, target) in enumerate(pairs)
    ]
    for copy in copies:
        copy.start()
    return copies


def stand_up(row):
    return jnp.broadcast_to(row, (8, row.shape[1])).T[:, :1]


def slot_marks(segment, b):
    row = segment[b : b + 1].astype(jnp.float32)
    return (stand_up(row), row)


def norm_rows(source, gains, first, target):
    gain, shift = (gains[first : first + 1], gains[first + 1 : first + 2])

    @pl.loop(0, source.shape[0] // 64)
    def _(t):
        part = tile_of(t, 64)
        target[part] = (row_norm(source[part])[0] * gain + shift).astype(target.dtype)


def forward_kernel(
    spans,
    base,
    state,
    gains,
    segment,
    mixing,
    mixing_out,
    upward,
    down,
    state_out,
    middle,
    mixed,
    heads_low,
    attended,
    normed_low,
    mixing_held,
    out_held,
    up_held,
    down_held,
    hidden,
    gain_query,
    gain_key,
    sem,
):
    mixing, mixing_out, upward, down = [
        ref.at[pl.ds(*span)] for ref, span in zip((mixing, mixing_out, upward, down), spans)
    ]
    loads = load_all(
        [(mixing, mixing_held), (mixing_out, out_held), (upward, up_held), (down, down_held)], sem
    )
    gain_query[...] = stand_up(gains[base + 4 : base + 5])
    gain_key[...] = stand_up(gains[base + 5 : base + 6])
    norm_rows(state, gains, base, heads_low)
    loads[0].wait()

    @pl.loop(0, 3 * D // TILE)
    def _(t):
        mixed[tile_of(t)] = contract_last(mixing_held[tile_of(t)], heads_low[...])

    parts, length = segment.shape
    for b in range(parts):
        column, row = slot_marks(segment, b)
        same = column == row
        tokens = slice(b * length, (b + 1) * length)

        @pl.loop(0, D // GROUP)
        def _(group):
            for head in range(GROUP // HD):
                first = group * GROUP + head * HD
                part = pl.ds(pl.multiple_of(first, HD), HD)
                query, key, value = [
                    mixed[pl.ds(pl.multiple_of(place * D + first, HD), HD), tokens]
                    for place in range(3)
                ]
                query_low = normed_head(query, gain_query[part])[0].astype(jnp.bfloat16)
                key_low = normed_head(key, gain_key[part])[0].astype(jnp.bfloat16)
                share = head_shares(query_low, key_low, same).astype(jnp.bfloat16)
                attended[part, tokens] = jnp.dot(
                    value.astype(jnp.bfloat16), share, preferred_element_type=jnp.float32
                ).astype(jnp.bfloat16)

    loads[1].wait()
    for t in range(state.shape[0] // TILE):
        part = slice(t * TILE, (t + 1) * TILE)
        middle[part] = state[part] + contract_first(attended[:, part], out_held[...])
    norm_rows(middle, gains, base + 2, normed_low)
    loads[2].wait()

    @pl.loop(0, FF // TILE)
    def _(t):
        value = contract_last(up_held[tile_of(t)], normed_low[...])
        hidden[tile_of(t)] = gelu_parts(value)[0].astype(jnp.bfloat16)

    loads[3].wait()
    for t in range(state.shape[0] // TILE):
        part = slice(t * TILE, (t + 1) * TILE)
        state_out[part] = middle[part] + contract_first(hidden[:, part], down_held[...])


def layer_weights(blocks):
    weights = [array.reshape(-1, D) for array, _, _ in blocks]
    return (weights, [(first * D, number * D) for _, first, number in blocks])


def layer_forward(state, blocks, gains, base, segment):
    tokens = state.shape[0]
    weights, spans = layer_weights(blocks)
    state_out, middle, mixed, heads_low, attended, normed_low = pl.pallas_call(
        functools.partial(forward_kernel, spans, base),
        out_shape=[
            jax.ShapeDtypeStruct((tokens, D), jnp.float32),
            jax.ShapeDtypeStruct((tokens, D), jnp.float32),
            jax.ShapeDtypeStruct((3 * D, tokens), jnp.float32),
            jax.ShapeDtypeStruct((tokens, D), jnp.bfloat16),
            jax.ShapeDtypeStruct((D, tokens), jnp.bfloat16),
            jax.ShapeDtypeStruct((tokens, D), jnp.bfloat16),
        ],
        in_specs=whole("vvvaaaa"),
        out_specs=whole("vvvvvv"),
        scratch_shapes=[pltpu.VMEM((number, D), jnp.bfloat16) for _, number in spans]
        + [
            pltpu.VMEM((FF, tokens), jnp.bfloat16),
            pltpu.VMEM((D, 1), jnp.float32),
            pltpu.VMEM((D, 1), jnp.float32),
            pltpu.SemaphoreType.DMA((4,)),
        ],
        compiler_params=pltpu.CompilerParams(vmem_limit_bytes=VMEM_LIMIT),
        name="layer_forward",
    )(state, gains, segment, *weights)
    return (state_out, (state, middle, mixed, heads_low, attended, normed_low))


def backward_kernel(
    spans,
    base,
    grad,
    middle,
    normed_low,
    gains,
    segment,
    state,
    mixed,
    heads_low,
    attended,
    mixing,
    mixing_out,
    upward,
    down,
    grad_out,
    gain_out,
    head_gain_out,
    grad_mixing,
    grad_mixing_out,
    grad_up,
    grad_down,
    state_held,
    mixed_held,
    heads_held,
    attended_held,
    mixing_held,
    out_held,
    up_held,
    down_held,
    low,
    inner,
    hidden_grad,
    mixed_low,
    attended_grad,
    made_up,
    made_down,
    made_mixing,
    made_out,
    gain_query,
    gain_key,
    sem,
    store_sem,
):
    mixing, mixing_out, upward, down = [
        ref.at[pl.ds(*span)] for ref, span in zip((mixing, mixing_out, upward, down), spans)
    ]
    loads = load_all(
        [
            (upward, up_held),
            (down, down_held),
            (mixing_out, out_held),
            (attended, attended_held),
            (mixed, mixed_held),
            (heads_low, heads_held),
            (mixing, mixing_held),
            (state, state_held),
        ],
        sem,
    )
    stores = [
        pltpu.make_async_copy(made_up, grad_up, store_sem.at[0]),
        pltpu.make_async_copy(made_down, grad_down, store_sem.at[1]),
        pltpu.make_async_copy(made_out, grad_mixing_out, store_sem.at[2]),
        pltpu.make_async_copy(made_mixing, grad_mixing, store_sem.at[3]),
    ]
    tokens = grad.shape[0]
    gain_out[...] = jnp.zeros_like(gain_out)
    gain_query[...] = stand_up(gains[base + 4 : base + 5])
    gain_key[...] = stand_up(gains[base + 5 : base + 6])

    @pl.loop(0, tokens // 64)
    def _(t):
        low[tile_of(t, 64)] = grad[tile_of(t, 64)].astype(jnp.bfloat16)

    loads[0].wait()
    loads[1].wait()

    @pl.loop(0, FF // TILE)
    def _(t):
        part = tile_of(t)
        value, slope = gelu_parts(contract_last(up_held[part], normed_low[...]))
        delta = (contract_last(down_held[part], low[...]) * slope).astype(jnp.bfloat16)
        hidden_grad[part] = delta
        made_down[part] = jnp.dot(
            value.astype(jnp.bfloat16), low[...], preferred_element_type=jnp.float32
        ).astype(jnp.bfloat16)
        made_up[part] = jnp.dot(
            delta, normed_low[...], preferred_element_type=jnp.float32
        ).astype(jnp.bfloat16)

    stores[0].start()
    stores[1].start()
    for t in range(tokens // TILE):
        part = slice(t * TILE, (t + 1) * TILE)
        inner[part] = contract_first(hidden_grad[:, part], up_held[...])

    def norm_back(source, first, previous, target, target_low):
        gain = gains[base + first : base + first + 1]

        @pl.loop(0, tokens // 64)
        def _(t):
            part = tile_of(t, 64)
            unit, scale = row_norm(source[part])
            delta = inner[part]
            gain_out[first : first + 1] += jnp.sum(delta * unit, 0, keepdims=True)
            gain_out[first + 1 : first + 2] += jnp.sum(delta, 0, keepdims=True)
            delta = delta * gain
            delta = delta - jnp.mean(delta, -1, keepdims=True) - unit * jnp.mean(
                delta * unit, -1, keepdims=True
            )
            value = previous[part] + delta * scale
            target[part] = value
            if target_low is not None:
                target_low[part] = value.astype(jnp.bfloat16)

    norm_back(middle, 2, grad, grad_out, low)
    loads[2].wait()
    loads[3].wait()

    @pl.loop(0, D // TILE)
    def _(t):
        part = tile_of(t)
        made_out[part] = jnp.dot(
            attended_held[part], low[...], preferred_element_type=jnp.float32
        ).astype(jnp.bfloat16)
        attended_grad[part] = contract_last(out_held[part], low[...]).astype(jnp.bfloat16)

    stores[2].start()
    loads[4].wait()
    parts, length = segment.shape
    for b in range(parts):
        column, row = slot_marks(segment, b)
        same = column == row
        span = slice(b * length, (b + 1) * length)

        @pl.loop(0, D // GROUP)
        def _(group):
            for head in range(GROUP // HD):
                first = group * GROUP + head * HD
                part = pl.ds(pl.multiple_of(first, HD), HD)
                where = [pl.ds(pl.multiple_of(place * D + first, HD), HD) for place in range(3)]
                query, key, value = [mixed_held[at, span] for at in where]
                query_value, query_unit, query_scale = normed_head(query, gain_query[part])
                key_value, key_unit, key_scale = normed_head(key, gain_key[part])
                query_low = query_value.astype(jnp.bfloat16)
                key_low = key_value.astype(jnp.bfloat16)
                value_low = value.astype(jnp.bfloat16)
                out_low = attended_grad[part, span]
                share = head_shares(query_low, key_low, same)
                mixed_low[where[2], span] = contract_last(
                    out_low, share.astype(jnp.bfloat16)
                ).astype(jnp.bfloat16)
                share_grad = contract_first(value_low, out_low)
                total = jnp.sum(share * share_grad, 0, keepdims=True)
                score_low = (share * (share_grad - total) * (1.0 / math.sqrt(HD))).astype(
                    jnp.bfloat16
                )
                query_grad = jnp.dot(key_low, score_low, preferred_element_type=jnp.float32)
                key_grad = contract_last(query_low, score_low)
                for place, (delta, unit, scale, gain) in enumerate(
                    (
                        (query_grad, query_unit, query_scale, gain_query[part]),
                        (key_grad, key_unit, key_scale, gain_key[part]),
                    )
                ):
                    head_gain_out[b, place, part] = jnp.sum(delta * unit, 1, keepdims=True)
                    delta = delta * gain
                    delta = delta - jnp.mean(delta, 0, keepdims=True) - unit * jnp.mean(
                        delta * unit, 0, keepdims=True
                    )
                    mixed_low[where[place], span] = (delta * scale).astype(jnp.bfloat16)

    loads[5].wait()

    @pl.loop(0, 3 * D // TILE)
    def _(t):
        part = tile_of(t)
        made_mixing[part] = jnp.dot(
            mixed_low[part], heads_held[...], preferred_element_type=jnp.float32
        ).astype(jnp.bfloat16)

    stores[3].start()
    loads[6].wait()
    for t in range(tokens // TILE):
        part = slice(t * TILE, (t + 1) * TILE)
        inner[part] = contract_first(mixed_low[:, part], mixing_held[...])
    loads[7].wait()
    norm_back(state_held, 0, grad_out, grad_out, None)
    for copy in stores:
        copy.wait()


def layer_backward(grad, kept, blocks, gains, base, segment):
    state, middle, mixed, heads_low, attended, normed_low = kept
    tokens = grad.shape[0]
    weights, spans = layer_weights(blocks)
    low = jnp.bfloat16
    grad, gain_grads, head_gains, *block_grads = pl.pallas_call(
        functools.partial(backward_kernel, spans, base),
        out_shape=[
            jax.ShapeDtypeStruct((tokens, D), jnp.float32),
            jax.ShapeDtypeStruct((8, D), jnp.float32),
            jax.ShapeDtypeStruct((segment.shape[0], 2, D, 1), jnp.float32),
        ]
        + [jax.ShapeDtypeStruct((number, D), low) for _, number in spans],
        in_specs=whole("vvvvvaaaaaaaa"),
        out_specs=whole("vvvaaaa"),
        scratch_shapes=[
            pltpu.VMEM(state.shape, jnp.float32),
            pltpu.VMEM(mixed.shape, jnp.float32),
            pltpu.VMEM(heads_low.shape, low),
            pltpu.VMEM(attended.shape, low),
        ]
        + [pltpu.VMEM((number, D), low) for _, number in spans]
        + [
            pltpu.VMEM((tokens, D), low),
            pltpu.VMEM((tokens, D), jnp.float32),
            pltpu.VMEM((FF, tokens), low),
            pltpu.VMEM((3 * D, tokens), low),
            pltpu.VMEM((D, tokens), low),
            pltpu.VMEM((FF, D), low),
            pltpu.VMEM((FF, D), low),
            pltpu.VMEM((3 * D, D), low),
            pltpu.VMEM((D, D), low),
            pltpu.VMEM((D, 1), jnp.float32),
            pltpu.VMEM((D, 1), jnp.float32),
            pltpu.SemaphoreType.DMA((8,)),
            pltpu.SemaphoreType.DMA((4,)),
        ],
        compiler_params=pltpu.CompilerParams(vmem_limit_bytes=60 * 1024 * 1024),
        name="layer_backward",
    )(grad, middle, normed_low, gains, segment, state, mixed, heads_low, attended, *weights)
    gain_grads = jnp.concatenate([gain_grads[:4], jnp.sum(head_gains[..., 0], 0)], 0)
    return (grad, block_grads, gain_grads)


HEAD_LANES = 128


def full_dot(left, right):
    return jnp.dot(left, right, preferred_element_type=jnp.float32, precision=HIGH)


def head_marks():
    entry = lax.broadcasted_iota(jnp.int32, (D, HEAD_LANES), 0)
    lane = lax.broadcasted_iota(jnp.int32, (D, HEAD_LANES), 1)
    return (entry // HD == lane).astype(jnp.float32)


def full_dot_last(left, right):
    return lax.dot_general(
        left,
        right,
        (((1,), (1,)), ((), ())),
        preferred_element_type=jnp.float32,
        precision=HIGH,
    )


def pool_sequence(state, gains, marks_of):
    unit, scale = row_norm(state)
    final = unit * gains[0:1] + gains[1:2]
    marks = head_marks()
    logits = full_dot(final * gains[2:3], marks) * (1.0 / math.sqrt(HD))
    rows, columns = marks_of
    slot = lax.broadcasted_iota(jnp.int32, (rows.shape[0], IMGS), 1)
    member = (rows == slot.astype(jnp.float32)).astype(jnp.float32)
    slot = lax.broadcasted_iota(jnp.int32, (IMGS, columns.shape[1]), 0)
    member_rows = (columns == slot.astype(jnp.float32)).astype(jnp.float32)
    tops = jnp.zeros_like(logits)
    for k in range(IMGS):
        here = rows == k
        top = jnp.max(jnp.where(here, logits, -1e30), 0, keepdims=True)
        tops = jnp.where(here, top, tops)
    exponent = jnp.exp(logits - tops)
    share = exponent / full_dot(member, full_dot(member_rows, exponent))
    spread_share = full_dot_last(share, marks)
    dead = (jnp.sum(member_rows, 1, keepdims=True) == 0.0).astype(jnp.float32)
    pooled = full_dot(member_rows, spread_share * final) + dead * jnp.mean(
        final, 0, keepdims=True
    )
    return (unit, scale, final, marks, member, member_rows, share, spread_share, dead, pooled)


def unit_scale(value):
    return lax.rsqrt(jnp.mean(value * value, -1, keepdims=True) + 1e-06)


def pool_kernel(base, state, gains, segment, matrix, pooled_low, embedded, image_low):
    parts, length = segment.shape
    for b in range(parts):
        pooled = pool_sequence(
            state[b * length : (b + 1) * length], gains[base : base + 3], slot_marks(segment, b)
        )[-1]
        pooled_low[b] = pooled.astype(jnp.bfloat16)
        value = jnp.dot(
            pooled.astype(jnp.bfloat16), matrix[...], preferred_element_type=jnp.float32
        )
        embedded[b] = value
        image_low[b] = (value * unit_scale(value) * (1.0 / math.sqrt(D))).astype(jnp.bfloat16)


def pool_forward(state, gains, base, segment, matrix):
    parts = segment.shape[0]
    shape = (parts, IMGS, D)
    return pl.pallas_call(
        functools.partial(pool_kernel, base),
        out_shape=[
            jax.ShapeDtypeStruct(shape, jnp.bfloat16),
            jax.ShapeDtypeStruct(shape, jnp.float32),
            jax.ShapeDtypeStruct(shape, jnp.bfloat16),
        ],
        in_specs=whole("vvvv"),
        out_specs=whole("vvv"),
        compiler_params=pltpu.CompilerParams(vmem_limit_bytes=VMEM_LIMIT),
        name="pool_forward",
    )(state, gains, segment, matrix)


def contrast_kernel(
    base,
    me,
    images,
    texts,
    alive_columns,
    alive_rows,
    own_images,
    own_live,
    state,
    all_gains,
    segment,
    matrix,
    pooled_low,
    embedded,
    loss,
    grad,
    grad_matrix,
    gain_out,
    text_side,
):
    parts, length = segment.shape
    gains = all_gains[base : base + 3]
    everyone = images.shape[1]
    count = jnp.zeros((1, 1), jnp.float32)
    for b in range(parts):
        count = count + jnp.sum(alive_columns[b], -1, keepdims=True)
    factor = 1.0 / (2.0 * count)
    first = me[0] * IMGS

    def rows_of(scores, alive, live, start):
        masked = jnp.where(alive > 0, scores, -1e30)
        top = jnp.max(masked, -1, keepdims=True)
        exponent = jnp.exp(masked - top)
        total = jnp.sum(exponent, -1, keepdims=True)
        line = lax.broadcasted_iota(jnp.int32, scores.shape, 0) + start
        column = lax.broadcasted_iota(jnp.int32, scores.shape, 1)
        target = (line == column).astype(jnp.float32)
        diagonal = jnp.sum(scores * target, -1, keepdims=True)
        term = (top + jnp.log(total) - diagonal) * live
        delta = (exponent * (1.0 / total) - target) * live
        return (term, (delta * factor * LOGIT_SCALE).astype(jnp.bfloat16))

    loss[...] = jnp.zeros_like(loss)
    grad_sum = jnp.zeros((D, D), jnp.float32)
    gain_out[...] = jnp.zeros_like(gain_out)
    for b in range(parts):
        forward = LOGIT_SCALE * contract_last(own_images[b], texts[b])
        term, forward_low = rows_of(forward, alive_columns[b], own_live[b], first)
        loss[...] += jnp.sum(term, 0, keepdims=True) * factor
        text_side[...] = jnp.zeros_like(text_side)

        @pl.loop(0, everyone // TILE)
        def _(t):
            part = tile_of(t)
            backward = LOGIT_SCALE * contract_last(texts[b, part], images[b])
            term, backward_low = rows_of(
                backward, alive_columns[b], alive_rows[b, part], t * TILE
            )
            line = lax.broadcasted_iota(jnp.int32, term.shape, 0) + t * TILE
            here = jnp.logical_and(line >= first, line < first + IMGS)
            loss[...] += jnp.sum(jnp.where(here, term, 0.0), 0, keepdims=True) * factor
            text_side[...] += contract_first(backward_low, texts[b, part])

        image_grad = jnp.dot(forward_low, texts[b], preferred_element_type=jnp.float32)
        image_grad = image_grad + text_side[pl.ds(pl.multiple_of(first, IMGS), IMGS)]
        value = embedded[b]
        scale = unit_scale(value)
        embed_low = (
            (
                image_grad * scale
                - value * (scale * scale * scale) * jnp.mean(value * image_grad, -1, keepdims=True)
            )
            * (1.0 / math.sqrt(D))
        ).astype(jnp.bfloat16)
        grad_sum = grad_sum + contract_first(pooled_low[b], embed_low)
        pooled_grad = contract_last(embed_low, matrix[...])
        unit, norm_scale, final, marks, member, member_rows, share, spread_share, dead, _ = (
            pool_sequence(
                state[b * length : (b + 1) * length], gains, slot_marks(segment, b)
            )
        )
        token_grad = full_dot(member, pooled_grad)
        share_grad = full_dot(final * token_grad, marks)
        inside = full_dot(member, full_dot(member_rows, share * share_grad))
        logit_grad = share * (share_grad - inside) * (1.0 / math.sqrt(HD))
        spread_logit = full_dot_last(logit_grad, marks)
        final_grad = (
            spread_share * token_grad
            + spread_logit * gains[2:3]
            + jnp.sum(dead * pooled_grad, 0, keepdims=True) * (1.0 / length)
        )
        gain_out[0:1] += jnp.sum(final_grad * unit, 0, keepdims=True)
        gain_out[1:2] += jnp.sum(final_grad, 0, keepdims=True)
        gain_out[2:3] += jnp.sum(spread_logit * final, 0, keepdims=True)
        delta = final_grad * gains[0:1]
        delta = delta - jnp.mean(delta, -1, keepdims=True) - unit * jnp.mean(
            delta * unit, -1, keepdims=True
        )
        grad[b * length : (b + 1) * length] = delta * norm_scale
    grad_matrix[...] = grad_sum.astype(jnp.bfloat16)


def contrast(me, images, texts, alive, own_images, live, state, gains, base, segment, matrix, pooled_low, embedded):
    parts, everyone = alive.shape
    loss, grad, grad_matrix, gain_grads = pl.pallas_call(
        functools.partial(contrast_kernel, base),
        out_shape=[
            jax.ShapeDtypeStruct((8, 128), jnp.float32),
            jax.ShapeDtypeStruct(state.shape, jnp.float32),
            jax.ShapeDtypeStruct((D, D), jnp.bfloat16),
            jax.ShapeDtypeStruct((8, D), jnp.float32),
        ],
        in_specs=[pl.BlockSpec(memory_space=pltpu.SMEM)] + whole("vvvvvvvvvvvv"),
        out_specs=whole("vvvv"),
        scratch_shapes=[pltpu.VMEM((everyone, D), jnp.float32)],
        compiler_params=pltpu.CompilerParams(vmem_limit_bytes=VMEM_LIMIT),
        name="contrast",
    )(
        me.reshape(1),
        images,
        texts,
        alive[:, None, :],
        alive[:, :, None],
        own_images,
        live[:, :, None],
        state,
        gains,
        segment,
        matrix,
        pooled_low,
        embedded,
    )
    return (loss[0, 0], grad, grad_matrix, gain_grads[:3])


def muon_groups():
    found = [(0, 1), (1, 1)]
    for index in range(LAYERS):
        base = 2 + 12 * index
        found = found + [(base, 3), (base + 3, 1), (base + 4, 4), (base + 8, 4)]
    return found


def lane_plan(lanes):
    plan = [[] for _ in range(lanes)]
    for start, number in sorted(muon_groups(), key=lambda group: -group[1]):
        lane = min(range(lanes), key=lambda i: (sum(n for _, n in plan[i]), len(plan[i]), i))
        plan[lane].append((start, number))
    plan.sort(key=lambda entry: (-entry[0][1] if entry else 0))
    if lanes == 8:
        plan = [plan[i] for i in (0, 1, 2, 3, 4, 6, 5, 7)]
    depth = max(len(entry) for entry in plan)
    widths = [
        max([entry[slot][1] for entry in plan if slot < len(entry)]) for slot in range(depth)
    ]
    return (plan, widths)


def lane_blocks(plan):
    rows = [[start + i for start, number in entry for i in range(number)] for entry in plan]
    most = max(len(row) for row in rows)
    return np.array([row + [-1] * (most - len(row)) for row in rows], np.int32)


def lane_tables(plan, widths):
    index = np.zeros((len(plan), sum(widths)), np.int32)
    mask = np.zeros((len(plan), sum(widths)), np.float32)
    number = np.ones((len(plan), sum(widths)), np.float32)
    home = {}
    for lane, entry in enumerate(plan):
        first = 0
        for slot, width in enumerate(widths):
            if slot < len(entry):
                start, count = entry[slot]
                for place in range(count):
                    index[lane, first + place] = start + place
                    mask[lane, first + place] = 1.0
                    number[lane, first + place] = count
                    home[start + place] = (lane, first + place)
            first += width
    return (index, mask, number, home)


def orthogonal_factor(gram):
    size = jnp.sqrt(jnp.trace(gram)) + 1e-07
    state = gram / (size * size)
    total = None
    for turn in range(NS_ITERS):
        low = rounded(state)
        change = COEF_B * state + COEF_C * jnp.dot(low, low, preferred_element_type=jnp.float32)
        change_low = rounded(change)
        if total is None:
            total = COEF_A * jnp.eye(D, dtype=jnp.float32) + change
        else:
            total = COEF_A * total + jnp.dot(
                rounded(total), change_low, preferred_element_type=jnp.float32
            )
        if turn < NS_ITERS - 1:
            for _ in range(2):
                state = COEF_A * state + jnp.dot(
                    rounded(state), change_low, preferred_element_type=jnp.float32
                )
    return total / size


def per_device(
    patches, grid, segments, text_ids, table, weights, momenta, gains, gains_m, gains_v, step
):
    fin = 6 * LAYERS
    base = fin + 3
    lanes = lax.axis_size("dp")
    slots = jnp.arange(IMGS, dtype=jnp.int32)
    live = jnp.any(segments[:, 0, None, :] == slots[None, :, None], -1).astype(jnp.float32)
    depth = lax.axis_size("fsdp")
    captions = MB * IMGS
    tokens = text_ids.shape[3]
    fast = depth == 4 and lanes == 8
    early = [(0, 1), (2, 3), (5, 1), (6, 4), (10, 4), (1, 1)]
    later = []
    for index in range(1, LAYERS):
        start = 2 + 12 * index
        early = early + [(start, 3), (start + 3, 1)]
        later = later + [(start + 4, 4), (start + 8, 4)]
    later_own = jnp.concatenate([weights[a : a + n] for a, n in later], 0)
    if fast:
        eighth = weights.shape[1] // lanes
        later_own = lax.dynamic_slice_in_dim(later_own, lax.axis_index("dp") * eighth, eighth, 1)
    later_blocks = gather_later(rounded(later_own))
    if fast:
        half = tokens // 2
        own_ids = jnp.transpose(text_ids.reshape(captions, 2, half), (2, 1, 0)).reshape(half, -1)
        place = jnp.arange(depth * 2 * captions, dtype=jnp.int32) // (2 * captions)
        own_ids = jnp.where(
            place[None] == lax.axis_index("fsdp"), jnp.tile(own_ids, (1, depth)), 0
        )
        (stem, *first_blocks), text_sum = fetch(weights, early, own_ids, table, captions, 1)
    else:
        stem, *first_blocks = [
            lax.all_gather(rounded(weights[a : a + n]), "fsdp", axis=1, tiled=True)
            for a, n in early
        ]
        ids = lax.all_gather(text_ids.reshape(captions, tokens), "fsdp", axis=0)
        picked = ids.reshape(depth * captions, -1) - lax.axis_index("fsdp") * table.shape[0]
        row = jnp.arange(table.shape[0], dtype=jnp.int32)
        hits = jnp.sum((picked[:, :, None] == row[None, None, :]).astype(jnp.int32), 1)
        text_sum = lax.psum_scatter(
            jnp.dot(
                rounded(hits.astype(jnp.float32)), table, preferred_element_type=jnp.float32
            ).reshape(depth, captions, D),
            "fsdp",
            scatter_dimension=0,
        )
    early_blocks = first_blocks[5:]
    pooling_matrix = first_blocks[4][0]
    first_blocks = first_blocks[:4]
    text_low = rounded(unit_rows(text_sum / text_ids.shape[-1]))
    me = lax.axis_index(("dp", "fsdp"))
    segment = segments[:, 0]
    rows_hot, cols_hot = jax.vmap(positions)(grid[:, 0])
    rows_hot = rows_hot.reshape(-1, POS)
    cols_hot = cols_hot.reshape(-1, POS)
    patch_low = patches.reshape(-1, D)
    state = product(patch_low, stem[0], "sd,rd->sr")
    state = state + jnp.dot(rows_hot, gains[base : base + POS], precision=HIGH)
    state = state + jnp.dot(cols_hot, gains[base + POS : base + 2 * POS], precision=HIGH)
    saved = []
    for index in range(LAYERS):
        if index == 0:
            blocks = [(array, 0, array.shape[0]) for array in first_blocks]
        else:
            first = 8 * index - 8
            blocks = [
                (array, 0, array.shape[0]) for array in early_blocks[2 * index - 2 : 2 * index]
            ] + [(later_blocks, first, 4), (later_blocks, first + 4, 4)]
        state, kept = layer_forward(state, blocks, gains, 6 * index, segment)
        saved.append((kept, blocks))
    pooled_low, embedded, image_low = pool_forward(state, gains, fin, segment, pooling_matrix)
    own_flags = jnp.broadcast_to(live.reshape(captions, 1), (captions, 128)).astype(jnp.bfloat16)
    both = jnp.stack([image_low.reshape(captions, D), text_low]).reshape(2 * captions, D)
    gathered, flags = share([both, own_flags], 8)
    gathered = gathered.reshape(-1, 2, MB, IMGS, D)
    flags = flags.reshape(-1, MB, IMGS, 128)[..., 0].astype(jnp.float32)
    images, texts = [
        jnp.moveaxis(gathered[:, i], 0, 1).reshape(MB, -1, D) for i in range(2)
    ]
    loss_part, grad, grad_pool, pool_gain_grads = contrast(
        me,
        images,
        texts,
        jnp.moveaxis(flags, 0, 1).reshape(MB, -1),
        image_low,
        live,
        state,
        gains,
        fin,
        segment,
        pooling_matrix,
        pooled_low,
        embedded,
    )
    gain_parts = [None] * LAYERS
    block_grads = [None] * LAYERS
    slices = [None] * LAYERS
    for index in reversed(range(LAYERS)):
        kept, blocks = saved[index]
        grad, block_grads[index], gain_parts[index] = layer_backward(
            grad, kept, blocks, gains, 6 * index, segment
        )
        if index == 1:
            block_grads[index].append(grad_pool)
        if fast and index > 0:
            (slices[index],) = reduce_grads(block_grads[index], 4 + index)
    grad_low = rounded(grad)
    grad_patch = rounded(product(grad_low, patch_low, "sr,sd->rd"))
    block_grads[0].append(grad_patch)
    grad_rows = jnp.dot(rows_hot.T, grad, precision=HIGH)
    grad_cols = jnp.dot(cols_hot.T, grad, precision=HIGH)
    gains_grad = jnp.concatenate(
        gain_parts
        + [pool_gain_grads, grad_rows, grad_cols],
        0,
    )
    plan, widths = lane_plan(lanes)
    index, mask, number, home = lane_tables(plan, widths)
    lane = lax.axis_index("dp")
    scale = np.ones((weights.shape[0],), np.float32)
    for start, count_blocks in muon_groups():
        scale[start : start + count_blocks] = MUON_RATE * math.sqrt(count_blocks)
    if fast:
        width = 256
        small = jnp.concatenate([gains_grad.reshape(-1), loss_part[None]])
        small = jnp.pad(small, (0, lanes * depth * 8 * width - small.shape[0]))
        blocks_here = lane_blocks(plan)
        origins = [(0, 12), (1, 12)] + [
            (index, block) for index in range(LAYERS) for block in range(12)
        ]
        slices[0], _, small, stats, mine, slices = reduce_grads(
            block_grads[0],
            4,
            small.reshape(lanes * depth, 8, width),
            (blocks_here, origins),
            slices[1],
        )
        flat = small.reshape(-1)
        gains_grad, loss = (flat[: gains.size].reshape(gains.shape), flat[gains.size])
        squares = jnp.sum(stats[:, :, 0, 0])
        norm = jnp.sqrt(squares + jnp.sum(gains_grad * gains_grad))
        clip = jnp.minimum(1.0, CLIP_LIMIT / (norm + 1e-06))
        own_momenta = jnp.stack(
            [
                jnp.where(
                    jnp.asarray(blocks_here >= 0)[lane, place],
                    lax.dynamic_index_in_dim(
                        momenta, jnp.maximum(jnp.asarray(blocks_here)[lane, place], 0), 0, False
                    ),
                    0.0,
                )
                for place in range(blocks_here.shape[1])
            ]
        )
        own = MOMENT * own_momenta + clip * mine.reshape(own_momenta.shape).astype(jnp.float32)
        two = jnp.asarray(np.array([len(entry) > 1 for entry in plan], np.int32))[lane]
        own_low = rounded(own)
        first_low = jnp.concatenate(
            [own_low[:1], jnp.where(two > 0, jnp.bfloat16(0), own_low[1:])], 0
        )
        grams = jnp.stack(
            [
                product(first_low, first_low, "brd,bre->de"),
                product(own_low[1], own_low[1], "rd,re->de"),
            ]
        )
        grams, shard_grads = sum_grams(grams, slices, 12)
        turned = spread(schulz(two.reshape(1), grams, own), 13)
        homes = {
            int(block): (lane_of, place)
            for lane_of, entry in enumerate(blocks_here)
            for place, block in enumerate(entry)
            if block >= 0
        }
        momenta_new, weights_new, weights_low = update(
            homes, scale, clip, momenta, shard_grads.reshape(weights.shape), weights, turned
        )
    else:
        stack = jnp.concatenate(
            [block_grads[index].pop().reshape(1, D, D) for index in range(LAYERS)]
            + [value.reshape(-1, D, D) for values in block_grads for value in values],
            0,
        )
        shard_grads = lax.psum(
            lax.psum_scatter(stack, "fsdp", scatter_dimension=1, tiled=True), "dp"
        ).astype(jnp.float32)
        gains_grad, loss = lax.psum((gains_grad, loss_part), ("dp", "fsdp"))
        squares = lax.psum(jnp.sum(shard_grads * shard_grads), "fsdp")
        norm = jnp.sqrt(squares + jnp.sum(gains_grad * gains_grad))
        clip = jnp.minimum(1.0, CLIP_LIMIT / (norm + 1e-06))
        momenta_new = MOMENT * momenta + clip * shard_grads
        own = jnp.stack(
            [
                lax.dynamic_index_in_dim(momenta_new, jnp.asarray(index)[lane, place], 0, False)
                * jnp.asarray(mask)[lane, place]
                for place in range(index.shape[1])
            ]
        )
        own_low = rounded(own)
        bounds = np.cumsum([0] + widths)
        grams = jnp.stack(
            [
                product(own_low[a:b], own_low[a:b], "brd,bre->de")
                for a, b in zip(bounds[:-1], bounds[1:])
            ]
        )
        grams = lax.psum(grams, "fsdp")
        turned = jnp.concatenate(
            [
                product(
                    own_low[bounds[slot] : bounds[slot + 1]],
                    rounded(orthogonal_factor(grams[slot])),
                    "brd,de->bre",
                )
                for slot in range(len(widths))
            ],
            0,
        )
        spread_rows = lax.all_gather(rounded(turned), "dp", axis=0)
        current = jnp.stack(
            [spread_rows[home[block][0], home[block][1]] for block in range(weights.shape[0])]
        ).astype(jnp.float32)
        weights_new = weights * (1.0 - MUON_RATE * MUON_DECAY) - jnp.asarray(scale)[:, None, None] * current
        weights_low = rounded(weights_new)
    grad_small = clip * gains_grad
    moment_one = BETA_ONE * gains_m + (1.0 - BETA_ONE) * grad_small
    moment_two = BETA_TWO * gains_v + (1.0 - BETA_TWO) * grad_small * grad_small
    count_steps = step[0].astype(jnp.float32)
    corrected_one = moment_one / (1.0 - jnp.power(BETA_ONE, count_steps))
    corrected_two = moment_two / (1.0 - jnp.power(BETA_TWO, count_steps))
    gains_new = gains - ADAM_RATE * (
        corrected_one / (jnp.sqrt(corrected_two) + ADAM_EPS) + ADAM_DECAY * gains
    )
    shift_grad = grad_small[fin + 1]
    return (
        loss,
        norm,
        weights_new,
        weights_low,
        momenta_new,
        gains_new,
        moment_one,
        moment_two,
        shift_grad,
    )


def solution(mesh):
    placed = (
        P(None, ("dp", "fsdp"), None, None),
        P(None, ("dp", "fsdp"), None, None),
        P(None, ("dp", "fsdp"), None),
        P(None, ("dp", "fsdp"), None, None),
        P("fsdp", None),
        P(None, "fsdp", None),
        P(None, "fsdp", None),
        P(),
        P(),
        P(),
        P(),
    )
    return jax.shard_map(
        per_device,
        mesh=mesh,
        in_specs=placed,
        out_specs=(
            P(),
            P(),
            P(None, "fsdp", None),
            P(None, "fsdp", None),
            P(None, "fsdp", None),
            P(),
            P(),
            P(),
            P(),
        ),
        check_vma=False,
    )
```

```python
import functools
import math

import jax
import jax.numpy as jnp
import numpy as np
from jax import lax
from jax.experimental import pallas as pl
from jax.experimental.pallas import tpu as pltpu
from jax.sharding import PartitionSpec as P

D = 768
HEADS = 12
FF = 3072
LAYERS = 2
IMGS = 8
POS = 32
MB = 2
NS_ITERS = 5
HD = 64


MESH = pl.DeviceIdType.MESH
VMEM_LIMIT = 56 * 1024 * 1024
HIGH = lax.Precision.HIGHEST
LOGIT_SCALE = 50.0
CLIP_LIMIT = 0.005
MOMENT = 0.95
MUON_RATE = 0.5
MUON_DECAY = 0.01
ADAM_RATE = 0.4
BETA_ONE = 0.9
BETA_TWO = 0.999
ADAM_EPS = 1e-08
ADAM_DECAY = 0.01
COEF_A = 3.4445
COEF_B = -4.775
COEF_C = 2.0315


def rounded(value):
    return value.astype(jnp.bfloat16)


def product(left, right, form):
    return jnp.einsum(form, left, right, preferred_element_type=jnp.float32)


def unit_rows(value):
    return (
        value
        * lax.rsqrt(jnp.mean(value * value, -1, keepdims=True) + 1e-06)
        * (1.0 / math.sqrt(value.shape[-1]))
    )


def positions(grid):
    slots = jnp.arange(POS, dtype=jnp.int32)
    row_index = grid[0] * POS // grid[2]
    col_index = grid[1] * POS // grid[3]
    return (
        (row_index[:, None] == slots[None]).astype(jnp.float32),
        (col_index[:, None] == slots[None]).astype(jnp.float32),
    )


def whole(kinds):
    memory = {"v": pltpu.VMEM, "a": pl.ANY}
    return [pl.BlockSpec(memory_space=memory[kind]) for kind in kinds]


def flip(index, bit):
    return index + bit - 2 * bit * lax.rem(index // bit, 2)


def greet(peers):
    barrier = pltpu.get_barrier_semaphore()
    for peer in peers:
        pl.semaphore_signal(barrier, inc=1, device_id=peer, device_id_type=MESH)
    pl.semaphore_wait(barrier, len(peers))


def places():
    d = lax.axis_index("dp")
    z = lax.axis_index("fsdp")
    return (d, z, [lax.rem(z + step, 4) for step in range(4)])


CAPTION_TILE = 400


def fetch_kernel(chunks, sizes, weights, ids, table, *refs):
    outs = refs[: len(sizes)]
    text_sum = refs[len(sizes)]
    (
        full,
        low,
        all_ids,
        pages,
        found,
        found_parts,
        from_z,
        load_sem,
        store_sem,
        send,
        recv,
        page_sem,
        id_send,
        id_recv,
        part_send,
        part_recv,
    ) = refs[len(sizes) + 1 :]
    d, z, zs = places()
    sib, near_x, near_y = flip(d, 1), flip(d, 2), flip(d, 4)
    diagonal = flip(near_x, 4)
    starts = [sum(chunk[3] for chunk in chunks[:k]) for k in range(len(chunks))]
    loads = []
    for k, (source, _, _, n) in enumerate(chunks):
        loads.append(
            pltpu.make_async_copy(
                weights.at[pl.ds(source, n)], full.at[pl.ds(starts[k], n)], load_sem.at[k]
            )
        )
        loads[k].start()
    page_count = table.shape[0] // CAPTION_TILE

    def page(t):
        return pltpu.make_async_copy(
            table.at[tile_of(t, CAPTION_TILE)], pages.at[lax.rem(t, 2)], page_sem.at[lax.rem(t, 2)]
        )

    page(0).start()
    greet([(d, zs[1]), (d, zs[2]), (d, zs[3]), (sib, z), (near_x, z), (near_y, z)])
    pending = []
    all_ids[z] = ids[...]
    id_copies = []
    for o in (1, 2, 3):
        id_copies.append(
            pltpu.make_async_remote_copy(
                src_ref=ids,
                dst_ref=all_ids.at[z],
                send_sem=id_send.at[o - 1],
                recv_sem=id_recv.at[o - 1],
                device_id=(d, zs[o]),
                device_id_type=MESH,
            )
        )
        id_copies[-1].start()

    def push(k, slot, first, n, zz, dd, to, source=None):
        out = outs[chunks[k][1]]
        rows = pl.ds(chunks[k][2] + first, n)
        copy = pltpu.make_async_remote_copy(
            src_ref=out.at[rows, zz, dd] if source is None else source,
            dst_ref=out.at[rows, zz, dd],
            send_sem=send.at[k, slot],
            recv_sem=recv.at[k, slot],
            device_id=to,
            device_id_type=MESH,
        )
        copy.start()
        pending.append(copy)
        return copy

    along_z = []
    stores = []
    for k, (_, out, offset, n) in enumerate(chunks):
        loads[k].wait()

        @pl.loop(starts[k], starts[k] + n)
        def _(i):
            low[i] = full[i].astype(low.dtype)

        along_z.append(
            [
                push(k, o - 1, 0, n, z, d, (d, zs[o]), low.at[pl.ds(starts[k], n), d])
                for o in (1, 2, 3)
            ]
        )
        stores.append(
            pltpu.make_async_copy(
                low.at[pl.ds(starts[k], n)],
                outs[out].at[pl.ds(offset, n), z],
                store_sem.at[k],
            )
        )
        stores[k].start()
    for copy in id_copies:
        copy.wait_recv()
    marks = all_ids[0] + all_ids[1] + all_ids[2] + all_ids[3]
    found[...] = jnp.zeros_like(found)

    def look_up(t):
        @pl.when(t + 1 < page_count)
        def _():
            page(t + 1).start()

        page(t).wait()
        row = lax.broadcasted_iota(jnp.int32, (CAPTION_TILE, marks.shape[1]), 0)
        row = row + (z * table.shape[0] + t * CAPTION_TILE)
        hits = jnp.zeros(row.shape, jnp.float32)
        for token in range(marks.shape[0]):
            hits = hits + jnp.where(row == marks[token : token + 1], 1.0, 0.0)
        found[...] += contract_first(hits.astype(jnp.bfloat16), pages[lax.rem(t, 2)])

    def look_up_span(first, last):
        @pl.loop(first, last)
        def _(t):
            look_up(t)

    share_of = -(-page_count // (len(chunks) - 1))
    part_copies = []

    def send_parts():
        captions = found_parts.shape[1]
        for owner in range(4):
            found_parts[owner] = (
                found[2 * owner * captions : (2 * owner + 1) * captions]
                + found[(2 * owner + 1) * captions : (2 * owner + 2) * captions]
            )
        for o in (1, 2, 3):
            part_copies.append(
                pltpu.make_async_remote_copy(
                    src_ref=found_parts.at[zs[o]],
                    dst_ref=from_z.at[o - 1],
                    send_sem=part_send.at[o - 1],
                    recv_sem=part_recv.at[o - 1],
                    device_id=(d, zs[o]),
                    device_id_type=MESH,
                )
            )
            part_copies[-1].start()

    along_x, along_y, turn_y, turn_x, last = {}, {}, {}, {}, []
    count = len(chunks)
    for step in range(count + 2):
        if step < count:
            k, n = step, chunks[step][3]
            along_x[k], along_y[k] = [], []
            for o in (1, 2, 3):
                zz = zs[4 - o]
                along_z[k][o - 1].wait_recv()
                along_x[k].append(push(k, 2 + o, 0, n, zz, d, (near_x, z)))
                along_y[k].append(push(k, 5 + o, 0, n, zz, d, (near_y, z)))
                last.append(push(k, 14 + o, 0, n, zz, d, (sib, z)))
        if 1 <= step <= count:
            k, n = step - 1, chunks[step - 1][3]
            half = n // 2
            turn_y[k], turn_x[k] = [], []
            for o in (1, 2, 3):
                zz = zs[4 - o]
                along_x[k][o - 1].wait_recv()
                if half:
                    turn_y[k].append(push(k, 8 + o, 0, half, zz, near_x, (near_y, z)))
                last.append(push(k, 17 + o, 0, n, zz, near_x, (sib, z)))
                along_y[k][o - 1].wait_recv()
                turn_x[k].append(push(k, 11 + o, half, n - half, zz, near_y, (near_x, z)))
                last.append(push(k, 20 + o, 0, n, zz, near_y, (sib, z)))
        if step * share_of < page_count:
            look_up_span(step * share_of, min((step + 1) * share_of, page_count))
        if step == count - 1:
            send_parts()
        if step >= 2:
            k, n = step - 2, chunks[step - 2][3]
            for o in (1, 2, 3):
                for copies in (turn_y[k], turn_x[k]):
                    if copies:
                        copies[o - 1].wait_recv()
                last.append(push(k, 23 + o, 0, n, zs[4 - o], diagonal, (sib, z)))
    for copy in last:
        copy.wait_recv()
    for copy in pending:
        copy.wait_send()
    for copy in stores:
        copy.wait()
    for copy in id_copies:
        copy.wait_send()
    for copy in part_copies:
        copy.wait()
    text_sum[...] = found_parts[z] + from_z[0] + from_z[1] + from_z[2]


def fetch(weights, pieces, ids, table, captions, collective):
    depth, eighths = lax.axis_size("fsdp"), lax.axis_size("dp")
    blocks, rows, width = weights.shape
    part = (eighths, rows // eighths, width)
    chunks = []
    for out, (a, n) in enumerate(pieces):
        for first in range(0, n, 2):
            chunks.append((a + first, out, first, min(2, n - first)))
    total = sum(n for _, n in pieces)
    outs = pl.pallas_call(
        functools.partial(fetch_kernel, chunks, [n for _, n in pieces]),
        out_shape=[
            jax.ShapeDtypeStruct((n, depth) + part, jnp.bfloat16) for _, n in pieces
        ]
        + [jax.ShapeDtypeStruct((captions, width), jnp.float32)],
        in_specs=whole("ava"),
        out_specs=whole("a" * len(pieces) + "v"),
        scratch_shapes=[
            pltpu.VMEM((total,) + part, jnp.float32),
            pltpu.VMEM((total,) + part, jnp.bfloat16),
            pltpu.VMEM((depth,) + ids.shape, jnp.int32),
            pltpu.VMEM((2, CAPTION_TILE, width), jnp.bfloat16),
            pltpu.VMEM((2 * depth * captions, width), jnp.float32),
            pltpu.VMEM((depth, captions, width), jnp.float32),
            pltpu.VMEM((3, captions, width), jnp.float32),
            pltpu.SemaphoreType.DMA((len(chunks),)),
            pltpu.SemaphoreType.DMA((len(chunks),)),
            pltpu.SemaphoreType.DMA((len(chunks), 27)),
            pltpu.SemaphoreType.DMA((len(chunks), 27)),
            pltpu.SemaphoreType.DMA((2,)),
            pltpu.SemaphoreType.DMA((3,)),
            pltpu.SemaphoreType.DMA((3,)),
            pltpu.SemaphoreType.DMA((3,)),
            pltpu.SemaphoreType.DMA((3,)),
        ],
        compiler_params=pltpu.CompilerParams(
            collective_id=collective, has_side_effects=True, vmem_limit_bytes=VMEM_LIMIT
        ),
        name=f"fetch_{collective}",
    )(weights.reshape((blocks,) + part), ids, table)
    return ([out.reshape(-1, width, width) for out in outs[:-1]], outs[-1])


def gather_later(own):
    depth, eighths = lax.axis_size("fsdp"), lax.axis_size("dp")
    if depth != 4 or eighths != 8:
        return lax.all_gather(own, "fsdp", axis=1, tiled=True)
    return lax.all_gather(own, ("fsdp", "dp"), axis=1).reshape(-1, D, D)


def share_kernel(count, *refs):
    owns, outs, (send, recv) = (refs[:count], refs[count : 2 * count], refs[2 * count :])
    d, z, zs = places()
    sib, near_x, near_y = flip(d, 1), flip(d, 2), flip(d, 4)
    diagonal = flip(near_x, 4)
    greet(
        [(d, zs[1]), (d, zs[2]), (d, zs[3]), (sib, z), (near_x, z), (near_y, z), (diagonal, z)]
    )
    for own, out in zip(owns, outs):
        out[d, z] = own[...]
    started = []

    def push(slot, origin, to, first=False):
        copies = []
        for i in range(count):
            copies.append(
                pltpu.make_async_remote_copy(
                    src_ref=owns[i] if first else outs[i].at[origin],
                    dst_ref=outs[i].at[origin, z] if first else outs[i].at[origin],
                    send_sem=send.at[i, slot],
                    recv_sem=recv.at[i, slot],
                    device_id=to,
                    device_id_type=MESH,
                )
            )
            copies[-1].start()
        started.extend(copies)
        return copies

    def arrive(copies):
        for copy in copies:
            copy.wait_recv()

    first = [push(o - 1, d, (d, zs[o]), True) for o in (1, 2, 3)]
    for copies in first:
        arrive(copies)
    second = [push(3 + i, d, (to, z)) for i, to in enumerate((near_x, near_y, diagonal))]
    last = [push(6, d, (sib, z))]
    for i, origin in enumerate((near_x, near_y, diagonal)):
        arrive(second[i])
        last.append(push(7 + i, origin, (sib, z)))
    for copies in last:
        arrive(copies)
    for copy in started:
        copy.wait_send()


def share(owns, collective):
    lanes, depth = lax.axis_size("dp"), lax.axis_size("fsdp")
    if depth != 4 or lanes != 8:
        return [
            lax.all_gather(own, ("dp", "fsdp"), axis=0).reshape((lanes, depth) + own.shape)
            for own in owns
        ]
    count = len(owns)
    return pl.pallas_call(
        functools.partial(share_kernel, count),
        out_shape=[jax.ShapeDtypeStruct((lanes, depth) + own.shape, own.dtype) for own in owns],
        in_specs=[pl.BlockSpec(memory_space=pltpu.VMEM)] * count,
        out_specs=[pl.BlockSpec(memory_space=pltpu.VMEM)] * count,
        scratch_shapes=[
            pltpu.SemaphoreType.DMA((count, 10)),
            pltpu.SemaphoreType.DMA((count, 10)),
        ],
        compiler_params=pltpu.CompilerParams(collective_id=collective, has_side_effects=True),
        name=f"share_{collective}",
    )(*owns)


class Reduction:
    def __init__(self, source, start, first, n, buffers, k, semaphores, spots):
        self.source, self.start, self.first, self.n, self.k = (source, start, first, n, k)
        self.held, self.from_core, self.from_near, self.from_turn, self.ready, self.from_z = buffers
        self.local_sem, self.send, self.recv = semaphores
        self.spots = spots
        self.rows = pl.ds(first, n)
        self.started = []

    def push(self, slot, source, target, to):
        copy = pltpu.make_async_remote_copy(
            src_ref=source,
            dst_ref=target,
            send_sem=self.send.at[self.k, slot],
            recv_sem=self.recv.at[self.k, slot],
            device_id=to,
            device_id_type=MESH,
        )
        copy.start()
        self.started.append(copy)
        return copy

    def begin(self):
        d, z, zs, x, y, c = self.spots
        blocks = pl.ds(self.start, self.n)
        self.local = pltpu.make_async_copy(
            self.source.at[blocks, :, :, :, c], self.held.at[self.rows], self.local_sem.at[self.k]
        )
        self.local.start()
        self.core = self.push(
            0,
            self.source.at[blocks, :, :, :, 1 - c],
            self.from_core.at[self.rows],
            (flip(d, 1), z),
        )

    def add(self, count, place):
        @pl.loop(0, self.n * count)
        def _(i):
            target, other = place(self.first + i // count, lax.rem(i, count))
            self.held[target] = self.held[target] + other

    def across_plane(self):
        d, z, zs, x, y, c = self.spots
        self.local.wait()
        self.core.wait_recv()

        def place(b, i):
            target = (b, i // 4, lax.rem(i // 2, 2), lax.rem(i, 2))
            return (target, self.from_core[target])

        self.add(16, place)
        self.near = [
            self.push(
                1,
                self.held.at[self.rows, 0:2, :, 1 - x],
                self.from_near.at[self.rows, 0:2],
                (flip(d, 2), z),
            ),
            self.push(
                2,
                self.held.at[self.rows, 2:4, 1 - y],
                self.from_near.at[self.rows, 2:4],
                (flip(d, 4), z),
            ),
        ]

    def turn(self):
        d, z, zs, x, y, c = self.spots

        def place_a(b, i):
            return ((b, i // 2, lax.rem(i, 2), x), self.from_near[b, i // 2, lax.rem(i, 2)])

        def place_b(b, i):
            return ((b, 2 + i // 2, y, lax.rem(i, 2)), self.from_near[b, 2 + i // 2, lax.rem(i, 2)])

        self.near[0].wait_recv()
        self.add(4, place_a)
        a = self.push(
            3,
            self.held.at[self.rows, 0:2, 1 - y, x],
            self.from_turn.at[self.rows, 0:2],
            (flip(d, 4), z),
        )
        self.near[1].wait_recv()
        self.add(4, place_b)
        b = self.push(
            4,
            self.held.at[self.rows, 2:4, y, 1 - x],
            self.from_turn.at[self.rows, 2:4],
            (flip(d, 2), z),
        )
        self.turned = [a, b]

    def along_z(self):
        d, z, zs, x, y, c = self.spots
        for copy in self.turned:
            copy.wait_recv()

        @pl.loop(0, self.n * 4)
        def _(i):
            b, zz = (self.first + i // 4, lax.rem(i, 4))
            self.ready[b, zz] = self.held[b, zz, y, x] + self.from_turn[b, zz]

        self.spread = [
            self.push(
                4 + o,
                self.ready.at[self.rows, zs[o]],
                self.from_z.at[self.rows, o - 1],
                (d, zs[o]),
            )
            for o in (1, 2, 3)
        ]

    def finish(self, out):
        d, z, zs, x, y, c = self.spots
        for copy in self.spread:
            copy.wait_recv()

        @pl.loop(self.first, self.first + self.n)
        def _(b):
            total = self.held[b, z, y, x].astype(jnp.float32) + self.from_turn[b, z].astype(
                jnp.float32
            )
            for o in range(3):
                total = total + self.from_z[b, o].astype(jnp.float32)
            out[b] = total

        for copy in self.started:
            copy.wait_send()


class Meeting:
    def __init__(self, blocks_of, sources, refs):
        self.blocks_of, self.sources = (blocks_of, sources)
        self.small_out, self.stats_out, self.mine, self.low = refs[:4]
        self.parts, self.stats, self.local_sem, self.send, self.recv = refs[4:9]
        self.part_send, self.part_recv = refs[9:]

    def push(self, slot, source, target, to, sems):
        copy = pltpu.make_async_remote_copy(
            src_ref=source,
            dst_ref=target,
            send_sem=sems[0].at[slot],
            recv_sem=sems[1].at[slot],
            device_id=to,
            device_id_type=MESH,
        )
        copy.start()
        return copy

    def run(self, small, results, spots, others):
        d, z, zs = spots[:3]
        total = jnp.zeros(results[0].shape[1:], jnp.float32)
        homes = {
            int(block): (lane, place)
            for lane, entry in enumerate(self.blocks_of)
            for place, block in enumerate(entry)
        }
        for block, (source, index) in enumerate(self.sources):
            value = results[source][index]
            total = total + value * value
            value = value.astype(self.low.dtype)
            self.low[block] = value
            lane, place = homes[block]
            self.parts[lane, place] = value
        for lane, entry in enumerate(self.blocks_of):
            for place, block in enumerate(entry):
                if block < 0:
                    self.parts[lane, place] = jnp.zeros_like(self.parts[lane, place])
        squares = jnp.sum(total, axis=(0, 1), keepdims=True)
        self.stats[...] = jnp.broadcast_to(squares, self.stats.shape)
        moved = [
            self.push(
                i,
                self.parts.at[other],
                self.mine.at[:, d],
                (other, z),
                (self.part_send, self.part_recv),
            )
            for i, other in enumerate(others)
        ]
        keep = pltpu.make_async_copy(self.parts.at[d], self.mine.at[:, d], self.local_sem)
        keep.start()
        pairs = [(small, self.small_out), (self.stats, self.stats_out)]
        for own, out in pairs:
            out[z, d] = own[...]
        started = []

        def push_all(slot, origin, to, first=False):
            copies = []
            for i, (own, out) in enumerate(pairs):
                copies.append(
                    self.push(
                        slot,
                        own if first else out.at[:, origin],
                        out.at[z, origin] if first else out.at[:, origin],
                        to,
                        (self.send.at[i], self.recv.at[i]),
                    )
                )
            started.extend(copies)
            return copies

        def arrive(copies):
            for copy in copies:
                copy.wait_recv()

        first = [push_all(o - 1, d, (d, zs[o]), True) for o in (1, 2, 3)]
        for copies in first:
            arrive(copies)
        second = [push_all(3 + i, d, (to, z)) for i, to in enumerate(others[:3])]
        last = [push_all(6, d, (others[3], z))]
        for i, origin in enumerate(others[:3]):
            arrive(second[i])
            last.append(push_all(7 + i, origin, (others[3], z)))
        for copies in last:
            arrive(copies)
        arrive(moved)
        for copy in started + moved:
            copy.wait_send()
        keep.wait()


def reduce_kernel(chunks, sources, sets, meeting, *refs):
    ins = refs[:sources]
    refs = refs[sources:]
    if meeting is not None:
        earlier, refs = (refs[0], refs[1:])
    outs = refs[:sets]
    refs = refs[sets:]
    if meeting is not None:
        outside, refs = (refs[:4], refs[4:])
    buffers = [refs[6 * i : 6 * i + 6] for i in range(sets)]
    semaphores = refs[6 * sets : 6 * sets + 3]
    d, z, zs = places()
    spots = (d, z, zs, lax.rem(d // 2, 2), d // 4, lax.rem(d, 2))
    sib, near_x, near_y = (flip(d, 1), flip(d, 2), flip(d, 4))
    diagonal = flip(near_x, 4)
    others = [near_x, near_y, diagonal, sib, flip(near_x, 1), flip(near_y, 1), flip(diagonal, 1)]
    if meeting is None:
        others = [near_x, near_y, sib]
    greet([(d, zs[1]), (d, zs[2]), (d, zs[3])] + [(other, z) for other in others])
    work = []
    for k, (source, start, first, n, which) in enumerate(chunks):
        work.append(
            Reduction(ins[source], start, first, n, buffers[which], k, semaphores, spots)
        )
        work[k].begin()
    count = len(chunks)
    for step in range(count + 3):
        if step < count:
            work[step].across_plane()
        if 1 <= step <= count:
            work[step - 1].turn()
        if 2 <= step <= count + 1:
            work[step - 2].along_z()
        if step >= 3:
            work[step - 3].finish(outs[chunks[step - 3][4]])
    if meeting is not None:
        tail = Meeting(*meeting, tuple(outside) + tuple(refs[6 * sets + 3 :]))
        tail.run(outs[1].at[0], (outs[0], earlier), spots, others)


def reduce_grads(grads, collective, small=None, meeting=None, earlier=None):
    lanes, depth = lax.axis_size("dp"), lax.axis_size("fsdp")
    rows = D // (lanes * depth)
    tail = (depth, 2, 2, 2)
    sources = [grad.reshape((-1,) + tail + (rows, D)) for grad in grads]
    chunks = []
    first = 0
    for i, source in enumerate(sources):
        for start in range(0, source.shape[0], 2):
            n = min(2, source.shape[0] - start)
            chunks.append((i, start, first, n, 0))
            first += n
    sets = [(first, (rows, D), jnp.bfloat16)]
    if small is not None:
        sources.append(small.reshape((1,) + tail + small.shape[1:]))
        chunks.insert(1, (len(sources) - 1, 0, 0, 1, 1))
        sets.append((1, small.shape[1:], jnp.float32))
    scratch = []
    for n, shape, kind in sets:
        scratch += [
            pltpu.VMEM((n, depth, 2, 2) + shape, kind),
            pltpu.VMEM((n, depth, 2, 2) + shape, kind),
            pltpu.VMEM((n, depth, 2) + shape, kind),
            pltpu.VMEM((n, depth) + shape, kind),
            pltpu.VMEM((n, depth) + shape, kind),
            pltpu.VMEM((n, 3) + shape, kind),
        ]
    scratch += [
        pltpu.SemaphoreType.DMA((len(chunks),)),
        pltpu.SemaphoreType.DMA((len(chunks), 8)),
        pltpu.SemaphoreType.DMA((len(chunks), 8)),
    ]
    out_shape = [jax.ShapeDtypeStruct((n,) + shape, jnp.float32) for n, shape, _ in sets]
    count = len(sources)
    if meeting is not None:
        blocks_of, origins = meeting
        most = len(blocks_of[0])
        out_shape += [
            jax.ShapeDtypeStruct((depth, lanes) + small.shape[1:], jnp.float32),
            jax.ShapeDtypeStruct((depth, lanes, 8, 128), jnp.float32),
            jax.ShapeDtypeStruct((most, lanes, rows, D), jnp.bfloat16),
            jax.ShapeDtypeStruct((len(origins), rows, D), jnp.bfloat16),
        ]
        scratch += [
            pltpu.VMEM((lanes, most, rows, D), jnp.bfloat16),
            pltpu.VMEM((8, 128), jnp.float32),
            pltpu.SemaphoreType.DMA,
            pltpu.SemaphoreType.DMA((2, 10)),
            pltpu.SemaphoreType.DMA((2, 10)),
            pltpu.SemaphoreType.DMA((7,)),
            pltpu.SemaphoreType.DMA((7,)),
        ]
        sources.append(earlier)
    return pl.pallas_call(
        functools.partial(reduce_kernel, chunks, count, len(sets), meeting),
        out_shape=out_shape,
        in_specs=whole("a" * count + "v" * (len(sources) - count)),
        out_specs=whole("v" * len(out_shape)),
        scratch_shapes=scratch,
        compiler_params=pltpu.CompilerParams(
            collective_id=collective, has_side_effects=True, vmem_limit_bytes=VMEM_LIMIT
        ),
        name=f"reduce_{collective}",
    )(*sources)


def spread_stages(own, out, local_sem, send, recv):
    d, z, _ = places()
    sib, near_x, near_y = flip(d, 1), flip(d, 2), flip(d, 4)
    diagonal = flip(near_x, 4)
    half = own.shape[0] // 2
    parts = (pl.ds(0, half), pl.ds(half, own.shape[0] - half))
    started = []
    last = []

    def push(slot, origin, part, to, source=None):
        copy = pltpu.make_async_remote_copy(
            src_ref=out.at[part, origin] if source is None else source,
            dst_ref=out.at[part, origin],
            send_sem=send.at[slot],
            recv_sem=recv.at[slot],
            device_id=to,
            device_id_type=MESH,
        )
        copy.start()
        started.append(copy)
        return copy

    keep = pltpu.make_async_copy(own, out.at[:, d], local_sem)
    near = {}
    turned = []

    def begin():
        for way, part in ((0, 0), (1, 1), (0, 1), (1, 0)):
            near[way, part] = push(
                2 * way + part, d, parts[part], ((near_x, near_y)[way], z), own.at[parts[part]]
            )
        keep.start()
        last.extend([push(4 + i, d, parts[i], (sib, z), own.at[parts[i]]) for i in (0, 1)])

    def forward():
        near[0, 0].wait_recv()
        turned.append(push(6, near_x, parts[0], (near_y, z)))
        last.append(push(7, near_x, parts[0], (sib, z)))
        near[1, 1].wait_recv()
        turned.append(push(8, near_y, parts[1], (near_x, z)))
        last.append(push(9, near_y, parts[1], (sib, z)))

    def collect():
        near[1, 0].wait_recv()
        last.append(push(10, near_y, parts[0], (sib, z)))
        near[0, 1].wait_recv()
        last.append(push(11, near_x, parts[1], (sib, z)))
        for i in (0, 1):
            turned[i].wait_recv()
            last.append(push(12 + i, diagonal, parts[i], (sib, z)))

    def finish():
        for copy in last:
            copy.wait_recv()
        for copy in started:
            copy.wait_send()
        keep.wait()

    return (begin, forward, collect, finish)


GRAM_TILE = 128


def gram_kernel(
    gram,
    rows,
    own,
    total,
    all_rows,
    shards,
    left,
    right,
    onward,
    back,
    sems,
    local_sem,
    send,
    recv,
    row_sems,
):
    d, z, _ = places()
    up, down = (z + 1, z - 1)
    two = jnp.logical_and(lax.rem(d, 2) == 1, d // 4 == 1)
    one = jnp.logical_not(two)
    sib, near_x, near_y = flip(d, 1), flip(d, 2), flip(d, 4)
    greet([(d, lax.rem(z + step, 4)) for step in (1, 2, 3)] + [(sib, z), (near_x, z), (near_y, z)])
    stages = spread_stages(own, shards, local_sem, send, recv)
    count = D // GRAM_TILE

    def at(ref, j):
        return ref.at[pl.ds(j * GRAM_TILE, GRAM_TILE), pl.ds(j * GRAM_TILE, D - j * GRAM_TILE)]

    def copy(source, target, j, way, to):
        return pltpu.make_async_remote_copy(
            src_ref=at(source, j),
            dst_ref=at(target, j),
            send_sem=sems.at[2 * way, j],
            recv_sem=sems.at[2 * way + 1, j],
            device_id=(d, to),
            device_id_type=MESH,
        )

    def add(target, j, *terms):
        @pl.loop(0, GRAM_TILE // 16)
        def _(i):
            part = pl.ds(pl.multiple_of(j * GRAM_TILE + i * 16, 16), 16)
            columns = pl.ds(j * GRAM_TILE, D - j * GRAM_TILE)
            value = terms[0][part, columns]
            for term in terms[1:]:
                value = value + term[part, columns]
            target[part, columns] = value

    def ends():
        @pl.when(z == 0)
        def _():
            for j in range(count):
                copy(gram, left, j, 0, up).start()

        @pl.when(z == 3)
        def _():
            for j in range(count):
                copy(gram, right, j, 1, down).start()

    def near(j):
        @pl.when(z == 1)
        def _():
            copy(onward, left, j, 0, up).wait_recv()
            add(onward, j, gram, left)
            copy(onward, left, j, 0, up).start()

        @pl.when(z == 2)
        def _():
            copy(back, right, j, 1, down).wait_recv()
            add(back, j, gram, right)
            copy(back, right, j, 1, down).start()

    def far(j):
        @pl.when(z == 1)
        def _():
            copy(back, right, j, 1, down).wait_recv()
            add(back, j, gram, right)
            copy(back, right, j, 1, down).start()
            add(total, j, onward, right)

        @pl.when(z == 2)
        def _():
            copy(onward, left, j, 0, up).wait_recv()
            add(onward, j, gram, left)
            copy(onward, left, j, 0, up).start()
            add(total, j, onward, right)

        @pl.when(z == 3)
        def _():
            copy(gram, left, j, 0, up).wait_recv()
            add(total, j, left, gram)

        @pl.when(z == 0)
        def _():
            copy(gram, right, j, 1, down).wait_recv()
            add(total, j, gram, right)

        lines = slice(j * GRAM_TILE, (j + 1) * GRAM_TILE)
        for k in range(j + 1, count):
            columns = slice(k * GRAM_TILE, (k + 1) * GRAM_TILE)
            total[columns, lines] = total[lines, columns].T

    def finish():
        for j in range(count):

            @pl.when(z == 0)
            def _():
                copy(gram, left, j, 0, up).wait_send()

            @pl.when(z == 3)
            def _():
                copy(gram, right, j, 1, down).wait_send()

            @pl.when(jnp.logical_and(z > 0, z < 3))
            def _():
                copy(onward, left, j, 0, up).wait_send()
                copy(back, right, j, 1, down).wait_send()

    def pass_on(origin, way, to, source=None):
        return pltpu.make_async_remote_copy(
            src_ref=all_rows.at[origin] if source is None else source,
            dst_ref=all_rows.at[origin],
            send_sem=row_sems.at[2 * way, origin],
            recv_sem=row_sems.at[2 * way + 1, origin],
            device_id=(d, to),
            device_id_type=MESH,
        )

    def line_of(here):
        started = []
        if here < 3:
            started.append(pass_on(here, 0, here + 1, rows))
            started[-1].start()
        if here > 0:
            started.append(pass_on(here, 1, here - 1, rows))
            started[-1].start()
        all_rows[here] = rows[...]
        from_left = list(range(here - 1, -1, -1))
        from_right = list(range(here + 1, 4))
        for i in range(3):
            if i < len(from_left):
                pass_on(from_left[i], 0, here).wait_recv()
                if here < 3:
                    started.append(pass_on(from_left[i], 0, here + 1))
                    started[-1].start()
            if i < len(from_right):
                pass_on(from_right[i], 1, here).wait_recv()
                if here > 0:
                    started.append(pass_on(from_right[i], 1, here - 1))
                    started[-1].start()
        return started

    pl.when(one)(ends)
    stages[0]()

    @pl.when(one)
    def _():
        near(0)
        near(1)
        near(2)
        far(0)

    @pl.when(two)
    def _():
        for here in range(4):

            @pl.when(z == here)
            def _():
                for started in line_of(here):
                    started.wait_send()

    stages[1]()

    @pl.when(one)
    def _():
        near(3)
        far(1)
        near(4)
        far(2)

    stages[2]()

    @pl.when(one)
    def _():
        near(5)
        far(3)
        far(4)
        far(5)
        finish()

    stages[3]()


def sum_grams(gram, rows, own, collective):
    lanes, depth = lax.axis_size("dp"), lax.axis_size("fsdp")
    square = pltpu.VMEM(gram.shape, jnp.float32)
    return pl.pallas_call(
        gram_kernel,
        out_shape=[
            jax.ShapeDtypeStruct(gram.shape, jnp.float32),
            jax.ShapeDtypeStruct((depth,) + rows.shape, rows.dtype),
            jax.ShapeDtypeStruct(own.shape[:1] + (lanes,) + own.shape[1:], own.dtype),
        ],
        in_specs=whole("vvv"),
        out_specs=whole("vva"),
        scratch_shapes=[
            square,
            square,
            square,
            square,
            pltpu.SemaphoreType.DMA((4, D // GRAM_TILE)),
            pltpu.SemaphoreType.DMA,
            pltpu.SemaphoreType.DMA((14,)),
            pltpu.SemaphoreType.DMA((14,)),
            pltpu.SemaphoreType.DMA((4, 4)),
        ],
        compiler_params=pltpu.CompilerParams(
            collective_id=collective, has_side_effects=True, vmem_limit_bytes=VMEM_LIMIT
        ),
        name=f"gram_{collective}",
    )(gram, rows, own)


def schulz_kernel(two, gram, all_rows, rows, out, state, state_low, change, current):
    def chains(parts):
        for slot, first, number in parts:
            if len(parts) == 1:
                value = gram[...]
            else:
                value = jnp.zeros((D, D), jnp.float32)
                for z in range(all_rows.shape[0]):
                    piece = all_rows[z, slot]
                    value = value + contract_first(piece, piece)
            line = lax.broadcasted_iota(jnp.int32, value.shape, 0)
            column = lax.broadcasted_iota(jnp.int32, value.shape, 1)
            total = jnp.sum(jnp.where(line == column, value, 0.0), axis=(0, 1), keepdims=True)
            inverse = 1.0 / (jnp.sqrt(total) + 1e-07)
            value = value * (inverse * inverse)
            state[slot] = value
            state_low[slot] = value.astype(jnp.bfloat16)
            for place in range(first, first + number):
                current[place] = rows[place] * inverse

        def turn(last):
            for slot, _, _ in parts:
                square = jnp.dot(
                    state_low[slot], state_low[slot], preferred_element_type=jnp.float32
                )
                change[slot] = (COEF_B * state[slot] + COEF_C * square).astype(jnp.bfloat16)
            for slot, first, number in parts:
                for place in range(first, first + number):
                    value = current[place]
                    current[place] = COEF_A * value + jnp.dot(
                        value.astype(jnp.bfloat16),
                        change[slot],
                        preferred_element_type=jnp.float32,
                    )
            if last:
                return
            for half in range(2):
                for slot, _, _ in parts:
                    value = COEF_A * state[slot] + jnp.dot(
                        state_low[slot], change[slot], preferred_element_type=jnp.float32
                    )
                    state[slot] = value
                    state_low[slot] = value.astype(jnp.bfloat16)

        @pl.loop(0, NS_ITERS - 1)
        def _(_):
            turn(False)

        turn(True)
        for slot, first, number in parts:
            for place in range(first, first + number):
                out[place] = current[place].astype(jnp.bfloat16)

    @pl.when(two[0] == 0)
    def _():
        chains([(0, 0, 4)])

    @pl.when(two[0] == 1)
    def _():
        chains([(0, 0, 1), (1, 1, 1)])
        for place in (2, 3):
            out[place] = jnp.zeros(out.shape[1:], jnp.bfloat16)


def schulz(two, gram, all_rows, rows):
    return pl.pallas_call(
        schulz_kernel,
        out_shape=jax.ShapeDtypeStruct(rows.shape, jnp.bfloat16),
        in_specs=[
            pl.BlockSpec(memory_space=pltpu.SMEM),
        ]
        + whole("vvv"),
        out_specs=pl.BlockSpec(memory_space=pltpu.VMEM),
        scratch_shapes=[
            pltpu.VMEM((2, D, D), jnp.float32),
            pltpu.VMEM((2, D, D), jnp.bfloat16),
            pltpu.VMEM((2, D, D), jnp.bfloat16),
            pltpu.VMEM(rows.shape, jnp.float32),
        ],
        compiler_params=pltpu.CompilerParams(vmem_limit_bytes=VMEM_LIMIT),
        name="schulz",
    )(two, gram, all_rows, rows)


def spread_kernel(own, out, local_sem, send, recv):
    d, z, _ = places()
    greet([(flip(d, 1), z), (flip(d, 2), z), (flip(d, 4), z)])
    for stage in spread_stages(own, out, local_sem, send, recv):
        stage()


def spread(own, collective):
    lanes = lax.axis_size("dp")
    return pl.pallas_call(
        spread_kernel,
        out_shape=jax.ShapeDtypeStruct(own.shape[:1] + (lanes,) + own.shape[1:], own.dtype),
        in_specs=[pl.BlockSpec(memory_space=pltpu.VMEM)],
        out_specs=pl.BlockSpec(memory_space=pl.ANY),
        scratch_shapes=[
            pltpu.SemaphoreType.DMA,
            pltpu.SemaphoreType.DMA((14,)),
            pltpu.SemaphoreType.DMA((14,)),
        ],
        compiler_params=pltpu.CompilerParams(
            collective_id=collective, has_side_effects=True, vmem_limit_bytes=VMEM_LIMIT
        ),
        name=f"spread_{collective}",
    )(own)


def update_kernel(
    table,
    scale,
    clip,
    momenta,
    grads,
    weights,
    turned_first,
    turned_second,
    momenta_new,
    weights_new,
    weights_low,
):
    pair = pl.program_id(0)
    for i, turned in enumerate((turned_first, turned_second)):
        momenta_new[i] = MOMENT * momenta[i] + clip[0] * grads[i].astype(jnp.float32)
        value = weights[i] * (1.0 - MUON_RATE * MUON_DECAY) - scale[2 * pair + i] * turned[
            0, 0
        ].astype(jnp.float32)
        weights_new[i] = value
        weights_low[i] = value.astype(jnp.bfloat16)


def update(home, scale, clip, momenta, grads, weights, turned):
    blocks, rows, width = weights.shape
    table = np.array(
        [home[block][1] for block in range(blocks)] + [home[block][0] for block in range(blocks)],
        np.int32,
    )
    pair = pl.BlockSpec((2, rows, width), lambda b, *_: (b, 0, 0))

    def turned_of(i):
        return pl.BlockSpec(
            (1, 1, rows, width),
            lambda b, table, *_: (table[2 * b + i], table[blocks + 2 * b + i], 0, 0),
        )

    return pl.pallas_call(
        update_kernel,
        grid_spec=pltpu.PrefetchScalarGridSpec(
            num_scalar_prefetch=3,
            grid=(blocks // 2,),
            in_specs=[pair, pair, pair, turned_of(0), turned_of(1)],
            out_specs=[pair, pair, pair],
        ),
        out_shape=[
            jax.ShapeDtypeStruct(weights.shape, jnp.float32),
            jax.ShapeDtypeStruct(weights.shape, jnp.float32),
            jax.ShapeDtypeStruct(weights.shape, jnp.bfloat16),
        ],
        compiler_params=pltpu.CompilerParams(vmem_limit_bytes=VMEM_LIMIT),
        name="update",
    )(
        jnp.asarray(table),
        jnp.asarray(scale),
        clip.reshape(1),
        momenta,
        grads,
        weights,
        turned,
        turned,
    )


GROUP = 4 * HD


def normed_head(value, gain):
    centred = value - jnp.mean(value, 0, keepdims=True)
    scale = lax.rsqrt(jnp.mean(centred * centred, 0, keepdims=True) + 1e-06)
    centred = centred * scale
    return (centred * gain, centred, scale)


def contract_first(left, right):
    return lax.dot_general(
        left, right, (((0,), (0,)), ((), ())), preferred_element_type=jnp.float32
    )


def contract_last(left, right):
    return lax.dot_general(
        left, right, (((1,), (1,)), ((), ())), preferred_element_type=jnp.float32
    )


def head_shares(query_low, key_low, same):
    scores = contract_first(key_low, query_low) * (1.0 / math.sqrt(HD))
    scores = jnp.where(same, scores, -1e30)
    exponent = jnp.exp(scores - jnp.max(scores, 0, keepdims=True))
    return exponent * (1.0 / jnp.sum(exponent, 0, keepdims=True))


TILE = 768
TOKENS = 256
SLOPE = math.sqrt(2.0 / math.pi)
CUBIC = 0.044715


def tile_of(t, size=TILE):
    return pl.ds(pl.multiple_of(t * size, size), size)


def row_norm(value):
    centred = value - jnp.mean(value, -1, keepdims=True)
    scale = lax.rsqrt(jnp.mean(centred * centred, -1, keepdims=True) + 1e-06)
    return (centred * scale, scale)


def gelu_parts(value):
    square = value * value
    bend = jnp.tanh(SLOPE * value * (1.0 + CUBIC * square))
    half = 0.5 + 0.5 * bend
    slope = half + 0.5 * value * (1.0 - bend * bend) * SLOPE * (1.0 + 3.0 * CUBIC * square)
    return (value * half, slope)


def load_all(pairs, sem):
    copies = [
        pltpu.make_async_copy(source, target, sem.at[i])
        for i, (source, target) in enumerate(pairs)
    ]
    for copy in copies:
        copy.start()
    return copies


def stand_up(row):
    return jnp.broadcast_to(row, (8, row.shape[1])).T[:, :1]


def slot_marks(segment, b):
    row = segment[b : b + 1].astype(jnp.float32)
    return (stand_up(row), row)


def norm_rows(source, gains, first, target):
    gain, shift = (gains[first : first + 1], gains[first + 1 : first + 2])

    @pl.loop(0, source.shape[0] // 64)
    def _(t):
        part = tile_of(t, 64)
        target[part] = (row_norm(source[part])[0] * gain + shift).astype(target.dtype)


def forward_kernel(
    spans,
    base,
    state,
    gains,
    segment,
    mixing,
    mixing_out,
    upward,
    down,
    state_out,
    middle,
    mixed,
    heads_low,
    attended,
    normed_low,
    mixing_held,
    out_held,
    up_held,
    down_held,
    hidden,
    gain_query,
    gain_key,
    sem,
):
    mixing, mixing_out, upward, down = [
        ref.at[pl.ds(*span)] for ref, span in zip((mixing, mixing_out, upward, down), spans)
    ]
    loads = load_all(
        [(mixing, mixing_held), (mixing_out, out_held), (upward, up_held), (down, down_held)], sem
    )
    gain_query[...] = stand_up(gains[base + 4 : base + 5])
    gain_key[...] = stand_up(gains[base + 5 : base + 6])
    norm_rows(state, gains, base, heads_low)
    loads[0].wait()

    @pl.loop(0, 3 * D // TILE)
    def _(t):
        mixed[tile_of(t)] = contract_last(mixing_held[tile_of(t)], heads_low[...])

    parts, length = segment.shape
    for b in range(parts):
        column, row = slot_marks(segment, b)
        same = column == row
        tokens = slice(b * length, (b + 1) * length)

        @pl.loop(0, D // GROUP)
        def _(group):
            for head in range(GROUP // HD):
                first = group * GROUP + head * HD
                part = pl.ds(pl.multiple_of(first, HD), HD)
                query, key, value = [
                    mixed[pl.ds(pl.multiple_of(place * D + first, HD), HD), tokens]
                    for place in range(3)
                ]
                query_low = normed_head(query, gain_query[part])[0].astype(jnp.bfloat16)
                key_low = normed_head(key, gain_key[part])[0].astype(jnp.bfloat16)
                share = head_shares(query_low, key_low, same).astype(jnp.bfloat16)
                attended[part, tokens] = jnp.dot(
                    value.astype(jnp.bfloat16), share, preferred_element_type=jnp.float32
                ).astype(jnp.bfloat16)

    loads[1].wait()
    for t in range(state.shape[0] // TOKENS):
        part = slice(t * TOKENS, (t + 1) * TOKENS)
        middle[part] = state[part] + contract_first(attended[:, part], out_held[...])
    norm_rows(middle, gains, base + 2, normed_low)
    loads[2].wait()

    @pl.loop(0, FF // TILE)
    def _(t):
        value = contract_last(up_held[tile_of(t)], normed_low[...])
        hidden[tile_of(t)] = gelu_parts(value)[0].astype(jnp.bfloat16)

    loads[3].wait()
    for t in range(state.shape[0] // TOKENS):
        part = slice(t * TOKENS, (t + 1) * TOKENS)
        state_out[part] = middle[part] + contract_first(hidden[:, part], down_held[...])


def layer_weights(blocks):
    weights = [array.reshape(-1, D) for array, _, _ in blocks]
    return (weights, [(first * D, number * D) for _, first, number in blocks])


def layer_forward(state, blocks, gains, base, segment):
    tokens = state.shape[0]
    weights, spans = layer_weights(blocks)
    state_out, middle, mixed, heads_low, attended, normed_low = pl.pallas_call(
        functools.partial(forward_kernel, spans, base),
        out_shape=[
            jax.ShapeDtypeStruct((tokens, D), jnp.float32),
            jax.ShapeDtypeStruct((tokens, D), jnp.float32),
            jax.ShapeDtypeStruct((3 * D, tokens), jnp.float32),
            jax.ShapeDtypeStruct((tokens, D), jnp.bfloat16),
            jax.ShapeDtypeStruct((D, tokens), jnp.bfloat16),
            jax.ShapeDtypeStruct((tokens, D), jnp.bfloat16),
        ],
        in_specs=whole("vvvaaaa"),
        out_specs=whole("vvvvvv"),
        scratch_shapes=[pltpu.VMEM((number, D), jnp.bfloat16) for _, number in spans]
        + [
            pltpu.VMEM((FF, tokens), jnp.bfloat16),
            pltpu.VMEM((D, 1), jnp.float32),
            pltpu.VMEM((D, 1), jnp.float32),
            pltpu.SemaphoreType.DMA((4,)),
        ],
        compiler_params=pltpu.CompilerParams(vmem_limit_bytes=VMEM_LIMIT),
        name="layer_forward",
    )(state, gains, segment, *weights)
    return (state_out, (state, middle, mixed, heads_low, attended, normed_low))


def backward_kernel(
    spans,
    base,
    grad,
    middle,
    normed_low,
    gains,
    segment,
    state,
    mixed,
    heads_low,
    attended,
    mixing,
    mixing_out,
    upward,
    down,
    grad_out,
    gain_out,
    grad_mixing,
    grad_mixing_out,
    grad_up,
    grad_down,
    state_held,
    mixed_held,
    heads_held,
    attended_held,
    mixing_held,
    out_held,
    up_held,
    down_held,
    low,
    inner,
    hidden_grad,
    mixed_low,
    attended_grad,
    made_up,
    made_down,
    made_mixing,
    made_out,
    gain_query,
    gain_key,
    head_gains,
    sem,
    store_sem,
):
    mixing, mixing_out, upward, down = [
        ref.at[pl.ds(*span)] for ref, span in zip((mixing, mixing_out, upward, down), spans)
    ]
    loads = load_all(
        [
            (upward, up_held),
            (down, down_held),
            (mixing_out, out_held),
            (attended, attended_held),
            (mixed, mixed_held),
            (heads_low, heads_held),
            (mixing, mixing_held),
            (state, state_held),
        ],
        sem,
    )
    stores = [
        pltpu.make_async_copy(made_up, grad_up, store_sem.at[0]),
        pltpu.make_async_copy(made_down, grad_down, store_sem.at[1]),
        pltpu.make_async_copy(made_out, grad_mixing_out, store_sem.at[2]),
        pltpu.make_async_copy(made_mixing, grad_mixing, store_sem.at[3]),
    ]
    tokens = grad.shape[0]
    gain_out[...] = jnp.zeros_like(gain_out)
    head_gains[...] = jnp.zeros_like(head_gains)
    gain_query[...] = stand_up(gains[base + 4 : base + 5])
    gain_key[...] = stand_up(gains[base + 5 : base + 6])

    @pl.loop(0, tokens // 64)
    def _(t):
        low[tile_of(t, 64)] = grad[tile_of(t, 64)].astype(jnp.bfloat16)

    loads[0].wait()
    loads[1].wait()

    @pl.loop(0, FF // TILE)
    def _(t):
        part = tile_of(t)
        value, slope = gelu_parts(contract_last(up_held[part], normed_low[...]))
        delta = (contract_last(down_held[part], low[...]) * slope).astype(jnp.bfloat16)
        hidden_grad[part] = delta
        made_down[part] = jnp.dot(
            value.astype(jnp.bfloat16), low[...], preferred_element_type=jnp.float32
        ).astype(jnp.bfloat16)
        made_up[part] = jnp.dot(
            delta, normed_low[...], preferred_element_type=jnp.float32
        ).astype(jnp.bfloat16)

    stores[0].start()
    stores[1].start()
    for t in range(tokens // TOKENS):
        part = slice(t * TOKENS, (t + 1) * TOKENS)
        inner[part] = contract_first(hidden_grad[:, part], up_held[...])

    def norm_back(source, first, previous, target, target_low):
        gain = gains[base + first : base + first + 1]

        @pl.loop(0, tokens // 64)
        def _(t):
            part = tile_of(t, 64)
            unit, scale = row_norm(source[part])
            delta = inner[part]
            gain_out[first : first + 1] += jnp.sum(delta * unit, 0, keepdims=True)
            gain_out[first + 1 : first + 2] += jnp.sum(delta, 0, keepdims=True)
            delta = delta * gain
            delta = delta - jnp.mean(delta, -1, keepdims=True) - unit * jnp.mean(
                delta * unit, -1, keepdims=True
            )
            value = previous[part] + delta * scale
            target[part] = value
            if target_low is not None:
                target_low[part] = value.astype(jnp.bfloat16)

    norm_back(middle, 2, grad, grad_out, low)
    loads[2].wait()
    loads[3].wait()

    @pl.loop(0, D // TILE)
    def _(t):
        part = tile_of(t)
        made_out[part] = jnp.dot(
            attended_held[part], low[...], preferred_element_type=jnp.float32
        ).astype(jnp.bfloat16)
        attended_grad[part] = contract_last(out_held[part], low[...]).astype(jnp.bfloat16)

    stores[2].start()
    loads[4].wait()
    parts, length = segment.shape
    for b in range(parts):
        column, row = slot_marks(segment, b)
        same = column == row
        span = slice(b * length, (b + 1) * length)

        @pl.loop(0, D // GROUP)
        def _(group):
            for head in range(GROUP // HD):
                first = group * GROUP + head * HD
                part = pl.ds(pl.multiple_of(first, HD), HD)
                where = [pl.ds(pl.multiple_of(place * D + first, HD), HD) for place in range(3)]
                query, key, value = [mixed_held[at, span] for at in where]
                query_value, query_unit, query_scale = normed_head(query, gain_query[part])
                key_value, key_unit, key_scale = normed_head(key, gain_key[part])
                query_low = query_value.astype(jnp.bfloat16)
                key_low = key_value.astype(jnp.bfloat16)
                value_low = value.astype(jnp.bfloat16)
                out_low = attended_grad[part, span]
                share = head_shares(query_low, key_low, same)
                mixed_low[where[2], span] = contract_last(
                    out_low, share.astype(jnp.bfloat16)
                ).astype(jnp.bfloat16)
                share_grad = contract_first(value_low, out_low)
                total = jnp.sum(share * share_grad, 0, keepdims=True)
                score_low = (share * (share_grad - total) * (1.0 / math.sqrt(HD))).astype(
                    jnp.bfloat16
                )
                query_grad = jnp.dot(key_low, score_low, preferred_element_type=jnp.float32)
                key_grad = contract_last(query_low, score_low)
                for place, (delta, unit, scale, gain) in enumerate(
                    (
                        (query_grad, query_unit, query_scale, gain_query[part]),
                        (key_grad, key_unit, key_scale, gain_key[part]),
                    )
                ):
                    head_gains[place, part] += jnp.sum(delta * unit, 1, keepdims=True)
                    delta = delta * gain
                    delta = delta - jnp.mean(delta, 0, keepdims=True) - unit * jnp.mean(
                        delta * unit, 0, keepdims=True
                    )
                    mixed_low[where[place], span] = (delta * scale).astype(jnp.bfloat16)

    for place in range(2):
        column = jnp.broadcast_to(head_gains[place], (D, 128))
        gain_out[4 + place : 5 + place] = column.T[:1]
    loads[5].wait()

    @pl.loop(0, 3 * D // TILE)
    def _(t):
        part = tile_of(t)
        made_mixing[part] = jnp.dot(
            mixed_low[part], heads_held[...], preferred_element_type=jnp.float32
        ).astype(jnp.bfloat16)

    stores[3].start()
    loads[6].wait()
    for t in range(tokens // TOKENS):
        part = slice(t * TOKENS, (t + 1) * TOKENS)
        inner[part] = contract_first(mixed_low[:, part], mixing_held[...])
    loads[7].wait()
    norm_back(state_held, 0, grad_out, grad_out, None)
    for copy in stores:
        copy.wait()


def layer_backward(grad, kept, blocks, gains, base, segment):
    state, middle, mixed, heads_low, attended, normed_low = kept
    tokens = grad.shape[0]
    weights, spans = layer_weights(blocks)
    low = jnp.bfloat16
    grad, gain_grads, *block_grads = pl.pallas_call(
        functools.partial(backward_kernel, spans, base),
        out_shape=[
            jax.ShapeDtypeStruct((tokens, D), jnp.float32),
            jax.ShapeDtypeStruct((8, D), jnp.float32),
        ]
        + [jax.ShapeDtypeStruct((number, D), low) for _, number in spans],
        in_specs=whole("vvvvvaaaaaaaa"),
        out_specs=whole("vvaaaa"),
        scratch_shapes=[
            pltpu.VMEM(state.shape, jnp.float32),
            pltpu.VMEM(mixed.shape, jnp.float32),
            pltpu.VMEM(heads_low.shape, low),
            pltpu.VMEM(attended.shape, low),
        ]
        + [pltpu.VMEM((number, D), low) for _, number in spans]
        + [
            pltpu.VMEM((tokens, D), low),
            pltpu.VMEM((tokens, D), jnp.float32),
            pltpu.VMEM((FF, tokens), low),
            pltpu.VMEM((3 * D, tokens), low),
            pltpu.VMEM((D, tokens), low),
            pltpu.VMEM((FF, D), low),
            pltpu.VMEM((FF, D), low),
            pltpu.VMEM((3 * D, D), low),
            pltpu.VMEM((D, D), low),
            pltpu.VMEM((D, 1), jnp.float32),
            pltpu.VMEM((D, 1), jnp.float32),
            pltpu.VMEM((2, D, 1), jnp.float32),
            pltpu.SemaphoreType.DMA((8,)),
            pltpu.SemaphoreType.DMA((4,)),
        ],
        compiler_params=pltpu.CompilerParams(vmem_limit_bytes=60 * 1024 * 1024),
        name="layer_backward",
    )(grad, middle, normed_low, gains, segment, state, mixed, heads_low, attended, *weights)
    return (grad, block_grads, gain_grads[:6])


HEAD_LANES = 128


def full_dot(left, right):
    return jnp.dot(left, right, preferred_element_type=jnp.float32, precision=HIGH)


def head_marks():
    entry = lax.broadcasted_iota(jnp.int32, (D, HEAD_LANES), 0)
    lane = lax.broadcasted_iota(jnp.int32, (D, HEAD_LANES), 1)
    return (entry // HD == lane).astype(jnp.float32)


def full_dot_last(left, right):
    return lax.dot_general(
        left,
        right,
        (((1,), (1,)), ((), ())),
        preferred_element_type=jnp.float32,
        precision=HIGH,
    )


def pool_sequence(state, gains, marks_of):
    unit, scale = row_norm(state)
    final = unit * gains[0:1] + gains[1:2]
    marks = head_marks()
    logits = full_dot(final * gains[2:3], marks) * (1.0 / math.sqrt(HD))
    rows, columns = marks_of
    slot = lax.broadcasted_iota(jnp.int32, (rows.shape[0], IMGS), 1)
    member = (rows == slot.astype(jnp.float32)).astype(jnp.float32)
    slot = lax.broadcasted_iota(jnp.int32, (IMGS, columns.shape[1]), 0)
    member_rows = (columns == slot.astype(jnp.float32)).astype(jnp.float32)
    tops = jnp.zeros_like(logits)
    for k in range(IMGS):
        here = rows == k
        top = jnp.max(jnp.where(here, logits, -1e30), 0, keepdims=True)
        tops = jnp.where(here, top, tops)
    exponent = jnp.exp(logits - tops)
    share = exponent / full_dot(member, full_dot(member_rows, exponent))
    spread_share = full_dot_last(share, marks)
    dead = (jnp.sum(member_rows, 1, keepdims=True) == 0.0).astype(jnp.float32)
    pooled = full_dot(member_rows, spread_share * final) + dead * jnp.mean(
        final, 0, keepdims=True
    )
    return (unit, scale, final, marks, member, member_rows, share, spread_share, dead, pooled)


def unit_scale(value):
    return lax.rsqrt(jnp.mean(value * value, -1, keepdims=True) + 1e-06)


def pool_kernel(base, state, gains, segment, matrix, pooled_low, embedded, image_low):
    parts, length = segment.shape
    for b in range(parts):
        pooled = pool_sequence(
            state[b * length : (b + 1) * length], gains[base : base + 3], slot_marks(segment, b)
        )[-1]
        pooled_low[b] = pooled.astype(jnp.bfloat16)
        value = jnp.dot(
            pooled.astype(jnp.bfloat16), matrix[...], preferred_element_type=jnp.float32
        )
        embedded[b] = value
        image_low[b] = (value * unit_scale(value) * (1.0 / math.sqrt(D))).astype(jnp.bfloat16)


def pool_forward(state, gains, base, segment, matrix):
    parts = segment.shape[0]
    shape = (parts, IMGS, D)
    return pl.pallas_call(
        functools.partial(pool_kernel, base),
        out_shape=[
            jax.ShapeDtypeStruct(shape, jnp.bfloat16),
            jax.ShapeDtypeStruct(shape, jnp.float32),
            jax.ShapeDtypeStruct(shape, jnp.bfloat16),
        ],
        in_specs=whole("vvvv"),
        out_specs=whole("vvv"),
        compiler_params=pltpu.CompilerParams(vmem_limit_bytes=VMEM_LIMIT),
        name="pool_forward",
    )(state, gains, segment, matrix)


def contrast_kernel(
    base,
    me,
    images,
    texts,
    alive_columns,
    alive_rows,
    own_images,
    own_live,
    state,
    all_gains,
    segment,
    matrix,
    pooled_low,
    embedded,
    loss,
    grad,
    grad_matrix,
    gain_out,
    text_side,
):
    parts, length = segment.shape
    gains = all_gains[base : base + 3]
    everyone = images.shape[1]
    count = jnp.zeros((1, 1), jnp.float32)
    for b in range(parts):
        count = count + jnp.sum(alive_columns[b], -1, keepdims=True)
    factor = 1.0 / (2.0 * count)
    first = me[0] * IMGS

    def rows_of(scores, alive, live, start):
        masked = jnp.where(alive > 0, scores, -1e30)
        top = jnp.max(masked, -1, keepdims=True)
        exponent = jnp.exp(masked - top)
        total = jnp.sum(exponent, -1, keepdims=True)
        line = lax.broadcasted_iota(jnp.int32, scores.shape, 0) + start
        column = lax.broadcasted_iota(jnp.int32, scores.shape, 1)
        target = (line == column).astype(jnp.float32)
        diagonal = jnp.sum(scores * target, -1, keepdims=True)
        term = (top + jnp.log(total) - diagonal) * live
        delta = (exponent * (1.0 / total) - target) * live
        return (term, (delta * factor * LOGIT_SCALE).astype(jnp.bfloat16))

    loss[...] = jnp.zeros_like(loss)
    grad_sum = jnp.zeros((D, D), jnp.float32)
    gain_out[...] = jnp.zeros_like(gain_out)
    for b in range(parts):
        forward = LOGIT_SCALE * contract_last(own_images[b], texts[b])
        term, forward_low = rows_of(forward, alive_columns[b], own_live[b], first)
        loss[...] += jnp.sum(term, 0, keepdims=True) * factor
        text_side[...] = jnp.zeros_like(text_side)

        @pl.loop(0, everyone // TOKENS)
        def _(t):
            part = tile_of(t, TOKENS)
            backward = LOGIT_SCALE * contract_last(texts[b, part], images[b])
            term, backward_low = rows_of(
                backward, alive_columns[b], alive_rows[b, part], t * TOKENS
            )
            line = lax.broadcasted_iota(jnp.int32, term.shape, 0) + t * TOKENS
            here = jnp.logical_and(line >= first, line < first + IMGS)
            loss[...] += jnp.sum(jnp.where(here, term, 0.0), 0, keepdims=True) * factor
            text_side[...] += contract_first(backward_low, texts[b, part])

        image_grad = jnp.dot(forward_low, texts[b], preferred_element_type=jnp.float32)
        image_grad = image_grad + text_side[pl.ds(pl.multiple_of(first, IMGS), IMGS)]
        value = embedded[b]
        scale = unit_scale(value)
        embed_low = (
            (
                image_grad * scale
                - value * (scale * scale * scale) * jnp.mean(value * image_grad, -1, keepdims=True)
            )
            * (1.0 / math.sqrt(D))
        ).astype(jnp.bfloat16)
        grad_sum = grad_sum + contract_first(pooled_low[b], embed_low)
        pooled_grad = contract_last(embed_low, matrix[...])
        unit, norm_scale, final, marks, member, member_rows, share, spread_share, dead, _ = (
            pool_sequence(
                state[b * length : (b + 1) * length], gains, slot_marks(segment, b)
            )
        )
        token_grad = full_dot(member, pooled_grad)
        share_grad = full_dot(final * token_grad, marks)
        inside = full_dot(member, full_dot(member_rows, share * share_grad))
        logit_grad = share * (share_grad - inside) * (1.0 / math.sqrt(HD))
        spread_logit = full_dot_last(logit_grad, marks)
        final_grad = (
            spread_share * token_grad
            + spread_logit * gains[2:3]
            + jnp.sum(dead * pooled_grad, 0, keepdims=True) * (1.0 / length)
        )
        gain_out[0:1] += jnp.sum(final_grad * unit, 0, keepdims=True)
        gain_out[1:2] += jnp.sum(final_grad, 0, keepdims=True)
        gain_out[2:3] += jnp.sum(spread_logit * final, 0, keepdims=True)
        delta = final_grad * gains[0:1]
        delta = delta - jnp.mean(delta, -1, keepdims=True) - unit * jnp.mean(
            delta * unit, -1, keepdims=True
        )
        grad[b * length : (b + 1) * length] = delta * norm_scale
    grad_matrix[...] = grad_sum.astype(jnp.bfloat16)


def contrast(me, images, texts, alive, own_images, live, state, gains, base, segment, matrix, pooled_low, embedded):
    parts, everyone = alive.shape
    loss, grad, grad_matrix, gain_grads = pl.pallas_call(
        functools.partial(contrast_kernel, base),
        out_shape=[
            jax.ShapeDtypeStruct((8, 128), jnp.float32),
            jax.ShapeDtypeStruct(state.shape, jnp.float32),
            jax.ShapeDtypeStruct((D, D), jnp.bfloat16),
            jax.ShapeDtypeStruct((8, D), jnp.float32),
        ],
        in_specs=[pl.BlockSpec(memory_space=pltpu.SMEM)] + whole("vvvvvvvvvvvv"),
        out_specs=whole("vvvv"),
        scratch_shapes=[pltpu.VMEM((everyone, D), jnp.float32)],
        compiler_params=pltpu.CompilerParams(vmem_limit_bytes=VMEM_LIMIT),
        name="contrast",
    )(
        me.reshape(1),
        images,
        texts,
        alive[:, None, :],
        alive[:, :, None],
        own_images,
        live[:, :, None],
        state,
        gains,
        segment,
        matrix,
        pooled_low,
        embedded,
    )
    return (loss[0, 0], grad, grad_matrix, gain_grads[:3])


def muon_groups():
    found = [(0, 1), (1, 1)]
    for index in range(LAYERS):
        base = 2 + 12 * index
        found = found + [(base, 3), (base + 3, 1), (base + 4, 4), (base + 8, 4)]
    return found


def lane_plan(lanes):
    plan = [[] for _ in range(lanes)]
    for start, number in sorted(muon_groups(), key=lambda group: -group[1]):
        lane = min(range(lanes), key=lambda i: (sum(n for _, n in plan[i]), len(plan[i]), i))
        plan[lane].append((start, number))
    plan.sort(key=lambda entry: (-entry[0][1] if entry else 0))
    if lanes == 8:
        plan = [plan[i] for i in (0, 1, 2, 3, 4, 6, 5, 7)]
    depth = max(len(entry) for entry in plan)
    widths = [
        max([entry[slot][1] for entry in plan if slot < len(entry)]) for slot in range(depth)
    ]
    return (plan, widths)


def lane_blocks(plan):
    rows = [[start + i for start, number in entry for i in range(number)] for entry in plan]
    most = max(len(row) for row in rows)
    return np.array([row + [-1] * (most - len(row)) for row in rows], np.int32)


def lane_tables(plan, widths):
    index = np.zeros((len(plan), sum(widths)), np.int32)
    mask = np.zeros((len(plan), sum(widths)), np.float32)
    number = np.ones((len(plan), sum(widths)), np.float32)
    home = {}
    for lane, entry in enumerate(plan):
        first = 0
        for slot, width in enumerate(widths):
            if slot < len(entry):
                start, count = entry[slot]
                for place in range(count):
                    index[lane, first + place] = start + place
                    mask[lane, first + place] = 1.0
                    number[lane, first + place] = count
                    home[start + place] = (lane, first + place)
            first += width
    return (index, mask, number, home)


def orthogonal_factor(gram):
    size = jnp.sqrt(jnp.trace(gram)) + 1e-07
    state = gram / (size * size)
    total = None
    for turn in range(NS_ITERS):
        low = rounded(state)
        change = COEF_B * state + COEF_C * jnp.dot(low, low, preferred_element_type=jnp.float32)
        change_low = rounded(change)
        if total is None:
            total = COEF_A * jnp.eye(D, dtype=jnp.float32) + change
        else:
            total = COEF_A * total + jnp.dot(
                rounded(total), change_low, preferred_element_type=jnp.float32
            )
        if turn < NS_ITERS - 1:
            for _ in range(2):
                state = COEF_A * state + jnp.dot(
                    rounded(state), change_low, preferred_element_type=jnp.float32
                )
    return total / size


def per_device(
    patches, grid, segments, text_ids, table, weights, momenta, gains, gains_m, gains_v, step
):
    fin = 6 * LAYERS
    base = fin + 3
    lanes = lax.axis_size("dp")
    slots = jnp.arange(IMGS, dtype=jnp.int32)
    live = jnp.any(segments[:, 0, None, :] == slots[None, :, None], -1).astype(jnp.float32)
    depth = lax.axis_size("fsdp")
    captions = MB * IMGS
    tokens = text_ids.shape[3]
    fast = depth == 4 and lanes == 8
    early = [(0, 1), (2, 3), (5, 1), (6, 4), (10, 4), (1, 1)]
    later = []
    for index in range(1, LAYERS):
        start = 2 + 12 * index
        early = early + [(start, 3), (start + 3, 1)]
        later = later + [(start + 4, 4), (start + 8, 4)]
    later_own = jnp.concatenate([weights[a : a + n] for a, n in later], 0)
    if fast:
        eighth = weights.shape[1] // lanes
        later_own = lax.dynamic_slice_in_dim(later_own, lax.axis_index("dp") * eighth, eighth, 1)
    later_blocks = gather_later(rounded(later_own))
    if fast:
        half = tokens // 2
        own_ids = jnp.transpose(text_ids.reshape(captions, 2, half), (2, 1, 0)).reshape(half, -1)
        place = jnp.arange(depth * 2 * captions, dtype=jnp.int32) // (2 * captions)
        own_ids = jnp.where(
            place[None] == lax.axis_index("fsdp"), jnp.tile(own_ids, (1, depth)), 0
        )
        (stem, *first_blocks), text_sum = fetch(weights, early, own_ids, table, captions, 1)
    else:
        stem, *first_blocks = [
            lax.all_gather(rounded(weights[a : a + n]), "fsdp", axis=1, tiled=True)
            for a, n in early
        ]
        ids = lax.all_gather(text_ids.reshape(captions, tokens), "fsdp", axis=0)
        picked = ids.reshape(depth * captions, -1) - lax.axis_index("fsdp") * table.shape[0]
        row = jnp.arange(table.shape[0], dtype=jnp.int32)
        hits = jnp.sum((picked[:, :, None] == row[None, None, :]).astype(jnp.int32), 1)
        text_sum = lax.psum_scatter(
            jnp.dot(
                rounded(hits.astype(jnp.float32)), table, preferred_element_type=jnp.float32
            ).reshape(depth, captions, D),
            "fsdp",
            scatter_dimension=0,
        )
    early_blocks = first_blocks[5:]
    pooling_matrix = first_blocks[4][0]
    first_blocks = first_blocks[:4]
    text_low = rounded(unit_rows(text_sum / text_ids.shape[-1]))
    me = lax.axis_index(("dp", "fsdp"))
    segment = segments[:, 0]
    rows_hot, cols_hot = jax.vmap(positions)(grid[:, 0])
    rows_hot = rows_hot.reshape(-1, POS)
    cols_hot = cols_hot.reshape(-1, POS)
    patch_low = patches.reshape(-1, D)
    state = product(patch_low, stem[0], "sd,rd->sr")
    state = state + jnp.dot(rows_hot, gains[base : base + POS], precision=HIGH)
    state = state + jnp.dot(cols_hot, gains[base + POS : base + 2 * POS], precision=HIGH)
    saved = []
    for index in range(LAYERS):
        if index == 0:
            blocks = [(array, 0, array.shape[0]) for array in first_blocks]
        else:
            first = 8 * index - 8
            blocks = [
                (array, 0, array.shape[0]) for array in early_blocks[2 * index - 2 : 2 * index]
            ] + [(later_blocks, first, 4), (later_blocks, first + 4, 4)]
        state, kept = layer_forward(state, blocks, gains, 6 * index, segment)
        saved.append((kept, blocks))
    pooled_low, embedded, image_low = pool_forward(state, gains, fin, segment, pooling_matrix)
    own_flags = jnp.broadcast_to(live.reshape(captions, 1), (captions, 128)).astype(jnp.bfloat16)
    both = jnp.stack([image_low.reshape(captions, D), text_low]).reshape(2 * captions, D)
    gathered, flags = share([both, own_flags], 8)
    gathered = gathered.reshape(-1, 2, MB, IMGS, D)
    flags = flags.reshape(-1, MB, IMGS, 128)[..., 0].astype(jnp.float32)
    images, texts = [
        jnp.moveaxis(gathered[:, i], 0, 1).reshape(MB, -1, D) for i in range(2)
    ]
    loss_part, grad, grad_pool, pool_gain_grads = contrast(
        me,
        images,
        texts,
        jnp.moveaxis(flags, 0, 1).reshape(MB, -1),
        image_low,
        live,
        state,
        gains,
        fin,
        segment,
        pooling_matrix,
        pooled_low,
        embedded,
    )
    gain_parts = [None] * LAYERS
    block_grads = [None] * LAYERS
    slices = [None] * LAYERS
    for index in reversed(range(LAYERS)):
        kept, blocks = saved[index]
        grad, block_grads[index], gain_parts[index] = layer_backward(
            grad, kept, blocks, gains, 6 * index, segment
        )
        if index == 1:
            block_grads[index].append(grad_pool)
        if fast and index > 0:
            (slices[index],) = reduce_grads(block_grads[index], 4 + index)
    grad_low = rounded(grad)
    grad_patch = rounded(product(grad_low, patch_low, "sr,sd->rd"))
    block_grads[0].append(grad_patch)
    grad_rows = jnp.dot(rows_hot.T, grad, precision=HIGH)
    grad_cols = jnp.dot(cols_hot.T, grad, precision=HIGH)
    gains_grad = jnp.concatenate(
        gain_parts
        + [pool_gain_grads, grad_rows, grad_cols],
        0,
    )
    plan, widths = lane_plan(lanes)
    index, mask, number, home = lane_tables(plan, widths)
    lane = lax.axis_index("dp")
    scale = np.ones((weights.shape[0],), np.float32)
    for start, count_blocks in muon_groups():
        scale[start : start + count_blocks] = MUON_RATE * math.sqrt(count_blocks)
    if fast:
        width = 256
        small = jnp.concatenate([gains_grad.reshape(-1), loss_part[None]])
        small = jnp.pad(small, (0, lanes * depth * 8 * width - small.shape[0]))
        blocks_here = lane_blocks(plan)
        origins = [(0, 12), (1, 12)] + [
            (index, block) for index in range(LAYERS) for block in range(12)
        ]
        slices[0], _, small, stats, mine, slices = reduce_grads(
            block_grads[0],
            4,
            small.reshape(lanes * depth, 8, width),
            (blocks_here, origins),
            slices[1],
        )
        flat = small.reshape(-1)
        gains_grad, loss = (flat[: gains.size].reshape(gains.shape), flat[gains.size])
        squares = jnp.sum(stats[:, :, 0, 0])
        norm = jnp.sqrt(squares + jnp.sum(gains_grad * gains_grad))
        clip = jnp.minimum(1.0, CLIP_LIMIT / (norm + 1e-06))
        own_momenta = jnp.stack(
            [
                jnp.where(
                    jnp.asarray(blocks_here >= 0)[lane, place],
                    lax.dynamic_index_in_dim(
                        momenta, jnp.maximum(jnp.asarray(blocks_here)[lane, place], 0), 0, False
                    ),
                    0.0,
                )
                for place in range(blocks_here.shape[1])
            ]
        )
        own = MOMENT * own_momenta + clip * mine.reshape(own_momenta.shape).astype(jnp.float32)
        two = jnp.asarray(np.array([len(entry) > 1 for entry in plan], np.int32))[lane]
        own_low = rounded(own)
        gram = product(own_low, own_low, "brd,bre->de")
        gram, all_rows, shard_grads = sum_grams(gram, own_low[:2], slices, 12)
        turned = spread(schulz(two.reshape(1), gram, all_rows, own), 13)
        homes = {
            int(block): (lane_of, place)
            for lane_of, entry in enumerate(blocks_here)
            for place, block in enumerate(entry)
            if block >= 0
        }
        momenta_new, weights_new, weights_low = update(
            homes, scale, clip, momenta, shard_grads.reshape(weights.shape), weights, turned
        )
    else:
        stack = jnp.concatenate(
            [block_grads[index].pop().reshape(1, D, D) for index in range(LAYERS)]
            + [value.reshape(-1, D, D) for values in block_grads for value in values],
            0,
        )
        shard_grads = lax.psum(
            lax.psum_scatter(stack, "fsdp", scatter_dimension=1, tiled=True), "dp"
        ).astype(jnp.float32)
        gains_grad, loss = lax.psum((gains_grad, loss_part), ("dp", "fsdp"))
        squares = lax.psum(jnp.sum(shard_grads * shard_grads), "fsdp")
        norm = jnp.sqrt(squares + jnp.sum(gains_grad * gains_grad))
        clip = jnp.minimum(1.0, CLIP_LIMIT / (norm + 1e-06))
        momenta_new = MOMENT * momenta + clip * shard_grads
        own = jnp.stack(
            [
                lax.dynamic_index_in_dim(momenta_new, jnp.asarray(index)[lane, place], 0, False)
                * jnp.asarray(mask)[lane, place]
                for place in range(index.shape[1])
            ]
        )
        own_low = rounded(own)
        bounds = np.cumsum([0] + widths)
        grams = jnp.stack(
            [
                product(own_low[a:b], own_low[a:b], "brd,bre->de")
                for a, b in zip(bounds[:-1], bounds[1:])
            ]
        )
        grams = lax.psum(grams, "fsdp")
        turned = jnp.concatenate(
            [
                product(
                    own_low[bounds[slot] : bounds[slot + 1]],
                    rounded(orthogonal_factor(grams[slot])),
                    "brd,de->bre",
                )
                for slot in range(len(widths))
            ],
            0,
        )
        spread_rows = lax.all_gather(rounded(turned), "dp", axis=0)
        current = jnp.stack(
            [spread_rows[home[block][0], home[block][1]] for block in range(weights.shape[0])]
        ).astype(jnp.float32)
        weights_new = weights * (1.0 - MUON_RATE * MUON_DECAY) - jnp.asarray(scale)[:, None, None] * current
        weights_low = rounded(weights_new)
    grad_small = clip * gains_grad
    moment_one = BETA_ONE * gains_m + (1.0 - BETA_ONE) * grad_small
    moment_two = BETA_TWO * gains_v + (1.0 - BETA_TWO) * grad_small * grad_small
    count_steps = step[0].astype(jnp.float32)
    corrected_one = moment_one / (1.0 - jnp.power(BETA_ONE, count_steps))
    corrected_two = moment_two / (1.0 - jnp.power(BETA_TWO, count_steps))
    gains_new = gains - ADAM_RATE * (
        corrected_one / (jnp.sqrt(corrected_two) + ADAM_EPS) + ADAM_DECAY * gains
    )
    shift_grad = grad_small[fin + 1]
    return (
        loss,
        norm,
        weights_new,
        weights_low,
        momenta_new,
        gains_new,
        moment_one,
        moment_two,
        shift_grad,
    )


def solution(mesh):
    placed = (
        P(None, ("dp", "fsdp"), None, None),
        P(None, ("dp", "fsdp"), None, None),
        P(None, ("dp", "fsdp"), None),
        P(None, ("dp", "fsdp"), None, None),
        P("fsdp", None),
        P(None, "fsdp", None),
        P(None, "fsdp", None),
        P(),
        P(),
        P(),
        P(),
    )
    return jax.shard_map(
        per_device,
        mesh=mesh,
        in_specs=placed,
        out_specs=(
            P(),
            P(),
            P(None, "fsdp", None),
            P(None, "fsdp", None),
            P(None, "fsdp", None),
            P(),
            P(),
            P(),
            P(),
        ),
        check_vma=False,
    )
```

```python
import functools
import math

import jax
import jax.numpy as jnp
import numpy as np
from jax import lax
from jax.experimental import pallas as pl
from jax.experimental.pallas import tpu as pltpu
from jax.sharding import PartitionSpec as P

D = 768
HEADS = 12
FF = 3072
LAYERS = 2
IMGS = 8
POS = 32
MB = 2
NS_ITERS = 5
HD = 64


MESH = pl.DeviceIdType.MESH
VMEM_LIMIT = 56 * 1024 * 1024
HIGH = lax.Precision.HIGHEST
LOGIT_SCALE = 50.0
CLIP_LIMIT = 0.005
MOMENT = 0.95
MUON_RATE = 0.5
MUON_DECAY = 0.01
ADAM_RATE = 0.4
BETA_ONE = 0.9
BETA_TWO = 0.999
ADAM_EPS = 1e-08
ADAM_DECAY = 0.01
COEF_A = 3.4445
COEF_B = -4.775
COEF_C = 2.0315


def rounded(value):
    return value.astype(jnp.bfloat16)


def product(left, right, form):
    return jnp.einsum(form, left, right, preferred_element_type=jnp.float32)


def unit_rows(value):
    return (
        value
        * lax.rsqrt(jnp.mean(value * value, -1, keepdims=True) + 1e-06)
        * (1.0 / math.sqrt(value.shape[-1]))
    )


def positions(grid):
    slots = jnp.arange(POS, dtype=jnp.int32)
    row_index = grid[0] * POS // grid[2]
    col_index = grid[1] * POS // grid[3]
    return (
        (row_index[:, None] == slots[None]).astype(jnp.float32),
        (col_index[:, None] == slots[None]).astype(jnp.float32),
    )


def whole(kinds):
    memory = {"v": pltpu.VMEM, "a": pl.ANY}
    return [pl.BlockSpec(memory_space=memory[kind]) for kind in kinds]


def flip(index, bit):
    return index + bit - 2 * bit * lax.rem(index // bit, 2)


def greet(peers):
    barrier = pltpu.get_barrier_semaphore()
    for peer in peers:
        pl.semaphore_signal(barrier, inc=1, device_id=peer, device_id_type=MESH)
    pl.semaphore_wait(barrier, len(peers))


def places():
    d = lax.axis_index("dp")
    z = lax.axis_index("fsdp")
    return (d, z, [lax.rem(z + step, 4) for step in range(4)])


CAPTION_TILE = 400


def fetch_kernel(chunks, sizes, weights, ids, table, *refs):
    outs = refs[: len(sizes)]
    text_sum = refs[len(sizes)]
    (
        full,
        low,
        all_ids,
        pages,
        found,
        found_parts,
        from_z,
        load_sem,
        store_sem,
        send,
        recv,
        page_sem,
        id_send,
        id_recv,
        part_send,
        part_recv,
    ) = refs[len(sizes) + 1 :]
    d, z, zs = places()
    sib, near_x, near_y = flip(d, 1), flip(d, 2), flip(d, 4)
    diagonal = flip(near_x, 4)
    starts = [sum(chunk[3] for chunk in chunks[:k]) for k in range(len(chunks))]
    loads = []
    for k, (source, _, _, n) in enumerate(chunks):
        loads.append(
            pltpu.make_async_copy(
                weights.at[pl.ds(source, n)], full.at[pl.ds(starts[k], n)], load_sem.at[k]
            )
        )
        loads[k].start()
    page_count = table.shape[0] // CAPTION_TILE

    def page(t):
        return pltpu.make_async_copy(
            table.at[tile_of(t, CAPTION_TILE)], pages.at[lax.rem(t, 2)], page_sem.at[lax.rem(t, 2)]
        )

    page(0).start()
    greet([(d, zs[1]), (d, zs[2]), (d, zs[3]), (sib, z), (near_x, z), (near_y, z)])
    pending = []
    all_ids[z] = ids[...]
    id_copies = []
    for o in (1, 2, 3):
        id_copies.append(
            pltpu.make_async_remote_copy(
                src_ref=ids,
                dst_ref=all_ids.at[z],
                send_sem=id_send.at[o - 1],
                recv_sem=id_recv.at[o - 1],
                device_id=(d, zs[o]),
                device_id_type=MESH,
            )
        )
        id_copies[-1].start()

    def push(k, slot, first, n, zz, dd, to, source=None):
        out = outs[chunks[k][1]]
        rows = pl.ds(chunks[k][2] + first, n)
        copy = pltpu.make_async_remote_copy(
            src_ref=out.at[rows, zz, dd] if source is None else source,
            dst_ref=out.at[rows, zz, dd],
            send_sem=send.at[k, slot],
            recv_sem=recv.at[k, slot],
            device_id=to,
            device_id_type=MESH,
        )
        copy.start()
        pending.append(copy)
        return copy

    along_z = []
    stores = []
    for k, (_, out, offset, n) in enumerate(chunks):
        loads[k].wait()

        @pl.loop(starts[k], starts[k] + n)
        def _(i):
            low[i] = full[i].astype(low.dtype)

        along_z.append(
            [
                push(k, o - 1, 0, n, z, d, (d, zs[o]), low.at[pl.ds(starts[k], n), d])
                for o in (1, 2, 3)
            ]
        )
        stores.append(
            pltpu.make_async_copy(
                low.at[pl.ds(starts[k], n)],
                outs[out].at[pl.ds(offset, n), z],
                store_sem.at[k],
            )
        )
        stores[k].start()
    for copy in id_copies:
        copy.wait_recv()
    marks = all_ids[0] + all_ids[1] + all_ids[2] + all_ids[3]
    found[...] = jnp.zeros_like(found)

    def look_up(t):
        @pl.when(t + 1 < page_count)
        def _():
            page(t + 1).start()

        page(t).wait()
        row = lax.broadcasted_iota(jnp.int32, (CAPTION_TILE, marks.shape[1]), 0)
        row = row + (z * table.shape[0] + t * CAPTION_TILE)
        hits = jnp.zeros(row.shape, jnp.float32)
        for token in range(marks.shape[0]):
            hits = hits + jnp.where(row == marks[token : token + 1], 1.0, 0.0)
        found[...] += contract_first(hits.astype(jnp.bfloat16), pages[lax.rem(t, 2)])

    def look_up_span(first, last):
        @pl.loop(first, last)
        def _(t):
            look_up(t)

    share_of = -(-page_count // (len(chunks) - 1))
    part_copies = []

    def send_parts():
        captions = found_parts.shape[1]
        for owner in range(4):
            found_parts[owner] = (
                found[2 * owner * captions : (2 * owner + 1) * captions]
                + found[(2 * owner + 1) * captions : (2 * owner + 2) * captions]
            )
        for o in (1, 2, 3):
            part_copies.append(
                pltpu.make_async_remote_copy(
                    src_ref=found_parts.at[zs[o]],
                    dst_ref=from_z.at[o - 1],
                    send_sem=part_send.at[o - 1],
                    recv_sem=part_recv.at[o - 1],
                    device_id=(d, zs[o]),
                    device_id_type=MESH,
                )
            )
            part_copies[-1].start()

    along_x, along_y, turn_y, turn_x, last = {}, {}, {}, {}, []
    count = len(chunks)
    for step in range(count + 2):
        if step < count:
            k, n = step, chunks[step][3]
            along_x[k], along_y[k] = [], []
            for o in (1, 2, 3):
                zz = zs[4 - o]
                along_z[k][o - 1].wait_recv()
                along_x[k].append(push(k, 2 + o, 0, n, zz, d, (near_x, z)))
                along_y[k].append(push(k, 5 + o, 0, n, zz, d, (near_y, z)))
                last.append(push(k, 14 + o, 0, n, zz, d, (sib, z)))
        if 1 <= step <= count:
            k, n = step - 1, chunks[step - 1][3]
            half = n // 2
            turn_y[k], turn_x[k] = [], []
            for o in (1, 2, 3):
                zz = zs[4 - o]
                along_x[k][o - 1].wait_recv()
                if half:
                    turn_y[k].append(push(k, 8 + o, 0, half, zz, near_x, (near_y, z)))
                last.append(push(k, 17 + o, 0, n, zz, near_x, (sib, z)))
                along_y[k][o - 1].wait_recv()
                turn_x[k].append(push(k, 11 + o, half, n - half, zz, near_y, (near_x, z)))
                last.append(push(k, 20 + o, 0, n, zz, near_y, (sib, z)))
        if step * share_of < page_count:
            look_up_span(step * share_of, min((step + 1) * share_of, page_count))
        if step == count - 1:
            send_parts()
        if step >= 2:
            k, n = step - 2, chunks[step - 2][3]
            for o in (1, 2, 3):
                for copies in (turn_y[k], turn_x[k]):
                    if copies:
                        copies[o - 1].wait_recv()
                last.append(push(k, 23 + o, 0, n, zs[4 - o], diagonal, (sib, z)))
    for copy in last:
        copy.wait_recv()
    for copy in pending:
        copy.wait_send()
    for copy in stores:
        copy.wait()
    for copy in id_copies:
        copy.wait_send()
    for copy in part_copies:
        copy.wait()
    text_sum[...] = found_parts[z] + from_z[0] + from_z[1] + from_z[2]


def fetch(weights, pieces, ids, table, captions, collective):
    depth, eighths = lax.axis_size("fsdp"), lax.axis_size("dp")
    blocks, rows, width = weights.shape
    part = (eighths, rows // eighths, width)
    chunks = []
    for out, (a, n) in enumerate(pieces):
        for first in range(0, n, 2):
            chunks.append((a + first, out, first, min(2, n - first)))
    total = sum(n for _, n in pieces)
    outs = pl.pallas_call(
        functools.partial(fetch_kernel, chunks, [n for _, n in pieces]),
        out_shape=[
            jax.ShapeDtypeStruct((n, depth) + part, jnp.bfloat16) for _, n in pieces
        ]
        + [jax.ShapeDtypeStruct((captions, width), jnp.float32)],
        in_specs=whole("ava"),
        out_specs=whole("a" * len(pieces) + "v"),
        scratch_shapes=[
            pltpu.VMEM((total,) + part, jnp.float32),
            pltpu.VMEM((total,) + part, jnp.bfloat16),
            pltpu.VMEM((depth,) + ids.shape, jnp.int32),
            pltpu.VMEM((2, CAPTION_TILE, width), jnp.bfloat16),
            pltpu.VMEM((2 * depth * captions, width), jnp.float32),
            pltpu.VMEM((depth, captions, width), jnp.float32),
            pltpu.VMEM((3, captions, width), jnp.float32),
            pltpu.SemaphoreType.DMA((len(chunks),)),
            pltpu.SemaphoreType.DMA((len(chunks),)),
            pltpu.SemaphoreType.DMA((len(chunks), 27)),
            pltpu.SemaphoreType.DMA((len(chunks), 27)),
            pltpu.SemaphoreType.DMA((2,)),
            pltpu.SemaphoreType.DMA((3,)),
            pltpu.SemaphoreType.DMA((3,)),
            pltpu.SemaphoreType.DMA((3,)),
            pltpu.SemaphoreType.DMA((3,)),
        ],
        compiler_params=pltpu.CompilerParams(
            collective_id=collective, has_side_effects=True, vmem_limit_bytes=VMEM_LIMIT
        ),
        name=f"fetch_{collective}",
    )(weights.reshape((blocks,) + part), ids, table)
    return ([out.reshape(-1, width, width) for out in outs[:-1]], outs[-1])


def gather_later(own):
    depth, eighths = lax.axis_size("fsdp"), lax.axis_size("dp")
    if depth != 4 or eighths != 8:
        return lax.all_gather(own, "fsdp", axis=1, tiled=True)
    return lax.all_gather(own, ("fsdp", "dp"), axis=1).reshape(-1, D, D)


def share_kernel(count, *refs):
    owns, outs, (send, recv) = (refs[:count], refs[count : 2 * count], refs[2 * count :])
    d, z, zs = places()
    sib, near_x, near_y = flip(d, 1), flip(d, 2), flip(d, 4)
    diagonal = flip(near_x, 4)
    greet(
        [(d, zs[1]), (d, zs[2]), (d, zs[3]), (sib, z), (near_x, z), (near_y, z), (diagonal, z)]
    )
    for own, out in zip(owns, outs):
        out[d, z] = own[...]
    started = []

    def push(slot, origin, to, first=False):
        copies = []
        for i in range(count):
            copies.append(
                pltpu.make_async_remote_copy(
                    src_ref=owns[i] if first else outs[i].at[origin],
                    dst_ref=outs[i].at[origin, z] if first else outs[i].at[origin],
                    send_sem=send.at[i, slot],
                    recv_sem=recv.at[i, slot],
                    device_id=to,
                    device_id_type=MESH,
                )
            )
            copies[-1].start()
        started.extend(copies)
        return copies

    def arrive(copies):
        for copy in copies:
            copy.wait_recv()

    first = [push(o - 1, d, (d, zs[o]), True) for o in (1, 2, 3)]
    for copies in first:
        arrive(copies)
    second = [push(3 + i, d, (to, z)) for i, to in enumerate((near_x, near_y, diagonal))]
    last = [push(6, d, (sib, z))]
    for i, origin in enumerate((near_x, near_y, diagonal)):
        arrive(second[i])
        last.append(push(7 + i, origin, (sib, z)))
    for copies in last:
        arrive(copies)
    for copy in started:
        copy.wait_send()


def share(owns, collective):
    lanes, depth = lax.axis_size("dp"), lax.axis_size("fsdp")
    if depth != 4 or lanes != 8:
        return [
            lax.all_gather(own, ("dp", "fsdp"), axis=0).reshape((lanes, depth) + own.shape)
            for own in owns
        ]
    count = len(owns)
    return pl.pallas_call(
        functools.partial(share_kernel, count),
        out_shape=[jax.ShapeDtypeStruct((lanes, depth) + own.shape, own.dtype) for own in owns],
        in_specs=[pl.BlockSpec(memory_space=pltpu.VMEM)] * count,
        out_specs=[pl.BlockSpec(memory_space=pltpu.VMEM)] * count,
        scratch_shapes=[
            pltpu.SemaphoreType.DMA((count, 10)),
            pltpu.SemaphoreType.DMA((count, 10)),
        ],
        compiler_params=pltpu.CompilerParams(collective_id=collective, has_side_effects=True),
        name=f"share_{collective}",
    )(*owns)


class Reduction:
    def __init__(self, source, start, first, n, buffers, k, semaphores, spots):
        self.source, self.start, self.first, self.n, self.k = (source, start, first, n, k)
        self.held, self.from_core, self.from_near, self.from_turn, self.ready, self.from_z = buffers
        self.local_sem, self.send, self.recv = semaphores
        self.spots = spots
        self.rows = pl.ds(first, n)
        self.started = []

    def push(self, slot, source, target, to):
        copy = pltpu.make_async_remote_copy(
            src_ref=source,
            dst_ref=target,
            send_sem=self.send.at[self.k, slot],
            recv_sem=self.recv.at[self.k, slot],
            device_id=to,
            device_id_type=MESH,
        )
        copy.start()
        self.started.append(copy)
        return copy

    def begin(self):
        d, z, zs, x, y, c = self.spots
        blocks = pl.ds(self.start, self.n)
        self.local = pltpu.make_async_copy(
            self.source.at[blocks, :, :, :, c], self.held.at[self.rows], self.local_sem.at[self.k]
        )
        self.local.start()
        self.core = self.push(
            0,
            self.source.at[blocks, :, :, :, 1 - c],
            self.from_core.at[self.rows],
            (flip(d, 1), z),
        )

    def add(self, count, place):
        @pl.loop(0, self.n * count)
        def _(i):
            target, other = place(self.first + i // count, lax.rem(i, count))
            self.held[target] = self.held[target] + other

    def across_plane(self):
        d, z, zs, x, y, c = self.spots
        self.local.wait()
        self.core.wait_recv()

        def place(b, i):
            target = (b, i // 4, lax.rem(i // 2, 2), lax.rem(i, 2))
            return (target, self.from_core[target])

        self.add(16, place)
        self.near = [
            self.push(
                1,
                self.held.at[self.rows, 0:2, :, 1 - x],
                self.from_near.at[self.rows, 0:2],
                (flip(d, 2), z),
            ),
            self.push(
                2,
                self.held.at[self.rows, 2:4, 1 - y],
                self.from_near.at[self.rows, 2:4],
                (flip(d, 4), z),
            ),
        ]

    def turn(self):
        d, z, zs, x, y, c = self.spots

        def place_a(b, i):
            return ((b, i // 2, lax.rem(i, 2), x), self.from_near[b, i // 2, lax.rem(i, 2)])

        def place_b(b, i):
            return ((b, 2 + i // 2, y, lax.rem(i, 2)), self.from_near[b, 2 + i // 2, lax.rem(i, 2)])

        self.near[0].wait_recv()
        self.add(4, place_a)
        a = self.push(
            3,
            self.held.at[self.rows, 0:2, 1 - y, x],
            self.from_turn.at[self.rows, 0:2],
            (flip(d, 4), z),
        )
        self.near[1].wait_recv()
        self.add(4, place_b)
        b = self.push(
            4,
            self.held.at[self.rows, 2:4, y, 1 - x],
            self.from_turn.at[self.rows, 2:4],
            (flip(d, 2), z),
        )
        self.turned = [a, b]

    def along_z(self):
        d, z, zs, x, y, c = self.spots
        for copy in self.turned:
            copy.wait_recv()

        @pl.loop(0, self.n * 4)
        def _(i):
            b, zz = (self.first + i // 4, lax.rem(i, 4))
            self.ready[b, zz] = self.held[b, zz, y, x] + self.from_turn[b, zz]

        self.spread = [
            self.push(
                4 + o,
                self.ready.at[self.rows, zs[o]],
                self.from_z.at[self.rows, o - 1],
                (d, zs[o]),
            )
            for o in (1, 2, 3)
        ]

    def finish(self, out):
        d, z, zs, x, y, c = self.spots
        for copy in self.spread:
            copy.wait_recv()

        @pl.loop(self.first, self.first + self.n)
        def _(b):
            total = self.held[b, z, y, x].astype(jnp.float32) + self.from_turn[b, z].astype(
                jnp.float32
            )
            for o in range(3):
                total = total + self.from_z[b, o].astype(jnp.float32)
            out[b] = total

        for copy in self.started:
            copy.wait_send()


class Meeting:
    def __init__(self, blocks_of, sources, refs):
        self.blocks_of, self.sources = (blocks_of, sources)
        self.small_out, self.stats_out, self.mine, self.low = refs[:4]
        self.parts, self.stats, self.local_sem, self.send, self.recv = refs[4:9]
        self.part_send, self.part_recv = refs[9:]

    def push(self, slot, source, target, to, sems):
        copy = pltpu.make_async_remote_copy(
            src_ref=source,
            dst_ref=target,
            send_sem=sems[0].at[slot],
            recv_sem=sems[1].at[slot],
            device_id=to,
            device_id_type=MESH,
        )
        copy.start()
        return copy

    def run(self, small, results, spots, others):
        d, z, zs = spots[:3]
        total = jnp.zeros(results[0].shape[1:], jnp.float32)
        homes = {
            int(block): (lane, place)
            for lane, entry in enumerate(self.blocks_of)
            for place, block in enumerate(entry)
        }
        for block, (source, index) in enumerate(self.sources):
            value = results[source][index]
            total = total + value * value
            value = value.astype(self.low.dtype)
            self.low[block] = value
            lane, place = homes[block]
            self.parts[lane, place] = value
        for lane, entry in enumerate(self.blocks_of):
            for place, block in enumerate(entry):
                if block < 0:
                    self.parts[lane, place] = jnp.zeros_like(self.parts[lane, place])
        squares = jnp.sum(total, axis=(0, 1), keepdims=True)
        self.stats[...] = jnp.broadcast_to(squares, self.stats.shape)
        moved = [
            self.push(
                i,
                self.parts.at[other],
                self.mine.at[:, d],
                (other, z),
                (self.part_send, self.part_recv),
            )
            for i, other in enumerate(others)
        ]
        keep = pltpu.make_async_copy(self.parts.at[d], self.mine.at[:, d], self.local_sem)
        keep.start()
        pairs = [(small, self.small_out), (self.stats, self.stats_out)]
        for own, out in pairs:
            out[z, d] = own[...]
        started = []

        def push_all(slot, origin, to, first=False):
            copies = []
            for i, (own, out) in enumerate(pairs):
                copies.append(
                    self.push(
                        slot,
                        own if first else out.at[:, origin],
                        out.at[z, origin] if first else out.at[:, origin],
                        to,
                        (self.send.at[i], self.recv.at[i]),
                    )
                )
            started.extend(copies)
            return copies

        def arrive(copies):
            for copy in copies:
                copy.wait_recv()

        first = [push_all(o - 1, d, (d, zs[o]), True) for o in (1, 2, 3)]
        for copies in first:
            arrive(copies)
        second = [push_all(3 + i, d, (to, z)) for i, to in enumerate(others[:3])]
        last = [push_all(6, d, (others[3], z))]
        for i, origin in enumerate(others[:3]):
            arrive(second[i])
            last.append(push_all(7 + i, origin, (others[3], z)))
        for copies in last:
            arrive(copies)
        arrive(moved)
        for copy in started + moved:
            copy.wait_send()
        keep.wait()


def reduce_kernel(chunks, sources, sets, meeting, *refs):
    ins = refs[:sources]
    refs = refs[sources:]
    if meeting is not None:
        earlier, refs = (refs[0], refs[1:])
    outs = refs[:sets]
    refs = refs[sets:]
    if meeting is not None:
        outside, refs = (refs[:4], refs[4:])
    buffers = [refs[6 * i : 6 * i + 6] for i in range(sets)]
    semaphores = refs[6 * sets : 6 * sets + 3]
    d, z, zs = places()
    spots = (d, z, zs, lax.rem(d // 2, 2), d // 4, lax.rem(d, 2))
    sib, near_x, near_y = (flip(d, 1), flip(d, 2), flip(d, 4))
    diagonal = flip(near_x, 4)
    others = [near_x, near_y, diagonal, sib, flip(near_x, 1), flip(near_y, 1), flip(diagonal, 1)]
    if meeting is None:
        others = [near_x, near_y, sib]
    greet([(d, zs[1]), (d, zs[2]), (d, zs[3])] + [(other, z) for other in others])
    work = []
    for k, (source, start, first, n, which) in enumerate(chunks):
        work.append(
            Reduction(ins[source], start, first, n, buffers[which], k, semaphores, spots)
        )
        work[k].begin()
    count = len(chunks)
    for step in range(count + 3):
        if step < count:
            work[step].across_plane()
        if 1 <= step <= count:
            work[step - 1].turn()
        if 2 <= step <= count + 1:
            work[step - 2].along_z()
        if step >= 3:
            work[step - 3].finish(outs[chunks[step - 3][4]])
    if meeting is not None:
        tail = Meeting(*meeting, tuple(outside) + tuple(refs[6 * sets + 3 :]))
        tail.run(outs[1].at[0], (outs[0], earlier), spots, others)


def reduce_grads(grads, collective, small=None, meeting=None, earlier=None):
    lanes, depth = lax.axis_size("dp"), lax.axis_size("fsdp")
    rows = D // (lanes * depth)
    tail = (depth, 2, 2, 2)
    sources = [grad.reshape((-1,) + tail + (rows, D)) for grad in grads]
    chunks = []
    first = 0
    for i, source in enumerate(sources):
        for start in range(0, source.shape[0], 2):
            n = min(2, source.shape[0] - start)
            chunks.append((i, start, first, n, 0))
            first += n
    sets = [(first, (rows, D), jnp.bfloat16)]
    if small is not None:
        sources.append(small.reshape((1,) + tail + small.shape[1:]))
        chunks.insert(1, (len(sources) - 1, 0, 0, 1, 1))
        sets.append((1, small.shape[1:], jnp.float32))
    scratch = []
    for n, shape, kind in sets:
        scratch += [
            pltpu.VMEM((n, depth, 2, 2) + shape, kind),
            pltpu.VMEM((n, depth, 2, 2) + shape, kind),
            pltpu.VMEM((n, depth, 2) + shape, kind),
            pltpu.VMEM((n, depth) + shape, kind),
            pltpu.VMEM((n, depth) + shape, kind),
            pltpu.VMEM((n, 3) + shape, kind),
        ]
    scratch += [
        pltpu.SemaphoreType.DMA((len(chunks),)),
        pltpu.SemaphoreType.DMA((len(chunks), 8)),
        pltpu.SemaphoreType.DMA((len(chunks), 8)),
    ]
    out_shape = [jax.ShapeDtypeStruct((n,) + shape, jnp.float32) for n, shape, _ in sets]
    count = len(sources)
    if meeting is not None:
        blocks_of, origins = meeting
        most = len(blocks_of[0])
        out_shape += [
            jax.ShapeDtypeStruct((depth, lanes) + small.shape[1:], jnp.float32),
            jax.ShapeDtypeStruct((depth, lanes, 8, 128), jnp.float32),
            jax.ShapeDtypeStruct((most, lanes, rows, D), jnp.bfloat16),
            jax.ShapeDtypeStruct((len(origins), rows, D), jnp.bfloat16),
        ]
        scratch += [
            pltpu.VMEM((lanes, most, rows, D), jnp.bfloat16),
            pltpu.VMEM((8, 128), jnp.float32),
            pltpu.SemaphoreType.DMA,
            pltpu.SemaphoreType.DMA((2, 10)),
            pltpu.SemaphoreType.DMA((2, 10)),
            pltpu.SemaphoreType.DMA((7,)),
            pltpu.SemaphoreType.DMA((7,)),
        ]
        sources.append(earlier)
    return pl.pallas_call(
        functools.partial(reduce_kernel, chunks, count, len(sets), meeting),
        out_shape=out_shape,
        in_specs=whole("a" * count + "v" * (len(sources) - count)),
        out_specs=whole("v" * len(out_shape)),
        scratch_shapes=scratch,
        compiler_params=pltpu.CompilerParams(
            collective_id=collective, has_side_effects=True, vmem_limit_bytes=VMEM_LIMIT
        ),
        name=f"reduce_{collective}",
    )(*sources)


def spread_stages(own, out, local_sem, send, recv):
    d, z, _ = places()
    sib, near_x, near_y = flip(d, 1), flip(d, 2), flip(d, 4)
    diagonal = flip(near_x, 4)
    half = own.shape[0] // 2
    parts = (pl.ds(0, half), pl.ds(half, own.shape[0] - half))
    started = []
    last = []

    def push(slot, origin, part, to, source=None):
        copy = pltpu.make_async_remote_copy(
            src_ref=out.at[part, origin] if source is None else source,
            dst_ref=out.at[part, origin],
            send_sem=send.at[slot],
            recv_sem=recv.at[slot],
            device_id=to,
            device_id_type=MESH,
        )
        copy.start()
        started.append(copy)
        return copy

    keep = pltpu.make_async_copy(own, out.at[:, d], local_sem)
    near = {}
    turned = []

    def begin():
        for way, part in ((0, 0), (1, 1), (0, 1), (1, 0)):
            near[way, part] = push(
                2 * way + part, d, parts[part], ((near_x, near_y)[way], z), own.at[parts[part]]
            )
        keep.start()
        last.extend([push(4 + i, d, parts[i], (sib, z), own.at[parts[i]]) for i in (0, 1)])

    def forward():
        near[0, 0].wait_recv()
        turned.append(push(6, near_x, parts[0], (near_y, z)))
        last.append(push(7, near_x, parts[0], (sib, z)))
        near[1, 1].wait_recv()
        turned.append(push(8, near_y, parts[1], (near_x, z)))
        last.append(push(9, near_y, parts[1], (sib, z)))

    def collect():
        near[1, 0].wait_recv()
        last.append(push(10, near_y, parts[0], (sib, z)))
        near[0, 1].wait_recv()
        last.append(push(11, near_x, parts[1], (sib, z)))
        for i in (0, 1):
            turned[i].wait_recv()
            last.append(push(12 + i, diagonal, parts[i], (sib, z)))

    def finish():
        for copy in last:
            copy.wait_recv()
        for copy in started:
            copy.wait_send()
        keep.wait()

    return (begin, forward, collect, finish)


GRAM_TILE = 128


def gram_kernel(
    gram,
    rows,
    own,
    total,
    all_rows,
    shards,
    left,
    right,
    onward,
    back,
    sems,
    local_sem,
    send,
    recv,
    row_sems,
):
    d, z, _ = places()
    up, down = (z + 1, z - 1)
    two = jnp.logical_and(lax.rem(d, 2) == 1, d // 4 == 1)
    one = jnp.logical_not(two)
    sib, near_x, near_y = flip(d, 1), flip(d, 2), flip(d, 4)
    greet([(d, lax.rem(z + step, 4)) for step in (1, 2, 3)] + [(sib, z), (near_x, z), (near_y, z)])
    stages = spread_stages(own, shards, local_sem, send, recv)
    count = D // GRAM_TILE

    def at(ref, j):
        return ref.at[pl.ds(j * GRAM_TILE, GRAM_TILE), pl.ds(j * GRAM_TILE, D - j * GRAM_TILE)]

    def copy(source, target, j, way, to):
        return pltpu.make_async_remote_copy(
            src_ref=at(source, j),
            dst_ref=at(target, j),
            send_sem=sems.at[2 * way, j],
            recv_sem=sems.at[2 * way + 1, j],
            device_id=(d, to),
            device_id_type=MESH,
        )

    def add(target, j, *terms):
        @pl.loop(0, GRAM_TILE // 16)
        def _(i):
            part = pl.ds(pl.multiple_of(j * GRAM_TILE + i * 16, 16), 16)
            columns = pl.ds(j * GRAM_TILE, D - j * GRAM_TILE)
            value = terms[0][part, columns]
            for term in terms[1:]:
                value = value + term[part, columns]
            target[part, columns] = value

    def ends():
        @pl.when(z == 0)
        def _():
            for j in range(count):
                copy(gram, left, j, 0, up).start()

        @pl.when(z == 3)
        def _():
            for j in range(count):
                copy(gram, right, j, 1, down).start()

    def near(j):
        @pl.when(z == 1)
        def _():
            copy(onward, left, j, 0, up).wait_recv()
            add(onward, j, gram, left)
            copy(onward, left, j, 0, up).start()

        @pl.when(z == 2)
        def _():
            copy(back, right, j, 1, down).wait_recv()
            add(back, j, gram, right)
            copy(back, right, j, 1, down).start()

    def far(j):
        @pl.when(z == 1)
        def _():
            copy(back, right, j, 1, down).wait_recv()
            add(back, j, gram, right)
            copy(back, right, j, 1, down).start()
            add(total, j, onward, right)

        @pl.when(z == 2)
        def _():
            copy(onward, left, j, 0, up).wait_recv()
            add(onward, j, gram, left)
            copy(onward, left, j, 0, up).start()
            add(total, j, onward, right)

        @pl.when(z == 3)
        def _():
            copy(gram, left, j, 0, up).wait_recv()
            add(total, j, left, gram)

        @pl.when(z == 0)
        def _():
            copy(gram, right, j, 1, down).wait_recv()
            add(total, j, gram, right)

        lines = slice(j * GRAM_TILE, (j + 1) * GRAM_TILE)
        for k in range(j + 1, count):
            columns = slice(k * GRAM_TILE, (k + 1) * GRAM_TILE)
            total[columns, lines] = total[lines, columns].T

    def finish():
        for j in range(count):

            @pl.when(z == 0)
            def _():
                copy(gram, left, j, 0, up).wait_send()

            @pl.when(z == 3)
            def _():
                copy(gram, right, j, 1, down).wait_send()

            @pl.when(jnp.logical_and(z > 0, z < 3))
            def _():
                copy(onward, left, j, 0, up).wait_send()
                copy(back, right, j, 1, down).wait_send()

    def pass_on(origin, way, to, source=None):
        return pltpu.make_async_remote_copy(
            src_ref=all_rows.at[origin] if source is None else source,
            dst_ref=all_rows.at[origin],
            send_sem=row_sems.at[2 * way, origin],
            recv_sem=row_sems.at[2 * way + 1, origin],
            device_id=(d, to),
            device_id_type=MESH,
        )

    def line_of(here):
        started = []
        if here < 3:
            started.append(pass_on(here, 0, here + 1, rows))
            started[-1].start()
        if here > 0:
            started.append(pass_on(here, 1, here - 1, rows))
            started[-1].start()
        all_rows[here] = rows[...]
        from_left = list(range(here - 1, -1, -1))
        from_right = list(range(here + 1, 4))
        for i in range(3):
            if i < len(from_left):
                pass_on(from_left[i], 0, here).wait_recv()
                if here < 3:
                    started.append(pass_on(from_left[i], 0, here + 1))
                    started[-1].start()
            if i < len(from_right):
                pass_on(from_right[i], 1, here).wait_recv()
                if here > 0:
                    started.append(pass_on(from_right[i], 1, here - 1))
                    started[-1].start()
        return started

    pl.when(one)(ends)
    stages[0]()

    @pl.when(one)
    def _():
        near(0)
        near(1)
        near(2)
        far(0)

    @pl.when(two)
    def _():
        for here in range(4):

            @pl.when(z == here)
            def _():
                for started in line_of(here):
                    started.wait_send()

    stages[1]()

    @pl.when(one)
    def _():
        near(3)
        far(1)
        near(4)
        far(2)

    stages[2]()

    @pl.when(one)
    def _():
        near(5)
        far(3)
        far(4)
        far(5)
        finish()

    stages[3]()


def sum_grams(gram, rows, own, collective):
    lanes, depth = lax.axis_size("dp"), lax.axis_size("fsdp")
    square = pltpu.VMEM(gram.shape, jnp.float32)
    return pl.pallas_call(
        gram_kernel,
        out_shape=[
            jax.ShapeDtypeStruct(gram.shape, jnp.float32),
            jax.ShapeDtypeStruct((depth,) + rows.shape, rows.dtype),
            jax.ShapeDtypeStruct(own.shape[:1] + (lanes,) + own.shape[1:], own.dtype),
        ],
        in_specs=whole("vvv"),
        out_specs=whole("vva"),
        scratch_shapes=[
            square,
            square,
            square,
            square,
            pltpu.SemaphoreType.DMA((4, D // GRAM_TILE)),
            pltpu.SemaphoreType.DMA,
            pltpu.SemaphoreType.DMA((14,)),
            pltpu.SemaphoreType.DMA((14,)),
            pltpu.SemaphoreType.DMA((4, 4)),
        ],
        compiler_params=pltpu.CompilerParams(
            collective_id=collective, has_side_effects=True, vmem_limit_bytes=VMEM_LIMIT
        ),
        name=f"gram_{collective}",
    )(gram, rows, own)


def schulz_kernel(two, gram, all_rows, rows, out, state, state_low, change, current):
    def chains(parts):
        for slot, first, number in parts:
            if len(parts) == 1:
                value = gram[...]
            else:
                value = jnp.zeros((D, D), jnp.float32)
                for z in range(all_rows.shape[0]):
                    piece = all_rows[z, slot]
                    value = value + contract_first(piece, piece)
            line = lax.broadcasted_iota(jnp.int32, value.shape, 0)
            column = lax.broadcasted_iota(jnp.int32, value.shape, 1)
            total = jnp.sum(jnp.where(line == column, value, 0.0), axis=(0, 1), keepdims=True)
            inverse = 1.0 / (jnp.sqrt(total) + 1e-07)
            value = value * (inverse * inverse)
            state[slot] = value
            state_low[slot] = value.astype(jnp.bfloat16)
            for place in range(first, first + number):
                current[place] = rows[place] * inverse

        def turn(last):
            for slot, _, _ in parts:
                square = jnp.dot(
                    state_low[slot], state_low[slot], preferred_element_type=jnp.float32
                )
                change[slot] = (COEF_B * state[slot] + COEF_C * square).astype(jnp.bfloat16)
            for slot, first, number in parts:
                for place in range(first, first + number):
                    value = current[place]
                    current[place] = COEF_A * value + jnp.dot(
                        value.astype(jnp.bfloat16),
                        change[slot],
                        preferred_element_type=jnp.float32,
                    )
            if last:
                return
            for half in range(2):
                for slot, _, _ in parts:
                    value = COEF_A * state[slot] + jnp.dot(
                        state_low[slot], change[slot], preferred_element_type=jnp.float32
                    )
                    state[slot] = value
                    state_low[slot] = value.astype(jnp.bfloat16)

        @pl.loop(0, NS_ITERS - 1)
        def _(_):
            turn(False)

        turn(True)
        for slot, first, number in parts:
            for place in range(first, first + number):
                out[place] = current[place].astype(jnp.bfloat16)

    @pl.when(two[0] == 0)
    def _():
        chains([(0, 0, 4)])

    @pl.when(two[0] == 1)
    def _():
        chains([(0, 0, 1), (1, 1, 1)])
        for place in (2, 3):
            out[place] = jnp.zeros(out.shape[1:], jnp.bfloat16)


def schulz(two, gram, all_rows, rows):
    return pl.pallas_call(
        schulz_kernel,
        out_shape=jax.ShapeDtypeStruct(rows.shape, jnp.bfloat16),
        in_specs=[
            pl.BlockSpec(memory_space=pltpu.SMEM),
        ]
        + whole("vvv"),
        out_specs=pl.BlockSpec(memory_space=pltpu.VMEM),
        scratch_shapes=[
            pltpu.VMEM((2, D, D), jnp.float32),
            pltpu.VMEM((2, D, D), jnp.bfloat16),
            pltpu.VMEM((2, D, D), jnp.bfloat16),
            pltpu.VMEM(rows.shape, jnp.float32),
        ],
        compiler_params=pltpu.CompilerParams(vmem_limit_bytes=VMEM_LIMIT),
        name="schulz",
    )(two, gram, all_rows, rows)


def spread_kernel(own, out, local_sem, send, recv):
    d, z, _ = places()
    greet([(flip(d, 1), z), (flip(d, 2), z), (flip(d, 4), z)])
    for stage in spread_stages(own, out, local_sem, send, recv):
        stage()


def spread(own, collective):
    lanes = lax.axis_size("dp")
    return pl.pallas_call(
        spread_kernel,
        out_shape=jax.ShapeDtypeStruct(own.shape[:1] + (lanes,) + own.shape[1:], own.dtype),
        in_specs=[pl.BlockSpec(memory_space=pltpu.VMEM)],
        out_specs=pl.BlockSpec(memory_space=pl.ANY),
        scratch_shapes=[
            pltpu.SemaphoreType.DMA,
            pltpu.SemaphoreType.DMA((14,)),
            pltpu.SemaphoreType.DMA((14,)),
        ],
        compiler_params=pltpu.CompilerParams(
            collective_id=collective, has_side_effects=True, vmem_limit_bytes=VMEM_LIMIT
        ),
        name=f"spread_{collective}",
    )(own)


def update_kernel(
    table,
    scale,
    clip,
    momenta,
    grads,
    weights,
    turned_first,
    turned_second,
    momenta_new,
    weights_new,
    weights_low,
):
    pair = pl.program_id(0)
    for i, turned in enumerate((turned_first, turned_second)):
        momenta_new[i] = MOMENT * momenta[i] + clip[0] * grads[i].astype(jnp.float32)
        value = weights[i] * (1.0 - MUON_RATE * MUON_DECAY) - scale[2 * pair + i] * turned[
            0, 0
        ].astype(jnp.float32)
        weights_new[i] = value
        weights_low[i] = value.astype(jnp.bfloat16)


def update(home, scale, clip, momenta, grads, weights, turned):
    blocks, rows, width = weights.shape
    table = np.array(
        [home[block][1] for block in range(blocks)] + [home[block][0] for block in range(blocks)],
        np.int32,
    )
    pair = pl.BlockSpec((2, rows, width), lambda b, *_: (b, 0, 0))

    def turned_of(i):
        return pl.BlockSpec(
            (1, 1, rows, width),
            lambda b, table, *_: (table[2 * b + i], table[blocks + 2 * b + i], 0, 0),
        )

    return pl.pallas_call(
        update_kernel,
        grid_spec=pltpu.PrefetchScalarGridSpec(
            num_scalar_prefetch=3,
            grid=(blocks // 2,),
            in_specs=[pair, pair, pair, turned_of(0), turned_of(1)],
            out_specs=[pair, pair, pair],
        ),
        out_shape=[
            jax.ShapeDtypeStruct(weights.shape, jnp.float32),
            jax.ShapeDtypeStruct(weights.shape, jnp.float32),
            jax.ShapeDtypeStruct(weights.shape, jnp.bfloat16),
        ],
        compiler_params=pltpu.CompilerParams(vmem_limit_bytes=VMEM_LIMIT),
        name="update",
    )(
        jnp.asarray(table),
        jnp.asarray(scale),
        clip.reshape(1),
        momenta,
        grads,
        weights,
        turned,
        turned,
    )


GROUP = 6 * HD


def normed_head(value, gain):
    centred = value - jnp.mean(value, 0, keepdims=True)
    scale = lax.rsqrt(jnp.mean(centred * centred, 0, keepdims=True) + 1e-06)
    centred = centred * scale
    return (centred * gain, centred, scale)


def contract_first(left, right):
    return lax.dot_general(
        left, right, (((0,), (0,)), ((), ())), preferred_element_type=jnp.float32
    )


def contract_last(left, right):
    return lax.dot_general(
        left, right, (((1,), (1,)), ((), ())), preferred_element_type=jnp.float32
    )


def shares_of(scores, same):
    scores = jnp.where(same, scores * (1.0 / math.sqrt(HD)), -1e30)
    exponent = jnp.exp(scores - jnp.max(scores, 0, keepdims=True))
    return exponent * (1.0 / jnp.sum(exponent, 0, keepdims=True))


TILE = 768
TOKENS = 256
SLOPE = math.sqrt(2.0 / math.pi)
CUBIC = 0.044715


def tile_of(t, size=TILE):
    return pl.ds(pl.multiple_of(t * size, size), size)


def row_norm(value):
    centred = value - jnp.mean(value, -1, keepdims=True)
    scale = lax.rsqrt(jnp.mean(centred * centred, -1, keepdims=True) + 1e-06)
    return (centred * scale, scale)


def gelu_parts(value):
    square = value * value
    bend = jnp.tanh(SLOPE * value * (1.0 + CUBIC * square))
    half = 0.5 + 0.5 * bend
    slope = half + 0.5 * value * (1.0 - bend * bend) * SLOPE * (1.0 + 3.0 * CUBIC * square)
    return (value * half, slope)


def load_all(pairs, sem):
    copies = [
        pltpu.make_async_copy(source, target, sem.at[i])
        for i, (source, target) in enumerate(pairs)
    ]
    for copy in copies:
        copy.start()
    return copies


def stand_up(row):
    return jnp.broadcast_to(row, (8, row.shape[1])).T[:, :1]


def slot_marks(segment, b):
    row = segment[b : b + 1].astype(jnp.float32)
    return (stand_up(row), row)


def norm_rows(source, gains, first, target):
    gain, shift = (gains[first : first + 1], gains[first + 1 : first + 2])

    @pl.loop(0, source.shape[0] // 64)
    def _(t):
        part = tile_of(t, 64)
        target[part] = (row_norm(source[part])[0] * gain + shift).astype(target.dtype)


def forward_kernel(
    spans,
    base,
    state,
    gains,
    segment,
    mixing,
    mixing_out,
    upward,
    down,
    state_out,
    middle,
    mixed,
    heads_low,
    attended,
    normed_low,
    mixing_held,
    out_held,
    up_held,
    down_held,
    hidden,
    gain_query,
    gain_key,
    sem,
):
    mixing, mixing_out, upward, down = [
        ref.at[pl.ds(*span)] for ref, span in zip((mixing, mixing_out, upward, down), spans)
    ]
    loads = load_all(
        [(mixing, mixing_held), (mixing_out, out_held), (upward, up_held), (down, down_held)], sem
    )
    gain_query[...] = stand_up(gains[base + 4 : base + 5])
    gain_key[...] = stand_up(gains[base + 5 : base + 6])
    norm_rows(state, gains, base, heads_low)
    loads[0].wait()

    @pl.loop(0, 3 * D // TILE)
    def _(t):
        mixed[tile_of(t)] = contract_last(mixing_held[tile_of(t)], heads_low[...])

    parts, length = segment.shape
    for b in range(parts):
        column, row = slot_marks(segment, b)
        same = column == row
        tokens = slice(b * length, (b + 1) * length)

        @pl.loop(0, D // GROUP)
        def _(group):
            held = []
            for head in range(GROUP // HD):
                first = group * GROUP + head * HD
                part = pl.ds(pl.multiple_of(first, HD), HD)
                query, key, value = [
                    mixed[pl.ds(pl.multiple_of(place * D + first, HD), HD), tokens]
                    for place in range(3)
                ]
                query_low = normed_head(query, gain_query[part])[0].astype(jnp.bfloat16)
                key_low = normed_head(key, gain_key[part])[0].astype(jnp.bfloat16)
                held.append((part, query_low, key_low, value.astype(jnp.bfloat16)))
            scores = [contract_first(key_low, query_low) for _, query_low, key_low, _ in held]
            shares = [shares_of(score, same).astype(jnp.bfloat16) for score in scores]
            for (part, _, _, value_low), share in zip(held, shares):
                attended[part, tokens] = jnp.dot(
                    value_low, share, preferred_element_type=jnp.float32
                ).astype(jnp.bfloat16)

    loads[1].wait()
    for t in range(state.shape[0] // TOKENS):
        part = slice(t * TOKENS, (t + 1) * TOKENS)
        middle[part] = state[part] + contract_first(attended[:, part], out_held[...])
    norm_rows(middle, gains, base + 2, normed_low)
    loads[2].wait()

    @pl.loop(0, FF // TILE)
    def _(t):
        value = contract_last(up_held[tile_of(t)], normed_low[...])
        hidden[tile_of(t)] = gelu_parts(value)[0].astype(jnp.bfloat16)

    loads[3].wait()
    for t in range(state.shape[0] // TOKENS):
        part = slice(t * TOKENS, (t + 1) * TOKENS)
        state_out[part] = middle[part] + contract_first(hidden[:, part], down_held[...])


def layer_weights(blocks):
    weights = [array.reshape(-1, D) for array, _, _ in blocks]
    return (weights, [(first * D, number * D) for _, first, number in blocks])


def layer_forward(state, blocks, gains, base, segment):
    tokens = state.shape[0]
    weights, spans = layer_weights(blocks)
    state_out, middle, mixed, heads_low, attended, normed_low = pl.pallas_call(
        functools.partial(forward_kernel, spans, base),
        out_shape=[
            jax.ShapeDtypeStruct((tokens, D), jnp.float32),
            jax.ShapeDtypeStruct((tokens, D), jnp.float32),
            jax.ShapeDtypeStruct((3 * D, tokens), jnp.float32),
            jax.ShapeDtypeStruct((tokens, D), jnp.bfloat16),
            jax.ShapeDtypeStruct((D, tokens), jnp.bfloat16),
            jax.ShapeDtypeStruct((tokens, D), jnp.bfloat16),
        ],
        in_specs=whole("vvvaaaa"),
        out_specs=whole("vvvvvv"),
        scratch_shapes=[pltpu.VMEM((number, D), jnp.bfloat16) for _, number in spans]
        + [
            pltpu.VMEM((FF, tokens), jnp.bfloat16),
            pltpu.VMEM((D, 1), jnp.float32),
            pltpu.VMEM((D, 1), jnp.float32),
            pltpu.SemaphoreType.DMA((4,)),
        ],
        compiler_params=pltpu.CompilerParams(vmem_limit_bytes=VMEM_LIMIT),
        name="layer_forward",
    )(state, gains, segment, *weights)
    return (state_out, (state, middle, mixed, heads_low, attended, normed_low))


def backward_kernel(
    spans,
    base,
    grad,
    middle,
    normed_low,
    gains,
    segment,
    state,
    mixed,
    heads_low,
    attended,
    mixing,
    mixing_out,
    upward,
    down,
    grad_out,
    gain_out,
    grad_mixing,
    grad_mixing_out,
    grad_up,
    grad_down,
    state_held,
    mixed_held,
    heads_held,
    attended_held,
    mixing_held,
    out_held,
    up_held,
    down_held,
    low,
    inner,
    hidden_grad,
    mixed_low,
    attended_grad,
    made_up,
    made_down,
    made_mixing,
    made_out,
    gain_query,
    gain_key,
    head_gains,
    sem,
    store_sem,
):
    mixing, mixing_out, upward, down = [
        ref.at[pl.ds(*span)] for ref, span in zip((mixing, mixing_out, upward, down), spans)
    ]
    loads = load_all(
        [
            (upward, up_held),
            (down, down_held),
            (mixing_out, out_held),
            (attended, attended_held),
            (mixed, mixed_held),
            (heads_low, heads_held),
            (mixing, mixing_held),
            (state, state_held),
        ],
        sem,
    )
    stores = [
        pltpu.make_async_copy(made_up, grad_up, store_sem.at[0]),
        pltpu.make_async_copy(made_down, grad_down, store_sem.at[1]),
        pltpu.make_async_copy(made_out, grad_mixing_out, store_sem.at[2]),
        pltpu.make_async_copy(made_mixing, grad_mixing, store_sem.at[3]),
    ]
    tokens = grad.shape[0]
    gain_out[...] = jnp.zeros_like(gain_out)
    head_gains[...] = jnp.zeros_like(head_gains)
    gain_query[...] = stand_up(gains[base + 4 : base + 5])
    gain_key[...] = stand_up(gains[base + 5 : base + 6])

    @pl.loop(0, tokens // 64)
    def _(t):
        low[tile_of(t, 64)] = grad[tile_of(t, 64)].astype(jnp.bfloat16)

    loads[0].wait()
    loads[1].wait()

    @pl.loop(0, FF // TILE)
    def _(t):
        part = tile_of(t)
        value, slope = gelu_parts(contract_last(up_held[part], normed_low[...]))
        delta = (contract_last(down_held[part], low[...]) * slope).astype(jnp.bfloat16)
        hidden_grad[part] = delta
        made_down[part] = jnp.dot(
            value.astype(jnp.bfloat16), low[...], preferred_element_type=jnp.float32
        ).astype(jnp.bfloat16)
        made_up[part] = jnp.dot(
            delta, normed_low[...], preferred_element_type=jnp.float32
        ).astype(jnp.bfloat16)

    stores[0].start()
    stores[1].start()
    for t in range(tokens // TOKENS):
        part = slice(t * TOKENS, (t + 1) * TOKENS)
        inner[part] = contract_first(hidden_grad[:, part], up_held[...])

    def norm_back(source, first, previous, target, target_low):
        gain = gains[base + first : base + first + 1]

        @pl.loop(0, tokens // 64)
        def _(t):
            part = tile_of(t, 64)
            unit, scale = row_norm(source[part])
            delta = inner[part]
            gain_out[first : first + 1] += jnp.sum(delta * unit, 0, keepdims=True)
            gain_out[first + 1 : first + 2] += jnp.sum(delta, 0, keepdims=True)
            delta = delta * gain
            delta = delta - jnp.mean(delta, -1, keepdims=True) - unit * jnp.mean(
                delta * unit, -1, keepdims=True
            )
            value = previous[part] + delta * scale
            target[part] = value
            if target_low is not None:
                target_low[part] = value.astype(jnp.bfloat16)

    norm_back(middle, 2, grad, grad_out, low)
    loads[2].wait()
    loads[3].wait()

    @pl.loop(0, D // TILE)
    def _(t):
        part = tile_of(t)
        made_out[part] = jnp.dot(
            attended_held[part], low[...], preferred_element_type=jnp.float32
        ).astype(jnp.bfloat16)
        attended_grad[part] = contract_last(out_held[part], low[...]).astype(jnp.bfloat16)

    stores[2].start()
    loads[4].wait()
    parts, length = segment.shape
    for b in range(parts):
        column, row = slot_marks(segment, b)
        same = column == row
        span = slice(b * length, (b + 1) * length)

        @pl.loop(0, D // GROUP)
        def _(group):
            held = []
            for head in range(GROUP // HD):
                first = group * GROUP + head * HD
                part = pl.ds(pl.multiple_of(first, HD), HD)
                where = [pl.ds(pl.multiple_of(place * D + first, HD), HD) for place in range(3)]
                query, key, value = [mixed_held[at, span] for at in where]
                query_low = normed_head(query, gain_query[part])[0].astype(jnp.bfloat16)
                key_low = normed_head(key, gain_key[part])[0].astype(jnp.bfloat16)
                held.append((part, where, query_low, key_low, value.astype(jnp.bfloat16)))
            scores = [contract_first(key_low, query_low) for _, _, query_low, key_low, _ in held]
            share_grads = [
                contract_first(value_low, attended_grad[part, span])
                for part, _, _, _, value_low in held
            ]
            shares = [shares_of(score, same) for score in scores]
            score_lows = []
            for share, share_grad in zip(shares, share_grads):
                total = jnp.sum(share * share_grad, 0, keepdims=True)
                score_lows.append(
                    (share * (share_grad - total) * (1.0 / math.sqrt(HD))).astype(jnp.bfloat16)
                )
            for (part, where, query_low, key_low, _), share, score_low in zip(
                held, shares, score_lows
            ):
                mixed_low[where[2], span] = contract_last(
                    attended_grad[part, span], share.astype(jnp.bfloat16)
                ).astype(jnp.bfloat16)
                deltas = (
                    jnp.dot(key_low, score_low, preferred_element_type=jnp.float32),
                    contract_last(query_low, score_low),
                )
                for place, (delta, gains_here) in enumerate(zip(deltas, (gain_query, gain_key))):
                    _, unit, scale = normed_head(mixed_held[where[place], span], gains_here[part])
                    head_gains[place, part] += jnp.sum(delta * unit, 1, keepdims=True)
                    delta = delta * gains_here[part]
                    delta = delta - jnp.mean(delta, 0, keepdims=True) - unit * jnp.mean(
                        delta * unit, 0, keepdims=True
                    )
                    mixed_low[where[place], span] = (delta * scale).astype(jnp.bfloat16)

    for place in range(2):
        column = jnp.broadcast_to(head_gains[place], (D, 128))
        gain_out[4 + place : 5 + place] = column.T[:1]
    loads[5].wait()

    @pl.loop(0, 3 * D // TILE)
    def _(t):
        part = tile_of(t)
        made_mixing[part] = jnp.dot(
            mixed_low[part], heads_held[...], preferred_element_type=jnp.float32
        ).astype(jnp.bfloat16)

    stores[3].start()
    loads[6].wait()
    for t in range(tokens // TOKENS):
        part = slice(t * TOKENS, (t + 1) * TOKENS)
        inner[part] = contract_first(mixed_low[:, part], mixing_held[...])
    loads[7].wait()
    norm_back(state_held, 0, grad_out, grad_out, None)
    for copy in stores:
        copy.wait()


def layer_backward(grad, kept, blocks, gains, base, segment):
    state, middle, mixed, heads_low, attended, normed_low = kept
    tokens = grad.shape[0]
    weights, spans = layer_weights(blocks)
    low = jnp.bfloat16
    grad, gain_grads, *block_grads = pl.pallas_call(
        functools.partial(backward_kernel, spans, base),
        out_shape=[
            jax.ShapeDtypeStruct((tokens, D), jnp.float32),
            jax.ShapeDtypeStruct((8, D), jnp.float32),
        ]
        + [jax.ShapeDtypeStruct((number, D), low) for _, number in spans],
        in_specs=whole("vvvvvaaaaaaaa"),
        out_specs=whole("vvaaaa"),
        scratch_shapes=[
            pltpu.VMEM(state.shape, jnp.float32),
            pltpu.VMEM(mixed.shape, jnp.float32),
            pltpu.VMEM(heads_low.shape, low),
            pltpu.VMEM(attended.shape, low),
        ]
        + [pltpu.VMEM((number, D), low) for _, number in spans]
        + [
            pltpu.VMEM((tokens, D), low),
            pltpu.VMEM((tokens, D), jnp.float32),
            pltpu.VMEM((FF, tokens), low),
            pltpu.VMEM((3 * D, tokens), low),
            pltpu.VMEM((D, tokens), low),
            pltpu.VMEM((FF, D), low),
            pltpu.VMEM((FF, D), low),
            pltpu.VMEM((3 * D, D), low),
            pltpu.VMEM((D, D), low),
            pltpu.VMEM((D, 1), jnp.float32),
            pltpu.VMEM((D, 1), jnp.float32),
            pltpu.VMEM((2, D, 1), jnp.float32),
            pltpu.SemaphoreType.DMA((8,)),
            pltpu.SemaphoreType.DMA((4,)),
        ],
        compiler_params=pltpu.CompilerParams(vmem_limit_bytes=60 * 1024 * 1024),
        name="layer_backward",
    )(grad, middle, normed_low, gains, segment, state, mixed, heads_low, attended, *weights)
    return (grad, block_grads, gain_grads[:6])


HEAD_LANES = 128


def full_dot(left, right):
    return jnp.dot(left, right, preferred_element_type=jnp.float32, precision=HIGH)


def head_marks():
    entry = lax.broadcasted_iota(jnp.int32, (D, HEAD_LANES), 0)
    lane = lax.broadcasted_iota(jnp.int32, (D, HEAD_LANES), 1)
    return (entry // HD == lane).astype(jnp.float32)


def full_dot_last(left, right):
    return lax.dot_general(
        left,
        right,
        (((1,), (1,)), ((), ())),
        preferred_element_type=jnp.float32,
        precision=HIGH,
    )


def pool_sequence(state, gains, marks_of):
    unit, scale = row_norm(state)
    final = unit * gains[0:1] + gains[1:2]
    marks = head_marks()
    logits = full_dot(final * gains[2:3], marks) * (1.0 / math.sqrt(HD))
    rows, columns = marks_of
    slot = lax.broadcasted_iota(jnp.int32, (rows.shape[0], IMGS), 1)
    member = (rows == slot.astype(jnp.float32)).astype(jnp.float32)
    slot = lax.broadcasted_iota(jnp.int32, (IMGS, columns.shape[1]), 0)
    member_rows = (columns == slot.astype(jnp.float32)).astype(jnp.float32)
    tops = jnp.zeros_like(logits)
    for k in range(IMGS):
        here = rows == k
        top = jnp.max(jnp.where(here, logits, -1e30), 0, keepdims=True)
        tops = jnp.where(here, top, tops)
    exponent = jnp.exp(logits - tops)
    share = exponent / full_dot(member, full_dot(member_rows, exponent))
    spread_share = full_dot_last(share, marks)
    dead = (jnp.sum(member_rows, 1, keepdims=True) == 0.0).astype(jnp.float32)
    pooled = full_dot(member_rows, spread_share * final) + dead * jnp.mean(
        final, 0, keepdims=True
    )
    return (unit, scale, final, marks, member, member_rows, share, spread_share, dead, pooled)


def unit_scale(value):
    return lax.rsqrt(jnp.mean(value * value, -1, keepdims=True) + 1e-06)


def pool_kernel(base, state, gains, segment, matrix, pooled_low, embedded, image_low):
    parts, length = segment.shape
    for b in range(parts):
        pooled = pool_sequence(
            state[b * length : (b + 1) * length], gains[base : base + 3], slot_marks(segment, b)
        )[-1]
        pooled_low[b] = pooled.astype(jnp.bfloat16)
        value = jnp.dot(
            pooled.astype(jnp.bfloat16), matrix[...], preferred_element_type=jnp.float32
        )
        embedded[b] = value
        image_low[b] = (value * unit_scale(value) * (1.0 / math.sqrt(D))).astype(jnp.bfloat16)


def pool_forward(state, gains, base, segment, matrix):
    parts = segment.shape[0]
    shape = (parts, IMGS, D)
    return pl.pallas_call(
        functools.partial(pool_kernel, base),
        out_shape=[
            jax.ShapeDtypeStruct(shape, jnp.bfloat16),
            jax.ShapeDtypeStruct(shape, jnp.float32),
            jax.ShapeDtypeStruct(shape, jnp.bfloat16),
        ],
        in_specs=whole("vvvv"),
        out_specs=whole("vvv"),
        compiler_params=pltpu.CompilerParams(vmem_limit_bytes=VMEM_LIMIT),
        name="pool_forward",
    )(state, gains, segment, matrix)


def contrast_kernel(
    base,
    me,
    images,
    texts,
    alive_columns,
    alive_rows,
    own_images,
    own_live,
    state,
    all_gains,
    segment,
    matrix,
    pooled_low,
    embedded,
    loss,
    grad,
    grad_matrix,
    gain_out,
    text_side,
):
    parts, length = segment.shape
    gains = all_gains[base : base + 3]
    everyone = images.shape[1]
    count = jnp.zeros((1, 1), jnp.float32)
    for b in range(parts):
        count = count + jnp.sum(alive_columns[b], -1, keepdims=True)
    factor = 1.0 / (2.0 * count)
    first = me[0] * IMGS

    def rows_of(scores, alive, live, start):
        masked = jnp.where(alive > 0, scores, -1e30)
        top = jnp.max(masked, -1, keepdims=True)
        exponent = jnp.exp(masked - top)
        total = jnp.sum(exponent, -1, keepdims=True)
        line = lax.broadcasted_iota(jnp.int32, scores.shape, 0) + start
        column = lax.broadcasted_iota(jnp.int32, scores.shape, 1)
        target = (line == column).astype(jnp.float32)
        diagonal = jnp.sum(scores * target, -1, keepdims=True)
        term = (top + jnp.log(total) - diagonal) * live
        delta = (exponent * (1.0 / total) - target) * live
        return (term, (delta * factor * LOGIT_SCALE).astype(jnp.bfloat16))

    loss[...] = jnp.zeros_like(loss)
    grad_sum = jnp.zeros((D, D), jnp.float32)
    gain_out[...] = jnp.zeros_like(gain_out)
    for b in range(parts):
        forward = LOGIT_SCALE * contract_last(own_images[b], texts[b])
        term, forward_low = rows_of(forward, alive_columns[b], own_live[b], first)
        loss[...] += jnp.sum(term, 0, keepdims=True) * factor
        text_side[...] = jnp.zeros_like(text_side)

        @pl.loop(0, everyone // TOKENS)
        def _(t):
            part = tile_of(t, TOKENS)
            backward = LOGIT_SCALE * contract_last(texts[b, part], images[b])
            term, backward_low = rows_of(
                backward, alive_columns[b], alive_rows[b, part], t * TOKENS
            )
            line = lax.broadcasted_iota(jnp.int32, term.shape, 0) + t * TOKENS
            here = jnp.logical_and(line >= first, line < first + IMGS)
            loss[...] += jnp.sum(jnp.where(here, term, 0.0), 0, keepdims=True) * factor
            text_side[...] += contract_first(backward_low, texts[b, part])

        image_grad = jnp.dot(forward_low, texts[b], preferred_element_type=jnp.float32)
        image_grad = image_grad + text_side[pl.ds(pl.multiple_of(first, IMGS), IMGS)]
        value = embedded[b]
        scale = unit_scale(value)
        embed_low = (
            (
                image_grad * scale
                - value * (scale * scale * scale) * jnp.mean(value * image_grad, -1, keepdims=True)
            )
            * (1.0 / math.sqrt(D))
        ).astype(jnp.bfloat16)
        grad_sum = grad_sum + contract_first(pooled_low[b], embed_low)
        pooled_grad = contract_last(embed_low, matrix[...])
        unit, norm_scale, final, marks, member, member_rows, share, spread_share, dead, _ = (
            pool_sequence(
                state[b * length : (b + 1) * length], gains, slot_marks(segment, b)
            )
        )
        token_grad = full_dot(member, pooled_grad)
        share_grad = full_dot(final * token_grad, marks)
        inside = full_dot(member, full_dot(member_rows, share * share_grad))
        logit_grad = share * (share_grad - inside) * (1.0 / math.sqrt(HD))
        spread_logit = full_dot_last(logit_grad, marks)
        final_grad = (
            spread_share * token_grad
            + spread_logit * gains[2:3]
            + jnp.sum(dead * pooled_grad, 0, keepdims=True) * (1.0 / length)
        )
        gain_out[0:1] += jnp.sum(final_grad * unit, 0, keepdims=True)
        gain_out[1:2] += jnp.sum(final_grad, 0, keepdims=True)
        gain_out[2:3] += jnp.sum(spread_logit * final, 0, keepdims=True)
        delta = final_grad * gains[0:1]
        delta = delta - jnp.mean(delta, -1, keepdims=True) - unit * jnp.mean(
            delta * unit, -1, keepdims=True
        )
        grad[b * length : (b + 1) * length] = delta * norm_scale
    grad_matrix[...] = grad_sum.astype(jnp.bfloat16)


def contrast(me, images, texts, alive, own_images, live, state, gains, base, segment, matrix, pooled_low, embedded):
    parts, everyone = alive.shape
    loss, grad, grad_matrix, gain_grads = pl.pallas_call(
        functools.partial(contrast_kernel, base),
        out_shape=[
            jax.ShapeDtypeStruct((8, 128), jnp.float32),
            jax.ShapeDtypeStruct(state.shape, jnp.float32),
            jax.ShapeDtypeStruct((D, D), jnp.bfloat16),
            jax.ShapeDtypeStruct((8, D), jnp.float32),
        ],
        in_specs=[pl.BlockSpec(memory_space=pltpu.SMEM)] + whole("vvvvvvvvvvvv"),
        out_specs=whole("vvvv"),
        scratch_shapes=[pltpu.VMEM((everyone, D), jnp.float32)],
        compiler_params=pltpu.CompilerParams(vmem_limit_bytes=VMEM_LIMIT),
        name="contrast",
    )(
        me.reshape(1),
        images,
        texts,
        alive[:, None, :],
        alive[:, :, None],
        own_images,
        live[:, :, None],
        state,
        gains,
        segment,
        matrix,
        pooled_low,
        embedded,
    )
    return (loss[0, 0], grad, grad_matrix, gain_grads[:3])


def muon_groups():
    found = [(0, 1), (1, 1)]
    for index in range(LAYERS):
        base = 2 + 12 * index
        found = found + [(base, 3), (base + 3, 1), (base + 4, 4), (base + 8, 4)]
    return found


def lane_plan(lanes):
    plan = [[] for _ in range(lanes)]
    for start, number in sorted(muon_groups(), key=lambda group: -group[1]):
        lane = min(range(lanes), key=lambda i: (sum(n for _, n in plan[i]), len(plan[i]), i))
        plan[lane].append((start, number))
    plan.sort(key=lambda entry: (-entry[0][1] if entry else 0))
    if lanes == 8:
        plan = [plan[i] for i in (0, 1, 2, 3, 4, 6, 5, 7)]
    depth = max(len(entry) for entry in plan)
    widths = [
        max([entry[slot][1] for entry in plan if slot < len(entry)]) for slot in range(depth)
    ]
    return (plan, widths)


def lane_blocks(plan):
    rows = [[start + i for start, number in entry for i in range(number)] for entry in plan]
    most = max(len(row) for row in rows)
    return np.array([row + [-1] * (most - len(row)) for row in rows], np.int32)


def lane_tables(plan, widths):
    index = np.zeros((len(plan), sum(widths)), np.int32)
    mask = np.zeros((len(plan), sum(widths)), np.float32)
    number = np.ones((len(plan), sum(widths)), np.float32)
    home = {}
    for lane, entry in enumerate(plan):
        first = 0
        for slot, width in enumerate(widths):
            if slot < len(entry):
                start, count = entry[slot]
                for place in range(count):
                    index[lane, first + place] = start + place
                    mask[lane, first + place] = 1.0
                    number[lane, first + place] = count
                    home[start + place] = (lane, first + place)
            first += width
    return (index, mask, number, home)


def orthogonal_factor(gram):
    size = jnp.sqrt(jnp.trace(gram)) + 1e-07
    state = gram / (size * size)
    total = None
    for turn in range(NS_ITERS):
        low = rounded(state)
        change = COEF_B * state + COEF_C * jnp.dot(low, low, preferred_element_type=jnp.float32)
        change_low = rounded(change)
        if total is None:
            total = COEF_A * jnp.eye(D, dtype=jnp.float32) + change
        else:
            total = COEF_A * total + jnp.dot(
                rounded(total), change_low, preferred_element_type=jnp.float32
            )
        if turn < NS_ITERS - 1:
            for _ in range(2):
                state = COEF_A * state + jnp.dot(
                    rounded(state), change_low, preferred_element_type=jnp.float32
                )
    return total / size


def per_device(
    patches, grid, segments, text_ids, table, weights, momenta, gains, gains_m, gains_v, step
):
    fin = 6 * LAYERS
    base = fin + 3
    lanes = lax.axis_size("dp")
    slots = jnp.arange(IMGS, dtype=jnp.int32)
    live = jnp.any(segments[:, 0, None, :] == slots[None, :, None], -1).astype(jnp.float32)
    depth = lax.axis_size("fsdp")
    captions = MB * IMGS
    tokens = text_ids.shape[3]
    fast = depth == 4 and lanes == 8
    early = [(0, 1), (2, 3), (5, 1), (6, 4), (10, 4), (1, 1)]
    later = []
    for index in range(1, LAYERS):
        start = 2 + 12 * index
        early = early + [(start, 3), (start + 3, 1)]
        later = later + [(start + 4, 4), (start + 8, 4)]
    later_own = jnp.concatenate([weights[a : a + n] for a, n in later], 0)
    if fast:
        eighth = weights.shape[1] // lanes
        later_own = lax.dynamic_slice_in_dim(later_own, lax.axis_index("dp") * eighth, eighth, 1)
    later_blocks = gather_later(rounded(later_own))
    if fast:
        half = tokens // 2
        own_ids = jnp.transpose(text_ids.reshape(captions, 2, half), (2, 1, 0)).reshape(half, -1)
        place = jnp.arange(depth * 2 * captions, dtype=jnp.int32) // (2 * captions)
        own_ids = jnp.where(
            place[None] == lax.axis_index("fsdp"), jnp.tile(own_ids, (1, depth)), 0
        )
        (stem, *first_blocks), text_sum = fetch(weights, early, own_ids, table, captions, 1)
    else:
        stem, *first_blocks = [
            lax.all_gather(rounded(weights[a : a + n]), "fsdp", axis=1, tiled=True)
            for a, n in early
        ]
        ids = lax.all_gather(text_ids.reshape(captions, tokens), "fsdp", axis=0)
        picked = ids.reshape(depth * captions, -1) - lax.axis_index("fsdp") * table.shape[0]
        row = jnp.arange(table.shape[0], dtype=jnp.int32)
        hits = jnp.sum((picked[:, :, None] == row[None, None, :]).astype(jnp.int32), 1)
        text_sum = lax.psum_scatter(
            jnp.dot(
                rounded(hits.astype(jnp.float32)), table, preferred_element_type=jnp.float32
            ).reshape(depth, captions, D),
            "fsdp",
            scatter_dimension=0,
        )
    early_blocks = first_blocks[5:]
    pooling_matrix = first_blocks[4][0]
    first_blocks = first_blocks[:4]
    text_low = rounded(unit_rows(text_sum / text_ids.shape[-1]))
    me = lax.axis_index(("dp", "fsdp"))
    segment = segments[:, 0]
    rows_hot, cols_hot = jax.vmap(positions)(grid[:, 0])
    rows_hot = rows_hot.reshape(-1, POS)
    cols_hot = cols_hot.reshape(-1, POS)
    patch_low = patches.reshape(-1, D)
    state = product(patch_low, stem[0], "sd,rd->sr")
    state = state + jnp.dot(rows_hot, gains[base : base + POS], precision=HIGH)
    state = state + jnp.dot(cols_hot, gains[base + POS : base + 2 * POS], precision=HIGH)
    saved = []
    for index in range(LAYERS):
        if index == 0:
            blocks = [(array, 0, array.shape[0]) for array in first_blocks]
        else:
            first = 8 * index - 8
            blocks = [
                (array, 0, array.shape[0]) for array in early_blocks[2 * index - 2 : 2 * index]
            ] + [(later_blocks, first, 4), (later_blocks, first + 4, 4)]
        state, kept = layer_forward(state, blocks, gains, 6 * index, segment)
        saved.append((kept, blocks))
    pooled_low, embedded, image_low = pool_forward(state, gains, fin, segment, pooling_matrix)
    own_flags = jnp.broadcast_to(live.reshape(captions, 1), (captions, 128)).astype(jnp.bfloat16)
    both = jnp.stack([image_low.reshape(captions, D), text_low]).reshape(2 * captions, D)
    gathered, flags = share([both, own_flags], 8)
    gathered = gathered.reshape(-1, 2, MB, IMGS, D)
    flags = flags.reshape(-1, MB, IMGS, 128)[..., 0].astype(jnp.float32)
    images, texts = [
        jnp.moveaxis(gathered[:, i], 0, 1).reshape(MB, -1, D) for i in range(2)
    ]
    loss_part, grad, grad_pool, pool_gain_grads = contrast(
        me,
        images,
        texts,
        jnp.moveaxis(flags, 0, 1).reshape(MB, -1),
        image_low,
        live,
        state,
        gains,
        fin,
        segment,
        pooling_matrix,
        pooled_low,
        embedded,
    )
    gain_parts = [None] * LAYERS
    block_grads = [None] * LAYERS
    slices = [None] * LAYERS
    for index in reversed(range(LAYERS)):
        kept, blocks = saved[index]
        grad, block_grads[index], gain_parts[index] = layer_backward(
            grad, kept, blocks, gains, 6 * index, segment
        )
        if index == 1:
            block_grads[index].append(grad_pool)
        if fast and index > 0:
            (slices[index],) = reduce_grads(block_grads[index], 4 + index)
    grad_low = rounded(grad)
    grad_patch = rounded(product(grad_low, patch_low, "sr,sd->rd"))
    block_grads[0].append(grad_patch)
    grad_rows = jnp.dot(rows_hot.T, grad, precision=HIGH)
    grad_cols = jnp.dot(cols_hot.T, grad, precision=HIGH)
    gains_grad = jnp.concatenate(
        gain_parts
        + [pool_gain_grads, grad_rows, grad_cols],
        0,
    )
    plan, widths = lane_plan(lanes)
    index, mask, number, home = lane_tables(plan, widths)
    lane = lax.axis_index("dp")
    scale = np.ones((weights.shape[0],), np.float32)
    for start, count_blocks in muon_groups():
        scale[start : start + count_blocks] = MUON_RATE * math.sqrt(count_blocks)
    if fast:
        width = 256
        small = jnp.concatenate([gains_grad.reshape(-1), loss_part[None]])
        small = jnp.pad(small, (0, lanes * depth * 8 * width - small.shape[0]))
        blocks_here = lane_blocks(plan)
        origins = [(0, 12), (1, 12)] + [
            (index, block) for index in range(LAYERS) for block in range(12)
        ]
        slices[0], _, small, stats, mine, slices = reduce_grads(
            block_grads[0],
            4,
            small.reshape(lanes * depth, 8, width),
            (blocks_here, origins),
            slices[1],
        )
        flat = small.reshape(-1)
        gains_grad, loss = (flat[: gains.size].reshape(gains.shape), flat[gains.size])
        squares = jnp.sum(stats[:, :, 0, 0])
        norm = jnp.sqrt(squares + jnp.sum(gains_grad * gains_grad))
        clip = jnp.minimum(1.0, CLIP_LIMIT / (norm + 1e-06))
        own_momenta = jnp.stack(
            [
                jnp.where(
                    jnp.asarray(blocks_here >= 0)[lane, place],
                    lax.dynamic_index_in_dim(
                        momenta, jnp.maximum(jnp.asarray(blocks_here)[lane, place], 0), 0, False
                    ),
                    0.0,
                )
                for place in range(blocks_here.shape[1])
            ]
        )
        own = MOMENT * own_momenta + clip * mine.reshape(own_momenta.shape).astype(jnp.float32)
        two = jnp.asarray(np.array([len(entry) > 1 for entry in plan], np.int32))[lane]
        own_low = rounded(own)
        gram = product(own_low, own_low, "brd,bre->de")
        gram, all_rows, shard_grads = sum_grams(gram, own_low[:2], slices, 12)
        turned = spread(schulz(two.reshape(1), gram, all_rows, own), 13)
        homes = {
            int(block): (lane_of, place)
            for lane_of, entry in enumerate(blocks_here)
            for place, block in enumerate(entry)
            if block >= 0
        }
        momenta_new, weights_new, weights_low = update(
            homes, scale, clip, momenta, shard_grads.reshape(weights.shape), weights, turned
        )
    else:
        stack = jnp.concatenate(
            [block_grads[index].pop().reshape(1, D, D) for index in range(LAYERS)]
            + [value.reshape(-1, D, D) for values in block_grads for value in values],
            0,
        )
        shard_grads = lax.psum(
            lax.psum_scatter(stack, "fsdp", scatter_dimension=1, tiled=True), "dp"
        ).astype(jnp.float32)
        gains_grad, loss = lax.psum((gains_grad, loss_part), ("dp", "fsdp"))
        squares = lax.psum(jnp.sum(shard_grads * shard_grads), "fsdp")
        norm = jnp.sqrt(squares + jnp.sum(gains_grad * gains_grad))
        clip = jnp.minimum(1.0, CLIP_LIMIT / (norm + 1e-06))
        momenta_new = MOMENT * momenta + clip * shard_grads
        own = jnp.stack(
            [
                lax.dynamic_index_in_dim(momenta_new, jnp.asarray(index)[lane, place], 0, False)
                * jnp.asarray(mask)[lane, place]
                for place in range(index.shape[1])
            ]
        )
        own_low = rounded(own)
        bounds = np.cumsum([0] + widths)
        grams = jnp.stack(
            [
                product(own_low[a:b], own_low[a:b], "brd,bre->de")
                for a, b in zip(bounds[:-1], bounds[1:])
            ]
        )
        grams = lax.psum(grams, "fsdp")
        turned = jnp.concatenate(
            [
                product(
                    own_low[bounds[slot] : bounds[slot + 1]],
                    rounded(orthogonal_factor(grams[slot])),
                    "brd,de->bre",
                )
                for slot in range(len(widths))
            ],
            0,
        )
        spread_rows = lax.all_gather(rounded(turned), "dp", axis=0)
        current = jnp.stack(
            [spread_rows[home[block][0], home[block][1]] for block in range(weights.shape[0])]
        ).astype(jnp.float32)
        weights_new = weights * (1.0 - MUON_RATE * MUON_DECAY) - jnp.asarray(scale)[:, None, None] * current
        weights_low = rounded(weights_new)
    grad_small = clip * gains_grad
    moment_one = BETA_ONE * gains_m + (1.0 - BETA_ONE) * grad_small
    moment_two = BETA_TWO * gains_v + (1.0 - BETA_TWO) * grad_small * grad_small
    count_steps = step[0].astype(jnp.float32)
    corrected_one = moment_one / (1.0 - jnp.power(BETA_ONE, count_steps))
    corrected_two = moment_two / (1.0 - jnp.power(BETA_TWO, count_steps))
    gains_new = gains - ADAM_RATE * (
        corrected_one / (jnp.sqrt(corrected_two) + ADAM_EPS) + ADAM_DECAY * gains
    )
    shift_grad = grad_small[fin + 1]
    return (
        loss,
        norm,
        weights_new,
        weights_low,
        momenta_new,
        gains_new,
        moment_one,
        moment_two,
        shift_grad,
    )


def solution(mesh):
    placed = (
        P(None, ("dp", "fsdp"), None, None),
        P(None, ("dp", "fsdp"), None, None),
        P(None, ("dp", "fsdp"), None),
        P(None, ("dp", "fsdp"), None, None),
        P("fsdp", None),
        P(None, "fsdp", None),
        P(None, "fsdp", None),
        P(),
        P(),
        P(),
        P(),
    )
    return jax.shard_map(
        per_device,
        mesh=mesh,
        in_specs=placed,
        out_specs=(
            P(),
            P(),
            P(None, "fsdp", None),
            P(None, "fsdp", None),
            P(None, "fsdp", None),
            P(),
            P(),
            P(),
            P(),
        ),
        check_vma=False,
    )
```

```python
import functools
import math

import jax
import jax.numpy as jnp
import numpy as np
from jax import lax
from jax.experimental import pallas as pl
from jax.experimental.pallas import tpu as pltpu
from jax.sharding import PartitionSpec as P

D = 768
HEADS = 12
FF = 3072
LAYERS = 2
IMGS = 8
POS = 32
MB = 2
NS_ITERS = 5
HD = 64


MESH = pl.DeviceIdType.MESH
VMEM_LIMIT = 56 * 1024 * 1024
HIGH = lax.Precision.HIGHEST
LOGIT_SCALE = 50.0
CLIP_LIMIT = 0.005
MOMENT = 0.95
MUON_RATE = 0.5
MUON_DECAY = 0.01
ADAM_RATE = 0.4
BETA_ONE = 0.9
BETA_TWO = 0.999
ADAM_EPS = 1e-08
ADAM_DECAY = 0.01
COEF_A = 3.4445
COEF_B = -4.775
COEF_C = 2.0315


def rounded(value):
    return value.astype(jnp.bfloat16)


def product(left, right, form):
    return jnp.einsum(form, left, right, preferred_element_type=jnp.float32)


def unit_rows(value):
    return (
        value
        * lax.rsqrt(jnp.mean(value * value, -1, keepdims=True) + 1e-06)
        * (1.0 / math.sqrt(value.shape[-1]))
    )


def positions(grid):
    slots = jnp.arange(POS, dtype=jnp.int32)
    row_index = grid[0] * POS // grid[2]
    col_index = grid[1] * POS // grid[3]
    return (
        (row_index[:, None] == slots[None]).astype(jnp.float32),
        (col_index[:, None] == slots[None]).astype(jnp.float32),
    )


def whole(kinds):
    memory = {"v": pltpu.VMEM, "a": pl.ANY}
    return [pl.BlockSpec(memory_space=memory[kind]) for kind in kinds]


def flip(index, bit):
    return index + bit - 2 * bit * lax.rem(index // bit, 2)


def greet(peers):
    barrier = pltpu.get_barrier_semaphore()
    for peer in peers:
        pl.semaphore_signal(barrier, inc=1, device_id=peer, device_id_type=MESH)
    pl.semaphore_wait(barrier, len(peers))


def places():
    d = lax.axis_index("dp")
    z = lax.axis_index("fsdp")
    return (d, z, [lax.rem(z + step, 4) for step in range(4)])


CAPTION_TILE = 400


def fetch_kernel(chunks, sizes, tokens, weights, ids, table, *refs):
    outs = refs[: len(sizes)]
    texts = refs[len(sizes)]
    (
        full,
        low,
        all_ids,
        pages,
        found,
        found_parts,
        from_z,
        load_sem,
        store_sem,
        send,
        recv,
        page_sem,
        id_send,
        id_recv,
        part_send,
        part_recv,
        own_text,
        text_send,
        text_recv,
    ) = refs[len(sizes) + 1 :]
    d, z, zs = places()
    sib, near_x, near_y = flip(d, 1), flip(d, 2), flip(d, 4)
    diagonal = flip(near_x, 4)
    starts = [sum(chunk[3] for chunk in chunks[:k]) for k in range(len(chunks))]
    loads = []
    for k, (source, _, _, n) in enumerate(chunks):
        loads.append(
            pltpu.make_async_copy(
                weights.at[pl.ds(source, n)], full.at[pl.ds(starts[k], n)], load_sem.at[k]
            )
        )
        loads[k].start()
    page_count = table.shape[0] // CAPTION_TILE

    def page(t):
        return pltpu.make_async_copy(
            table.at[tile_of(t, CAPTION_TILE)], pages.at[lax.rem(t, 2)], page_sem.at[lax.rem(t, 2)]
        )

    page(0).start()
    greet(
        [(d, zs[1]), (d, zs[2]), (d, zs[3]), (sib, z), (near_x, z), (near_y, z), (diagonal, z)]
    )
    pending = []
    all_ids[z] = ids[...]
    id_copies = []
    for o in (1, 2, 3):
        id_copies.append(
            pltpu.make_async_remote_copy(
                src_ref=ids,
                dst_ref=all_ids.at[z],
                send_sem=id_send.at[o - 1],
                recv_sem=id_recv.at[o - 1],
                device_id=(d, zs[o]),
                device_id_type=MESH,
            )
        )
        id_copies[-1].start()

    def push(k, slot, first, n, zz, dd, to, source=None):
        out = outs[chunks[k][1]]
        rows = pl.ds(chunks[k][2] + first, n)
        copy = pltpu.make_async_remote_copy(
            src_ref=out.at[rows, zz, dd] if source is None else source,
            dst_ref=out.at[rows, zz, dd],
            send_sem=send.at[k, slot],
            recv_sem=recv.at[k, slot],
            device_id=to,
            device_id_type=MESH,
        )
        copy.start()
        pending.append(copy)
        return copy

    along_z = []
    stores = []
    for k, (_, out, offset, n) in enumerate(chunks):
        loads[k].wait()

        @pl.loop(starts[k], starts[k] + n)
        def _(i):
            low[i] = full[i].astype(low.dtype)

        along_z.append(
            [
                push(k, o - 1, 0, n, z, d, (d, zs[o]), low.at[pl.ds(starts[k], n), d])
                for o in (1, 2, 3)
            ]
        )
        stores.append(
            pltpu.make_async_copy(
                low.at[pl.ds(starts[k], n)],
                outs[out].at[pl.ds(offset, n), z],
                store_sem.at[k],
            )
        )
        stores[k].start()
    for copy in id_copies:
        copy.wait_recv()
    marks = all_ids[0] + all_ids[1] + all_ids[2] + all_ids[3]
    found[...] = jnp.zeros_like(found)

    def look_up(t):
        @pl.when(t + 1 < page_count)
        def _():
            page(t + 1).start()

        page(t).wait()
        row = lax.broadcasted_iota(jnp.int32, (CAPTION_TILE, marks.shape[1]), 0)
        row = row + (z * table.shape[0] + t * CAPTION_TILE)
        hits = jnp.zeros(row.shape, jnp.float32)
        for token in range(marks.shape[0]):
            hits = hits + jnp.where(row == marks[token : token + 1], 1.0, 0.0)
        found[...] += contract_first(hits.astype(jnp.bfloat16), pages[lax.rem(t, 2)])

    def look_up_span(first, last):
        @pl.loop(first, last)
        def _(t):
            look_up(t)

    share_of = -(-page_count // (len(chunks) - 4))
    part_copies = []
    text_copies = []

    def push_text(slot, source, target, to):
        text_copies.append(
            pltpu.make_async_remote_copy(
                src_ref=source,
                dst_ref=target,
                send_sem=text_send.at[slot],
                recv_sem=text_recv.at[slot],
                device_id=to,
                device_id_type=MESH,
            )
        )
        text_copies[-1].start()

    def text_along_z():
        for copy in part_copies:
            copy.wait_recv()
        value = (found_parts[z] + from_z[0] + from_z[1] + from_z[2]) * (1.0 / tokens)
        value = unit_rows(value).astype(own_text.dtype)
        own_text[...] = value
        texts[d, z] = value
        for o in (1, 2, 3):
            push_text(o - 1, own_text, texts.at[d, z], (d, zs[o]))

    def text_across_plane():
        for copy in text_copies[:3]:
            copy.wait_recv()
        for i, to in enumerate((near_x, near_y, diagonal, sib)):
            push_text(3 + i, texts.at[d], texts.at[d], (to, z))

    def text_to_core():
        for i, origin in enumerate((near_x, near_y, diagonal)):
            text_copies[3 + i].wait_recv()
            push_text(7 + i, texts.at[origin], texts.at[origin], (sib, z))

    def send_parts():
        captions = found_parts.shape[1]
        for owner in range(4):
            found_parts[owner] = (
                found[2 * owner * captions : (2 * owner + 1) * captions]
                + found[(2 * owner + 1) * captions : (2 * owner + 2) * captions]
            )
        for o in (1, 2, 3):
            part_copies.append(
                pltpu.make_async_remote_copy(
                    src_ref=found_parts.at[zs[o]],
                    dst_ref=from_z.at[o - 1],
                    send_sem=part_send.at[o - 1],
                    recv_sem=part_recv.at[o - 1],
                    device_id=(d, zs[o]),
                    device_id_type=MESH,
                )
            )
            part_copies[-1].start()

    along_x, along_y, turn_y, turn_x, last = {}, {}, {}, {}, []
    count = len(chunks)
    for step in range(count + 2):
        if step < count:
            k, n = step, chunks[step][3]
            along_x[k], along_y[k] = [], []
            for o in (1, 2, 3):
                zz = zs[4 - o]
                along_z[k][o - 1].wait_recv()
                along_x[k].append(push(k, 2 + o, 0, n, zz, d, (near_x, z)))
                along_y[k].append(push(k, 5 + o, 0, n, zz, d, (near_y, z)))
                last.append(push(k, 14 + o, 0, n, zz, d, (sib, z)))
        if 1 <= step <= count:
            k, n = step - 1, chunks[step - 1][3]
            half = n // 2
            turn_y[k], turn_x[k] = [], []
            for o in (1, 2, 3):
                zz = zs[4 - o]
                along_x[k][o - 1].wait_recv()
                if half:
                    turn_y[k].append(push(k, 8 + o, 0, half, zz, near_x, (near_y, z)))
                last.append(push(k, 17 + o, 0, n, zz, near_x, (sib, z)))
                along_y[k][o - 1].wait_recv()
                turn_x[k].append(push(k, 11 + o, half, n - half, zz, near_y, (near_x, z)))
                last.append(push(k, 20 + o, 0, n, zz, near_y, (sib, z)))
        if step * share_of < page_count:
            look_up_span(step * share_of, min((step + 1) * share_of, page_count))
        for at, action in (
            (count - 4, send_parts),
            (count - 2, text_along_z),
            (count - 1, text_across_plane),
            (count + 1, text_to_core),
        ):
            if step == at:
                action()
        if step >= 2:
            k, n = step - 2, chunks[step - 2][3]
            for o in (1, 2, 3):
                for copies in (turn_y[k], turn_x[k]):
                    if copies:
                        copies[o - 1].wait_recv()
                last.append(push(k, 23 + o, 0, n, zs[4 - o], diagonal, (sib, z)))
    for copy in last:
        copy.wait_recv()
    for copy in pending:
        copy.wait_send()
    for copy in stores:
        copy.wait()
    for copy in id_copies:
        copy.wait_send()
    for copy in part_copies:
        copy.wait_send()
    for copy in text_copies[6:]:
        copy.wait_recv()
    for copy in text_copies:
        copy.wait_send()


def fetch(weights, pieces, ids, table, captions, tokens, collective):
    depth, eighths = lax.axis_size("fsdp"), lax.axis_size("dp")
    blocks, rows, width = weights.shape
    part = (eighths, rows // eighths, width)
    chunks = []
    for out, (a, n) in enumerate(pieces):
        for first in range(0, n, 2):
            chunks.append((a + first, out, first, min(2, n - first)))
    total = sum(n for _, n in pieces)
    outs = pl.pallas_call(
        functools.partial(fetch_kernel, chunks, [n for _, n in pieces], tokens),
        out_shape=[
            jax.ShapeDtypeStruct((n, depth) + part, jnp.bfloat16) for _, n in pieces
        ]
        + [jax.ShapeDtypeStruct((eighths, depth, captions, width), jnp.bfloat16)],
        in_specs=whole("ava"),
        out_specs=whole("a" * len(pieces) + "v"),
        scratch_shapes=[
            pltpu.VMEM((total,) + part, jnp.float32),
            pltpu.VMEM((total,) + part, jnp.bfloat16),
            pltpu.VMEM((depth,) + ids.shape, jnp.int32),
            pltpu.VMEM((2, CAPTION_TILE, width), jnp.bfloat16),
            pltpu.VMEM((2 * depth * captions, width), jnp.float32),
            pltpu.VMEM((depth, captions, width), jnp.float32),
            pltpu.VMEM((3, captions, width), jnp.float32),
            pltpu.SemaphoreType.DMA((len(chunks),)),
            pltpu.SemaphoreType.DMA((len(chunks),)),
            pltpu.SemaphoreType.DMA((len(chunks), 27)),
            pltpu.SemaphoreType.DMA((len(chunks), 27)),
            pltpu.SemaphoreType.DMA((2,)),
            pltpu.SemaphoreType.DMA((3,)),
            pltpu.SemaphoreType.DMA((3,)),
            pltpu.SemaphoreType.DMA((3,)),
            pltpu.SemaphoreType.DMA((3,)),
            pltpu.VMEM((captions, width), jnp.bfloat16),
            pltpu.SemaphoreType.DMA((10,)),
            pltpu.SemaphoreType.DMA((10,)),
        ],
        compiler_params=pltpu.CompilerParams(
            collective_id=collective, has_side_effects=True, vmem_limit_bytes=VMEM_LIMIT
        ),
        name=f"fetch_{collective}",
    )(weights.reshape((blocks,) + part), ids, table)
    return ([out.reshape(-1, width, width) for out in outs[:-1]], outs[-1])


def gather_later(own):
    depth, eighths = lax.axis_size("fsdp"), lax.axis_size("dp")
    if depth != 4 or eighths != 8:
        return lax.all_gather(own, "fsdp", axis=1, tiled=True)
    return lax.all_gather(own, ("fsdp", "dp"), axis=1).reshape(-1, D, D)


def share_kernel(count, *refs):
    owns, outs, (send, recv) = (refs[:count], refs[count : 2 * count], refs[2 * count :])
    d, z, zs = places()
    sib, near_x, near_y = flip(d, 1), flip(d, 2), flip(d, 4)
    diagonal = flip(near_x, 4)
    greet(
        [(d, zs[1]), (d, zs[2]), (d, zs[3]), (sib, z), (near_x, z), (near_y, z), (diagonal, z)]
    )
    for own, out in zip(owns, outs):
        out[d, z] = own[...]
    started = []

    def push(slot, origin, to, first=False):
        copies = []
        for i in range(count):
            copies.append(
                pltpu.make_async_remote_copy(
                    src_ref=owns[i] if first else outs[i].at[origin],
                    dst_ref=outs[i].at[origin, z] if first else outs[i].at[origin],
                    send_sem=send.at[i, slot],
                    recv_sem=recv.at[i, slot],
                    device_id=to,
                    device_id_type=MESH,
                )
            )
            copies[-1].start()
        started.extend(copies)
        return copies

    def arrive(copies):
        for copy in copies:
            copy.wait_recv()

    first = [push(o - 1, d, (d, zs[o]), True) for o in (1, 2, 3)]
    for copies in first:
        arrive(copies)
    second = [push(3 + i, d, (to, z)) for i, to in enumerate((near_x, near_y, diagonal))]
    last = [push(6, d, (sib, z))]
    for i, origin in enumerate((near_x, near_y, diagonal)):
        arrive(second[i])
        last.append(push(7 + i, origin, (sib, z)))
    for copies in last:
        arrive(copies)
    for copy in started:
        copy.wait_send()


def share(owns, collective):
    lanes, depth = lax.axis_size("dp"), lax.axis_size("fsdp")
    if depth != 4 or lanes != 8:
        return [
            lax.all_gather(own, ("dp", "fsdp"), axis=0).reshape((lanes, depth) + own.shape)
            for own in owns
        ]
    count = len(owns)
    return pl.pallas_call(
        functools.partial(share_kernel, count),
        out_shape=[jax.ShapeDtypeStruct((lanes, depth) + own.shape, own.dtype) for own in owns],
        in_specs=[pl.BlockSpec(memory_space=pltpu.VMEM)] * count,
        out_specs=[pl.BlockSpec(memory_space=pltpu.VMEM)] * count,
        scratch_shapes=[
            pltpu.SemaphoreType.DMA((count, 10)),
            pltpu.SemaphoreType.DMA((count, 10)),
        ],
        compiler_params=pltpu.CompilerParams(collective_id=collective, has_side_effects=True),
        name=f"share_{collective}",
    )(*owns)


class Reduction:
    def __init__(self, source, start, first, n, buffers, k, semaphores, spots):
        self.source, self.start, self.first, self.n, self.k = (source, start, first, n, k)
        self.held, self.from_core, self.from_near, self.from_turn, self.ready, self.from_z = buffers
        self.local_sem, self.send, self.recv = semaphores
        self.spots = spots
        self.rows = pl.ds(first, n)
        self.started = []

    def push(self, slot, source, target, to):
        copy = pltpu.make_async_remote_copy(
            src_ref=source,
            dst_ref=target,
            send_sem=self.send.at[self.k, slot],
            recv_sem=self.recv.at[self.k, slot],
            device_id=to,
            device_id_type=MESH,
        )
        copy.start()
        self.started.append(copy)
        return copy

    def begin(self):
        d, z, zs, x, y, c = self.spots
        blocks = pl.ds(self.start, self.n)
        self.local = pltpu.make_async_copy(
            self.source.at[blocks, :, :, :, c], self.held.at[self.rows], self.local_sem.at[self.k]
        )
        self.local.start()
        self.core = self.push(
            0,
            self.source.at[blocks, :, :, :, 1 - c],
            self.from_core.at[self.rows],
            (flip(d, 1), z),
        )

    def add(self, count, place):
        @pl.loop(0, self.n * count)
        def _(i):
            target, other = place(self.first + i // count, lax.rem(i, count))
            self.held[target] = self.held[target] + other

    def across_plane(self):
        d, z, zs, x, y, c = self.spots
        self.local.wait()
        self.core.wait_recv()

        def place(b, i):
            target = (b, i // 4, lax.rem(i // 2, 2), lax.rem(i, 2))
            return (target, self.from_core[target])

        self.add(16, place)
        self.near = [
            self.push(
                1,
                self.held.at[self.rows, 0:2, :, 1 - x],
                self.from_near.at[self.rows, 0:2],
                (flip(d, 2), z),
            ),
            self.push(
                2,
                self.held.at[self.rows, 2:4, 1 - y],
                self.from_near.at[self.rows, 2:4],
                (flip(d, 4), z),
            ),
        ]

    def turn(self):
        d, z, zs, x, y, c = self.spots

        def place_a(b, i):
            return ((b, i // 2, lax.rem(i, 2), x), self.from_near[b, i // 2, lax.rem(i, 2)])

        def place_b(b, i):
            return ((b, 2 + i // 2, y, lax.rem(i, 2)), self.from_near[b, 2 + i // 2, lax.rem(i, 2)])

        self.near[0].wait_recv()
        self.add(4, place_a)
        a = self.push(
            3,
            self.held.at[self.rows, 0:2, 1 - y, x],
            self.from_turn.at[self.rows, 0:2],
            (flip(d, 4), z),
        )
        self.near[1].wait_recv()
        self.add(4, place_b)
        b = self.push(
            4,
            self.held.at[self.rows, 2:4, y, 1 - x],
            self.from_turn.at[self.rows, 2:4],
            (flip(d, 2), z),
        )
        self.turned = [a, b]

    def along_z(self):
        d, z, zs, x, y, c = self.spots
        for copy in self.turned:
            copy.wait_recv()

        @pl.loop(0, self.n * 4)
        def _(i):
            b, zz = (self.first + i // 4, lax.rem(i, 4))
            self.ready[b, zz] = self.held[b, zz, y, x] + self.from_turn[b, zz]

        self.spread = [
            self.push(
                4 + o,
                self.ready.at[self.rows, zs[o]],
                self.from_z.at[self.rows, o - 1],
                (d, zs[o]),
            )
            for o in (1, 2, 3)
        ]

    def finish(self, out):
        d, z, zs, x, y, c = self.spots
        for copy in self.spread:
            copy.wait_recv()

        @pl.loop(self.first, self.first + self.n)
        def _(b):
            total = self.held[b, z, y, x].astype(jnp.float32) + self.from_turn[b, z].astype(
                jnp.float32
            )
            for o in range(3):
                total = total + self.from_z[b, o].astype(jnp.float32)
            out[b] = total

        for copy in self.started:
            copy.wait_send()


class Meeting:
    def __init__(self, blocks_of, sources, refs):
        self.blocks_of, self.sources = (blocks_of, sources)
        self.small_out, self.stats_out, self.mine, self.low = refs[:4]
        self.parts, self.stats, self.local_sem, self.send, self.recv = refs[4:9]
        self.part_send, self.part_recv = refs[9:]

    def push(self, slot, source, target, to, sems):
        copy = pltpu.make_async_remote_copy(
            src_ref=source,
            dst_ref=target,
            send_sem=sems[0].at[slot],
            recv_sem=sems[1].at[slot],
            device_id=to,
            device_id_type=MESH,
        )
        copy.start()
        return copy

    def run(self, small, results, spots, others):
        d, z, zs = spots[:3]
        total = jnp.zeros(results[0].shape[1:], jnp.float32)
        homes = {
            int(block): (lane, place)
            for lane, entry in enumerate(self.blocks_of)
            for place, block in enumerate(entry)
        }
        for block, (source, index) in enumerate(self.sources):
            value = results[source][index]
            total = total + value * value
            value = value.astype(self.low.dtype)
            self.low[block] = value
            lane, place = homes[block]
            self.parts[lane, place] = value
        for lane, entry in enumerate(self.blocks_of):
            for place, block in enumerate(entry):
                if block < 0:
                    self.parts[lane, place] = jnp.zeros_like(self.parts[lane, place])
        squares = jnp.sum(total, axis=(0, 1), keepdims=True)
        self.stats[...] = jnp.broadcast_to(squares, self.stats.shape)
        moved = [
            self.push(
                i,
                self.parts.at[other],
                self.mine.at[:, d],
                (other, z),
                (self.part_send, self.part_recv),
            )
            for i, other in enumerate(others)
        ]
        keep = pltpu.make_async_copy(self.parts.at[d], self.mine.at[:, d], self.local_sem)
        keep.start()
        pairs = [(small, self.small_out), (self.stats, self.stats_out)]
        for own, out in pairs:
            out[z, d] = own[...]
        started = []

        def push_all(slot, origin, to, first=False):
            copies = []
            for i, (own, out) in enumerate(pairs):
                copies.append(
                    self.push(
                        slot,
                        own if first else out.at[:, origin],
                        out.at[z, origin] if first else out.at[:, origin],
                        to,
                        (self.send.at[i], self.recv.at[i]),
                    )
                )
            started.extend(copies)
            return copies

        def arrive(copies):
            for copy in copies:
                copy.wait_recv()

        first = [push_all(o - 1, d, (d, zs[o]), True) for o in (1, 2, 3)]
        for copies in first:
            arrive(copies)
        second = [push_all(3 + i, d, (to, z)) for i, to in enumerate(others[:3])]
        last = [push_all(6, d, (others[3], z))]
        for i, origin in enumerate(others[:3]):
            arrive(second[i])
            last.append(push_all(7 + i, origin, (others[3], z)))
        for copies in last:
            arrive(copies)
        arrive(moved)
        for copy in started + moved:
            copy.wait_send()
        keep.wait()


def reduce_kernel(chunks, sources, sets, meeting, *refs):
    ins = refs[:sources]
    refs = refs[sources:]
    if meeting is not None:
        earlier, refs = (refs[0], refs[1:])
    outs = refs[:sets]
    refs = refs[sets:]
    if meeting is not None:
        outside, refs = (refs[:4], refs[4:])
    buffers = [refs[6 * i : 6 * i + 6] for i in range(sets)]
    semaphores = refs[6 * sets : 6 * sets + 3]
    d, z, zs = places()
    spots = (d, z, zs, lax.rem(d // 2, 2), d // 4, lax.rem(d, 2))
    sib, near_x, near_y = (flip(d, 1), flip(d, 2), flip(d, 4))
    diagonal = flip(near_x, 4)
    others = [near_x, near_y, diagonal, sib, flip(near_x, 1), flip(near_y, 1), flip(diagonal, 1)]
    if meeting is None:
        others = [near_x, near_y, sib]
    greet([(d, zs[1]), (d, zs[2]), (d, zs[3])] + [(other, z) for other in others])
    work = []
    for k, (source, start, first, n, which) in enumerate(chunks):
        work.append(
            Reduction(ins[source], start, first, n, buffers[which], k, semaphores, spots)
        )
        work[k].begin()
    count = len(chunks)
    for step in range(count + 3):
        if step < count:
            work[step].across_plane()
        if 1 <= step <= count:
            work[step - 1].turn()
        if 2 <= step <= count + 1:
            work[step - 2].along_z()
        if step >= 3:
            work[step - 3].finish(outs[chunks[step - 3][4]])
    if meeting is not None:
        tail = Meeting(*meeting, tuple(outside) + tuple(refs[6 * sets + 3 :]))
        tail.run(outs[1].at[0], (outs[0], earlier), spots, others)


def reduce_grads(grads, collective, small=None, meeting=None, earlier=None):
    lanes, depth = lax.axis_size("dp"), lax.axis_size("fsdp")
    rows = D // (lanes * depth)
    tail = (depth, 2, 2, 2)
    sources = [grad.reshape((-1,) + tail + (rows, D)) for grad in grads]
    chunks = []
    first = 0
    for i, source in enumerate(sources):
        for start in range(0, source.shape[0], 2):
            n = min(2, source.shape[0] - start)
            chunks.append((i, start, first, n, 0))
            first += n
    sets = [(first, (rows, D), jnp.bfloat16)]
    if small is not None:
        sources.append(small.reshape((1,) + tail + small.shape[1:]))
        chunks.insert(1, (len(sources) - 1, 0, 0, 1, 1))
        sets.append((1, small.shape[1:], jnp.float32))
    scratch = []
    for n, shape, kind in sets:
        scratch += [
            pltpu.VMEM((n, depth, 2, 2) + shape, kind),
            pltpu.VMEM((n, depth, 2, 2) + shape, kind),
            pltpu.VMEM((n, depth, 2) + shape, kind),
            pltpu.VMEM((n, depth) + shape, kind),
            pltpu.VMEM((n, depth) + shape, kind),
            pltpu.VMEM((n, 3) + shape, kind),
        ]
    scratch += [
        pltpu.SemaphoreType.DMA((len(chunks),)),
        pltpu.SemaphoreType.DMA((len(chunks), 8)),
        pltpu.SemaphoreType.DMA((len(chunks), 8)),
    ]
    out_shape = [jax.ShapeDtypeStruct((n,) + shape, jnp.float32) for n, shape, _ in sets]
    count = len(sources)
    if meeting is not None:
        blocks_of, origins = meeting
        most = len(blocks_of[0])
        out_shape += [
            jax.ShapeDtypeStruct((depth, lanes) + small.shape[1:], jnp.float32),
            jax.ShapeDtypeStruct((depth, lanes, 8, 128), jnp.float32),
            jax.ShapeDtypeStruct((most, lanes, rows, D), jnp.bfloat16),
            jax.ShapeDtypeStruct((len(origins), rows, D), jnp.bfloat16),
        ]
        scratch += [
            pltpu.VMEM((lanes, most, rows, D), jnp.bfloat16),
            pltpu.VMEM((8, 128), jnp.float32),
            pltpu.SemaphoreType.DMA,
            pltpu.SemaphoreType.DMA((2, 10)),
            pltpu.SemaphoreType.DMA((2, 10)),
            pltpu.SemaphoreType.DMA((7,)),
            pltpu.SemaphoreType.DMA((7,)),
        ]
        sources.append(earlier)
    return pl.pallas_call(
        functools.partial(reduce_kernel, chunks, count, len(sets), meeting),
        out_shape=out_shape,
        in_specs=whole("a" * count + "v" * (len(sources) - count)),
        out_specs=whole("v" * len(out_shape)),
        scratch_shapes=scratch,
        compiler_params=pltpu.CompilerParams(
            collective_id=collective, has_side_effects=True, vmem_limit_bytes=VMEM_LIMIT
        ),
        name=f"reduce_{collective}",
    )(*sources)


def spread_stages(own, out, local_sem, send, recv):
    d, z, _ = places()
    sib, near_x, near_y = flip(d, 1), flip(d, 2), flip(d, 4)
    diagonal = flip(near_x, 4)
    half = own.shape[0] // 2
    parts = (pl.ds(0, half), pl.ds(half, own.shape[0] - half))
    started = []
    last = []

    def push(slot, origin, part, to, source=None):
        copy = pltpu.make_async_remote_copy(
            src_ref=out.at[part, origin] if source is None else source,
            dst_ref=out.at[part, origin],
            send_sem=send.at[slot],
            recv_sem=recv.at[slot],
            device_id=to,
            device_id_type=MESH,
        )
        copy.start()
        started.append(copy)
        return copy

    keep = pltpu.make_async_copy(own, out.at[:, d], local_sem)
    near = {}
    turned = []

    def begin():
        for way, part in ((0, 0), (1, 1), (0, 1), (1, 0)):
            near[way, part] = push(
                2 * way + part, d, parts[part], ((near_x, near_y)[way], z), own.at[parts[part]]
            )
        keep.start()
        last.extend([push(4 + i, d, parts[i], (sib, z), own.at[parts[i]]) for i in (0, 1)])

    def forward():
        near[0, 0].wait_recv()
        turned.append(push(6, near_x, parts[0], (near_y, z)))
        last.append(push(7, near_x, parts[0], (sib, z)))
        near[1, 1].wait_recv()
        turned.append(push(8, near_y, parts[1], (near_x, z)))
        last.append(push(9, near_y, parts[1], (sib, z)))

    def collect():
        near[1, 0].wait_recv()
        last.append(push(10, near_y, parts[0], (sib, z)))
        near[0, 1].wait_recv()
        last.append(push(11, near_x, parts[1], (sib, z)))
        for i in (0, 1):
            turned[i].wait_recv()
            last.append(push(12 + i, diagonal, parts[i], (sib, z)))

    def finish():
        for copy in last:
            copy.wait_recv()
        for copy in started:
            copy.wait_send()
        keep.wait()

    return (begin, forward, collect, finish)


GRAM_TILE = 128


def gram_kernel(
    gram,
    rows,
    own,
    total,
    all_rows,
    shards,
    left,
    right,
    onward,
    back,
    sems,
    local_sem,
    send,
    recv,
    row_sems,
):
    d, z, _ = places()
    up, down = (z + 1, z - 1)
    two = jnp.logical_and(lax.rem(d, 2) == 1, d // 4 == 1)
    one = jnp.logical_not(two)
    sib, near_x, near_y = flip(d, 1), flip(d, 2), flip(d, 4)
    greet([(d, lax.rem(z + step, 4)) for step in (1, 2, 3)] + [(sib, z), (near_x, z), (near_y, z)])
    stages = spread_stages(own, shards, local_sem, send, recv)
    count = D // GRAM_TILE

    def at(ref, j):
        return ref.at[pl.ds(j * GRAM_TILE, GRAM_TILE), pl.ds(j * GRAM_TILE, D - j * GRAM_TILE)]

    def copy(source, target, j, way, to):
        return pltpu.make_async_remote_copy(
            src_ref=at(source, j),
            dst_ref=at(target, j),
            send_sem=sems.at[2 * way, j],
            recv_sem=sems.at[2 * way + 1, j],
            device_id=(d, to),
            device_id_type=MESH,
        )

    def add(target, j, *terms):
        @pl.loop(0, GRAM_TILE // 16)
        def _(i):
            part = pl.ds(pl.multiple_of(j * GRAM_TILE + i * 16, 16), 16)
            columns = pl.ds(j * GRAM_TILE, D - j * GRAM_TILE)
            value = terms[0][part, columns]
            for term in terms[1:]:
                value = value + term[part, columns]
            target[part, columns] = value

    def ends():
        @pl.when(z == 0)
        def _():
            for j in range(count):
                copy(gram, left, j, 0, up).start()

        @pl.when(z == 3)
        def _():
            for j in range(count):
                copy(gram, right, j, 1, down).start()

    def near(j):
        @pl.when(z == 1)
        def _():
            copy(onward, left, j, 0, up).wait_recv()
            add(onward, j, gram, left)
            copy(onward, left, j, 0, up).start()

        @pl.when(z == 2)
        def _():
            copy(back, right, j, 1, down).wait_recv()
            add(back, j, gram, right)
            copy(back, right, j, 1, down).start()

    def far(j):
        @pl.when(z == 1)
        def _():
            copy(back, right, j, 1, down).wait_recv()
            add(back, j, gram, right)
            copy(back, right, j, 1, down).start()
            add(total, j, onward, right)

        @pl.when(z == 2)
        def _():
            copy(onward, left, j, 0, up).wait_recv()
            add(onward, j, gram, left)
            copy(onward, left, j, 0, up).start()
            add(total, j, onward, right)

        @pl.when(z == 3)
        def _():
            copy(gram, left, j, 0, up).wait_recv()
            add(total, j, left, gram)

        @pl.when(z == 0)
        def _():
            copy(gram, right, j, 1, down).wait_recv()
            add(total, j, gram, right)

        lines = slice(j * GRAM_TILE, (j + 1) * GRAM_TILE)
        for k in range(j + 1, count):
            columns = slice(k * GRAM_TILE, (k + 1) * GRAM_TILE)
            total[columns, lines] = total[lines, columns].T

    def finish():
        for j in range(count):

            @pl.when(z == 0)
            def _():
                copy(gram, left, j, 0, up).wait_send()

            @pl.when(z == 3)
            def _():
                copy(gram, right, j, 1, down).wait_send()

            @pl.when(jnp.logical_and(z > 0, z < 3))
            def _():
                copy(onward, left, j, 0, up).wait_send()
                copy(back, right, j, 1, down).wait_send()

    def pass_on(origin, way, to, source=None):
        return pltpu.make_async_remote_copy(
            src_ref=all_rows.at[origin] if source is None else source,
            dst_ref=all_rows.at[origin],
            send_sem=row_sems.at[2 * way, origin],
            recv_sem=row_sems.at[2 * way + 1, origin],
            device_id=(d, to),
            device_id_type=MESH,
        )

    def line_of(here):
        started = []
        if here < 3:
            started.append(pass_on(here, 0, here + 1, rows))
            started[-1].start()
        if here > 0:
            started.append(pass_on(here, 1, here - 1, rows))
            started[-1].start()
        all_rows[here] = rows[...]
        from_left = list(range(here - 1, -1, -1))
        from_right = list(range(here + 1, 4))
        for i in range(3):
            if i < len(from_left):
                pass_on(from_left[i], 0, here).wait_recv()
                if here < 3:
                    started.append(pass_on(from_left[i], 0, here + 1))
                    started[-1].start()
            if i < len(from_right):
                pass_on(from_right[i], 1, here).wait_recv()
                if here > 0:
                    started.append(pass_on(from_right[i], 1, here - 1))
                    started[-1].start()
        return started

    pl.when(one)(ends)
    stages[0]()

    @pl.when(one)
    def _():
        near(0)
        near(1)
        near(2)
        far(0)

    @pl.when(two)
    def _():
        for here in range(4):

            @pl.when(z == here)
            def _():
                for started in line_of(here):
                    started.wait_send()

    stages[1]()

    @pl.when(one)
    def _():
        near(3)
        far(1)
        near(4)
        far(2)

    stages[2]()

    @pl.when(one)
    def _():
        near(5)
        far(3)
        far(4)
        far(5)
        finish()

    stages[3]()


def sum_grams(gram, rows, own, collective):
    lanes, depth = lax.axis_size("dp"), lax.axis_size("fsdp")
    square = pltpu.VMEM(gram.shape, jnp.float32)
    return pl.pallas_call(
        gram_kernel,
        out_shape=[
            jax.ShapeDtypeStruct(gram.shape, jnp.float32),
            jax.ShapeDtypeStruct((depth,) + rows.shape, rows.dtype),
            jax.ShapeDtypeStruct(own.shape[:1] + (lanes,) + own.shape[1:], own.dtype),
        ],
        in_specs=whole("vvv"),
        out_specs=whole("vva"),
        scratch_shapes=[
            square,
            square,
            square,
            square,
            pltpu.SemaphoreType.DMA((4, D // GRAM_TILE)),
            pltpu.SemaphoreType.DMA,
            pltpu.SemaphoreType.DMA((14,)),
            pltpu.SemaphoreType.DMA((14,)),
            pltpu.SemaphoreType.DMA((4, 4)),
        ],
        compiler_params=pltpu.CompilerParams(
            collective_id=collective, has_side_effects=True, vmem_limit_bytes=VMEM_LIMIT
        ),
        name=f"gram_{collective}",
    )(gram, rows, own)


def schulz_kernel(two, gram, all_rows, rows, out, state, state_low, change, current):
    def chains(parts):
        for slot, first, number in parts:
            if len(parts) == 1:
                value = gram[...]
            else:
                value = jnp.zeros((D, D), jnp.float32)
                for z in range(all_rows.shape[0]):
                    piece = all_rows[z, slot]
                    value = value + contract_first(piece, piece)
            line = lax.broadcasted_iota(jnp.int32, value.shape, 0)
            column = lax.broadcasted_iota(jnp.int32, value.shape, 1)
            total = jnp.sum(jnp.where(line == column, value, 0.0), axis=(0, 1), keepdims=True)
            inverse = 1.0 / (jnp.sqrt(total) + 1e-07)
            value = value * (inverse * inverse)
            state[slot] = value
            state_low[slot] = value.astype(jnp.bfloat16)
            for place in range(first, first + number):
                current[place] = rows[place] * inverse

        def turn(last):
            for slot, _, _ in parts:
                square = jnp.dot(
                    state_low[slot], state_low[slot], preferred_element_type=jnp.float32
                )
                change[slot] = (COEF_B * state[slot] + COEF_C * square).astype(jnp.bfloat16)
            for slot, first, number in parts:
                for place in range(first, first + number):
                    value = current[place]
                    current[place] = COEF_A * value + jnp.dot(
                        value.astype(jnp.bfloat16),
                        change[slot],
                        preferred_element_type=jnp.float32,
                    )
            if last:
                return
            for half in range(2):
                for slot, _, _ in parts:
                    value = COEF_A * state[slot] + jnp.dot(
                        state_low[slot], change[slot], preferred_element_type=jnp.float32
                    )
                    state[slot] = value
                    state_low[slot] = value.astype(jnp.bfloat16)

        @pl.loop(0, NS_ITERS - 1)
        def _(_):
            turn(False)

        turn(True)
        for slot, first, number in parts:
            for place in range(first, first + number):
                out[place] = current[place].astype(jnp.bfloat16)

    @pl.when(two[0] == 0)
    def _():
        chains([(0, 0, 4)])

    @pl.when(two[0] == 1)
    def _():
        chains([(0, 0, 1), (1, 1, 1)])
        for place in (2, 3):
            out[place] = jnp.zeros(out.shape[1:], jnp.bfloat16)


def schulz(two, gram, all_rows, rows):
    return pl.pallas_call(
        schulz_kernel,
        out_shape=jax.ShapeDtypeStruct(rows.shape, jnp.bfloat16),
        in_specs=[
            pl.BlockSpec(memory_space=pltpu.SMEM),
        ]
        + whole("vvv"),
        out_specs=pl.BlockSpec(memory_space=pltpu.VMEM),
        scratch_shapes=[
            pltpu.VMEM((2, D, D), jnp.float32),
            pltpu.VMEM((2, D, D), jnp.bfloat16),
            pltpu.VMEM((2, D, D), jnp.bfloat16),
            pltpu.VMEM(rows.shape, jnp.float32),
        ],
        compiler_params=pltpu.CompilerParams(vmem_limit_bytes=VMEM_LIMIT),
        name="schulz",
    )(two, gram, all_rows, rows)


def spread_kernel(own, out, local_sem, send, recv):
    d, z, _ = places()
    greet([(flip(d, 1), z), (flip(d, 2), z), (flip(d, 4), z)])
    for stage in spread_stages(own, out, local_sem, send, recv):
        stage()


def spread(own, collective):
    lanes = lax.axis_size("dp")
    return pl.pallas_call(
        spread_kernel,
        out_shape=jax.ShapeDtypeStruct(own.shape[:1] + (lanes,) + own.shape[1:], own.dtype),
        in_specs=[pl.BlockSpec(memory_space=pltpu.VMEM)],
        out_specs=pl.BlockSpec(memory_space=pl.ANY),
        scratch_shapes=[
            pltpu.SemaphoreType.DMA,
            pltpu.SemaphoreType.DMA((14,)),
            pltpu.SemaphoreType.DMA((14,)),
        ],
        compiler_params=pltpu.CompilerParams(
            collective_id=collective, has_side_effects=True, vmem_limit_bytes=VMEM_LIMIT
        ),
        name=f"spread_{collective}",
    )(own)


def update_kernel(
    table,
    scale,
    clip,
    momenta,
    grads,
    weights,
    turned_first,
    turned_second,
    momenta_new,
    weights_new,
    weights_low,
):
    pair = pl.program_id(0)
    for i, turned in enumerate((turned_first, turned_second)):
        momenta_new[i] = MOMENT * momenta[i] + clip[0] * grads[i].astype(jnp.float32)
        value = weights[i] * (1.0 - MUON_RATE * MUON_DECAY) - scale[2 * pair + i] * turned[
            0, 0
        ].astype(jnp.float32)
        weights_new[i] = value
        weights_low[i] = value.astype(jnp.bfloat16)


def update(home, scale, clip, momenta, grads, weights, turned):
    blocks, rows, width = weights.shape
    table = np.array(
        [home[block][1] for block in range(blocks)] + [home[block][0] for block in range(blocks)],
        np.int32,
    )
    pair = pl.BlockSpec((2, rows, width), lambda b, *_: (b, 0, 0))

    def turned_of(i):
        return pl.BlockSpec(
            (1, 1, rows, width),
            lambda b, table, *_: (table[2 * b + i], table[blocks + 2 * b + i], 0, 0),
        )

    return pl.pallas_call(
        update_kernel,
        grid_spec=pltpu.PrefetchScalarGridSpec(
            num_scalar_prefetch=3,
            grid=(blocks // 2,),
            in_specs=[pair, pair, pair, turned_of(0), turned_of(1)],
            out_specs=[pair, pair, pair],
        ),
        out_shape=[
            jax.ShapeDtypeStruct(weights.shape, jnp.float32),
            jax.ShapeDtypeStruct(weights.shape, jnp.float32),
            jax.ShapeDtypeStruct(weights.shape, jnp.bfloat16),
        ],
        compiler_params=pltpu.CompilerParams(vmem_limit_bytes=VMEM_LIMIT),
        name="update",
    )(
        jnp.asarray(table),
        jnp.asarray(scale),
        clip.reshape(1),
        momenta,
        grads,
        weights,
        turned,
        turned,
    )


GROUP = 6 * HD


def normed_head(value, gain):
    centred = value - jnp.mean(value, 0, keepdims=True)
    scale = lax.rsqrt(jnp.mean(centred * centred, 0, keepdims=True) + 1e-06)
    centred = centred * scale
    return (centred * gain, centred, scale)


def contract_first(left, right):
    return lax.dot_general(
        left, right, (((0,), (0,)), ((), ())), preferred_element_type=jnp.float32
    )


def contract_last(left, right):
    return lax.dot_general(
        left, right, (((1,), (1,)), ((), ())), preferred_element_type=jnp.float32
    )


def shares_of(scores, same):
    scores = jnp.where(same, scores * (1.0 / math.sqrt(HD)), -1e30)
    exponent = jnp.exp(scores - jnp.max(scores, 0, keepdims=True))
    return exponent * (1.0 / jnp.sum(exponent, 0, keepdims=True))


TILE = 768
TOKENS = 256
SLOPE = math.sqrt(2.0 / math.pi)
CUBIC = 0.044715


def tile_of(t, size=TILE):
    return pl.ds(pl.multiple_of(t * size, size), size)


def row_norm(value):
    centred = value - jnp.mean(value, -1, keepdims=True)
    scale = lax.rsqrt(jnp.mean(centred * centred, -1, keepdims=True) + 1e-06)
    return (centred * scale, scale)


def gelu_parts(value):
    square = value * value
    bend = jnp.tanh(SLOPE * value * (1.0 + CUBIC * square))
    half = 0.5 + 0.5 * bend
    slope = half + 0.5 * value * (1.0 - bend * bend) * SLOPE * (1.0 + 3.0 * CUBIC * square)
    return (value * half, slope)


def load_all(pairs, sem):
    copies = [
        pltpu.make_async_copy(source, target, sem.at[i])
        for i, (source, target) in enumerate(pairs)
    ]
    for copy in copies:
        copy.start()
    return copies


def stand_up(row):
    return jnp.broadcast_to(row, (8, row.shape[1])).T[:, :1]


def slot_marks(segment, b):
    row = segment[b : b + 1].astype(jnp.float32)
    return (stand_up(row), row)


def norm_rows(source, gains, first, target):
    gain, shift = (gains[first : first + 1], gains[first + 1 : first + 2])

    @pl.loop(0, source.shape[0] // 64)
    def _(t):
        part = tile_of(t, 64)
        target[part] = (row_norm(source[part])[0] * gain + shift).astype(target.dtype)


def forward_kernel(
    spans,
    base,
    state,
    gains,
    segment,
    mixing,
    mixing_out,
    upward,
    down,
    state_out,
    middle,
    mixed,
    heads_low,
    attended,
    normed_low,
    mixing_held,
    out_held,
    up_held,
    down_held,
    hidden,
    gain_query,
    gain_key,
    sem,
):
    mixing, mixing_out, upward, down = [
        ref.at[pl.ds(*span)] for ref, span in zip((mixing, mixing_out, upward, down), spans)
    ]
    loads = load_all(
        [(mixing, mixing_held), (mixing_out, out_held), (upward, up_held), (down, down_held)], sem
    )
    gain_query[...] = stand_up(gains[base + 4 : base + 5])
    gain_key[...] = stand_up(gains[base + 5 : base + 6])
    norm_rows(state, gains, base, heads_low)
    loads[0].wait()

    @pl.loop(0, 3 * D // TILE)
    def _(t):
        mixed[tile_of(t)] = contract_last(mixing_held[tile_of(t)], heads_low[...])

    parts, length = segment.shape
    for b in range(parts):
        column, row = slot_marks(segment, b)
        same = column == row
        tokens = slice(b * length, (b + 1) * length)

        @pl.loop(0, D // GROUP)
        def _(group):
            held = []
            for head in range(GROUP // HD):
                first = group * GROUP + head * HD
                part = pl.ds(pl.multiple_of(first, HD), HD)
                query, key, value = [
                    mixed[pl.ds(pl.multiple_of(place * D + first, HD), HD), tokens]
                    for place in range(3)
                ]
                query_low = normed_head(query, gain_query[part])[0].astype(jnp.bfloat16)
                key_low = normed_head(key, gain_key[part])[0].astype(jnp.bfloat16)
                held.append((part, query_low, key_low, value.astype(jnp.bfloat16)))
            scores = [contract_first(key_low, query_low) for _, query_low, key_low, _ in held]
            shares = [shares_of(score, same).astype(jnp.bfloat16) for score in scores]
            for (part, _, _, value_low), share in zip(held, shares):
                attended[part, tokens] = jnp.dot(
                    value_low, share, preferred_element_type=jnp.float32
                ).astype(jnp.bfloat16)

    loads[1].wait()
    for t in range(state.shape[0] // TOKENS):
        part = slice(t * TOKENS, (t + 1) * TOKENS)
        middle[part] = state[part] + contract_first(attended[:, part], out_held[...])
    norm_rows(middle, gains, base + 2, normed_low)
    loads[2].wait()

    @pl.loop(0, FF // TILE)
    def _(t):
        value = contract_last(up_held[tile_of(t)], normed_low[...])
        hidden[tile_of(t)] = gelu_parts(value)[0].astype(jnp.bfloat16)

    loads[3].wait()
    for t in range(state.shape[0] // TOKENS):
        part = slice(t * TOKENS, (t + 1) * TOKENS)
        state_out[part] = middle[part] + contract_first(hidden[:, part], down_held[...])


def layer_weights(blocks):
    weights = [array.reshape(-1, D) for array, _, _ in blocks]
    return (weights, [(first * D, number * D) for _, first, number in blocks])


def layer_forward(state, blocks, gains, base, segment):
    tokens = state.shape[0]
    weights, spans = layer_weights(blocks)
    state_out, middle, mixed, heads_low, attended, normed_low = pl.pallas_call(
        functools.partial(forward_kernel, spans, base),
        out_shape=[
            jax.ShapeDtypeStruct((tokens, D), jnp.float32),
            jax.ShapeDtypeStruct((tokens, D), jnp.float32),
            jax.ShapeDtypeStruct((3 * D, tokens), jnp.float32),
            jax.ShapeDtypeStruct((tokens, D), jnp.bfloat16),
            jax.ShapeDtypeStruct((D, tokens), jnp.bfloat16),
            jax.ShapeDtypeStruct((tokens, D), jnp.bfloat16),
        ],
        in_specs=whole("vvvaaaa"),
        out_specs=whole("vvvvvv"),
        scratch_shapes=[pltpu.VMEM((number, D), jnp.bfloat16) for _, number in spans]
        + [
            pltpu.VMEM((FF, tokens), jnp.bfloat16),
            pltpu.VMEM((D, 1), jnp.float32),
            pltpu.VMEM((D, 1), jnp.float32),
            pltpu.SemaphoreType.DMA((4,)),
        ],
        compiler_params=pltpu.CompilerParams(vmem_limit_bytes=VMEM_LIMIT),
        name="layer_forward",
    )(state, gains, segment, *weights)
    return (state_out, (state, middle, mixed, heads_low, attended, normed_low))


def backward_kernel(
    spans,
    base,
    grad,
    middle,
    normed_low,
    gains,
    segment,
    state,
    mixed,
    heads_low,
    attended,
    mixing,
    mixing_out,
    upward,
    down,
    grad_out,
    gain_out,
    grad_mixing,
    grad_mixing_out,
    grad_up,
    grad_down,
    state_held,
    mixed_held,
    heads_held,
    attended_held,
    mixing_held,
    out_held,
    up_held,
    down_held,
    low,
    inner,
    hidden_grad,
    mixed_low,
    attended_grad,
    made_up,
    made_down,
    made_mixing,
    made_out,
    gain_query,
    gain_key,
    head_gains,
    sem,
    store_sem,
):
    mixing, mixing_out, upward, down = [
        ref.at[pl.ds(*span)] for ref, span in zip((mixing, mixing_out, upward, down), spans)
    ]
    loads = load_all(
        [
            (upward, up_held),
            (down, down_held),
            (mixing_out, out_held),
            (attended, attended_held),
            (mixed, mixed_held),
            (heads_low, heads_held),
            (mixing, mixing_held),
            (state, state_held),
        ],
        sem,
    )
    stores = [
        pltpu.make_async_copy(made_up, grad_up, store_sem.at[0]),
        pltpu.make_async_copy(made_down, grad_down, store_sem.at[1]),
        pltpu.make_async_copy(made_out, grad_mixing_out, store_sem.at[2]),
        pltpu.make_async_copy(made_mixing, grad_mixing, store_sem.at[3]),
    ]
    tokens = grad.shape[0]
    gain_out[...] = jnp.zeros_like(gain_out)
    head_gains[...] = jnp.zeros_like(head_gains)
    gain_query[...] = stand_up(gains[base + 4 : base + 5])
    gain_key[...] = stand_up(gains[base + 5 : base + 6])

    @pl.loop(0, tokens // 64)
    def _(t):
        low[tile_of(t, 64)] = grad[tile_of(t, 64)].astype(jnp.bfloat16)

    loads[0].wait()
    loads[1].wait()

    @pl.loop(0, FF // TILE)
    def _(t):
        part = tile_of(t)
        value, slope = gelu_parts(contract_last(up_held[part], normed_low[...]))
        delta = (contract_last(down_held[part], low[...]) * slope).astype(jnp.bfloat16)
        hidden_grad[part] = delta
        made_down[part] = jnp.dot(
            value.astype(jnp.bfloat16), low[...], preferred_element_type=jnp.float32
        ).astype(jnp.bfloat16)
        made_up[part] = jnp.dot(
            delta, normed_low[...], preferred_element_type=jnp.float32
        ).astype(jnp.bfloat16)

    stores[0].start()
    stores[1].start()
    for t in range(tokens // TOKENS):
        part = slice(t * TOKENS, (t + 1) * TOKENS)
        inner[part] = contract_first(hidden_grad[:, part], up_held[...])

    def norm_back(source, first, previous, target, target_low):
        gain = gains[base + first : base + first + 1]

        @pl.loop(0, tokens // 64)
        def _(t):
            part = tile_of(t, 64)
            unit, scale = row_norm(source[part])
            delta = inner[part]
            gain_out[first : first + 1] += jnp.sum(delta * unit, 0, keepdims=True)
            gain_out[first + 1 : first + 2] += jnp.sum(delta, 0, keepdims=True)
            delta = delta * gain
            delta = delta - jnp.mean(delta, -1, keepdims=True) - unit * jnp.mean(
                delta * unit, -1, keepdims=True
            )
            value = previous[part] + delta * scale
            target[part] = value
            if target_low is not None:
                target_low[part] = value.astype(jnp.bfloat16)

    norm_back(middle, 2, grad, grad_out, low)
    loads[2].wait()
    loads[3].wait()

    @pl.loop(0, D // TILE)
    def _(t):
        part = tile_of(t)
        made_out[part] = jnp.dot(
            attended_held[part], low[...], preferred_element_type=jnp.float32
        ).astype(jnp.bfloat16)
        attended_grad[part] = contract_last(out_held[part], low[...]).astype(jnp.bfloat16)

    stores[2].start()
    loads[4].wait()
    parts, length = segment.shape
    for b in range(parts):
        column, row = slot_marks(segment, b)
        same = column == row
        span = slice(b * length, (b + 1) * length)

        @pl.loop(0, D // GROUP)
        def _(group):
            held = []
            for head in range(GROUP // HD):
                first = group * GROUP + head * HD
                part = pl.ds(pl.multiple_of(first, HD), HD)
                where = [pl.ds(pl.multiple_of(place * D + first, HD), HD) for place in range(3)]
                query, key, value = [mixed_held[at, span] for at in where]
                query_low = normed_head(query, gain_query[part])[0].astype(jnp.bfloat16)
                key_low = normed_head(key, gain_key[part])[0].astype(jnp.bfloat16)
                held.append((part, where, query_low, key_low, value.astype(jnp.bfloat16)))
            scores = [contract_first(key_low, query_low) for _, _, query_low, key_low, _ in held]
            share_grads = [
                contract_first(value_low, attended_grad[part, span])
                for part, _, _, _, value_low in held
            ]
            shares = [shares_of(score, same) for score in scores]
            score_lows = []
            for share, share_grad in zip(shares, share_grads):
                total = jnp.sum(share * share_grad, 0, keepdims=True)
                score_lows.append(
                    (share * (share_grad - total) * (1.0 / math.sqrt(HD))).astype(jnp.bfloat16)
                )
            for (part, where, query_low, key_low, _), share, score_low in zip(
                held, shares, score_lows
            ):
                mixed_low[where[2], span] = contract_last(
                    attended_grad[part, span], share.astype(jnp.bfloat16)
                ).astype(jnp.bfloat16)
                deltas = (
                    jnp.dot(key_low, score_low, preferred_element_type=jnp.float32),
                    contract_last(query_low, score_low),
                )
                for place, (delta, gains_here) in enumerate(zip(deltas, (gain_query, gain_key))):
                    _, unit, scale = normed_head(mixed_held[where[place], span], gains_here[part])
                    head_gains[place, part] += jnp.sum(delta * unit, 1, keepdims=True)
                    delta = delta * gains_here[part]
                    delta = delta - jnp.mean(delta, 0, keepdims=True) - unit * jnp.mean(
                        delta * unit, 0, keepdims=True
                    )
                    mixed_low[where[place], span] = (delta * scale).astype(jnp.bfloat16)

    for place in range(2):
        column = jnp.broadcast_to(head_gains[place], (D, 128))
        gain_out[4 + place : 5 + place] = column.T[:1]
    loads[5].wait()

    @pl.loop(0, 3 * D // TILE)
    def _(t):
        part = tile_of(t)
        made_mixing[part] = jnp.dot(
            mixed_low[part], heads_held[...], preferred_element_type=jnp.float32
        ).astype(jnp.bfloat16)

    stores[3].start()
    loads[6].wait()
    for t in range(tokens // TOKENS):
        part = slice(t * TOKENS, (t + 1) * TOKENS)
        inner[part] = contract_first(mixed_low[:, part], mixing_held[...])
    loads[7].wait()
    norm_back(state_held, 0, grad_out, grad_out, None)
    for copy in stores:
        copy.wait()


def layer_backward(grad, kept, blocks, gains, base, segment):
    state, middle, mixed, heads_low, attended, normed_low = kept
    tokens = grad.shape[0]
    weights, spans = layer_weights(blocks)
    low = jnp.bfloat16
    grad, gain_grads, *block_grads = pl.pallas_call(
        functools.partial(backward_kernel, spans, base),
        out_shape=[
            jax.ShapeDtypeStruct((tokens, D), jnp.float32),
            jax.ShapeDtypeStruct((8, D), jnp.float32),
        ]
        + [jax.ShapeDtypeStruct((number, D), low) for _, number in spans],
        in_specs=whole("vvvvvaaaaaaaa"),
        out_specs=whole("vvaaaa"),
        scratch_shapes=[
            pltpu.VMEM(state.shape, jnp.float32),
            pltpu.VMEM(mixed.shape, jnp.float32),
            pltpu.VMEM(heads_low.shape, low),
            pltpu.VMEM(attended.shape, low),
        ]
        + [pltpu.VMEM((number, D), low) for _, number in spans]
        + [
            pltpu.VMEM((tokens, D), low),
            pltpu.VMEM((tokens, D), jnp.float32),
            pltpu.VMEM((FF, tokens), low),
            pltpu.VMEM((3 * D, tokens), low),
            pltpu.VMEM((D, tokens), low),
            pltpu.VMEM((FF, D), low),
            pltpu.VMEM((FF, D), low),
            pltpu.VMEM((3 * D, D), low),
            pltpu.VMEM((D, D), low),
            pltpu.VMEM((D, 1), jnp.float32),
            pltpu.VMEM((D, 1), jnp.float32),
            pltpu.VMEM((2, D, 1), jnp.float32),
            pltpu.SemaphoreType.DMA((8,)),
            pltpu.SemaphoreType.DMA((4,)),
        ],
        compiler_params=pltpu.CompilerParams(vmem_limit_bytes=60 * 1024 * 1024),
        name="layer_backward",
    )(grad, middle, normed_low, gains, segment, state, mixed, heads_low, attended, *weights)
    return (grad, block_grads, gain_grads[:6])


HEAD_LANES = 128


def full_dot(left, right):
    return jnp.dot(left, right, preferred_element_type=jnp.float32, precision=HIGH)


def head_marks():
    entry = lax.broadcasted_iota(jnp.int32, (D, HEAD_LANES), 0)
    lane = lax.broadcasted_iota(jnp.int32, (D, HEAD_LANES), 1)
    return (entry // HD == lane).astype(jnp.float32)


def full_dot_last(left, right):
    return lax.dot_general(
        left,
        right,
        (((1,), (1,)), ((), ())),
        preferred_element_type=jnp.float32,
        precision=HIGH,
    )


def pool_sequence(state, gains, marks_of):
    unit, scale = row_norm(state)
    final = unit * gains[0:1] + gains[1:2]
    marks = head_marks()
    logits = full_dot(final * gains[2:3], marks) * (1.0 / math.sqrt(HD))
    rows, columns = marks_of
    slot = lax.broadcasted_iota(jnp.int32, (rows.shape[0], IMGS), 1)
    member = (rows == slot.astype(jnp.float32)).astype(jnp.float32)
    slot = lax.broadcasted_iota(jnp.int32, (IMGS, columns.shape[1]), 0)
    member_rows = (columns == slot.astype(jnp.float32)).astype(jnp.float32)
    tops = jnp.zeros_like(logits)
    for k in range(IMGS):
        here = rows == k
        top = jnp.max(jnp.where(here, logits, -1e30), 0, keepdims=True)
        tops = jnp.where(here, top, tops)
    exponent = jnp.exp(logits - tops)
    share = exponent / full_dot(member, full_dot(member_rows, exponent))
    spread_share = full_dot_last(share, marks)
    dead = (jnp.sum(member_rows, 1, keepdims=True) == 0.0).astype(jnp.float32)
    pooled = full_dot(member_rows, spread_share * final) + dead * jnp.mean(
        final, 0, keepdims=True
    )
    return (unit, scale, final, marks, member, member_rows, share, spread_share, dead, pooled)


def unit_scale(value):
    return lax.rsqrt(jnp.mean(value * value, -1, keepdims=True) + 1e-06)


def pool_kernel(base, state, gains, segment, matrix, pooled_low, embedded, image_low):
    parts, length = segment.shape
    for b in range(parts):
        pooled = pool_sequence(
            state[b * length : (b + 1) * length], gains[base : base + 3], slot_marks(segment, b)
        )[-1]
        pooled_low[b] = pooled.astype(jnp.bfloat16)
        value = jnp.dot(
            pooled.astype(jnp.bfloat16), matrix[...], preferred_element_type=jnp.float32
        )
        embedded[b] = value
        image_low[b] = (value * unit_scale(value) * (1.0 / math.sqrt(D))).astype(jnp.bfloat16)


def pool_forward(state, gains, base, segment, matrix):
    parts = segment.shape[0]
    shape = (parts, IMGS, D)
    return pl.pallas_call(
        functools.partial(pool_kernel, base),
        out_shape=[
            jax.ShapeDtypeStruct(shape, jnp.bfloat16),
            jax.ShapeDtypeStruct(shape, jnp.float32),
            jax.ShapeDtypeStruct(shape, jnp.bfloat16),
        ],
        in_specs=whole("vvvv"),
        out_specs=whole("vvv"),
        compiler_params=pltpu.CompilerParams(vmem_limit_bytes=VMEM_LIMIT),
        name="pool_forward",
    )(state, gains, segment, matrix)


def contrast_kernel(
    base,
    me,
    images,
    texts,
    alive_columns,
    alive_rows,
    own_images,
    own_live,
    state,
    all_gains,
    segment,
    matrix,
    pooled_low,
    embedded,
    loss,
    grad,
    grad_matrix,
    gain_out,
    text_side,
):
    parts, length = segment.shape
    gains = all_gains[base : base + 3]
    everyone = images.shape[1]
    count = jnp.zeros((1, 1), jnp.float32)
    for b in range(parts):
        count = count + jnp.sum(alive_columns[b], -1, keepdims=True)
    factor = 1.0 / (2.0 * count)
    first = me[0] * IMGS

    def rows_of(scores, alive, live, start):
        masked = jnp.where(alive > 0, scores, -1e30)
        top = jnp.max(masked, -1, keepdims=True)
        exponent = jnp.exp(masked - top)
        total = jnp.sum(exponent, -1, keepdims=True)
        line = lax.broadcasted_iota(jnp.int32, scores.shape, 0) + start
        column = lax.broadcasted_iota(jnp.int32, scores.shape, 1)
        target = (line == column).astype(jnp.float32)
        diagonal = jnp.sum(scores * target, -1, keepdims=True)
        term = (top + jnp.log(total) - diagonal) * live
        delta = (exponent * (1.0 / total) - target) * live
        return (term, (delta * factor * LOGIT_SCALE).astype(jnp.bfloat16))

    loss[...] = jnp.zeros_like(loss)
    grad_sum = jnp.zeros((D, D), jnp.float32)
    gain_out[...] = jnp.zeros_like(gain_out)
    for b in range(parts):
        forward = LOGIT_SCALE * contract_last(own_images[b], texts[b])
        term, forward_low = rows_of(forward, alive_columns[b], own_live[b], first)
        loss[...] += jnp.sum(term, 0, keepdims=True) * factor
        text_side[...] = jnp.zeros_like(text_side)

        @pl.loop(0, everyone // TOKENS)
        def _(t):
            part = tile_of(t, TOKENS)
            backward = LOGIT_SCALE * contract_last(texts[b, part], images[b])
            term, backward_low = rows_of(
                backward, alive_columns[b], alive_rows[b, part], t * TOKENS
            )
            line = lax.broadcasted_iota(jnp.int32, term.shape, 0) + t * TOKENS
            here = jnp.logical_and(line >= first, line < first + IMGS)
            loss[...] += jnp.sum(jnp.where(here, term, 0.0), 0, keepdims=True) * factor
            text_side[...] += contract_first(backward_low, texts[b, part])

        image_grad = jnp.dot(forward_low, texts[b], preferred_element_type=jnp.float32)
        image_grad = image_grad + text_side[pl.ds(pl.multiple_of(first, IMGS), IMGS)]
        value = embedded[b]
        scale = unit_scale(value)
        embed_low = (
            (
                image_grad * scale
                - value * (scale * scale * scale) * jnp.mean(value * image_grad, -1, keepdims=True)
            )
            * (1.0 / math.sqrt(D))
        ).astype(jnp.bfloat16)
        grad_sum = grad_sum + contract_first(pooled_low[b], embed_low)
        pooled_grad = contract_last(embed_low, matrix[...])
        unit, norm_scale, final, marks, member, member_rows, share, spread_share, dead, _ = (
            pool_sequence(
                state[b * length : (b + 1) * length], gains, slot_marks(segment, b)
            )
        )
        token_grad = full_dot(member, pooled_grad)
        share_grad = full_dot(final * token_grad, marks)
        inside = full_dot(member, full_dot(member_rows, share * share_grad))
        logit_grad = share * (share_grad - inside) * (1.0 / math.sqrt(HD))
        spread_logit = full_dot_last(logit_grad, marks)
        final_grad = (
            spread_share * token_grad
            + spread_logit * gains[2:3]
            + jnp.sum(dead * pooled_grad, 0, keepdims=True) * (1.0 / length)
        )
        gain_out[0:1] += jnp.sum(final_grad * unit, 0, keepdims=True)
        gain_out[1:2] += jnp.sum(final_grad, 0, keepdims=True)
        gain_out[2:3] += jnp.sum(spread_logit * final, 0, keepdims=True)
        delta = final_grad * gains[0:1]
        delta = delta - jnp.mean(delta, -1, keepdims=True) - unit * jnp.mean(
            delta * unit, -1, keepdims=True
        )
        grad[b * length : (b + 1) * length] = delta * norm_scale
    grad_matrix[...] = grad_sum.astype(jnp.bfloat16)


def contrast(me, images, texts, alive, own_images, live, state, gains, base, segment, matrix, pooled_low, embedded):
    parts, everyone = alive.shape
    loss, grad, grad_matrix, gain_grads = pl.pallas_call(
        functools.partial(contrast_kernel, base),
        out_shape=[
            jax.ShapeDtypeStruct((8, 128), jnp.float32),
            jax.ShapeDtypeStruct(state.shape, jnp.float32),
            jax.ShapeDtypeStruct((D, D), jnp.bfloat16),
            jax.ShapeDtypeStruct((8, D), jnp.float32),
        ],
        in_specs=[pl.BlockSpec(memory_space=pltpu.SMEM)] + whole("vvvvvvvvvvvv"),
        out_specs=whole("vvvv"),
        scratch_shapes=[pltpu.VMEM((everyone, D), jnp.float32)],
        compiler_params=pltpu.CompilerParams(vmem_limit_bytes=VMEM_LIMIT),
        name="contrast",
    )(
        me.reshape(1),
        images,
        texts,
        alive[:, None, :],
        alive[:, :, None],
        own_images,
        live[:, :, None],
        state,
        gains,
        segment,
        matrix,
        pooled_low,
        embedded,
    )
    return (loss[0, 0], grad, grad_matrix, gain_grads[:3])


def muon_groups():
    found = [(0, 1), (1, 1)]
    for index in range(LAYERS):
        base = 2 + 12 * index
        found = found + [(base, 3), (base + 3, 1), (base + 4, 4), (base + 8, 4)]
    return found


def lane_plan(lanes):
    plan = [[] for _ in range(lanes)]
    for start, number in sorted(muon_groups(), key=lambda group: -group[1]):
        lane = min(range(lanes), key=lambda i: (sum(n for _, n in plan[i]), len(plan[i]), i))
        plan[lane].append((start, number))
    plan.sort(key=lambda entry: (-entry[0][1] if entry else 0))
    if lanes == 8:
        plan = [plan[i] for i in (0, 1, 2, 3, 4, 6, 5, 7)]
    depth = max(len(entry) for entry in plan)
    widths = [
        max([entry[slot][1] for entry in plan if slot < len(entry)]) for slot in range(depth)
    ]
    return (plan, widths)


def lane_blocks(plan):
    rows = [[start + i for start, number in entry for i in range(number)] for entry in plan]
    most = max(len(row) for row in rows)
    return np.array([row + [-1] * (most - len(row)) for row in rows], np.int32)


def lane_tables(plan, widths):
    index = np.zeros((len(plan), sum(widths)), np.int32)
    mask = np.zeros((len(plan), sum(widths)), np.float32)
    number = np.ones((len(plan), sum(widths)), np.float32)
    home = {}
    for lane, entry in enumerate(plan):
        first = 0
        for slot, width in enumerate(widths):
            if slot < len(entry):
                start, count = entry[slot]
                for place in range(count):
                    index[lane, first + place] = start + place
                    mask[lane, first + place] = 1.0
                    number[lane, first + place] = count
                    home[start + place] = (lane, first + place)
            first += width
    return (index, mask, number, home)


def orthogonal_factor(gram):
    size = jnp.sqrt(jnp.trace(gram)) + 1e-07
    state = gram / (size * size)
    total = None
    for turn in range(NS_ITERS):
        low = rounded(state)
        change = COEF_B * state + COEF_C * jnp.dot(low, low, preferred_element_type=jnp.float32)
        change_low = rounded(change)
        if total is None:
            total = COEF_A * jnp.eye(D, dtype=jnp.float32) + change
        else:
            total = COEF_A * total + jnp.dot(
                rounded(total), change_low, preferred_element_type=jnp.float32
            )
        if turn < NS_ITERS - 1:
            for _ in range(2):
                state = COEF_A * state + jnp.dot(
                    rounded(state), change_low, preferred_element_type=jnp.float32
                )
    return total / size


def per_device(
    patches, grid, segments, text_ids, table, weights, momenta, gains, gains_m, gains_v, step
):
    fin = 6 * LAYERS
    base = fin + 3
    lanes = lax.axis_size("dp")
    slots = jnp.arange(IMGS, dtype=jnp.int32)
    live = jnp.any(segments[:, 0, None, :] == slots[None, :, None], -1).astype(jnp.float32)
    depth = lax.axis_size("fsdp")
    captions = MB * IMGS
    tokens = text_ids.shape[3]
    fast = depth == 4 and lanes == 8
    early = [(0, 1), (2, 3), (5, 1), (6, 4), (10, 4), (1, 1)]
    later = []
    for index in range(1, LAYERS):
        start = 2 + 12 * index
        early = early + [(start, 3), (start + 3, 1)]
        later = later + [(start + 4, 4), (start + 8, 4)]
    later_own = jnp.concatenate([weights[a : a + n] for a, n in later], 0)
    if fast:
        eighth = weights.shape[1] // lanes
        later_own = lax.dynamic_slice_in_dim(later_own, lax.axis_index("dp") * eighth, eighth, 1)
    later_blocks = gather_later(rounded(later_own))
    if fast:
        half = tokens // 2
        own_ids = jnp.transpose(text_ids.reshape(captions, 2, half), (2, 1, 0)).reshape(half, -1)
        place = jnp.arange(depth * 2 * captions, dtype=jnp.int32) // (2 * captions)
        own_ids = jnp.where(
            place[None] == lax.axis_index("fsdp"), jnp.tile(own_ids, (1, depth)), 0
        )
        (stem, *first_blocks), texts = fetch(
            weights, early, own_ids, table, captions, tokens, 1
        )
    else:
        stem, *first_blocks = [
            lax.all_gather(rounded(weights[a : a + n]), "fsdp", axis=1, tiled=True)
            for a, n in early
        ]
        ids = lax.all_gather(text_ids.reshape(captions, tokens), "fsdp", axis=0)
        picked = ids.reshape(depth * captions, -1) - lax.axis_index("fsdp") * table.shape[0]
        row = jnp.arange(table.shape[0], dtype=jnp.int32)
        hits = jnp.sum((picked[:, :, None] == row[None, None, :]).astype(jnp.int32), 1)
        text_sum = lax.psum_scatter(
            jnp.dot(
                rounded(hits.astype(jnp.float32)), table, preferred_element_type=jnp.float32
            ).reshape(depth, captions, D),
            "fsdp",
            scatter_dimension=0,
        )
        (texts,) = share([rounded(unit_rows(text_sum / tokens))], 7)
    early_blocks = first_blocks[5:]
    pooling_matrix = first_blocks[4][0]
    first_blocks = first_blocks[:4]
    me = lax.axis_index(("dp", "fsdp"))
    segment = segments[:, 0]
    rows_hot, cols_hot = jax.vmap(positions)(grid[:, 0])
    rows_hot = rows_hot.reshape(-1, POS)
    cols_hot = cols_hot.reshape(-1, POS)
    patch_low = patches.reshape(-1, D)
    state = product(patch_low, stem[0], "sd,rd->sr")
    state = state + jnp.dot(rows_hot, gains[base : base + POS], precision=HIGH)
    state = state + jnp.dot(cols_hot, gains[base + POS : base + 2 * POS], precision=HIGH)
    saved = []
    for index in range(LAYERS):
        if index == 0:
            blocks = [(array, 0, array.shape[0]) for array in first_blocks]
        else:
            first = 8 * index - 8
            blocks = [
                (array, 0, array.shape[0]) for array in early_blocks[2 * index - 2 : 2 * index]
            ] + [(later_blocks, first, 4), (later_blocks, first + 4, 4)]
        state, kept = layer_forward(state, blocks, gains, 6 * index, segment)
        saved.append((kept, blocks))
    pooled_low, embedded, image_low = pool_forward(state, gains, fin, segment, pooling_matrix)
    own_flags = jnp.broadcast_to(live.reshape(captions, 1), (captions, 128)).astype(jnp.bfloat16)
    images, flags = share([image_low.reshape(captions, D), own_flags], 8)
    flags = flags.reshape(-1, MB, IMGS, 128)[..., 0].astype(jnp.float32)
    images, texts = [
        jnp.moveaxis(value.reshape(-1, MB, IMGS, D), 0, 1).reshape(MB, -1, D)
        for value in (images, texts)
    ]
    loss_part, grad, grad_pool, pool_gain_grads = contrast(
        me,
        images,
        texts,
        jnp.moveaxis(flags, 0, 1).reshape(MB, -1),
        image_low,
        live,
        state,
        gains,
        fin,
        segment,
        pooling_matrix,
        pooled_low,
        embedded,
    )
    gain_parts = [None] * LAYERS
    block_grads = [None] * LAYERS
    slices = [None] * LAYERS
    for index in reversed(range(LAYERS)):
        kept, blocks = saved[index]
        grad, block_grads[index], gain_parts[index] = layer_backward(
            grad, kept, blocks, gains, 6 * index, segment
        )
        if index == 1:
            block_grads[index].append(grad_pool)
        if fast and index > 0:
            (slices[index],) = reduce_grads(block_grads[index], 4 + index)
    grad_low = rounded(grad)
    grad_patch = rounded(product(grad_low, patch_low, "sr,sd->rd"))
    block_grads[0].append(grad_patch)
    grad_rows = jnp.dot(rows_hot.T, grad, precision=HIGH)
    grad_cols = jnp.dot(cols_hot.T, grad, precision=HIGH)
    gains_grad = jnp.concatenate(
        gain_parts
        + [pool_gain_grads, grad_rows, grad_cols],
        0,
    )
    plan, widths = lane_plan(lanes)
    index, mask, number, home = lane_tables(plan, widths)
    lane = lax.axis_index("dp")
    scale = np.ones((weights.shape[0],), np.float32)
    for start, count_blocks in muon_groups():
        scale[start : start + count_blocks] = MUON_RATE * math.sqrt(count_blocks)
    if fast:
        width = 256
        small = jnp.concatenate([gains_grad.reshape(-1), loss_part[None]])
        small = jnp.pad(small, (0, lanes * depth * 8 * width - small.shape[0]))
        blocks_here = lane_blocks(plan)
        origins = [(0, 12), (1, 12)] + [
            (index, block) for index in range(LAYERS) for block in range(12)
        ]
        slices[0], _, small, stats, mine, slices = reduce_grads(
            block_grads[0],
            4,
            small.reshape(lanes * depth, 8, width),
            (blocks_here, origins),
            slices[1],
        )
        flat = small.reshape(-1)
        gains_grad, loss = (flat[: gains.size].reshape(gains.shape), flat[gains.size])
        squares = jnp.sum(stats[:, :, 0, 0])
        norm = jnp.sqrt(squares + jnp.sum(gains_grad * gains_grad))
        clip = jnp.minimum(1.0, CLIP_LIMIT / (norm + 1e-06))
        own_momenta = jnp.stack(
            [
                jnp.where(
                    jnp.asarray(blocks_here >= 0)[lane, place],
                    lax.dynamic_index_in_dim(
                        momenta, jnp.maximum(jnp.asarray(blocks_here)[lane, place], 0), 0, False
                    ),
                    0.0,
                )
                for place in range(blocks_here.shape[1])
            ]
        )
        own = MOMENT * own_momenta + clip * mine.reshape(own_momenta.shape).astype(jnp.float32)
        two = jnp.asarray(np.array([len(entry) > 1 for entry in plan], np.int32))[lane]
        own_low = rounded(own)
        gram = product(own_low, own_low, "brd,bre->de")
        gram, all_rows, shard_grads = sum_grams(gram, own_low[:2], slices, 12)
        turned = spread(schulz(two.reshape(1), gram, all_rows, own), 13)
        homes = {
            int(block): (lane_of, place)
            for lane_of, entry in enumerate(blocks_here)
            for place, block in enumerate(entry)
            if block >= 0
        }
        momenta_new, weights_new, weights_low = update(
            homes, scale, clip, momenta, shard_grads.reshape(weights.shape), weights, turned
        )
    else:
        stack = jnp.concatenate(
            [block_grads[index].pop().reshape(1, D, D) for index in range(LAYERS)]
            + [value.reshape(-1, D, D) for values in block_grads for value in values],
            0,
        )
        shard_grads = lax.psum(
            lax.psum_scatter(stack, "fsdp", scatter_dimension=1, tiled=True), "dp"
        ).astype(jnp.float32)
        gains_grad, loss = lax.psum((gains_grad, loss_part), ("dp", "fsdp"))
        squares = lax.psum(jnp.sum(shard_grads * shard_grads), "fsdp")
        norm = jnp.sqrt(squares + jnp.sum(gains_grad * gains_grad))
        clip = jnp.minimum(1.0, CLIP_LIMIT / (norm + 1e-06))
        momenta_new = MOMENT * momenta + clip * shard_grads
        own = jnp.stack(
            [
                lax.dynamic_index_in_dim(momenta_new, jnp.asarray(index)[lane, place], 0, False)
                * jnp.asarray(mask)[lane, place]
                for place in range(index.shape[1])
            ]
        )
        own_low = rounded(own)
        bounds = np.cumsum([0] + widths)
        grams = jnp.stack(
            [
                product(own_low[a:b], own_low[a:b], "brd,bre->de")
                for a, b in zip(bounds[:-1], bounds[1:])
            ]
        )
        grams = lax.psum(grams, "fsdp")
        turned = jnp.concatenate(
            [
                product(
                    own_low[bounds[slot] : bounds[slot + 1]],
                    rounded(orthogonal_factor(grams[slot])),
                    "brd,de->bre",
                )
                for slot in range(len(widths))
            ],
            0,
        )
        spread_rows = lax.all_gather(rounded(turned), "dp", axis=0)
        current = jnp.stack(
            [spread_rows[home[block][0], home[block][1]] for block in range(weights.shape[0])]
        ).astype(jnp.float32)
        weights_new = weights * (1.0 - MUON_RATE * MUON_DECAY) - jnp.asarray(scale)[:, None, None] * current
        weights_low = rounded(weights_new)
    grad_small = clip * gains_grad
    moment_one = BETA_ONE * gains_m + (1.0 - BETA_ONE) * grad_small
    moment_two = BETA_TWO * gains_v + (1.0 - BETA_TWO) * grad_small * grad_small
    count_steps = step[0].astype(jnp.float32)
    corrected_one = moment_one / (1.0 - jnp.power(BETA_ONE, count_steps))
    corrected_two = moment_two / (1.0 - jnp.power(BETA_TWO, count_steps))
    gains_new = gains - ADAM_RATE * (
        corrected_one / (jnp.sqrt(corrected_two) + ADAM_EPS) + ADAM_DECAY * gains
    )
    shift_grad = grad_small[fin + 1]
    return (
        loss,
        norm,
        weights_new,
        weights_low,
        momenta_new,
        gains_new,
        moment_one,
        moment_two,
        shift_grad,
    )


def solution(mesh):
    placed = (
        P(None, ("dp", "fsdp"), None, None),
        P(None, ("dp", "fsdp"), None, None),
        P(None, ("dp", "fsdp"), None),
        P(None, ("dp", "fsdp"), None, None),
        P("fsdp", None),
        P(None, "fsdp", None),
        P(None, "fsdp", None),
        P(),
        P(),
        P(),
        P(),
    )
    return jax.shard_map(
        per_device,
        mesh=mesh,
        in_specs=placed,
        out_specs=(
            P(),
            P(),
            P(None, "fsdp", None),
            P(None, "fsdp", None),
            P(None, "fsdp", None),
            P(),
            P(),
            P(),
            P(),
        ),
        check_vma=False,
    )
```

```python
import functools
import math

import jax
import jax.numpy as jnp
import numpy as np
from jax import lax
from jax.experimental import pallas as pl
from jax.experimental.pallas import tpu as pltpu
from jax.sharding import PartitionSpec as P

D = 768
HEADS = 12
FF = 3072
LAYERS = 2
IMGS = 8
POS = 32
MB = 2
NS_ITERS = 5
HD = 64


MESH = pl.DeviceIdType.MESH
VMEM_LIMIT = 56 * 1024 * 1024
HIGH = lax.Precision.HIGHEST
LOGIT_SCALE = 50.0
CLIP_LIMIT = 0.005
MOMENT = 0.95
MUON_RATE = 0.5
MUON_DECAY = 0.01
ADAM_RATE = 0.4
BETA_ONE = 0.9
BETA_TWO = 0.999
ADAM_EPS = 1e-08
ADAM_DECAY = 0.01
COEF_A = 3.4445
COEF_B = -4.775
COEF_C = 2.0315


def rounded(value):
    return value.astype(jnp.bfloat16)


def product(left, right, form):
    return jnp.einsum(form, left, right, preferred_element_type=jnp.float32)


def unit_rows(value):
    return (
        value
        * lax.rsqrt(jnp.mean(value * value, -1, keepdims=True) + 1e-06)
        * (1.0 / math.sqrt(value.shape[-1]))
    )


def positions(grid):
    slots = jnp.arange(POS, dtype=jnp.int32)
    row_index = grid[0] * POS // grid[2]
    col_index = grid[1] * POS // grid[3]
    return (
        (row_index[:, None] == slots[None]).astype(jnp.float32),
        (col_index[:, None] == slots[None]).astype(jnp.float32),
    )


def whole(kinds):
    memory = {"v": pltpu.VMEM, "a": pl.ANY}
    return [pl.BlockSpec(memory_space=memory[kind]) for kind in kinds]


def flip(index, bit):
    return index + bit - 2 * bit * lax.rem(index // bit, 2)


def greet(peers):
    barrier = pltpu.get_barrier_semaphore()
    for peer in peers:
        pl.semaphore_signal(barrier, inc=1, device_id=peer, device_id_type=MESH)
    pl.semaphore_wait(barrier, len(peers))


def places():
    d = lax.axis_index("dp")
    z = lax.axis_index("fsdp")
    return (d, z, [lax.rem(z + step, 4) for step in range(4)])


CAPTION_TILE = 400


def fetch_kernel(chunks, sizes, tokens, weights, ids, table, *refs):
    outs = refs[: len(sizes)]
    texts = refs[len(sizes)]
    (
        full,
        low,
        all_ids,
        pages,
        found,
        found_parts,
        from_z,
        load_sem,
        store_sem,
        send,
        recv,
        page_sem,
        id_send,
        id_recv,
        part_send,
        part_recv,
        own_text,
        text_send,
        text_recv,
    ) = refs[len(sizes) + 1 :]
    d, z, zs = places()
    sib, near_x, near_y = flip(d, 1), flip(d, 2), flip(d, 4)
    diagonal = flip(near_x, 4)
    starts = [sum(chunk[3] for chunk in chunks[:k]) for k in range(len(chunks))]
    loads = []
    for k, (source, _, _, n) in enumerate(chunks):
        loads.append(
            pltpu.make_async_copy(
                weights.at[pl.ds(source, n)], full.at[pl.ds(starts[k], n)], load_sem.at[k]
            )
        )
        loads[k].start()
    page_count = table.shape[0] // CAPTION_TILE

    def page(t):
        return pltpu.make_async_copy(
            table.at[tile_of(t, CAPTION_TILE)], pages.at[lax.rem(t, 2)], page_sem.at[lax.rem(t, 2)]
        )

    page(0).start()
    greet(
        [(d, zs[1]), (d, zs[2]), (d, zs[3]), (sib, z), (near_x, z), (near_y, z), (diagonal, z)]
    )
    pending = []
    all_ids[z] = ids[...]
    id_copies = []
    for o in (1, 2, 3):
        id_copies.append(
            pltpu.make_async_remote_copy(
                src_ref=ids,
                dst_ref=all_ids.at[z],
                send_sem=id_send.at[o - 1],
                recv_sem=id_recv.at[o - 1],
                device_id=(d, zs[o]),
                device_id_type=MESH,
            )
        )
        id_copies[-1].start()

    def push(k, slot, first, n, zz, dd, to, source=None):
        out = outs[chunks[k][1]]
        rows = pl.ds(chunks[k][2] + first, n)
        copy = pltpu.make_async_remote_copy(
            src_ref=out.at[rows, zz, dd] if source is None else source,
            dst_ref=out.at[rows, zz, dd],
            send_sem=send.at[k, slot],
            recv_sem=recv.at[k, slot],
            device_id=to,
            device_id_type=MESH,
        )
        copy.start()
        pending.append(copy)
        return copy

    along_z = []
    stores = []
    for k, (_, out, offset, n) in enumerate(chunks):
        loads[k].wait()

        @pl.loop(starts[k], starts[k] + n)
        def _(i):
            low[i] = full[i].astype(low.dtype)

        along_z.append(
            [
                push(k, o - 1, 0, n, z, d, (d, zs[o]), low.at[pl.ds(starts[k], n), d])
                for o in (1, 2, 3)
            ]
        )
        stores.append(
            pltpu.make_async_copy(
                low.at[pl.ds(starts[k], n)],
                outs[out].at[pl.ds(offset, n), z],
                store_sem.at[k],
            )
        )
        stores[k].start()
    for copy in id_copies:
        copy.wait_recv()
    marks = all_ids[0] + all_ids[1] + all_ids[2] + all_ids[3]
    found[...] = jnp.zeros_like(found)

    def look_up(t):
        @pl.when(t + 1 < page_count)
        def _():
            page(t + 1).start()

        page(t).wait()
        row = lax.broadcasted_iota(jnp.int32, (CAPTION_TILE, marks.shape[1]), 0)
        row = row + (z * table.shape[0] + t * CAPTION_TILE)
        hits = jnp.zeros(row.shape, jnp.float32)
        for token in range(marks.shape[0]):
            hits = hits + jnp.where(row == marks[token : token + 1], 1.0, 0.0)
        found[...] += contract_first(hits.astype(jnp.bfloat16), pages[lax.rem(t, 2)])

    def look_up_span(first, last):
        @pl.loop(first, last)
        def _(t):
            look_up(t)

    share_of = -(-page_count // (len(chunks) - 4))
    part_copies = []
    text_copies = []

    def push_text(slot, source, target, to):
        text_copies.append(
            pltpu.make_async_remote_copy(
                src_ref=source,
                dst_ref=target,
                send_sem=text_send.at[slot],
                recv_sem=text_recv.at[slot],
                device_id=to,
                device_id_type=MESH,
            )
        )
        text_copies[-1].start()

    def text_along_z():
        for copy in part_copies:
            copy.wait_recv()
        value = (found_parts[z] + from_z[0] + from_z[1] + from_z[2]) * (1.0 / tokens)
        value = unit_rows(value).astype(own_text.dtype)
        own_text[...] = value
        texts[d, z] = value
        for o in (1, 2, 3):
            push_text(o - 1, own_text, texts.at[d, z], (d, zs[o]))

    def text_across_plane():
        for copy in text_copies[:3]:
            copy.wait_recv()
        for i, to in enumerate((near_x, near_y, diagonal, sib)):
            push_text(3 + i, texts.at[d], texts.at[d], (to, z))

    def text_to_core():
        for i, origin in enumerate((near_x, near_y, diagonal)):
            text_copies[3 + i].wait_recv()
            push_text(7 + i, texts.at[origin], texts.at[origin], (sib, z))

    def send_parts():
        captions = found_parts.shape[1]
        for owner in range(4):
            found_parts[owner] = (
                found[2 * owner * captions : (2 * owner + 1) * captions]
                + found[(2 * owner + 1) * captions : (2 * owner + 2) * captions]
            )
        for o in (1, 2, 3):
            part_copies.append(
                pltpu.make_async_remote_copy(
                    src_ref=found_parts.at[zs[o]],
                    dst_ref=from_z.at[o - 1],
                    send_sem=part_send.at[o - 1],
                    recv_sem=part_recv.at[o - 1],
                    device_id=(d, zs[o]),
                    device_id_type=MESH,
                )
            )
            part_copies[-1].start()

    along_x, along_y, turn_y, turn_x, last = {}, {}, {}, {}, []
    count = len(chunks)
    for step in range(count + 2):
        if step < count:
            k, n = step, chunks[step][3]
            along_x[k], along_y[k] = [], []
            for o in (1, 2, 3):
                zz = zs[4 - o]
                along_z[k][o - 1].wait_recv()
                along_x[k].append(push(k, 2 + o, 0, n, zz, d, (near_x, z)))
                along_y[k].append(push(k, 5 + o, 0, n, zz, d, (near_y, z)))
                last.append(push(k, 14 + o, 0, n, zz, d, (sib, z)))
        if 1 <= step <= count:
            k, n = step - 1, chunks[step - 1][3]
            half = n // 2
            turn_y[k], turn_x[k] = [], []
            for o in (1, 2, 3):
                zz = zs[4 - o]
                along_x[k][o - 1].wait_recv()
                if half:
                    turn_y[k].append(push(k, 8 + o, 0, half, zz, near_x, (near_y, z)))
                last.append(push(k, 17 + o, 0, n, zz, near_x, (sib, z)))
                along_y[k][o - 1].wait_recv()
                turn_x[k].append(push(k, 11 + o, half, n - half, zz, near_y, (near_x, z)))
                last.append(push(k, 20 + o, 0, n, zz, near_y, (sib, z)))
        if step * share_of < page_count:
            look_up_span(step * share_of, min((step + 1) * share_of, page_count))
        for at, action in (
            (count - 4, send_parts),
            (count - 2, text_along_z),
            (count - 1, text_across_plane),
            (count + 1, text_to_core),
        ):
            if step == at:
                action()
        if step >= 2:
            k, n = step - 2, chunks[step - 2][3]
            for o in (1, 2, 3):
                for copies in (turn_y[k], turn_x[k]):
                    if copies:
                        copies[o - 1].wait_recv()
                last.append(push(k, 23 + o, 0, n, zs[4 - o], diagonal, (sib, z)))
    for copy in last:
        copy.wait_recv()
    for copy in pending:
        copy.wait_send()
    for copy in stores:
        copy.wait()
    for copy in id_copies:
        copy.wait_send()
    for copy in part_copies:
        copy.wait_send()
    for copy in text_copies[6:]:
        copy.wait_recv()
    for copy in text_copies:
        copy.wait_send()


def fetch(weights, pieces, ids, table, captions, tokens, collective):
    depth, eighths = lax.axis_size("fsdp"), lax.axis_size("dp")
    blocks, rows, width = weights.shape
    part = (eighths, rows // eighths, width)
    chunks = []
    for out, (a, n) in enumerate(pieces):
        for first in range(0, n, 2):
            chunks.append((a + first, out, first, min(2, n - first)))
    total = sum(n for _, n in pieces)
    outs = pl.pallas_call(
        functools.partial(fetch_kernel, chunks, [n for _, n in pieces], tokens),
        out_shape=[
            jax.ShapeDtypeStruct((n, depth) + part, jnp.bfloat16) for _, n in pieces
        ]
        + [jax.ShapeDtypeStruct((eighths, depth, captions, width), jnp.bfloat16)],
        in_specs=whole("ava"),
        out_specs=whole("a" * len(pieces) + "v"),
        scratch_shapes=[
            pltpu.VMEM((total,) + part, jnp.float32),
            pltpu.VMEM((total,) + part, jnp.bfloat16),
            pltpu.VMEM((depth,) + ids.shape, jnp.int32),
            pltpu.VMEM((2, CAPTION_TILE, width), jnp.bfloat16),
            pltpu.VMEM((2 * depth * captions, width), jnp.float32),
            pltpu.VMEM((depth, captions, width), jnp.float32),
            pltpu.VMEM((3, captions, width), jnp.float32),
            pltpu.SemaphoreType.DMA((len(chunks),)),
            pltpu.SemaphoreType.DMA((len(chunks),)),
            pltpu.SemaphoreType.DMA((len(chunks), 27)),
            pltpu.SemaphoreType.DMA((len(chunks), 27)),
            pltpu.SemaphoreType.DMA((2,)),
            pltpu.SemaphoreType.DMA((3,)),
            pltpu.SemaphoreType.DMA((3,)),
            pltpu.SemaphoreType.DMA((3,)),
            pltpu.SemaphoreType.DMA((3,)),
            pltpu.VMEM((captions, width), jnp.bfloat16),
            pltpu.SemaphoreType.DMA((10,)),
            pltpu.SemaphoreType.DMA((10,)),
        ],
        compiler_params=pltpu.CompilerParams(
            collective_id=collective, has_side_effects=True, vmem_limit_bytes=VMEM_LIMIT
        ),
        name=f"fetch_{collective}",
    )(weights.reshape((blocks,) + part), ids, table)
    return ([out.reshape(-1, width, width) for out in outs[:-1]], outs[-1])


def gather_later(own):
    depth, eighths = lax.axis_size("fsdp"), lax.axis_size("dp")
    if depth != 4 or eighths != 8:
        return lax.all_gather(own, "fsdp", axis=1, tiled=True)
    return lax.all_gather(own, ("fsdp", "dp"), axis=1).reshape(-1, D, D)


def share_kernel(count, *refs):
    owns, outs, (send, recv) = (refs[:count], refs[count : 2 * count], refs[2 * count :])
    d, z, zs = places()
    sib, near_x, near_y = flip(d, 1), flip(d, 2), flip(d, 4)
    diagonal = flip(near_x, 4)
    greet(
        [(d, zs[1]), (d, zs[2]), (d, zs[3]), (sib, z), (near_x, z), (near_y, z), (diagonal, z)]
    )
    for own, out in zip(owns, outs):
        out[d, z] = own[...]
    started = []

    def push(slot, origin, to, first=False):
        copies = []
        for i in range(count):
            copies.append(
                pltpu.make_async_remote_copy(
                    src_ref=owns[i] if first else outs[i].at[origin],
                    dst_ref=outs[i].at[origin, z] if first else outs[i].at[origin],
                    send_sem=send.at[i, slot],
                    recv_sem=recv.at[i, slot],
                    device_id=to,
                    device_id_type=MESH,
                )
            )
            copies[-1].start()
        started.extend(copies)
        return copies

    def arrive(copies):
        for copy in copies:
            copy.wait_recv()

    first = [push(o - 1, d, (d, zs[o]), True) for o in (1, 2, 3)]
    for copies in first:
        arrive(copies)
    second = [push(3 + i, d, (to, z)) for i, to in enumerate((near_x, near_y, diagonal))]
    last = [push(6, d, (sib, z))]
    for i, origin in enumerate((near_x, near_y, diagonal)):
        arrive(second[i])
        last.append(push(7 + i, origin, (sib, z)))
    for copies in last:
        arrive(copies)
    for copy in started:
        copy.wait_send()


def share(owns, collective):
    lanes, depth = lax.axis_size("dp"), lax.axis_size("fsdp")
    if depth != 4 or lanes != 8:
        return [
            lax.all_gather(own, ("dp", "fsdp"), axis=0).reshape((lanes, depth) + own.shape)
            for own in owns
        ]
    count = len(owns)
    return pl.pallas_call(
        functools.partial(share_kernel, count),
        out_shape=[jax.ShapeDtypeStruct((lanes, depth) + own.shape, own.dtype) for own in owns],
        in_specs=[pl.BlockSpec(memory_space=pltpu.VMEM)] * count,
        out_specs=[pl.BlockSpec(memory_space=pltpu.VMEM)] * count,
        scratch_shapes=[
            pltpu.SemaphoreType.DMA((count, 10)),
            pltpu.SemaphoreType.DMA((count, 10)),
        ],
        compiler_params=pltpu.CompilerParams(collective_id=collective, has_side_effects=True),
        name=f"share_{collective}",
    )(*owns)


class Reduction:
    def __init__(self, source, start, first, n, buffers, k, semaphores, spots):
        self.source, self.start, self.first, self.n, self.k = (source, start, first, n, k)
        self.held, self.from_core, self.from_near, self.from_turn, self.ready, self.from_z = buffers
        self.local_sem, self.send, self.recv = semaphores
        self.spots = spots
        self.rows = pl.ds(first, n)
        self.started = []

    def push(self, slot, source, target, to):
        copy = pltpu.make_async_remote_copy(
            src_ref=source,
            dst_ref=target,
            send_sem=self.send.at[self.k, slot],
            recv_sem=self.recv.at[self.k, slot],
            device_id=to,
            device_id_type=MESH,
        )
        copy.start()
        self.started.append(copy)
        return copy

    def begin(self):
        d, z, zs, x, y, c = self.spots
        blocks = pl.ds(self.start, self.n)
        self.local = pltpu.make_async_copy(
            self.source.at[blocks, :, :, :, c], self.held.at[self.rows], self.local_sem.at[self.k]
        )
        self.local.start()
        self.core = self.push(
            0,
            self.source.at[blocks, :, :, :, 1 - c],
            self.from_core.at[self.rows],
            (flip(d, 1), z),
        )

    def add(self, count, place):
        @pl.loop(0, self.n * count)
        def _(i):
            target, other = place(self.first + i // count, lax.rem(i, count))
            self.held[target] = self.held[target] + other

    def across_plane(self):
        d, z, zs, x, y, c = self.spots
        self.local.wait()
        self.core.wait_recv()

        def place(b, i):
            target = (b, i // 4, lax.rem(i // 2, 2), lax.rem(i, 2))
            return (target, self.from_core[target])

        self.add(16, place)
        self.near = [
            self.push(
                1,
                self.held.at[self.rows, 0:2, :, 1 - x],
                self.from_near.at[self.rows, 0:2],
                (flip(d, 2), z),
            ),
            self.push(
                2,
                self.held.at[self.rows, 2:4, 1 - y],
                self.from_near.at[self.rows, 2:4],
                (flip(d, 4), z),
            ),
        ]

    def turn(self):
        d, z, zs, x, y, c = self.spots

        def place_a(b, i):
            return ((b, i // 2, lax.rem(i, 2), x), self.from_near[b, i // 2, lax.rem(i, 2)])

        def place_b(b, i):
            return ((b, 2 + i // 2, y, lax.rem(i, 2)), self.from_near[b, 2 + i // 2, lax.rem(i, 2)])

        self.near[0].wait_recv()
        self.add(4, place_a)
        a = self.push(
            3,
            self.held.at[self.rows, 0:2, 1 - y, x],
            self.from_turn.at[self.rows, 0:2],
            (flip(d, 4), z),
        )
        self.near[1].wait_recv()
        self.add(4, place_b)
        b = self.push(
            4,
            self.held.at[self.rows, 2:4, y, 1 - x],
            self.from_turn.at[self.rows, 2:4],
            (flip(d, 2), z),
        )
        self.turned = [a, b]

    def along_z(self):
        d, z, zs, x, y, c = self.spots
        for copy in self.turned:
            copy.wait_recv()

        @pl.loop(0, self.n * 4)
        def _(i):
            b, zz = (self.first + i // 4, lax.rem(i, 4))
            self.ready[b, zz] = self.held[b, zz, y, x] + self.from_turn[b, zz]

        self.spread = [
            self.push(
                4 + o,
                self.ready.at[self.rows, zs[o]],
                self.from_z.at[self.rows, o - 1],
                (d, zs[o]),
            )
            for o in (1, 2, 3)
        ]

    def finish(self, out):
        d, z, zs, x, y, c = self.spots
        for copy in self.spread:
            copy.wait_recv()

        @pl.loop(self.first, self.first + self.n)
        def _(b):
            total = self.held[b, z, y, x].astype(jnp.float32) + self.from_turn[b, z].astype(
                jnp.float32
            )
            for o in range(3):
                total = total + self.from_z[b, o].astype(jnp.float32)
            out[b] = total

        for copy in self.started:
            copy.wait_send()


class Meeting:
    def __init__(self, blocks_of, sources, refs):
        self.blocks_of, self.sources = (blocks_of, sources)
        self.small_out, self.stats_out, self.mine, self.low = refs[:4]
        self.parts, self.stats, self.local_sem, self.send, self.recv = refs[4:9]
        self.part_send, self.part_recv = refs[9:]

    def push(self, slot, source, target, to, sems):
        copy = pltpu.make_async_remote_copy(
            src_ref=source,
            dst_ref=target,
            send_sem=sems[0].at[slot],
            recv_sem=sems[1].at[slot],
            device_id=to,
            device_id_type=MESH,
        )
        copy.start()
        return copy

    def run(self, small, results, spots, others):
        d, z, zs = spots[:3]
        total = jnp.zeros(results[0].shape[1:], jnp.float32)
        homes = {
            int(block): (lane, place)
            for lane, entry in enumerate(self.blocks_of)
            for place, block in enumerate(entry)
        }
        for block, (source, index) in enumerate(self.sources):
            value = results[source][index]
            total = total + value * value
            value = value.astype(self.low.dtype)
            self.low[block] = value
            lane, place = homes[block]
            self.parts[lane, place] = value
        for lane, entry in enumerate(self.blocks_of):
            for place, block in enumerate(entry):
                if block < 0:
                    self.parts[lane, place] = jnp.zeros_like(self.parts[lane, place])
        squares = jnp.sum(total, axis=(0, 1), keepdims=True)
        self.stats[...] = jnp.broadcast_to(squares, self.stats.shape)
        moved = [
            self.push(
                i,
                self.parts.at[other],
                self.mine.at[:, d],
                (other, z),
                (self.part_send, self.part_recv),
            )
            for i, other in enumerate(others)
        ]
        keep = pltpu.make_async_copy(self.parts.at[d], self.mine.at[:, d], self.local_sem)
        keep.start()
        pairs = [(small, self.small_out), (self.stats, self.stats_out)]
        for own, out in pairs:
            out[z, d] = own[...]
        started = []

        def push_all(slot, origin, to, first=False):
            copies = []
            for i, (own, out) in enumerate(pairs):
                copies.append(
                    self.push(
                        slot,
                        own if first else out.at[:, origin],
                        out.at[z, origin] if first else out.at[:, origin],
                        to,
                        (self.send.at[i], self.recv.at[i]),
                    )
                )
            started.extend(copies)
            return copies

        def arrive(copies):
            for copy in copies:
                copy.wait_recv()

        first = [push_all(o - 1, d, (d, zs[o]), True) for o in (1, 2, 3)]
        for copies in first:
            arrive(copies)
        second = [push_all(3 + i, d, (to, z)) for i, to in enumerate(others[:3])]
        last = [push_all(6, d, (others[3], z))]
        for i, origin in enumerate(others[:3]):
            arrive(second[i])
            last.append(push_all(7 + i, origin, (others[3], z)))
        for copies in last:
            arrive(copies)
        arrive(moved)
        for copy in started + moved:
            copy.wait_send()
        keep.wait()


def reduce_kernel(chunks, sources, sets, meeting, *refs):
    ins = refs[:sources]
    refs = refs[sources:]
    if meeting is not None:
        earlier, refs = (refs[0], refs[1:])
    outs = refs[:sets]
    refs = refs[sets:]
    if meeting is not None:
        outside, refs = (refs[:4], refs[4:])
    buffers = [refs[6 * i : 6 * i + 6] for i in range(sets)]
    semaphores = refs[6 * sets : 6 * sets + 3]
    d, z, zs = places()
    spots = (d, z, zs, lax.rem(d // 2, 2), d // 4, lax.rem(d, 2))
    sib, near_x, near_y = (flip(d, 1), flip(d, 2), flip(d, 4))
    diagonal = flip(near_x, 4)
    others = [near_x, near_y, diagonal, sib, flip(near_x, 1), flip(near_y, 1), flip(diagonal, 1)]
    if meeting is None:
        others = [near_x, near_y, sib]
    greet([(d, zs[1]), (d, zs[2]), (d, zs[3])] + [(other, z) for other in others])
    work = []
    for k, (source, start, first, n, which) in enumerate(chunks):
        work.append(
            Reduction(ins[source], start, first, n, buffers[which], k, semaphores, spots)
        )
        work[k].begin()
    count = len(chunks)
    for step in range(count + 3):
        if step < count:
            work[step].across_plane()
        if 1 <= step <= count:
            work[step - 1].turn()
        if 2 <= step <= count + 1:
            work[step - 2].along_z()
        if step >= 3:
            work[step - 3].finish(outs[chunks[step - 3][4]])
    if meeting is not None:
        tail = Meeting(*meeting, tuple(outside) + tuple(refs[6 * sets + 3 :]))
        tail.run(outs[1].at[0], (outs[0], earlier), spots, others)


def reduce_grads(grads, collective, small=None, meeting=None, earlier=None):
    lanes, depth = lax.axis_size("dp"), lax.axis_size("fsdp")
    rows = D // (lanes * depth)
    tail = (depth, 2, 2, 2)
    sources = [grad.reshape((-1,) + tail + (rows, D)) for grad in grads]
    chunks = []
    first = 0
    for i, source in enumerate(sources):
        for start in range(source.shape[0]):
            chunks.append((i, start, first, 1, 0))
            first += 1
    sets = [(first, (rows, D), jnp.bfloat16)]
    if small is not None:
        sources.append(small.reshape((1,) + tail + small.shape[1:]))
        chunks.insert(1, (len(sources) - 1, 0, 0, 1, 1))
        sets.append((1, small.shape[1:], jnp.float32))
    scratch = []
    for n, shape, kind in sets:
        scratch += [
            pltpu.VMEM((n, depth, 2, 2) + shape, kind),
            pltpu.VMEM((n, depth, 2, 2) + shape, kind),
            pltpu.VMEM((n, depth, 2) + shape, kind),
            pltpu.VMEM((n, depth) + shape, kind),
            pltpu.VMEM((n, depth) + shape, kind),
            pltpu.VMEM((n, 3) + shape, kind),
        ]
    scratch += [
        pltpu.SemaphoreType.DMA((len(chunks),)),
        pltpu.SemaphoreType.DMA((len(chunks), 8)),
        pltpu.SemaphoreType.DMA((len(chunks), 8)),
    ]
    out_shape = [jax.ShapeDtypeStruct((n,) + shape, jnp.float32) for n, shape, _ in sets]
    count = len(sources)
    if meeting is not None:
        blocks_of, origins = meeting
        most = len(blocks_of[0])
        out_shape += [
            jax.ShapeDtypeStruct((depth, lanes) + small.shape[1:], jnp.float32),
            jax.ShapeDtypeStruct((depth, lanes, 8, 128), jnp.float32),
            jax.ShapeDtypeStruct((most, lanes, rows, D), jnp.bfloat16),
            jax.ShapeDtypeStruct((len(origins), rows, D), jnp.bfloat16),
        ]
        scratch += [
            pltpu.VMEM((lanes, most, rows, D), jnp.bfloat16),
            pltpu.VMEM((8, 128), jnp.float32),
            pltpu.SemaphoreType.DMA,
            pltpu.SemaphoreType.DMA((2, 10)),
            pltpu.SemaphoreType.DMA((2, 10)),
            pltpu.SemaphoreType.DMA((7,)),
            pltpu.SemaphoreType.DMA((7,)),
        ]
        sources.append(earlier)
    return pl.pallas_call(
        functools.partial(reduce_kernel, chunks, count, len(sets), meeting),
        out_shape=out_shape,
        in_specs=whole("a" * count + "v" * (len(sources) - count)),
        out_specs=whole("v" * len(out_shape)),
        scratch_shapes=scratch,
        compiler_params=pltpu.CompilerParams(
            collective_id=collective, has_side_effects=True, vmem_limit_bytes=VMEM_LIMIT
        ),
        name=f"reduce_{collective}",
    )(*sources)


def spread_stages(own, out, local_sem, send, recv):
    d, z, _ = places()
    sib, near_x, near_y = flip(d, 1), flip(d, 2), flip(d, 4)
    diagonal = flip(near_x, 4)
    half = own.shape[0] // 2
    parts = (pl.ds(0, half), pl.ds(half, own.shape[0] - half))
    started = []
    last = []

    def push(slot, origin, part, to, source=None):
        copy = pltpu.make_async_remote_copy(
            src_ref=out.at[part, origin] if source is None else source,
            dst_ref=out.at[part, origin],
            send_sem=send.at[slot],
            recv_sem=recv.at[slot],
            device_id=to,
            device_id_type=MESH,
        )
        copy.start()
        started.append(copy)
        return copy

    keep = pltpu.make_async_copy(own, out.at[:, d], local_sem)
    near = {}
    turned = []

    def begin():
        for way, part in ((0, 0), (1, 1), (0, 1), (1, 0)):
            near[way, part] = push(
                2 * way + part, d, parts[part], ((near_x, near_y)[way], z), own.at[parts[part]]
            )
        keep.start()
        last.extend([push(4 + i, d, parts[i], (sib, z), own.at[parts[i]]) for i in (0, 1)])

    def forward():
        near[0, 0].wait_recv()
        turned.append(push(6, near_x, parts[0], (near_y, z)))
        last.append(push(7, near_x, parts[0], (sib, z)))
        near[1, 1].wait_recv()
        turned.append(push(8, near_y, parts[1], (near_x, z)))
        last.append(push(9, near_y, parts[1], (sib, z)))

    def collect():
        near[1, 0].wait_recv()
        last.append(push(10, near_y, parts[0], (sib, z)))
        near[0, 1].wait_recv()
        last.append(push(11, near_x, parts[1], (sib, z)))
        for i in (0, 1):
            turned[i].wait_recv()
            last.append(push(12 + i, diagonal, parts[i], (sib, z)))

    def finish():
        for copy in last:
            copy.wait_recv()
        for copy in started:
            copy.wait_send()
        keep.wait()

    return (begin, forward, collect, finish)


GRAM_TILE = 128


def gram_kernel(
    gram,
    rows,
    own,
    total,
    all_rows,
    shards,
    left,
    right,
    onward,
    back,
    sems,
    local_sem,
    send,
    recv,
    row_sems,
):
    d, z, _ = places()
    up, down = (z + 1, z - 1)
    two = jnp.logical_and(lax.rem(d, 2) == 1, d // 4 == 1)
    one = jnp.logical_not(two)
    sib, near_x, near_y = flip(d, 1), flip(d, 2), flip(d, 4)
    greet([(d, lax.rem(z + step, 4)) for step in (1, 2, 3)] + [(sib, z), (near_x, z), (near_y, z)])
    stages = spread_stages(own, shards, local_sem, send, recv)
    count = D // GRAM_TILE

    def at(ref, j):
        return ref.at[pl.ds(j * GRAM_TILE, GRAM_TILE), pl.ds(j * GRAM_TILE, D - j * GRAM_TILE)]

    def copy(source, target, j, way, to):
        return pltpu.make_async_remote_copy(
            src_ref=at(source, j),
            dst_ref=at(target, j),
            send_sem=sems.at[2 * way, j],
            recv_sem=sems.at[2 * way + 1, j],
            device_id=(d, to),
            device_id_type=MESH,
        )

    def add(target, j, *terms):
        @pl.loop(0, GRAM_TILE // 16)
        def _(i):
            part = pl.ds(pl.multiple_of(j * GRAM_TILE + i * 16, 16), 16)
            columns = pl.ds(j * GRAM_TILE, D - j * GRAM_TILE)
            value = terms[0][part, columns]
            for term in terms[1:]:
                value = value + term[part, columns]
            target[part, columns] = value

    def ends():
        @pl.when(z == 0)
        def _():
            for j in range(count):
                copy(gram, left, j, 0, up).start()

        @pl.when(z == 3)
        def _():
            for j in range(count):
                copy(gram, right, j, 1, down).start()

    def near(j):
        @pl.when(z == 1)
        def _():
            copy(onward, left, j, 0, up).wait_recv()
            add(onward, j, gram, left)
            copy(onward, left, j, 0, up).start()

        @pl.when(z == 2)
        def _():
            copy(back, right, j, 1, down).wait_recv()
            add(back, j, gram, right)
            copy(back, right, j, 1, down).start()

    def far(j):
        @pl.when(z == 1)
        def _():
            copy(back, right, j, 1, down).wait_recv()
            add(back, j, gram, right)
            copy(back, right, j, 1, down).start()
            add(total, j, onward, right)

        @pl.when(z == 2)
        def _():
            copy(onward, left, j, 0, up).wait_recv()
            add(onward, j, gram, left)
            copy(onward, left, j, 0, up).start()
            add(total, j, onward, right)

        @pl.when(z == 3)
        def _():
            copy(gram, left, j, 0, up).wait_recv()
            add(total, j, left, gram)

        @pl.when(z == 0)
        def _():
            copy(gram, right, j, 1, down).wait_recv()
            add(total, j, gram, right)

        lines = slice(j * GRAM_TILE, (j + 1) * GRAM_TILE)
        for k in range(j + 1, count):
            columns = slice(k * GRAM_TILE, (k + 1) * GRAM_TILE)
            total[columns, lines] = total[lines, columns].T

    def finish():
        for j in range(count):

            @pl.when(z == 0)
            def _():
                copy(gram, left, j, 0, up).wait_send()

            @pl.when(z == 3)
            def _():
                copy(gram, right, j, 1, down).wait_send()

            @pl.when(jnp.logical_and(z > 0, z < 3))
            def _():
                copy(onward, left, j, 0, up).wait_send()
                copy(back, right, j, 1, down).wait_send()

    def pass_on(origin, way, to, source=None):
        return pltpu.make_async_remote_copy(
            src_ref=all_rows.at[origin] if source is None else source,
            dst_ref=all_rows.at[origin],
            send_sem=row_sems.at[2 * way, origin],
            recv_sem=row_sems.at[2 * way + 1, origin],
            device_id=(d, to),
            device_id_type=MESH,
        )

    def line_of(here):
        started = []
        if here < 3:
            started.append(pass_on(here, 0, here + 1, rows))
            started[-1].start()
        if here > 0:
            started.append(pass_on(here, 1, here - 1, rows))
            started[-1].start()
        all_rows[here] = rows[...]
        from_left = list(range(here - 1, -1, -1))
        from_right = list(range(here + 1, 4))
        for i in range(3):
            if i < len(from_left):
                pass_on(from_left[i], 0, here).wait_recv()
                if here < 3:
                    started.append(pass_on(from_left[i], 0, here + 1))
                    started[-1].start()
            if i < len(from_right):
                pass_on(from_right[i], 1, here).wait_recv()
                if here > 0:
                    started.append(pass_on(from_right[i], 1, here - 1))
                    started[-1].start()
        return started

    pl.when(one)(ends)
    stages[0]()

    @pl.when(one)
    def _():
        near(0)
        near(1)
        near(2)
        far(0)

    @pl.when(two)
    def _():
        for here in range(4):

            @pl.when(z == here)
            def _():
                for started in line_of(here):
                    started.wait_send()

    stages[1]()

    @pl.when(one)
    def _():
        near(3)
        far(1)
        near(4)
        far(2)

    stages[2]()

    @pl.when(one)
    def _():
        near(5)
        far(3)
        far(4)
        far(5)
        finish()

    stages[3]()


def sum_grams(gram, rows, own, collective):
    lanes, depth = lax.axis_size("dp"), lax.axis_size("fsdp")
    square = pltpu.VMEM(gram.shape, jnp.float32)
    return pl.pallas_call(
        gram_kernel,
        out_shape=[
            jax.ShapeDtypeStruct(gram.shape, jnp.float32),
            jax.ShapeDtypeStruct((depth,) + rows.shape, rows.dtype),
            jax.ShapeDtypeStruct(own.shape[:1] + (lanes,) + own.shape[1:], own.dtype),
        ],
        in_specs=whole("vvv"),
        out_specs=whole("vva"),
        scratch_shapes=[
            square,
            square,
            square,
            square,
            pltpu.SemaphoreType.DMA((4, D // GRAM_TILE)),
            pltpu.SemaphoreType.DMA,
            pltpu.SemaphoreType.DMA((14,)),
            pltpu.SemaphoreType.DMA((14,)),
            pltpu.SemaphoreType.DMA((4, 4)),
        ],
        compiler_params=pltpu.CompilerParams(
            collective_id=collective, has_side_effects=True, vmem_limit_bytes=VMEM_LIMIT
        ),
        name=f"gram_{collective}",
    )(gram, rows, own)


def schulz_kernel(two, gram, all_rows, rows, out, state, state_low, change, current):
    def chains(parts):
        for slot, first, number in parts:
            if len(parts) == 1:
                value = gram[...]
            else:
                value = jnp.zeros((D, D), jnp.float32)
                for z in range(all_rows.shape[0]):
                    piece = all_rows[z, slot]
                    value = value + contract_first(piece, piece)
            line = lax.broadcasted_iota(jnp.int32, value.shape, 0)
            column = lax.broadcasted_iota(jnp.int32, value.shape, 1)
            total = jnp.sum(jnp.where(line == column, value, 0.0), axis=(0, 1), keepdims=True)
            inverse = 1.0 / (jnp.sqrt(total) + 1e-07)
            value = value * (inverse * inverse)
            state[slot] = value
            state_low[slot] = value.astype(jnp.bfloat16)
            for place in range(first, first + number):
                current[place] = rows[place] * inverse

        def turn(last):
            for slot, _, _ in parts:
                square = jnp.dot(
                    state_low[slot], state_low[slot], preferred_element_type=jnp.float32
                )
                change[slot] = (COEF_B * state[slot] + COEF_C * square).astype(jnp.bfloat16)
            for slot, first, number in parts:
                for place in range(first, first + number):
                    value = current[place]
                    current[place] = COEF_A * value + jnp.dot(
                        value.astype(jnp.bfloat16),
                        change[slot],
                        preferred_element_type=jnp.float32,
                    )
            if last:
                return
            for half in range(2):
                for slot, _, _ in parts:
                    value = COEF_A * state[slot] + jnp.dot(
                        state_low[slot], change[slot], preferred_element_type=jnp.float32
                    )
                    state[slot] = value
                    state_low[slot] = value.astype(jnp.bfloat16)

        @pl.loop(0, NS_ITERS - 1)
        def _(_):
            turn(False)

        turn(True)
        for slot, first, number in parts:
            for place in range(first, first + number):
                out[place] = current[place].astype(jnp.bfloat16)

    @pl.when(two[0] == 0)
    def _():
        chains([(0, 0, 4)])

    @pl.when(two[0] == 1)
    def _():
        chains([(0, 0, 1), (1, 1, 1)])
        for place in (2, 3):
            out[place] = jnp.zeros(out.shape[1:], jnp.bfloat16)


def schulz(two, gram, all_rows, rows):
    return pl.pallas_call(
        schulz_kernel,
        out_shape=jax.ShapeDtypeStruct(rows.shape, jnp.bfloat16),
        in_specs=[
            pl.BlockSpec(memory_space=pltpu.SMEM),
        ]
        + whole("vvv"),
        out_specs=pl.BlockSpec(memory_space=pltpu.VMEM),
        scratch_shapes=[
            pltpu.VMEM((2, D, D), jnp.float32),
            pltpu.VMEM((2, D, D), jnp.bfloat16),
            pltpu.VMEM((2, D, D), jnp.bfloat16),
            pltpu.VMEM(rows.shape, jnp.float32),
        ],
        compiler_params=pltpu.CompilerParams(vmem_limit_bytes=VMEM_LIMIT),
        name="schulz",
    )(two, gram, all_rows, rows)


def spread_kernel(own, out, local_sem, send, recv):
    d, z, _ = places()
    greet([(flip(d, 1), z), (flip(d, 2), z), (flip(d, 4), z)])
    for stage in spread_stages(own, out, local_sem, send, recv):
        stage()


def spread(own, collective):
    lanes = lax.axis_size("dp")
    return pl.pallas_call(
        spread_kernel,
        out_shape=jax.ShapeDtypeStruct(own.shape[:1] + (lanes,) + own.shape[1:], own.dtype),
        in_specs=[pl.BlockSpec(memory_space=pltpu.VMEM)],
        out_specs=pl.BlockSpec(memory_space=pl.ANY),
        scratch_shapes=[
            pltpu.SemaphoreType.DMA,
            pltpu.SemaphoreType.DMA((14,)),
            pltpu.SemaphoreType.DMA((14,)),
        ],
        compiler_params=pltpu.CompilerParams(
            collective_id=collective, has_side_effects=True, vmem_limit_bytes=VMEM_LIMIT
        ),
        name=f"spread_{collective}",
    )(own)


def update_kernel(
    table,
    scale,
    clip,
    momenta,
    grads,
    weights,
    turned_first,
    turned_second,
    momenta_new,
    weights_new,
    weights_low,
):
    pair = pl.program_id(0)
    for i, turned in enumerate((turned_first, turned_second)):
        momenta_new[i] = MOMENT * momenta[i] + clip[0] * grads[i].astype(jnp.float32)
        value = weights[i] * (1.0 - MUON_RATE * MUON_DECAY) - scale[2 * pair + i] * turned[
            0, 0
        ].astype(jnp.float32)
        weights_new[i] = value
        weights_low[i] = value.astype(jnp.bfloat16)


def update(home, scale, clip, momenta, grads, weights, turned):
    blocks, rows, width = weights.shape
    table = np.array(
        [home[block][1] for block in range(blocks)] + [home[block][0] for block in range(blocks)],
        np.int32,
    )
    pair = pl.BlockSpec((2, rows, width), lambda b, *_: (b, 0, 0))

    def turned_of(i):
        return pl.BlockSpec(
            (1, 1, rows, width),
            lambda b, table, *_: (table[2 * b + i], table[blocks + 2 * b + i], 0, 0),
        )

    return pl.pallas_call(
        update_kernel,
        grid_spec=pltpu.PrefetchScalarGridSpec(
            num_scalar_prefetch=3,
            grid=(blocks // 2,),
            in_specs=[pair, pair, pair, turned_of(0), turned_of(1)],
            out_specs=[pair, pair, pair],
        ),
        out_shape=[
            jax.ShapeDtypeStruct(weights.shape, jnp.float32),
            jax.ShapeDtypeStruct(weights.shape, jnp.float32),
            jax.ShapeDtypeStruct(weights.shape, jnp.bfloat16),
        ],
        compiler_params=pltpu.CompilerParams(vmem_limit_bytes=VMEM_LIMIT),
        name="update",
    )(
        jnp.asarray(table),
        jnp.asarray(scale),
        clip.reshape(1),
        momenta,
        grads,
        weights,
        turned,
        turned,
    )


GROUP = 6 * HD


def normed_head(value, gain):
    centred = value - jnp.mean(value, 0, keepdims=True)
    scale = lax.rsqrt(jnp.mean(centred * centred, 0, keepdims=True) + 1e-06)
    centred = centred * scale
    return (centred * gain, centred, scale)


def contract_first(left, right):
    return lax.dot_general(
        left, right, (((0,), (0,)), ((), ())), preferred_element_type=jnp.float32
    )


def contract_last(left, right):
    return lax.dot_general(
        left, right, (((1,), (1,)), ((), ())), preferred_element_type=jnp.float32
    )


def shares_of(scores, same):
    scores = jnp.where(same, scores * (1.0 / math.sqrt(HD)), -1e30)
    exponent = jnp.exp(scores - jnp.max(scores, 0, keepdims=True))
    return exponent * (1.0 / jnp.sum(exponent, 0, keepdims=True))


TILE = 768
TOKENS = 256
SLOPE = math.sqrt(2.0 / math.pi)
CUBIC = 0.044715


def tile_of(t, size=TILE):
    return pl.ds(pl.multiple_of(t * size, size), size)


def row_norm(value):
    centred = value - jnp.mean(value, -1, keepdims=True)
    scale = lax.rsqrt(jnp.mean(centred * centred, -1, keepdims=True) + 1e-06)
    return (centred * scale, scale)


def gelu_parts(value):
    square = value * value
    bend = jnp.tanh(SLOPE * value * (1.0 + CUBIC * square))
    half = 0.5 + 0.5 * bend
    slope = half + 0.5 * value * (1.0 - bend * bend) * SLOPE * (1.0 + 3.0 * CUBIC * square)
    return (value * half, slope)


def load_all(pairs, sem):
    copies = [
        pltpu.make_async_copy(source, target, sem.at[i])
        for i, (source, target) in enumerate(pairs)
    ]
    for copy in copies:
        copy.start()
    return copies


def stand_up(row):
    return jnp.broadcast_to(row, (8, row.shape[1])).T[:, :1]


def slot_marks(segment, b):
    row = segment[b : b + 1].astype(jnp.float32)
    return (stand_up(row), row)


def norm_rows(source, gains, first, target):
    gain, shift = (gains[first : first + 1], gains[first + 1 : first + 2])

    @pl.loop(0, source.shape[0] // 64)
    def _(t):
        part = tile_of(t, 64)
        target[part] = (row_norm(source[part])[0] * gain + shift).astype(target.dtype)


def forward_kernel(
    spans,
    base,
    state,
    gains,
    segment,
    mixing,
    mixing_out,
    upward,
    down,
    state_out,
    middle,
    mixed,
    heads_low,
    attended,
    normed_low,
    mixing_held,
    out_held,
    up_held,
    down_held,
    hidden,
    gain_query,
    gain_key,
    sem,
):
    mixing, mixing_out, upward, down = [
        ref.at[pl.ds(*span)] for ref, span in zip((mixing, mixing_out, upward, down), spans)
    ]
    loads = load_all(
        [(mixing, mixing_held), (mixing_out, out_held), (upward, up_held), (down, down_held)], sem
    )
    gain_query[...] = stand_up(gains[base + 4 : base + 5])
    gain_key[...] = stand_up(gains[base + 5 : base + 6])
    norm_rows(state, gains, base, heads_low)
    loads[0].wait()

    @pl.loop(0, 3 * D // TILE)
    def _(t):
        mixed[tile_of(t)] = contract_last(mixing_held[tile_of(t)], heads_low[...])

    parts, length = segment.shape
    for b in range(parts):
        column, row = slot_marks(segment, b)
        same = column == row
        tokens = slice(b * length, (b + 1) * length)

        @pl.loop(0, D // GROUP)
        def _(group):
            held = []
            for head in range(GROUP // HD):
                first = group * GROUP + head * HD
                part = pl.ds(pl.multiple_of(first, HD), HD)
                query, key, value = [
                    mixed[pl.ds(pl.multiple_of(place * D + first, HD), HD), tokens]
                    for place in range(3)
                ]
                query_low = normed_head(query, gain_query[part])[0].astype(jnp.bfloat16)
                key_low = normed_head(key, gain_key[part])[0].astype(jnp.bfloat16)
                held.append((part, query_low, key_low, value.astype(jnp.bfloat16)))
            scores = [contract_first(key_low, query_low) for _, query_low, key_low, _ in held]
            shares = [shares_of(score, same).astype(jnp.bfloat16) for score in scores]
            for (part, _, _, value_low), share in zip(held, shares):
                attended[part, tokens] = jnp.dot(
                    value_low, share, preferred_element_type=jnp.float32
                ).astype(jnp.bfloat16)

    loads[1].wait()
    for t in range(state.shape[0] // TOKENS):
        part = slice(t * TOKENS, (t + 1) * TOKENS)
        middle[part] = state[part] + contract_first(attended[:, part], out_held[...])
    norm_rows(middle, gains, base + 2, normed_low)
    loads[2].wait()

    @pl.loop(0, FF // TILE)
    def _(t):
        value = contract_last(up_held[tile_of(t)], normed_low[...])
        hidden[tile_of(t)] = gelu_parts(value)[0].astype(jnp.bfloat16)

    loads[3].wait()
    for t in range(state.shape[0] // TOKENS):
        part = slice(t * TOKENS, (t + 1) * TOKENS)
        state_out[part] = middle[part] + contract_first(hidden[:, part], down_held[...])


def layer_weights(blocks):
    weights = [array.reshape(-1, D) for array, _, _ in blocks]
    return (weights, [(first * D, number * D) for _, first, number in blocks])


def layer_forward(state, blocks, gains, base, segment):
    tokens = state.shape[0]
    weights, spans = layer_weights(blocks)
    state_out, middle, mixed, heads_low, attended, normed_low = pl.pallas_call(
        functools.partial(forward_kernel, spans, base),
        out_shape=[
            jax.ShapeDtypeStruct((tokens, D), jnp.float32),
            jax.ShapeDtypeStruct((tokens, D), jnp.float32),
            jax.ShapeDtypeStruct((3 * D, tokens), jnp.float32),
            jax.ShapeDtypeStruct((tokens, D), jnp.bfloat16),
            jax.ShapeDtypeStruct((D, tokens), jnp.bfloat16),
            jax.ShapeDtypeStruct((tokens, D), jnp.bfloat16),
        ],
        in_specs=whole("vvvaaaa"),
        out_specs=whole("vvvvvv"),
        scratch_shapes=[pltpu.VMEM((number, D), jnp.bfloat16) for _, number in spans]
        + [
            pltpu.VMEM((FF, tokens), jnp.bfloat16),
            pltpu.VMEM((D, 1), jnp.float32),
            pltpu.VMEM((D, 1), jnp.float32),
            pltpu.SemaphoreType.DMA((4,)),
        ],
        compiler_params=pltpu.CompilerParams(vmem_limit_bytes=VMEM_LIMIT),
        name="layer_forward",
    )(state, gains, segment, *weights)
    return (state_out, (state, middle, mixed, heads_low, attended, normed_low))


def backward_kernel(
    spans,
    base,
    grad,
    middle,
    normed_low,
    gains,
    segment,
    state,
    mixed,
    heads_low,
    attended,
    mixing,
    mixing_out,
    upward,
    down,
    grad_out,
    gain_out,
    grad_mixing,
    grad_mixing_out,
    grad_up,
    grad_down,
    state_held,
    mixed_held,
    heads_held,
    attended_held,
    mixing_held,
    out_held,
    up_held,
    down_held,
    low,
    inner,
    hidden_grad,
    mixed_low,
    attended_grad,
    made_up,
    made_down,
    made_mixing,
    made_out,
    gain_query,
    gain_key,
    head_gains,
    sem,
    store_sem,
):
    mixing, mixing_out, upward, down = [
        ref.at[pl.ds(*span)] for ref, span in zip((mixing, mixing_out, upward, down), spans)
    ]
    loads = load_all(
        [
            (upward, up_held),
            (down, down_held),
            (mixing_out, out_held),
            (attended, attended_held),
            (mixed, mixed_held),
            (heads_low, heads_held),
            (mixing, mixing_held),
            (state, state_held),
        ],
        sem,
    )
    stores = [
        pltpu.make_async_copy(made_up, grad_up, store_sem.at[0]),
        pltpu.make_async_copy(made_down, grad_down, store_sem.at[1]),
        pltpu.make_async_copy(made_out, grad_mixing_out, store_sem.at[2]),
        pltpu.make_async_copy(made_mixing, grad_mixing, store_sem.at[3]),
    ]
    tokens = grad.shape[0]
    gain_out[...] = jnp.zeros_like(gain_out)
    head_gains[...] = jnp.zeros_like(head_gains)
    gain_query[...] = stand_up(gains[base + 4 : base + 5])
    gain_key[...] = stand_up(gains[base + 5 : base + 6])

    @pl.loop(0, tokens // 64)
    def _(t):
        low[tile_of(t, 64)] = grad[tile_of(t, 64)].astype(jnp.bfloat16)

    loads[0].wait()
    loads[1].wait()

    @pl.loop(0, FF // TILE)
    def _(t):
        part = tile_of(t)
        value, slope = gelu_parts(contract_last(up_held[part], normed_low[...]))
        delta = (contract_last(down_held[part], low[...]) * slope).astype(jnp.bfloat16)
        hidden_grad[part] = delta
        made_down[part] = jnp.dot(
            value.astype(jnp.bfloat16), low[...], preferred_element_type=jnp.float32
        ).astype(jnp.bfloat16)
        made_up[part] = jnp.dot(
            delta, normed_low[...], preferred_element_type=jnp.float32
        ).astype(jnp.bfloat16)

    stores[0].start()
    stores[1].start()
    for t in range(tokens // TOKENS):
        part = slice(t * TOKENS, (t + 1) * TOKENS)
        inner[part] = contract_first(hidden_grad[:, part], up_held[...])

    def norm_back(source, first, previous, target, target_low):
        gain = gains[base + first : base + first + 1]

        @pl.loop(0, tokens // 64)
        def _(t):
            part = tile_of(t, 64)
            unit, scale = row_norm(source[part])
            delta = inner[part]
            gain_out[first : first + 1] += jnp.sum(delta * unit, 0, keepdims=True)
            gain_out[first + 1 : first + 2] += jnp.sum(delta, 0, keepdims=True)
            delta = delta * gain
            delta = delta - jnp.mean(delta, -1, keepdims=True) - unit * jnp.mean(
                delta * unit, -1, keepdims=True
            )
            value = previous[part] + delta * scale
            target[part] = value
            if target_low is not None:
                target_low[part] = value.astype(jnp.bfloat16)

    norm_back(middle, 2, grad, grad_out, low)
    loads[2].wait()
    loads[3].wait()

    @pl.loop(0, D // TILE)
    def _(t):
        part = tile_of(t)
        made_out[part] = jnp.dot(
            attended_held[part], low[...], preferred_element_type=jnp.float32
        ).astype(jnp.bfloat16)
        attended_grad[part] = contract_last(out_held[part], low[...]).astype(jnp.bfloat16)

    stores[2].start()
    loads[4].wait()
    parts, length = segment.shape
    for b in range(parts):
        column, row = slot_marks(segment, b)
        same = column == row
        span = slice(b * length, (b + 1) * length)

        @pl.loop(0, D // GROUP)
        def _(group):
            held = []
            for head in range(GROUP // HD):
                first = group * GROUP + head * HD
                part = pl.ds(pl.multiple_of(first, HD), HD)
                where = [pl.ds(pl.multiple_of(place * D + first, HD), HD) for place in range(3)]
                query, key, value = [mixed_held[at, span] for at in where]
                query_low = normed_head(query, gain_query[part])[0].astype(jnp.bfloat16)
                key_low = normed_head(key, gain_key[part])[0].astype(jnp.bfloat16)
                held.append((part, where, query_low, key_low, value.astype(jnp.bfloat16)))
            scores = [contract_first(key_low, query_low) for _, _, query_low, key_low, _ in held]
            share_grads = [
                contract_first(value_low, attended_grad[part, span])
                for part, _, _, _, value_low in held
            ]
            shares = [shares_of(score, same) for score in scores]
            score_lows = []
            for share, share_grad in zip(shares, share_grads):
                total = jnp.sum(share * share_grad, 0, keepdims=True)
                score_lows.append(
                    (share * (share_grad - total) * (1.0 / math.sqrt(HD))).astype(jnp.bfloat16)
                )
            for (part, where, query_low, key_low, _), share, score_low in zip(
                held, shares, score_lows
            ):
                mixed_low[where[2], span] = contract_last(
                    attended_grad[part, span], share.astype(jnp.bfloat16)
                ).astype(jnp.bfloat16)
                deltas = (
                    jnp.dot(key_low, score_low, preferred_element_type=jnp.float32),
                    contract_last(query_low, score_low),
                )
                for place, (delta, gains_here) in enumerate(zip(deltas, (gain_query, gain_key))):
                    _, unit, scale = normed_head(mixed_held[where[place], span], gains_here[part])
                    head_gains[place, part] += jnp.sum(delta * unit, 1, keepdims=True)
                    delta = delta * gains_here[part]
                    delta = delta - jnp.mean(delta, 0, keepdims=True) - unit * jnp.mean(
                        delta * unit, 0, keepdims=True
                    )
                    mixed_low[where[place], span] = (delta * scale).astype(jnp.bfloat16)

    for place in range(2):
        column = jnp.broadcast_to(head_gains[place], (D, 128))
        gain_out[4 + place : 5 + place] = column.T[:1]
    loads[5].wait()

    @pl.loop(0, 3 * D // TILE)
    def _(t):
        part = tile_of(t)
        made_mixing[part] = jnp.dot(
            mixed_low[part], heads_held[...], preferred_element_type=jnp.float32
        ).astype(jnp.bfloat16)

    stores[3].start()
    loads[6].wait()
    for t in range(tokens // TOKENS):
        part = slice(t * TOKENS, (t + 1) * TOKENS)
        inner[part] = contract_first(mixed_low[:, part], mixing_held[...])
    loads[7].wait()
    norm_back(state_held, 0, grad_out, grad_out, None)
    for copy in stores:
        copy.wait()


def layer_backward(grad, kept, blocks, gains, base, segment):
    state, middle, mixed, heads_low, attended, normed_low = kept
    tokens = grad.shape[0]
    weights, spans = layer_weights(blocks)
    low = jnp.bfloat16
    grad, gain_grads, *block_grads = pl.pallas_call(
        functools.partial(backward_kernel, spans, base),
        out_shape=[
            jax.ShapeDtypeStruct((tokens, D), jnp.float32),
            jax.ShapeDtypeStruct((8, D), jnp.float32),
        ]
        + [jax.ShapeDtypeStruct((number, D), low) for _, number in spans],
        in_specs=whole("vvvvvaaaaaaaa"),
        out_specs=whole("vvaaaa"),
        scratch_shapes=[
            pltpu.VMEM(state.shape, jnp.float32),
            pltpu.VMEM(mixed.shape, jnp.float32),
            pltpu.VMEM(heads_low.shape, low),
            pltpu.VMEM(attended.shape, low),
        ]
        + [pltpu.VMEM((number, D), low) for _, number in spans]
        + [
            pltpu.VMEM((tokens, D), low),
            pltpu.VMEM((tokens, D), jnp.float32),
            pltpu.VMEM((FF, tokens), low),
            pltpu.VMEM((3 * D, tokens), low),
            pltpu.VMEM((D, tokens), low),
            pltpu.VMEM((FF, D), low),
            pltpu.VMEM((FF, D), low),
            pltpu.VMEM((3 * D, D), low),
            pltpu.VMEM((D, D), low),
            pltpu.VMEM((D, 1), jnp.float32),
            pltpu.VMEM((D, 1), jnp.float32),
            pltpu.VMEM((2, D, 1), jnp.float32),
            pltpu.SemaphoreType.DMA((8,)),
            pltpu.SemaphoreType.DMA((4,)),
        ],
        compiler_params=pltpu.CompilerParams(vmem_limit_bytes=60 * 1024 * 1024),
        name="layer_backward",
    )(grad, middle, normed_low, gains, segment, state, mixed, heads_low, attended, *weights)
    return (grad, block_grads, gain_grads[:6])


HEAD_LANES = 128


def full_dot(left, right):
    return jnp.dot(left, right, preferred_element_type=jnp.float32, precision=HIGH)


def head_marks():
    entry = lax.broadcasted_iota(jnp.int32, (D, HEAD_LANES), 0)
    lane = lax.broadcasted_iota(jnp.int32, (D, HEAD_LANES), 1)
    return (entry // HD == lane).astype(jnp.float32)


def full_dot_last(left, right):
    return lax.dot_general(
        left,
        right,
        (((1,), (1,)), ((), ())),
        preferred_element_type=jnp.float32,
        precision=HIGH,
    )


def pool_sequence(state, gains, marks_of):
    unit, scale = row_norm(state)
    final = unit * gains[0:1] + gains[1:2]
    marks = head_marks()
    logits = full_dot(final * gains[2:3], marks) * (1.0 / math.sqrt(HD))
    rows, columns = marks_of
    slot = lax.broadcasted_iota(jnp.int32, (rows.shape[0], IMGS), 1)
    member = (rows == slot.astype(jnp.float32)).astype(jnp.float32)
    slot = lax.broadcasted_iota(jnp.int32, (IMGS, columns.shape[1]), 0)
    member_rows = (columns == slot.astype(jnp.float32)).astype(jnp.float32)
    tops = jnp.zeros_like(logits)
    for k in range(IMGS):
        here = rows == k
        top = jnp.max(jnp.where(here, logits, -1e30), 0, keepdims=True)
        tops = jnp.where(here, top, tops)
    exponent = jnp.exp(logits - tops)
    share = exponent / full_dot(member, full_dot(member_rows, exponent))
    spread_share = full_dot_last(share, marks)
    dead = (jnp.sum(member_rows, 1, keepdims=True) == 0.0).astype(jnp.float32)
    pooled = full_dot(member_rows, spread_share * final) + dead * jnp.mean(
        final, 0, keepdims=True
    )
    return (unit, scale, final, marks, member, member_rows, share, spread_share, dead, pooled)


def unit_scale(value):
    return lax.rsqrt(jnp.mean(value * value, -1, keepdims=True) + 1e-06)


def pool_kernel(base, state, gains, segment, matrix, pooled_low, embedded, image_low):
    parts, length = segment.shape
    for b in range(parts):
        pooled = pool_sequence(
            state[b * length : (b + 1) * length], gains[base : base + 3], slot_marks(segment, b)
        )[-1]
        pooled_low[b] = pooled.astype(jnp.bfloat16)
        value = jnp.dot(
            pooled.astype(jnp.bfloat16), matrix[...], preferred_element_type=jnp.float32
        )
        embedded[b] = value
        image_low[b] = (value * unit_scale(value) * (1.0 / math.sqrt(D))).astype(jnp.bfloat16)


def pool_forward(state, gains, base, segment, matrix):
    parts = segment.shape[0]
    shape = (parts, IMGS, D)
    return pl.pallas_call(
        functools.partial(pool_kernel, base),
        out_shape=[
            jax.ShapeDtypeStruct(shape, jnp.bfloat16),
            jax.ShapeDtypeStruct(shape, jnp.float32),
            jax.ShapeDtypeStruct(shape, jnp.bfloat16),
        ],
        in_specs=whole("vvvv"),
        out_specs=whole("vvv"),
        compiler_params=pltpu.CompilerParams(vmem_limit_bytes=VMEM_LIMIT),
        name="pool_forward",
    )(state, gains, segment, matrix)


def contrast_kernel(
    base,
    me,
    images,
    texts,
    alive_columns,
    alive_rows,
    own_images,
    own_live,
    state,
    all_gains,
    segment,
    matrix,
    pooled_low,
    embedded,
    loss,
    grad,
    grad_matrix,
    gain_out,
    text_side,
):
    parts, length = segment.shape
    gains = all_gains[base : base + 3]
    everyone = images.shape[1]
    count = jnp.zeros((1, 1), jnp.float32)
    for b in range(parts):
        count = count + jnp.sum(alive_columns[b], -1, keepdims=True)
    factor = 1.0 / (2.0 * count)
    first = me[0] * IMGS

    def rows_of(scores, alive, live, start):
        masked = jnp.where(alive > 0, scores, -1e30)
        top = jnp.max(masked, -1, keepdims=True)
        exponent = jnp.exp(masked - top)
        total = jnp.sum(exponent, -1, keepdims=True)
        line = lax.broadcasted_iota(jnp.int32, scores.shape, 0) + start
        column = lax.broadcasted_iota(jnp.int32, scores.shape, 1)
        target = (line == column).astype(jnp.float32)
        diagonal = jnp.sum(scores * target, -1, keepdims=True)
        term = (top + jnp.log(total) - diagonal) * live
        delta = (exponent * (1.0 / total) - target) * live
        return (term, (delta * factor * LOGIT_SCALE).astype(jnp.bfloat16))

    loss[...] = jnp.zeros_like(loss)
    grad_sum = jnp.zeros((D, D), jnp.float32)
    gain_out[...] = jnp.zeros_like(gain_out)
    for b in range(parts):
        forward = LOGIT_SCALE * contract_last(own_images[b], texts[b])
        term, forward_low = rows_of(forward, alive_columns[b], own_live[b], first)
        loss[...] += jnp.sum(term, 0, keepdims=True) * factor
        text_side[...] = jnp.zeros_like(text_side)

        @pl.loop(0, everyone // TOKENS)
        def _(t):
            part = tile_of(t, TOKENS)
            backward = LOGIT_SCALE * contract_last(texts[b, part], images[b])
            term, backward_low = rows_of(
                backward, alive_columns[b], alive_rows[b, part], t * TOKENS
            )
            line = lax.broadcasted_iota(jnp.int32, term.shape, 0) + t * TOKENS
            here = jnp.logical_and(line >= first, line < first + IMGS)
            loss[...] += jnp.sum(jnp.where(here, term, 0.0), 0, keepdims=True) * factor
            text_side[...] += contract_first(backward_low, texts[b, part])

        image_grad = jnp.dot(forward_low, texts[b], preferred_element_type=jnp.float32)
        image_grad = image_grad + text_side[pl.ds(pl.multiple_of(first, IMGS), IMGS)]
        value = embedded[b]
        scale = unit_scale(value)
        embed_low = (
            (
                image_grad * scale
                - value * (scale * scale * scale) * jnp.mean(value * image_grad, -1, keepdims=True)
            )
            * (1.0 / math.sqrt(D))
        ).astype(jnp.bfloat16)
        grad_sum = grad_sum + contract_first(pooled_low[b], embed_low)
        pooled_grad = contract_last(embed_low, matrix[...])
        unit, norm_scale, final, marks, member, member_rows, share, spread_share, dead, _ = (
            pool_sequence(
                state[b * length : (b + 1) * length], gains, slot_marks(segment, b)
            )
        )
        token_grad = full_dot(member, pooled_grad)
        share_grad = full_dot(final * token_grad, marks)
        inside = full_dot(member, full_dot(member_rows, share * share_grad))
        logit_grad = share * (share_grad - inside) * (1.0 / math.sqrt(HD))
        spread_logit = full_dot_last(logit_grad, marks)
        final_grad = (
            spread_share * token_grad
            + spread_logit * gains[2:3]
            + jnp.sum(dead * pooled_grad, 0, keepdims=True) * (1.0 / length)
        )
        gain_out[0:1] += jnp.sum(final_grad * unit, 0, keepdims=True)
        gain_out[1:2] += jnp.sum(final_grad, 0, keepdims=True)
        gain_out[2:3] += jnp.sum(spread_logit * final, 0, keepdims=True)
        delta = final_grad * gains[0:1]
        delta = delta - jnp.mean(delta, -1, keepdims=True) - unit * jnp.mean(
            delta * unit, -1, keepdims=True
        )
        grad[b * length : (b + 1) * length] = delta * norm_scale
    grad_matrix[...] = grad_sum.astype(jnp.bfloat16)


def contrast(me, images, texts, alive, own_images, live, state, gains, base, segment, matrix, pooled_low, embedded):
    parts, everyone = alive.shape
    loss, grad, grad_matrix, gain_grads = pl.pallas_call(
        functools.partial(contrast_kernel, base),
        out_shape=[
            jax.ShapeDtypeStruct((8, 128), jnp.float32),
            jax.ShapeDtypeStruct(state.shape, jnp.float32),
            jax.ShapeDtypeStruct((D, D), jnp.bfloat16),
            jax.ShapeDtypeStruct((8, D), jnp.float32),
        ],
        in_specs=[pl.BlockSpec(memory_space=pltpu.SMEM)] + whole("vvvvvvvvvvvv"),
        out_specs=whole("vvvv"),
        scratch_shapes=[pltpu.VMEM((everyone, D), jnp.float32)],
        compiler_params=pltpu.CompilerParams(vmem_limit_bytes=VMEM_LIMIT),
        name="contrast",
    )(
        me.reshape(1),
        images,
        texts,
        alive[:, None, :],
        alive[:, :, None],
        own_images,
        live[:, :, None],
        state,
        gains,
        segment,
        matrix,
        pooled_low,
        embedded,
    )
    return (loss[0, 0], grad, grad_matrix, gain_grads[:3])


def muon_groups():
    found = [(0, 1), (1, 1)]
    for index in range(LAYERS):
        base = 2 + 12 * index
        found = found + [(base, 3), (base + 3, 1), (base + 4, 4), (base + 8, 4)]
    return found


def lane_plan(lanes):
    plan = [[] for _ in range(lanes)]
    for start, number in sorted(muon_groups(), key=lambda group: -group[1]):
        lane = min(range(lanes), key=lambda i: (sum(n for _, n in plan[i]), len(plan[i]), i))
        plan[lane].append((start, number))
    plan.sort(key=lambda entry: (-entry[0][1] if entry else 0))
    if lanes == 8:
        plan = [plan[i] for i in (0, 1, 2, 3, 4, 6, 5, 7)]
    depth = max(len(entry) for entry in plan)
    widths = [
        max([entry[slot][1] for entry in plan if slot < len(entry)]) for slot in range(depth)
    ]
    return (plan, widths)


def lane_blocks(plan):
    rows = [[start + i for start, number in entry for i in range(number)] for entry in plan]
    most = max(len(row) for row in rows)
    return np.array([row + [-1] * (most - len(row)) for row in rows], np.int32)


def lane_tables(plan, widths):
    index = np.zeros((len(plan), sum(widths)), np.int32)
    mask = np.zeros((len(plan), sum(widths)), np.float32)
    number = np.ones((len(plan), sum(widths)), np.float32)
    home = {}
    for lane, entry in enumerate(plan):
        first = 0
        for slot, width in enumerate(widths):
            if slot < len(entry):
                start, count = entry[slot]
                for place in range(count):
                    index[lane, first + place] = start + place
                    mask[lane, first + place] = 1.0
                    number[lane, first + place] = count
                    home[start + place] = (lane, first + place)
            first += width
    return (index, mask, number, home)


def orthogonal_factor(gram):
    size = jnp.sqrt(jnp.trace(gram)) + 1e-07
    state = gram / (size * size)
    total = None
    for turn in range(NS_ITERS):
        low = rounded(state)
        change = COEF_B * state + COEF_C * jnp.dot(low, low, preferred_element_type=jnp.float32)
        change_low = rounded(change)
        if total is None:
            total = COEF_A * jnp.eye(D, dtype=jnp.float32) + change
        else:
            total = COEF_A * total + jnp.dot(
                rounded(total), change_low, preferred_element_type=jnp.float32
            )
        if turn < NS_ITERS - 1:
            for _ in range(2):
                state = COEF_A * state + jnp.dot(
                    rounded(state), change_low, preferred_element_type=jnp.float32
                )
    return total / size


def per_device(
    patches, grid, segments, text_ids, table, weights, momenta, gains, gains_m, gains_v, step
):
    fin = 6 * LAYERS
    base = fin + 3
    lanes = lax.axis_size("dp")
    slots = jnp.arange(IMGS, dtype=jnp.int32)
    live = jnp.any(segments[:, 0, None, :] == slots[None, :, None], -1).astype(jnp.float32)
    depth = lax.axis_size("fsdp")
    captions = MB * IMGS
    tokens = text_ids.shape[3]
    fast = depth == 4 and lanes == 8
    early = [(0, 1), (2, 3), (5, 1), (6, 4), (10, 4), (1, 1)]
    later = []
    for index in range(1, LAYERS):
        start = 2 + 12 * index
        early = early + [(start, 3), (start + 3, 1)]
        later = later + [(start + 4, 4), (start + 8, 4)]
    later_own = jnp.concatenate([weights[a : a + n] for a, n in later], 0)
    if fast:
        eighth = weights.shape[1] // lanes
        later_own = lax.dynamic_slice_in_dim(later_own, lax.axis_index("dp") * eighth, eighth, 1)
    later_blocks = gather_later(rounded(later_own))
    if fast:
        half = tokens // 2
        own_ids = jnp.transpose(text_ids.reshape(captions, 2, half), (2, 1, 0)).reshape(half, -1)
        place = jnp.arange(depth * 2 * captions, dtype=jnp.int32) // (2 * captions)
        own_ids = jnp.where(
            place[None] == lax.axis_index("fsdp"), jnp.tile(own_ids, (1, depth)), 0
        )
        (stem, *first_blocks), texts = fetch(
            weights, early, own_ids, table, captions, tokens, 1
        )
    else:
        stem, *first_blocks = [
            lax.all_gather(rounded(weights[a : a + n]), "fsdp", axis=1, tiled=True)
            for a, n in early
        ]
        ids = lax.all_gather(text_ids.reshape(captions, tokens), "fsdp", axis=0)
        picked = ids.reshape(depth * captions, -1) - lax.axis_index("fsdp") * table.shape[0]
        row = jnp.arange(table.shape[0], dtype=jnp.int32)
        hits = jnp.sum((picked[:, :, None] == row[None, None, :]).astype(jnp.int32), 1)
        text_sum = lax.psum_scatter(
            jnp.dot(
                rounded(hits.astype(jnp.float32)), table, preferred_element_type=jnp.float32
            ).reshape(depth, captions, D),
            "fsdp",
            scatter_dimension=0,
        )
        (texts,) = share([rounded(unit_rows(text_sum / tokens))], 7)
    early_blocks = first_blocks[5:]
    pooling_matrix = first_blocks[4][0]
    first_blocks = first_blocks[:4]
    me = lax.axis_index(("dp", "fsdp"))
    segment = segments[:, 0]
    rows_hot, cols_hot = jax.vmap(positions)(grid[:, 0])
    rows_hot = rows_hot.reshape(-1, POS)
    cols_hot = cols_hot.reshape(-1, POS)
    patch_low = patches.reshape(-1, D)
    state = product(patch_low, stem[0], "sd,rd->sr")
    state = state + jnp.dot(rows_hot, gains[base : base + POS], precision=HIGH)
    state = state + jnp.dot(cols_hot, gains[base + POS : base + 2 * POS], precision=HIGH)
    saved = []
    for index in range(LAYERS):
        if index == 0:
            blocks = [(array, 0, array.shape[0]) for array in first_blocks]
        else:
            first = 8 * index - 8
            blocks = [
                (array, 0, array.shape[0]) for array in early_blocks[2 * index - 2 : 2 * index]
            ] + [(later_blocks, first, 4), (later_blocks, first + 4, 4)]
        state, kept = layer_forward(state, blocks, gains, 6 * index, segment)
        saved.append((kept, blocks))
    pooled_low, embedded, image_low = pool_forward(state, gains, fin, segment, pooling_matrix)
    own_flags = jnp.broadcast_to(live.reshape(captions, 1), (captions, 128)).astype(jnp.bfloat16)
    images, flags = share([image_low.reshape(captions, D), own_flags], 8)
    flags = flags.reshape(-1, MB, IMGS, 128)[..., 0].astype(jnp.float32)
    images, texts = [
        jnp.moveaxis(value.reshape(-1, MB, IMGS, D), 0, 1).reshape(MB, -1, D)
        for value in (images, texts)
    ]
    loss_part, grad, grad_pool, pool_gain_grads = contrast(
        me,
        images,
        texts,
        jnp.moveaxis(flags, 0, 1).reshape(MB, -1),
        image_low,
        live,
        state,
        gains,
        fin,
        segment,
        pooling_matrix,
        pooled_low,
        embedded,
    )
    gain_parts = [None] * LAYERS
    block_grads = [None] * LAYERS
    slices = [None] * LAYERS
    for index in reversed(range(LAYERS)):
        kept, blocks = saved[index]
        grad, block_grads[index], gain_parts[index] = layer_backward(
            grad, kept, blocks, gains, 6 * index, segment
        )
        if index == 1:
            block_grads[index].append(grad_pool)
        if fast and index > 0:
            (slices[index],) = reduce_grads(block_grads[index], 4 + index)
    grad_low = rounded(grad)
    grad_patch = rounded(product(grad_low, patch_low, "sr,sd->rd"))
    block_grads[0].append(grad_patch)
    grad_rows = jnp.dot(rows_hot.T, grad, precision=HIGH)
    grad_cols = jnp.dot(cols_hot.T, grad, precision=HIGH)
    gains_grad = jnp.concatenate(
        gain_parts
        + [pool_gain_grads, grad_rows, grad_cols],
        0,
    )
    plan, widths = lane_plan(lanes)
    index, mask, number, home = lane_tables(plan, widths)
    lane = lax.axis_index("dp")
    scale = np.ones((weights.shape[0],), np.float32)
    for start, count_blocks in muon_groups():
        scale[start : start + count_blocks] = MUON_RATE * math.sqrt(count_blocks)
    if fast:
        width = 256
        small = jnp.concatenate([gains_grad.reshape(-1), loss_part[None]])
        small = jnp.pad(small, (0, lanes * depth * 8 * width - small.shape[0]))
        blocks_here = lane_blocks(plan)
        origins = [(0, 12), (1, 12)] + [
            (index, block) for index in range(LAYERS) for block in range(12)
        ]
        slices[0], _, small, stats, mine, slices = reduce_grads(
            block_grads[0],
            4,
            small.reshape(lanes * depth, 8, width),
            (blocks_here, origins),
            slices[1],
        )
        flat = small.reshape(-1)
        gains_grad, loss = (flat[: gains.size].reshape(gains.shape), flat[gains.size])
        squares = jnp.sum(stats[:, :, 0, 0])
        norm = jnp.sqrt(squares + jnp.sum(gains_grad * gains_grad))
        clip = jnp.minimum(1.0, CLIP_LIMIT / (norm + 1e-06))
        own_momenta = jnp.stack(
            [
                jnp.where(
                    jnp.asarray(blocks_here >= 0)[lane, place],
                    lax.dynamic_index_in_dim(
                        momenta, jnp.maximum(jnp.asarray(blocks_here)[lane, place], 0), 0, False
                    ),
                    0.0,
                )
                for place in range(blocks_here.shape[1])
            ]
        )
        own = MOMENT * own_momenta + clip * mine.reshape(own_momenta.shape).astype(jnp.float32)
        two = jnp.asarray(np.array([len(entry) > 1 for entry in plan], np.int32))[lane]
        own_low = rounded(own)
        gram = product(own_low, own_low, "brd,bre->de")
        gram, all_rows, shard_grads = sum_grams(gram, own_low[:2], slices, 12)
        turned = spread(schulz(two.reshape(1), gram, all_rows, own), 13)
        homes = {
            int(block): (lane_of, place)
            for lane_of, entry in enumerate(blocks_here)
            for place, block in enumerate(entry)
            if block >= 0
        }
        momenta_new, weights_new, weights_low = update(
            homes, scale, clip, momenta, shard_grads.reshape(weights.shape), weights, turned
        )
    else:
        stack = jnp.concatenate(
            [block_grads[index].pop().reshape(1, D, D) for index in range(LAYERS)]
            + [value.reshape(-1, D, D) for values in block_grads for value in values],
            0,
        )
        shard_grads = lax.psum(
            lax.psum_scatter(stack, "fsdp", scatter_dimension=1, tiled=True), "dp"
        ).astype(jnp.float32)
        gains_grad, loss = lax.psum((gains_grad, loss_part), ("dp", "fsdp"))
        squares = lax.psum(jnp.sum(shard_grads * shard_grads), "fsdp")
        norm = jnp.sqrt(squares + jnp.sum(gains_grad * gains_grad))
        clip = jnp.minimum(1.0, CLIP_LIMIT / (norm + 1e-06))
        momenta_new = MOMENT * momenta + clip * shard_grads
        own = jnp.stack(
            [
                lax.dynamic_index_in_dim(momenta_new, jnp.asarray(index)[lane, place], 0, False)
                * jnp.asarray(mask)[lane, place]
                for place in range(index.shape[1])
            ]
        )
        own_low = rounded(own)
        bounds = np.cumsum([0] + widths)
        grams = jnp.stack(
            [
                product(own_low[a:b], own_low[a:b], "brd,bre->de")
                for a, b in zip(bounds[:-1], bounds[1:])
            ]
        )
        grams = lax.psum(grams, "fsdp")
        turned = jnp.concatenate(
            [
                product(
                    own_low[bounds[slot] : bounds[slot + 1]],
                    rounded(orthogonal_factor(grams[slot])),
                    "brd,de->bre",
                )
                for slot in range(len(widths))
            ],
            0,
        )
        spread_rows = lax.all_gather(rounded(turned), "dp", axis=0)
        current = jnp.stack(
            [spread_rows[home[block][0], home[block][1]] for block in range(weights.shape[0])]
        ).astype(jnp.float32)
        weights_new = weights * (1.0 - MUON_RATE * MUON_DECAY) - jnp.asarray(scale)[:, None, None] * current
        weights_low = rounded(weights_new)
    grad_small = clip * gains_grad
    moment_one = BETA_ONE * gains_m + (1.0 - BETA_ONE) * grad_small
    moment_two = BETA_TWO * gains_v + (1.0 - BETA_TWO) * grad_small * grad_small
    count_steps = step[0].astype(jnp.float32)
    corrected_one = moment_one / (1.0 - jnp.power(BETA_ONE, count_steps))
    corrected_two = moment_two / (1.0 - jnp.power(BETA_TWO, count_steps))
    gains_new = gains - ADAM_RATE * (
        corrected_one / (jnp.sqrt(corrected_two) + ADAM_EPS) + ADAM_DECAY * gains
    )
    shift_grad = grad_small[fin + 1]
    return (
        loss,
        norm,
        weights_new,
        weights_low,
        momenta_new,
        gains_new,
        moment_one,
        moment_two,
        shift_grad,
    )


def solution(mesh):
    placed = (
        P(None, ("dp", "fsdp"), None, None),
        P(None, ("dp", "fsdp"), None, None),
        P(None, ("dp", "fsdp"), None),
        P(None, ("dp", "fsdp"), None, None),
        P("fsdp", None),
        P(None, "fsdp", None),
        P(None, "fsdp", None),
        P(),
        P(),
        P(),
        P(),
    )
    return jax.shard_map(
        per_device,
        mesh=mesh,
        in_specs=placed,
        out_specs=(
            P(),
            P(),
            P(None, "fsdp", None),
            P(None, "fsdp", None),
            P(None, "fsdp", None),
            P(),
            P(),
            P(),
            P(),
        ),
        check_vma=False,
    )
```
